32 devices in a mesh: fsdp: 4 (over z), cp: 2 (over x), tp: 4 (over y, core).
Axes of the slice: x: 2, y: 2, z: 4, core: 2. Of those that a mesh axis runs over, the one named last changes fastest.
Arguments:
- tokens: bfloat16 [8, 1024, 2304], P('fsdp', ('cp', 'tp')), may hold values from -6 to 6
- seq_lengths: int32 [8], P('fsdp'), may hold values from 256 to 1024, as said below
- attention_gain: bfloat16 [2304], replicated, may hold values from 0.5 to 1.5
- query_weight: bfloat16 [2304, 2304], P(('fsdp', 'cp'), 'tp'), may hold values from -0.1875 to 0.1875
- key_weight: bfloat16 [2304, 2304], P(('fsdp', 'cp'), 'tp'), may hold values from -0.1875 to 0.1875
- value_weight: bfloat16 [2304, 2304], P(('fsdp', 'cp'), 'tp'), may hold values from -0.125 to 0.125
- out_weight: bfloat16 [2304, 2304], P('tp', ('fsdp', 'cp')), may hold values from -3 to 3
- feedforward_gain: bfloat16 [2304], replicated, may hold values from 0.5 to 1.5
- gate_weight: bfloat16 [2304, 5760], P(('fsdp', 'cp'), 'tp'), may hold values from -0.125 to 0.125
- up_weight: bfloat16 [2304, 5760], P(('fsdp', 'cp'), 'tp'), may hold values from -0.125 to 0.125
- down_weight: bfloat16 [5760, 2304], P('tp', ('fsdp', 'cp')), may hold values from -0.4375 to 0.4375
- cotangent: bfloat16 [8, 1024, 2304], P('fsdp', ('cp', 'tp')), may hold values from -6 to 6
Outputs:
- output: bfloat16 [8, 1024, 2304], P('fsdp', ('cp', 'tp'))
- grad_tokens: bfloat16 [8, 1024, 2304], P('fsdp', ('cp', 'tp'))
- grad_query_weight: float32 [2304, 2304], P(('fsdp', 'cp'), 'tp')
- grad_key_weight: float32 [2304, 2304], P(('fsdp', 'cp'), 'tp')
- grad_value_weight: float32 [2304, 2304], P(('fsdp', 'cp'), 'tp')
- grad_out_weight: float32 [2304, 2304], P('tp', ('fsdp', 'cp'))
- grad_attention_gain: float32 [2304], replicated
- grad_gate_weight: float32 [2304, 5760], P(('fsdp', 'cp'), 'tp')
- grad_up_weight: float32 [2304, 5760], P(('fsdp', 'cp'), 'tp')
- grad_down_weight: float32 [5760, 2304], P('tp', ('fsdp', 'cp'))
- grad_feedforward_gain: float32 [2304], replicated
The draws below stay inside these ranges and needn't reach their ends.
Inputs may be any that keep to these rules, and one draw needn't show every extreme that they name: `seq_lengths`: real tokens of each sequence; positions from this count on are padding. In every draw one sequence has exactly 1024 and another exactly 256.
All inputs are finite; a program needn't handle non-finite values.
Results may differ from the reference program's by a relative error of at most 0.015.
Values may be sent and summed in bfloat16 or wider, within the bound.
A program may use at most 320 MiB of HBM per device.

```python
import math
import jax
import jax.numpy as jnp
from jax import lax

D = 2304
HEADS = 36
HD = 64
FF = 5760
SEQ = 1024
LEN_MIN = 256
SLOTS = 8


def draw_seq_lengths(key, part):
    first_key = jax.random.fold_in(key, 11)
    second_key = jax.random.fold_in(key, 12)
    third_key = jax.random.fold_in(key, 13)
    counts = jax.random.randint(first_key, (SLOTS,), LEN_MIN, SEQ + 1)
    longest = jax.random.randint(second_key, (), 0, SLOTS)
    shortest = (longest + 1 + jax.random.randint(third_key, (), 0, SLOTS - 1)) % SLOTS
    slot_index = jnp.arange(SLOTS, dtype=jnp.int32)
    counts = jnp.where(slot_index == longest, SEQ, counts)
    counts = jnp.where(slot_index == shortest, LEN_MIN, counts)
    return counts.astype(jnp.int32)


def level_of(key, shape, split, low, largest):
    def one(position, parts):
        draws = jax.random.uniform(jax.random.fold_in(jax.random.fold_in(key, 6), position), (parts,), jnp.float32, low / len(split), largest / len(split))
        return jnp.repeat(jnp.exp(draws), shape[position] // parts).reshape((-1,) + (1,) * (len(shape) - position - 1))

    factor_of = one(*split[0])
    for cut in split[1:]:
        factor_of = factor_of * one(*cut)
    return factor_of


def centred(rng, dims, spread, most, split=(), kind=jnp.bfloat16):
    entries = jax.random.normal(rng, dims, jnp.float32) * spread
    if len(split) > 0:
        entries = level_of(rng, dims, split, -0.22, 0.18) * entries
    return jnp.clip(entries, min=-most, max=most).astype(kind)


def setup_inputs(seed: int = 0) -> dict:
    key_list = jax.random.split(jax.random.key(seed), 13)
    tokens = centred(key_list[0], (SLOTS, SEQ, D), 1.0, 6.0, ((0, 4), (1, 8)))
    seq_lengths = draw_seq_lengths(jax.random.fold_in(key_list[12], 71), 0)
    attention_gain = jnp.clip(1.0 + 0.1 * jax.random.normal(key_list[2], (D,), jnp.float32), 0.5, 1.5).astype(jnp.bfloat16)
    query_weight = centred(key_list[3], (D, D), (D // 2) ** -0.5, 0.1875, ((0, 8), (1, 4)))
    key_weight = centred(key_list[4], (D, D), (D // 2) ** -0.5, 0.1875, ((0, 8), (1, 4)))
    value_weight = centred(key_list[5], (D, D), D ** -0.5, 0.125, ((0, 8), (1, 4)))
    out_weight = centred(key_list[6], (D, D), (max(D // 512, 1)) ** -0.5, 3.0, ((0, 4), (1, 8)))
    feedforward_gain = jnp.clip(1.0 + 0.1 * jax.random.normal(key_list[7], (D,), jnp.float32), 0.5, 1.5).astype(jnp.bfloat16)
    gate_weight = centred(key_list[8], (D, FF), D ** -0.5, 0.125, ((0, 8), (1, 4)))
    up_weight = centred(key_list[9], (D, FF), D ** -0.5, 0.125, ((0, 8), (1, 4)))
    down_weight = centred(key_list[10], (FF, D), (max(FF // 32, 1)) ** -0.5, 0.4375, ((0, 4), (1, 8)))
    cotangent = centred(key_list[11], (SLOTS, SEQ, D), 1.0, 6.0, ((0, 4), (1, 8)))
    return dict(tokens=tokens, seq_lengths=seq_lengths, attention_gain=attention_gain, query_weight=query_weight, key_weight=key_weight, value_weight=value_weight, out_weight=out_weight, feedforward_gain=feedforward_gain, gate_weight=gate_weight, up_weight=up_weight, down_weight=down_weight, cotangent=cotangent)


EPSILON = 1e-05
BRANCH = 1.4 / math.sqrt(40.0)
HIGHEST = lax.Precision.HIGHEST

@jax.custom_vjp
def low(v):
    return lax.optimization_barrier(v.astype(jnp.bfloat16)).astype(jnp.float32)

@jax.custom_vjp
def low_back(v):
    return v

def low_keep(v):
    return (low(v), None)

def low_pass(kept, grad):
    return (grad,)

def back_keep(v):
    return (v, None)

def back_low(kept, grad):
    return (low(grad),)
low.defvjp(low_keep, low_pass)
low_back.defvjp(back_keep, back_low)

def dense(left, right):
    return jnp.dot(left, right, precision=HIGHEST)

def normalize(values):
    return values * lax.rsqrt(lax.optimization_barrier(jnp.mean(values * values, axis=-1, keepdims=True)) + EPSILON)

def angles(places):
    frequency = jnp.power(10000.0, -2.0 * jnp.arange(HD // 2, dtype=jnp.float32) / HD)
    phase_angle = places[:, None] * frequency[None, :]
    return (jnp.cos(phase_angle)[:, None, :], jnp.sin(phase_angle)[:, None, :])

def rotate(values, cosine_table, sine_table):
    half_dim = values.shape[-1] // 2
    first = values[..., :half_dim]
    second = values[..., half_dim:]
    return jnp.concatenate([first * cosine_table - second * sine_table, second * cosine_table + first * sine_table], axis=-1)

def softmax_rows(scores):
    row_top = lax.optimization_barrier(jnp.max(scores, axis=-1, keepdims=True))
    exponent = jnp.exp(scores - row_top)
    return exponent / lax.optimization_barrier(jnp.sum(exponent, axis=-1, keepdims=True))

def silu_product(gate_pre, up_pre):
    return gate_pre / (1.0 + jnp.exp(-gate_pre)) * up_pre

def block_forward(inputs, attention_gain, query_weight, key_weight, value_weight, out_weight, feedforward_gain, gate_weight, up_weight, down_weight, length):
    row_count = inputs.shape[0]
    positions = jnp.arange(row_count, dtype=jnp.int32)
    cosine_table, sine_table = angles(positions.astype(jnp.float32))
    normed_one = low(normalize(inputs) * attention_gain)
    queries = low(rotate(low_back(dense(normed_one, query_weight)).reshape(row_count, HEADS, HD), cosine_table, sine_table))
    keys = low(rotate(low_back(dense(normed_one, key_weight)).reshape(row_count, HEADS, HD), cosine_table, sine_table))
    values = low(low_back(dense(normed_one, value_weight))).reshape(row_count, HEADS, HD)
    scores = low_back(jnp.einsum('qhd,khd->hqk', queries, keys, precision=HIGHEST) * (1.0 / math.sqrt(HD)))
    allowed = (positions[None, :] <= positions[:, None]) & (positions[None, :] < length)
    scores = jnp.where(allowed[None], scores, -1e+30)
    probabilities = softmax_rows(scores)
    context = low(low_back(jnp.einsum('hqk,khd->qhd', low(probabilities), values, precision=HIGHEST))).reshape(row_count, D)
    attention = low_back(dense(context, out_weight))
    middle = inputs + BRANCH * attention
    normed_two = low(normalize(middle) * feedforward_gain)
    gate_pre = low_back(dense(normed_two, gate_weight))
    up_pre = low_back(dense(normed_two, up_weight))
    hidden = low(silu_product(gate_pre, up_pre))
    return middle + BRANCH * low_back(dense(hidden, down_weight))

def reference(tokens, seq_lengths, attention_gain, query_weight, key_weight, value_weight, out_weight, feedforward_gain, gate_weight, up_weight, down_weight, cotangent):
    params = tuple((matrix.astype(jnp.float32) for matrix in (attention_gain, query_weight, key_weight, value_weight, out_weight, feedforward_gain, gate_weight, up_weight, down_weight)))

    def per_slot(totals, slot_data):
        inputs, length, upstream = slot_data

        def forward(inputs_exact, *weights):
            return block_forward(inputs_exact, *weights, length)
        result, pullback = jax.vjp(forward, inputs.astype(jnp.float32), *params)
        gradients = pullback(upstream.astype(jnp.float32))
        new_totals = tuple((earlier + later for earlier, later in zip(totals, gradients[1:])))
        return (new_totals, (result.astype(jnp.bfloat16), gradients[0].astype(jnp.bfloat16)))
    initial = tuple((jnp.zeros(matrix.shape, jnp.float32) for matrix in params))
    totals, stacked = lax.scan(per_slot, initial, (tokens, seq_lengths, cotangent))
    return (stacked[0], stacked[1], totals[1], totals[2], totals[3], totals[4], totals[0], totals[6], totals[7], totals[8], totals[5])
```

```python
import functools
import math

import jax
import jax.numpy as jnp
import numpy as np
from jax import lax
from jax.experimental import pallas as pl
from jax.experimental.pallas import tpu as pltpu
from jax.sharding import PartitionSpec as P

HD = 64
EPSILON = 1e-05
BRANCH = 1.4 / math.sqrt(40.0)
BF = jnp.bfloat16
F32 = jnp.float32
TILE = 128
QUERY_ROWS = 256


def turned(values, cosine, sine):
    lane = lax.broadcasted_iota(jnp.int32, values.shape, 1)
    partner = jnp.where(
        lane % HD < HD // 2,
        pltpu.roll(values, TILE - HD // 2, 1),
        pltpu.roll(values, HD // 2, 1),
    )
    return values * cosine + partner * sine


def row_blocks(seq, sets, local):
    lanes = seq // sets // local
    return [
        ((t * sets + h) * local, (h * lanes + t) * local)
        for t in range(lanes)
        for h in range(sets)
    ]


def key_mask(length, first, rows, columns):
    place = first + lax.broadcasted_iota(jnp.int32, (rows, columns), 0)
    return place < length


def scores_of(keys, queries, length, first_query):
    raw = lax.dot_general(keys, queries, (((1,), (1,)), ((), ())), preferred_element_type=F32)
    key_place = lax.broadcasted_iota(jnp.int32, raw.shape, 0)
    query_place = first_query + lax.broadcasted_iota(jnp.int32, raw.shape, 1)
    return jnp.where((key_place <= query_place) & (key_place < length), raw, -1e30)


def attention_kernel(
    blocks, length_ref, projected, cosine, sine, context, q_heads, k_heads, v_heads, level, kept
):
    heads, seq, _ = q_heads.shape
    local = seq // len(blocks)
    length = length_ref[0]
    for gathered, ordered in blocks:
        source, target = pl.ds(gathered, local), pl.ds(ordered, local)
        for tile in range(-(-3 * heads // 2)):
            width = min(TILE, 3 * heads * HD - tile * TILE)
            values = projected[source, tile * TILE : tile * TILE + width]
            if tile * 2 < 2 * heads:
                values = turned(values, cosine[target, :], sine[target, :])
            for which in range(width // HD):
                index = tile * 2 + which
                piece = values[:, which * HD : (which + 1) * HD]
                if index < heads:
                    q_heads[index, target, :] = (piece * (1.0 / math.sqrt(HD))).astype(BF)
                elif index < 2 * heads:
                    k_heads[index - heads, target, :] = piece.astype(BF)
                else:
                    v_heads[index - 2 * heads, target, :] = piece.astype(BF)

    def one_head(head, carry):
        for first in range(0, seq, QUERY_ROWS):
            most = first + QUERY_ROWS
            queries = q_heads[head, first:most, :]
            keys = k_heads[head, :most, :]
            values = v_heads[head, :most, :]
            scores = scores_of(keys, queries, length, first)
            top = jnp.max(scores, axis=0, keepdims=True)
            exponent = jnp.exp(scores - top)
            total = jnp.sum(exponent, axis=0, keepdims=True)
            probabilities = (exponent * (1.0 / total)).astype(BF)
            level[head, :, first:most] = top + jnp.log(total)
            mixed = lax.dot_general(
                values, probabilities, (((0,), (0,)), ((), ())), preferred_element_type=F32
            )
            kept[head, first:most, :] = mixed.T.astype(BF)
        return carry

    lax.fori_loop(0, heads, one_head, 0)
    for gathered, ordered in blocks:
        source, target = pl.ds(ordered, local), pl.ds(gathered, local)
        for head in range(0, heads, 2):
            parts = [kept[index, source, :] for index in range(head, min(head + 2, heads))]
            joined = parts[0] if len(parts) == 1 else jnp.concatenate(parts, axis=1)
            context[target, head * HD : head * HD + joined.shape[1]] = joined


def attention(blocks, heads, length, projected, cosine, sine):
    seq = projected.shape[0]
    per_head = jax.ShapeDtypeStruct((heads, seq, HD), BF)
    vmem = pl.BlockSpec(memory_space=pltpu.VMEM)
    return pl.pallas_call(
        functools.partial(attention_kernel, blocks),
        out_shape=(
            jax.ShapeDtypeStruct((seq, heads * HD), BF),
            per_head,
            per_head,
            per_head,
            jax.ShapeDtypeStruct((heads, 1, seq), F32),
        ),
        in_specs=[pl.BlockSpec(memory_space=pltpu.SMEM), vmem, vmem, vmem],
        out_specs=(vmem,) * 5,
        scratch_shapes=[pltpu.VMEM((heads, seq, HD), BF)],
        compiler_params=pltpu.CompilerParams(vmem_limit_bytes=48 << 20),
        cost_estimate=pl.CostEstimate(
            flops=4 * heads * seq * seq * HD, transcendentals=heads * seq * seq, bytes_accessed=20 << 20
        ),
    )(length, projected, cosine, sine)


def attention_back_kernel(
    blocks, length_ref, grad_context, q_heads, k_heads, v_heads, level, cosine, sine,
    grad_projected, g_heads, dq, dk, dv,
):
    heads, seq, _ = q_heads.shape
    local = seq // len(blocks)
    length = length_ref[0]
    for gathered, ordered in blocks:
        source, target = pl.ds(gathered, local), pl.ds(ordered, local)
        for head in range(heads):
            g_heads[head, target, :] = grad_context[source, head * HD : (head + 1) * HD]

    def one_head(head, carry):
        keys_turned = k_heads[head].T
        for first in reversed(range(0, seq, QUERY_ROWS)):
            most = first + QUERY_ROWS
            queries = q_heads[head, first:most, :]
            upstream = g_heads[head, first:most, :]
            keys = k_heads[head, :most, :]
            values = v_heads[head, :most, :]
            scores = scores_of(keys, queries, length, first)
            probabilities = jnp.exp(scores - level[head, :, first:most])
            grad_probabilities = lax.dot_general(
                values, upstream, (((1,), (1,)), ((), ())), preferred_element_type=F32
            )
            weighted = probabilities * grad_probabilities
            balance = jnp.sum(weighted, axis=0, keepdims=True)
            grad_scores = (weighted - probabilities * balance).astype(BF)
            grad_keys = jnp.dot(grad_scores, queries, preferred_element_type=F32)
            grad_values = jnp.dot(
                probabilities.astype(BF), upstream, preferred_element_type=F32
            )
            if most == seq:
                dk[head, :, :] = grad_keys
                dv[head, :, :] = grad_values
            else:
                dk[head, :most, :] += grad_keys
                dv[head, :most, :] += grad_values
            grad_queries = jnp.dot(
                keys_turned[:, :most], grad_scores, preferred_element_type=F32
            )
            dq[head, first:most, :] = grad_queries.T * (1.0 / math.sqrt(HD))
        return carry

    lax.fori_loop(0, heads, one_head, 0)
    sources = [dq] * heads + [dk] * heads + [dv] * heads
    for gathered, ordered in blocks:
        source, target = pl.ds(ordered, local), pl.ds(gathered, local)
        for tile in range(-(-3 * heads // 2)):
            indices = range(tile * 2, min(tile * 2 + 2, 3 * heads))
            parts = [sources[index][index % heads, source, :] for index in indices]
            joined = parts[0] if len(parts) == 1 else jnp.concatenate(parts, axis=1)
            if tile * 2 < 2 * heads:
                joined = turned(joined, cosine[source, :], -sine[source, :])
            grad_projected[target, tile * TILE : tile * TILE + joined.shape[1]] = joined.astype(BF)


def attention_back(blocks, heads, length, grad_context, q_heads, k_heads, v_heads, level, cosine, sine):
    seq = grad_context.shape[0]
    vmem = pl.BlockSpec(memory_space=pltpu.VMEM)
    return pl.pallas_call(
        functools.partial(attention_back_kernel, blocks),
        out_shape=jax.ShapeDtypeStruct((seq, 3 * heads * HD), BF),
        in_specs=[pl.BlockSpec(memory_space=pltpu.SMEM)] + [vmem] * 7,
        out_specs=vmem,
        scratch_shapes=[
            pltpu.VMEM((heads, seq, HD), BF),
            pltpu.VMEM((heads, seq, HD), F32),
            pltpu.VMEM((heads, seq, HD), F32),
            pltpu.VMEM((heads, seq, HD), F32),
        ],
        compiler_params=pltpu.CompilerParams(vmem_limit_bytes=56 << 20),
        cost_estimate=pl.CostEstimate(
            flops=10 * heads * seq * seq * HD, transcendentals=heads * seq * seq, bytes_accessed=20 << 20
        ),
    )(length, grad_context, q_heads, k_heads, v_heads, level, cosine, sine)


def tables(seq):
    frequency = jnp.power(10000.0, -2.0 * jnp.arange(HD // 2, dtype=F32) / HD)
    angle = jnp.arange(seq, dtype=F32)[:, None] * frequency[None, :]
    cosine, sine = jnp.cos(angle), jnp.sin(angle)
    return jnp.tile(cosine, (1, 4)), jnp.concatenate([-sine, sine, -sine, sine], axis=1)


MESH = pl.DeviceIdType.MESH


def greet(count):
    barrier = pltpu.get_barrier_semaphore()
    z, c, t = lax.axis_index("fsdp"), lax.axis_index("cp"), lax.axis_index("tp")

    def hello(**place):
        pl.semaphore_signal(barrier, inc=1, device_id=place, device_id_type=MESH)

    hello(cp=1 - c)
    hello(tp=t + 1 - 2 * (t % 2))
    hello(tp=(t + 2) % 4)
    pl.when(z > 0)(lambda: hello(fsdp=z - 1))
    pl.when(z < count - 1)(lambda: hello(fsdp=z + 1))
    peers = 3 + jnp.minimum(z, 1) + jnp.minimum(count - 1 - z, 1)
    pl.semaphore_wait(barrier, peers)


class Mail:
    def __init__(self, send, recv):
        self.send, self.recv, self.used, self.open = send, recv, 0, []

    def slot(self):
        self.used += 1
        return self.used - 1

    def copy(self, slot, source, target, **place):
        return pltpu.make_async_remote_copy(
            src_ref=source,
            dst_ref=target,
            send_sem=self.send.at[slot],
            recv_sem=self.recv.at[slot],
            device_id=place,
            device_id_type=MESH,
        )

    def start(self, slot, source, target, when=None, **place):
        made = self.copy(slot, source, target, **place)
        if when is None:
            made.start()
        else:
            pl.when(when)(made.start)
        self.open.append((made, when))

    def arrive(self, slot, target, when=None, **place):
        made = self.copy(slot, target, target, **place)
        if when is None:
            made.wait_recv()
        else:
            pl.when(when)(made.wait_recv)

    def finish(self):
        for made, when in self.open:
            if when is None:
                made.wait_send()
            else:
                pl.when(when)(made.wait_send)


class Line:
    def __init__(self, mail, count, own, at, low=None, high=None):
        self.mail, self.count, self.own, self.at = mail, count, own, at
        self.low, self.high = low, high
        self.z = lax.axis_index("fsdp")
        self.up = [mail.slot() for _ in range(count)]
        self.down = [mail.slot() for _ in range(count)]

    def has_low(self, hop):
        return self.z >= hop

    def has_high(self, hop):
        return self.z <= self.count - 1 - hop

    def send(self, hop):
        z, count, mail = self.z, self.count, self.mail
        low, high = jnp.maximum(z - hop + 1, 0), jnp.minimum(z + hop - 1, count - 1)
        from_low = from_high = self.own
        if hop > 1:
            ready = hop == 2 and self.low is not None
            from_low = self.low if ready else self.at(low)
            from_high = self.high if ready else self.at(high)
        mail.start(
            self.up[hop], from_low, self.at(low),
            when=(z >= hop - 1) & (z < count - 1), fsdp=jnp.minimum(z + 1, count - 1),
        )
        mail.start(
            self.down[hop], from_high, self.at(high),
            when=(z <= count - hop) & (z > 0), fsdp=jnp.maximum(z - 1, 0),
        )

    def arrive(self, hop):
        z, count = self.z, self.count
        self.mail.arrive(
            self.up[hop], self.at(jnp.maximum(z - hop, 0)), when=self.has_low(hop), fsdp=z
        )
        self.mail.arrive(
            self.down[hop], self.at(jnp.minimum(z + hop, count - 1)), when=self.has_high(hop), fsdp=z
        )


class Across:
    def __init__(self, line, own, mine_at, other_at):
        self.line, self.own, self.mine_at, self.other_at = line, own, mine_at, other_at
        self.c = lax.axis_index("cp")
        self.low = [line.mail.slot() for _ in range(line.count)]
        self.high = [line.mail.slot() for _ in range(line.count)]

    def send(self, hop):
        line, mail = self.line, self.line.mail
        z, count, other = line.z, line.count, 1 - self.c
        if hop == 0:
            mail.start(self.low[0], self.own, self.mine_at(z), cp=other)
            return
        low, high = jnp.maximum(z - hop, 0), jnp.minimum(z + hop, count - 1)
        mail.start(self.low[hop], self.mine_at(low), self.mine_at(low), when=line.has_low(hop), cp=other)
        mail.start(self.high[hop], self.mine_at(high), self.mine_at(high), when=line.has_high(hop), cp=other)

    def arrive(self, hop):
        line, mail = self.line, self.line.mail
        z, count, other = line.z, line.count, 1 - self.c
        if hop == 0:
            mail.arrive(self.low[0], self.other_at(z), cp=other)
            return
        low, high = jnp.maximum(z - hop, 0), jnp.minimum(z + hop, count - 1)
        mail.arrive(self.low[hop], self.other_at(low), when=line.has_low(hop), cp=other)
        mail.arrive(self.high[hop], self.other_at(high), when=line.has_high(hop), cp=other)


def first_gather_kernel(
    count, normed, qkv, turned_out, wide, normed_full, qkv_full, out_half, low, high,
    send, recv, local,
):
    z, c, t = lax.axis_index("fsdp"), lax.axis_index("cp"), lax.axis_index("tp")
    beside, yonder = t + 1 - 2 * (t % 2), (t + 2) % 4
    mail = Mail(send, recv)
    greet(count)
    kept = [
        pltpu.make_async_copy(qkv, qkv_full.at[z, c], local.at[0]),
        pltpu.make_async_copy(turned_out, out_half.at[z], local.at[1]),
        pltpu.make_async_copy(normed.at[c], normed_full.at[t, c], local.at[2]),
    ]
    for copy in kept:
        copy.start()

    heads = Line(mail, count, qkv, lambda j: qkv_full.at[j, c])
    heads_across = Across(
        heads, qkv, lambda j: qkv_full.at[j, c], lambda j: qkv_full.at[j, 1 - c]
    )
    outs = Line(mail, count, turned_out, lambda j: out_half.at[j])
    wide_up, wide_down = mail.slot(), mail.slot()
    rows_x = mail.slot()
    rows_y = [mail.slot() for _ in range(2)]
    rows_core = [mail.slot() for _ in range(4)]

    mail.start(rows_x, normed.at[1 - c], normed_full.at[t, c], cp=1 - c)
    heads.send(1)
    heads_across.send(0)
    mail.start(rows_y[0], normed.at[c], normed_full.at[t, c], tp=yonder)
    mail.start(rows_core[0], normed.at[c], normed_full.at[t, c], tp=beside)
    mail.arrive(rows_x, normed_full.at[t, 1 - c], cp=1 - c)
    mail.start(rows_y[1], normed_full.at[t, 1 - c], normed_full.at[t, 1 - c], tp=yonder)
    mail.start(rows_core[1], normed_full.at[t, 1 - c], normed_full.at[t, 1 - c], tp=beside)

    def rows_on(k, half):
        mail.arrive(rows_y[k], normed_full.at[yonder, half], tp=yonder)
        mail.start(
            rows_core[2 + k], normed_full.at[yonder, half], normed_full.at[yonder, half], tp=beside
        )

    for hop in range(1, count):
        heads.arrive(hop)
        if hop + 1 < count:
            heads.send(hop + 1)
        if hop > 1:
            outs.arrive(hop - 1)
        outs.send(hop)
        heads_across.send(hop)
        if hop == 1:
            rows_on(0, c)
            rows_on(1, 1 - c)
    mail.start(wide_up, wide, low, when=z < count - 1, fsdp=jnp.minimum(z + 1, count - 1))
    mail.start(wide_down, wide, high, when=z > 0, fsdp=jnp.maximum(z - 1, 0))
    if count > 1:
        outs.arrive(count - 1)
    for hop in range(count):
        heads_across.arrive(hop)
    mail.arrive(rows_core[0], normed_full.at[beside, c], tp=beside)
    mail.arrive(rows_core[1], normed_full.at[beside, 1 - c], tp=beside)
    far = (beside + 2) % 4
    mail.arrive(rows_core[2], normed_full.at[far, c], tp=beside)
    mail.arrive(rows_core[3], normed_full.at[far, 1 - c], tp=beside)
    mail.arrive(wide_up, low, when=z > 0, fsdp=z)
    mail.arrive(wide_down, high, when=z < count - 1, fsdp=z)
    for copy in kept:
        copy.wait()
    mail.finish()


def first_gather(count, normed, qkv, turned_out, wide):
    slots = 6 * count + 9
    anywhere = pl.BlockSpec(memory_space=pl.ANY)
    share = qkv.shape[0]
    return pl.pallas_call(
        functools.partial(first_gather_kernel, count),
        out_shape=(
            jax.ShapeDtypeStruct((4,) + normed.shape, BF),
            jax.ShapeDtypeStruct((count, 2) + qkv.shape, BF),
            jax.ShapeDtypeStruct((count,) + turned_out.shape, BF),
            jax.ShapeDtypeStruct(wide.shape, BF),
            jax.ShapeDtypeStruct(wide.shape, BF),
        ),
        in_specs=[anywhere] * 4,
        out_specs=(anywhere,) * 5,
        scratch_shapes=[
            pltpu.SemaphoreType.DMA((slots,)),
            pltpu.SemaphoreType.DMA((slots,)),
            pltpu.SemaphoreType.DMA((3,)),
        ],
        compiler_params=pltpu.CompilerParams(collective_id=1, has_side_effects=True),
    )(normed, qkv, turned_out, wide)


def in_pieces(rows, body, size=16):
    lax.fori_loop(0, rows // size, lambda i, carry: (body(pl.ds(i * size, size)), carry)[1], 0)


class Spread:
    def __init__(self, mail, own, at):
        self.mail, self.own, self.at = mail, own, at
        self.c, self.t = lax.axis_index("cp"), lax.axis_index("tp")
        self.beside, self.yonder = self.t + 1 - 2 * (self.t % 2), (self.t + 2) % 4
        self.x = [mail.slot() for _ in range(3)]
        self.y = [mail.slot() for _ in range(3)]
        self.core = {}

    def to_core(self, c_is_own, t_is_own, piece):
        slot = self.core[c_is_own, t_is_own, piece] = self.mail.slot()
        c = self.c if c_is_own else 1 - self.c
        t = self.t if t_is_own else self.yonder
        source = self.own(piece) if c_is_own and t_is_own else self.at(c, t, piece)
        self.mail.start(slot, source, self.at(c, t, piece), tp=self.beside)

    def begin(self, piece):
        c, t = self.c, self.t
        if piece == 0:
            self.mail.start(self.x[0], self.own(0), self.at(c, t, 0), cp=1 - c)
        else:
            self.mail.start(self.y[0], self.own(1), self.at(c, t, 1), tp=self.yonder)
            self.mail.start(self.x[1], self.own(1), self.at(c, t, 1), cp=1 - c)
            self.mail.start(self.y[1], self.own(0), self.at(c, t, 0), tp=self.yonder)
        self.to_core(True, True, piece)

    def turn(self):
        c, t, mail, yonder = self.c, self.t, self.mail, self.yonder
        mail.arrive(self.x[0], self.at(1 - c, t, 0), cp=1 - c)
        mail.start(self.y[2], self.at(1 - c, t, 0), self.at(1 - c, t, 0), tp=yonder)
        self.to_core(False, True, 0)
        mail.arrive(self.y[0], self.at(c, yonder, 1), tp=yonder)
        mail.start(self.x[2], self.at(c, yonder, 1), self.at(c, yonder, 1), cp=1 - c)
        self.to_core(True, False, 1)

    def end(self):
        c, t, mail, yonder = self.c, self.t, self.mail, self.yonder
        mail.arrive(self.x[1], self.at(1 - c, t, 1), cp=1 - c)
        self.to_core(False, True, 1)
        mail.arrive(self.y[1], self.at(c, yonder, 0), tp=yonder)
        self.to_core(True, False, 0)
        mail.arrive(self.x[2], self.at(1 - c, yonder, 1), cp=1 - c)
        self.to_core(False, False, 1)
        mail.arrive(self.y[2], self.at(1 - c, yonder, 0), tp=yonder)
        self.to_core(False, False, 0)
        far = (self.beside + 2) % 4
        for (c_is_own, t_is_own, piece), slot in self.core.items():
            place = self.at(
                c if c_is_own else 1 - c, self.beside if t_is_own else far, piece
            )
            mail.arrive(slot, place, tp=self.beside)


def second_gather_kernel(
    count, part, tokens, gain, wide, wide_low, wide_high, wide_other,
    middle, normed_full, wide_full,
    own, from_core, to_yonder, from_yonder, normed,
    send, recv, local,
):
    z, c, t = lax.axis_index("fsdp"), lax.axis_index("cp"), lax.axis_index("tp")
    beside, yonder = t + 1 - 2 * (t % 2), (t + 2) % 4
    far = (beside + 2) % 4
    rows = tokens.shape[0]
    half = rows // 2
    mail = Mail(send, recv)
    greet(count)

    mine = Line(mail, count, None, lambda j: wide_full.at[:, j, c], wide_low, wide_high)
    other = Line(mail, count, wide_other, lambda j: wide_full.at[:, j, 1 - c])
    core = [mail.slot() for _ in range(2)]
    across = [mail.slot() for _ in range(2)]
    spread = Spread(
        mail, lambda piece: normed.at[piece], lambda c, t, piece: normed_full.at[c, t, piece]
    )

    mail.start(core[1], part.at[far], from_core.at[1], tp=beside)
    mail.start(core[0], part.at[beside], from_core.at[0], tp=beside)
    kept = [
        (pltpu.make_async_copy(part.at[yonder], own.at[1], local.at[0]), None),
        (pltpu.make_async_copy(part.at[t], own.at[0], local.at[1]), None),
        (pltpu.make_async_copy(wide, wide_full.at[:, z, c], local.at[2]), None),
        (pltpu.make_async_copy(wide_other, wide_full.at[:, z, 1 - c], local.at[3]), None),
        (
            pltpu.make_async_copy(
                wide_low, wide_full.at[:, jnp.maximum(z - 1, 0), c], local.at[4]
            ),
            z > 0,
        ),
        (
            pltpu.make_async_copy(
                wide_high, wide_full.at[:, jnp.minimum(z + 1, count - 1), c], local.at[5]
            ),
            z < count - 1,
        ),
    ]
    for copy, when in kept:
        copy.start() if when is None else pl.when(when)(copy.start)
    if count > 2:
        mine.send(2)
    if count > 1:
        other.send(1)

    kept[0][0].wait()
    mail.arrive(core[1], from_core.at[1], tp=beside)
    for piece in range(2):

        def add(place, piece=piece):
            place = pl.ds(place.start + piece * half, place.size)
            to_yonder[place, :] = (
                own[1, place, :].astype(F32) + from_core[1, place, :].astype(F32)
            ).astype(BF)

        in_pieces(half, add)
        block = pl.ds(piece * half, half)
        mail.start(across[piece], to_yonder.at[block], from_yonder.at[block], tp=yonder)

    kept[1][0].wait()
    mail.arrive(core[0], from_core.at[0], tp=beside)
    for piece in range(2):
        block = pl.ds(piece * half, half)
        mail.arrive(across[piece], from_yonder.at[block], tp=yonder)

        def norm(place, piece=piece):
            row = pl.ds(place.start + piece * half, place.size)
            attended = (
                own[0, row, :].astype(F32)
                + from_core[0, row, :].astype(F32)
                + from_yonder[row, :].astype(F32)
            )
            values = tokens[row, :].astype(F32) + BRANCH * attended
            middle[row, :] = values
            normed[piece, place, :] = (normalize(values) * gain[...]).astype(BF)

        in_pieces(half, norm)
        spread.begin(piece)
    keep_normed = pltpu.make_async_copy(normed, normed_full.at[c, t], local.at[0])
    keep_normed.start()
    spread.turn()

    for hop in range(1, count):
        if hop + 1 < count:
            mine.arrive(hop + 1)
            if hop + 2 < count:
                mine.send(hop + 2)
        other.arrive(hop)
        if hop + 1 < count:
            other.send(hop + 1)
        if hop == 1:
            spread.end()
    if count == 1:
        spread.end()
    keep_normed.wait()
    for copy, when in kept[2:]:
        copy.wait() if when is None else pl.when(when)(copy.wait)
    mail.finish()


def second_gather(count, part, tokens, gain, wide, wide_low, wide_high, wide_other):
    slots = 4 * count + 20
    rows, width = tokens.shape
    anywhere = pl.BlockSpec(memory_space=pl.ANY)
    vmem = pl.BlockSpec(memory_space=pltpu.VMEM)
    return pl.pallas_call(
        functools.partial(second_gather_kernel, count),
        out_shape=(
            jax.ShapeDtypeStruct((rows, width), F32),
            jax.ShapeDtypeStruct((2, 4, 2, rows // 2, width), BF),
            jax.ShapeDtypeStruct((3, count, 2) + wide.shape[1:], BF),
        ),
        in_specs=[anywhere, vmem, vmem] + [anywhere] * 4,
        out_specs=(vmem, anywhere, anywhere),
        scratch_shapes=[
            pltpu.VMEM((2, rows, width), BF),
            pltpu.VMEM((2, rows, width), BF),
            pltpu.VMEM((rows, width), BF),
            pltpu.VMEM((rows, width), BF),
            pltpu.VMEM((2, rows // 2, width), BF),
            pltpu.SemaphoreType.DMA((slots,)),
            pltpu.SemaphoreType.DMA((slots,)),
            pltpu.SemaphoreType.DMA((6,)),
        ],
        compiler_params=pltpu.CompilerParams(
            collective_id=2, has_side_effects=True, vmem_limit_bytes=40 << 20
        ),
    )(part, tokens, gain, wide, wide_low, wide_high, wide_other)


def normalize(values):
    return values * lax.rsqrt(jnp.mean(values * values, axis=-1, keepdims=True) + EPSILON)


def scaled_norm(values, gain_values):
    return normalize(values) * gain_values


def silu_product(gate_pre, up_pre):
    return gate_pre / (1.0 + jnp.exp(-gate_pre)) * up_pre


def matmul(left, right):
    return jnp.dot(left, right, preferred_element_type=F32)


def rows_inner(left, right):
    return lax.dot_general(left, right, (((0,), (0,)), ((), ())), preferred_element_type=F32)


def cols_inner(left, right):
    return lax.dot_general(left, right, (((1,), (1,)), ((), ())), preferred_element_type=F32)


def after(value, *earlier):
    return lax.optimization_barrier((value, *earlier))[0]


def swap(value):
    return lax.ppermute(value, "cp", [(0, 1), (1, 0)])


def in_order(place, mine, other, axis):
    return jnp.where(
        place == 0,
        jnp.concatenate([mine, other], axis=axis),
        jnp.concatenate([other, mine], axis=axis),
    )


def gather_line(block, gates=None):
    count = lax.axis_size("fsdp")
    z = lax.axis_index("fsdp")
    from_low, from_high = [], []
    low = high = block
    for step in range(1, count):
        if gates is not None and step - 1 < len(gates):
            low, high = after((low, high), *gates[step - 1])
        low = lax.ppermute(low, "fsdp", [(i, i + 1) for i in range(step - 1, count - 1)])
        high = lax.ppermute(high, "fsdp", [(i, i - 1) for i in range(1, count - step + 1)])
        from_low.append(low)
        from_high.append(high)
    blocks = [block]
    for step in range(1, count):
        blocks.append(jnp.where(z >= step, from_low[step - 1], from_high[count - step - 1]))
    return blocks, list(zip(from_low, from_high))


def placed(blocks, axis=0):
    count = lax.axis_size("fsdp")
    z = lax.axis_index("fsdp")
    rows = blocks[0].shape[axis]
    shape = list(blocks[0].shape)
    shape[axis] = rows * count
    full = jnp.zeros(shape, blocks[0].dtype)
    for step, block in enumerate(blocks):
        start = lax.rem(z - step + count, count) * rows
        full = lax.dynamic_update_slice_in_dim(full, block, start, axis)
    return full


def reduce_line(part):
    count = lax.axis_size("fsdp")
    z = lax.axis_index("fsdp")
    low = high = None
    for step in range(1, count):
        up_part = part(jnp.clip(z + count - step, 0, count - 1))
        down_part = part(jnp.clip(z - count + step, 0, count - 1))
        if low is not None:
            up_part = (up_part.astype(F32) + low.astype(F32)).astype(BF)
            down_part = (down_part.astype(F32) + high.astype(F32)).astype(BF)
        low = lax.ppermute(up_part, "fsdp", [(i, i + 1) for i in range(0, step)])
        high = lax.ppermute(down_part, "fsdp", [(i, i - 1) for i in range(count - step, count)])
    total = part(z).astype(F32)
    if low is not None:
        total = total + low.astype(F32) + high.astype(F32)
    return total


def farthest_first(count):
    return np.array(
        [sorted(range(count), key=lambda j: (-abs(j - z), j)) for z in range(count)], np.int32
    )


def on_device(
    tokens,
    seq_lengths,
    attention_gain,
    query_weight,
    key_weight,
    value_weight,
    out_weight,
    feedforward_gain,
    gate_weight,
    up_weight,
    down_weight,
    cotangent,
):
    c = lax.axis_index("cp")
    z = lax.axis_index("fsdp")
    sets = lax.axis_size("cp")
    count = lax.axis_size("fsdp")
    lanes = lax.axis_size("tp")
    slots, local, width = tokens.shape
    share = query_weight.shape[0]
    heads_width = query_weight.shape[1]
    head_count = heads_width // HD
    hidden_width = gate_weight.shape[1] // sets
    rows = sets * local
    seq = rows * lanes
    blocks = row_blocks(seq, sets, local)
    everyone = ("cp", "tp")

    def pick(value, which, axis=0):
        return lax.dynamic_index_in_dim(value, which, axis, keepdims=False)

    def to_sequence(value):
        mine = pick(value, c)
        other = swap(pick(value, 1 - c))
        return in_order(c, mine, other, 0)

    def from_sequence(value):
        value = value.reshape(sets, local, width)
        mine = pick(value, c)
        other = swap(pick(value, 1 - c))
        return in_order(c, mine[None], other[None], 0)

    token_rows = to_sequence(tokens)
    inputs = token_rows.astype(F32)
    upstream = to_sequence(cotangent).astype(F32)
    length = pick(seq_lengths, c)[None]
    gain_one = attention_gain.astype(F32)
    gain_two = feedforward_gain.astype(F32)

    def normed_rows(values):
        return (normalize(values.astype(F32)) * gain_one).astype(BF)

    qkv = jnp.concatenate([query_weight, key_weight, value_weight], axis=1)
    wide = jnp.stack([gate_weight, up_weight, down_weight.T]).reshape(3, share, sets, hidden_width)
    own_wide = pick(wide, c, 2)
    normed_one, full_qkv, out_half, wide_low, wide_high = first_gather(
        count, normed_rows(tokens), qkv, out_weight.T, own_wide
    )
    normed_one = normed_one.reshape(seq, width)
    full_qkv = full_qkv.reshape(width, 3 * heads_width)
    out_other, wide_other = after((out_half, pick(wide, 1 - c, 2)), full_qkv)
    wide_other = swap(wide_other)
    full_out = in_order(c, out_half[:, None], swap(out_other)[:, None], 1)
    full_out = full_out.reshape(width, heads_width)

    cosine_table, sine_table = tables(seq)
    projected = matmul(normed_one, full_qkv)
    context, q_heads, k_heads, v_heads, level = attention(
        blocks, head_count, length, projected, cosine_table, sine_table
    )
    part = cols_inner(context, full_out).astype(BF)

    middle, normed_two, full_wide = second_gather(
        count, part.reshape(lanes, rows, width), token_rows, gain_two[None], own_wide,
        wide_low, wide_high, wide_other,
    )
    normed_two = normed_two.reshape(sets * seq, width)
    full_gate, full_up, full_down = full_wide.reshape(3, width, hidden_width)
    _, norm_two_back = jax.vjp(scaled_norm, middle, gain_two)
    _, norm_one_back = jax.vjp(scaled_norm, inputs, gain_one)
    grad_branch = lax.all_gather((BRANCH * upstream).astype(BF), everyone, axis=0, tiled=True)
    gate_pre = matmul(normed_two, full_gate)
    up_pre = matmul(normed_two, full_up)
    hidden_exact, silu_back = jax.vjp(silu_product, gate_pre, up_pre)
    hidden = hidden_exact.astype(BF)

    def line_part(gradient):
        pieces = gradient.reshape(count, gradient.shape[0] // count, gradient.shape[1])
        return lambda j: pick(pieces, j)

    def reduced_halves(gradient):
        total = reduce_line(line_part(gradient))
        total = total.reshape(sets, share, hidden_width)
        mine = pick(total, c)
        other = swap(pick(total, 1 - c).astype(BF)).astype(F32)
        return in_order(c, mine, other, 1)

    grad_down = reduced_halves(rows_inner(grad_branch, hidden).astype(BF)).T
    grad_hidden = matmul(grad_branch, full_down)
    grad_gate_exact, grad_up_exact = silu_back(grad_hidden)
    grad_gate_pre = grad_gate_exact.astype(BF)
    grad_up_pre = grad_up_exact.astype(BF)
    grad_normed_two = cols_inner(grad_gate_pre, full_gate) + cols_inner(grad_up_pre, full_up)
    grad_norm_two = lax.psum_scatter(
        grad_normed_two.astype(BF), everyone, scatter_dimension=0, tiled=True
    ).astype(F32)
    grad_gate = reduced_halves(rows_inner(normed_two, grad_gate_pre).astype(BF))
    grad_up = reduced_halves(rows_inner(normed_two, grad_up_pre).astype(BF))

    grad_middle_norm, grad_gain_two = norm_two_back(grad_norm_two)
    grad_middle = upstream + grad_middle_norm
    grad_attention = lax.all_gather((BRANCH * grad_middle).astype(BF), "tp", axis=0, tiled=True)

    feedforward = lax.psum_scatter(
        after(cols_inner(hidden, full_down).astype(BF), grad_attention),
        everyone, scatter_dimension=0, tiled=True,
    )
    output = from_sequence((middle + BRANCH * feedforward.astype(F32)).astype(BF))

    order = jnp.asarray(farthest_first(count))[z]

    def reduced_rows(gradient):
        pieces = gradient.reshape(count, sets, share, gradient.shape[1])
        mine = pick(pieces, c, 1)
        other = pick(pieces, 1 - c, 1)
        summed = []
        for k in range(count):
            got = swap(pick(other, order[k]))
            summed.append((pick(mine, order[k]).astype(F32) + got.astype(F32)).astype(BF))

        def part(j):
            found = summed[0]
            for k in range(1, count):
                found = jnp.where(order[k] == j, summed[k], found)
            return found

        return reduce_line(part)

    grad_out = reduced_rows(rows_inner(grad_attention, context).astype(BF)).T
    grad_context = matmul(grad_attention, full_out).astype(BF)
    grad_projected = attention_back(
        blocks, head_count, length, grad_context, q_heads, k_heads, v_heads, level,
        cosine_table, sine_table,
    )
    grad_qkv = reduced_rows(rows_inner(normed_one, grad_projected).astype(BF))
    grad_norm_one = lax.psum_scatter(
        cols_inner(grad_projected, full_qkv).astype(BF), "tp", scatter_dimension=0, tiled=True
    ).astype(F32)
    grad_inputs_norm, grad_gain_one = norm_one_back(grad_norm_one)
    grad_tokens = from_sequence((grad_middle + grad_inputs_norm).astype(BF))
    gain_sums = lax.psum(jnp.stack([grad_gain_one, grad_gain_two]), ("fsdp", "cp", "tp"))
    return (
        output,
        grad_tokens,
        grad_qkv[:, :heads_width],
        grad_qkv[:, heads_width : 2 * heads_width],
        grad_qkv[:, 2 * heads_width :],
        grad_out,
        gain_sums[0],
        grad_gate,
        grad_up,
        grad_down,
        gain_sums[1],
    )


def solution(mesh):
    in_specs = (
        P("fsdp", ("cp", "tp"), None),
        P("fsdp"),
        P(),
        P(("fsdp", "cp"), "tp"),
        P(("fsdp", "cp"), "tp"),
        P(("fsdp", "cp"), "tp"),
        P("tp", ("fsdp", "cp")),
        P(),
        P(("fsdp", "cp"), "tp"),
        P(("fsdp", "cp"), "tp"),
        P("tp", ("fsdp", "cp")),
        P("fsdp", ("cp", "tp"), None),
    )
    out_specs = (
        P("fsdp", ("cp", "tp"), None),
        P("fsdp", ("cp", "tp"), None),
        P(("fsdp", "cp"), "tp"),
        P(("fsdp", "cp"), "tp"),
        P(("fsdp", "cp"), "tp"),
        P("tp", ("fsdp", "cp")),
        P(),
        P(("fsdp", "cp"), "tp"),
        P(("fsdp", "cp"), "tp"),
        P("tp", ("fsdp", "cp")),
        P(),
    )
    return jax.shard_map(
        on_device, mesh=mesh, in_specs=in_specs, out_specs=out_specs, check_vma=False
    )
```

```python
import functools
import math

import jax
import jax.numpy as jnp
import numpy as np
from jax import lax
from jax.experimental import pallas as pl
from jax.experimental.pallas import tpu as pltpu
from jax.sharding import PartitionSpec as P

HD = 64
EPSILON = 1e-05
BRANCH = 1.4 / math.sqrt(40.0)
BF = jnp.bfloat16
F32 = jnp.float32
TILE = 128
QUERY_ROWS = 256


def turned(values, cosine, sine):
    lane = lax.broadcasted_iota(jnp.int32, values.shape, 1)
    partner = jnp.where(
        lane % HD < HD // 2,
        pltpu.roll(values, TILE - HD // 2, 1),
        pltpu.roll(values, HD // 2, 1),
    )
    return values * cosine + partner * sine


def row_blocks(seq, sets, local):
    lanes = seq // sets // local
    return [
        ((t * sets + h) * local, (h * lanes + t) * local)
        for t in range(lanes)
        for h in range(sets)
    ]


def key_mask(length, first, rows, columns):
    place = first + lax.broadcasted_iota(jnp.int32, (rows, columns), 0)
    return place < length


def scores_of(keys, queries, length, first_query):
    raw = lax.dot_general(keys, queries, (((1,), (1,)), ((), ())), preferred_element_type=F32)
    key_place = lax.broadcasted_iota(jnp.int32, raw.shape, 0)
    query_place = first_query + lax.broadcasted_iota(jnp.int32, raw.shape, 1)
    return jnp.where((key_place <= query_place) & (key_place < length), raw, -1e30)


def attention_kernel(
    blocks, length_ref, projected, cosine, sine, context, q_heads, k_heads, v_heads, level, kept
):
    heads, seq, _ = q_heads.shape
    local = seq // len(blocks)
    length = length_ref[0]
    for gathered, ordered in blocks:
        source, target = pl.ds(gathered, local), pl.ds(ordered, local)
        for tile in range(-(-3 * heads // 2)):
            width = min(TILE, 3 * heads * HD - tile * TILE)
            values = projected[source, tile * TILE : tile * TILE + width]
            if tile * 2 < 2 * heads:
                values = turned(values, cosine[target, :], sine[target, :])
            for which in range(width // HD):
                index = tile * 2 + which
                piece = values[:, which * HD : (which + 1) * HD]
                if index < heads:
                    q_heads[index, target, :] = (piece * (1.0 / math.sqrt(HD))).astype(BF)
                elif index < 2 * heads:
                    k_heads[index - heads, target, :] = piece.astype(BF)
                else:
                    v_heads[index - 2 * heads, target, :] = piece.astype(BF)

    def one_head(head, carry):
        for first in range(0, seq, QUERY_ROWS):
            most = first + QUERY_ROWS
            queries = q_heads[head, first:most, :]
            keys = k_heads[head, :most, :]
            values = v_heads[head, :most, :]
            scores = scores_of(keys, queries, length, first)
            top = jnp.max(scores, axis=0, keepdims=True)
            exponent = jnp.exp(scores - top)
            total = jnp.sum(exponent, axis=0, keepdims=True)
            probabilities = (exponent * (1.0 / total)).astype(BF)
            level[head, :, first:most] = top + jnp.log(total)
            mixed = lax.dot_general(
                values, probabilities, (((0,), (0,)), ((), ())), preferred_element_type=F32
            )
            kept[head, first:most, :] = mixed.T.astype(BF)
        return carry

    lax.fori_loop(0, heads, one_head, 0)
    for gathered, ordered in blocks:
        source, target = pl.ds(ordered, local), pl.ds(gathered, local)
        for head in range(0, heads, 2):
            parts = [kept[index, source, :] for index in range(head, min(head + 2, heads))]
            joined = parts[0] if len(parts) == 1 else jnp.concatenate(parts, axis=1)
            context[target, head * HD : head * HD + joined.shape[1]] = joined


def attention(blocks, heads, length, projected, cosine, sine):
    seq = projected.shape[0]
    per_head = jax.ShapeDtypeStruct((heads, seq, HD), BF)
    vmem = pl.BlockSpec(memory_space=pltpu.VMEM)
    return pl.pallas_call(
        functools.partial(attention_kernel, blocks),
        out_shape=(
            jax.ShapeDtypeStruct((seq, heads * HD), BF),
            per_head,
            per_head,
            per_head,
            jax.ShapeDtypeStruct((heads, 1, seq), F32),
        ),
        in_specs=[pl.BlockSpec(memory_space=pltpu.SMEM), vmem, vmem, vmem],
        out_specs=(vmem,) * 5,
        scratch_shapes=[pltpu.VMEM((heads, seq, HD), BF)],
        compiler_params=pltpu.CompilerParams(vmem_limit_bytes=48 << 20),
        cost_estimate=pl.CostEstimate(
            flops=4 * heads * seq * seq * HD, transcendentals=heads * seq * seq, bytes_accessed=20 << 20
        ),
    )(length, projected, cosine, sine)


def attention_back_kernel(
    blocks, length_ref, grad_context, q_heads, k_heads, v_heads, level, cosine, sine,
    grad_projected, g_heads, dq, dk, dv,
):
    heads, seq, _ = q_heads.shape
    local = seq // len(blocks)
    length = length_ref[0]
    for gathered, ordered in blocks:
        source, target = pl.ds(gathered, local), pl.ds(ordered, local)
        for head in range(heads):
            g_heads[head, target, :] = grad_context[source, head * HD : (head + 1) * HD]

    def one_head(head, carry):
        keys_turned = k_heads[head].T
        for first in reversed(range(0, seq, QUERY_ROWS)):
            most = first + QUERY_ROWS
            queries = q_heads[head, first:most, :]
            upstream = g_heads[head, first:most, :]
            keys = k_heads[head, :most, :]
            values = v_heads[head, :most, :]
            scores = scores_of(keys, queries, length, first)
            probabilities = jnp.exp(scores - level[head, :, first:most])
            grad_probabilities = lax.dot_general(
                values, upstream, (((1,), (1,)), ((), ())), preferred_element_type=F32
            )
            weighted = probabilities * grad_probabilities
            balance = jnp.sum(weighted, axis=0, keepdims=True)
            grad_scores = (weighted - probabilities * balance).astype(BF)
            grad_keys = jnp.dot(grad_scores, queries, preferred_element_type=F32)
            grad_values = jnp.dot(
                probabilities.astype(BF), upstream, preferred_element_type=F32
            )
            if most == seq:
                dk[head, :, :] = grad_keys
                dv[head, :, :] = grad_values
            else:
                dk[head, :most, :] += grad_keys
                dv[head, :most, :] += grad_values
            grad_queries = jnp.dot(
                keys_turned[:, :most], grad_scores, preferred_element_type=F32
            )
            dq[head, first:most, :] = grad_queries.T * (1.0 / math.sqrt(HD))
        return carry

    lax.fori_loop(0, heads, one_head, 0)
    sources = [dq] * heads + [dk] * heads + [dv] * heads
    for gathered, ordered in blocks:
        source, target = pl.ds(ordered, local), pl.ds(gathered, local)
        for tile in range(-(-3 * heads // 2)):
            indices = range(tile * 2, min(tile * 2 + 2, 3 * heads))
            parts = [sources[index][index % heads, source, :] for index in indices]
            joined = parts[0] if len(parts) == 1 else jnp.concatenate(parts, axis=1)
            if tile * 2 < 2 * heads:
                joined = turned(joined, cosine[source, :], -sine[source, :])
            grad_projected[target, tile * TILE : tile * TILE + joined.shape[1]] = joined.astype(BF)


def attention_back(blocks, heads, length, grad_context, q_heads, k_heads, v_heads, level, cosine, sine):
    seq = grad_context.shape[0]
    vmem = pl.BlockSpec(memory_space=pltpu.VMEM)
    return pl.pallas_call(
        functools.partial(attention_back_kernel, blocks),
        out_shape=jax.ShapeDtypeStruct((seq, 3 * heads * HD), BF),
        in_specs=[pl.BlockSpec(memory_space=pltpu.SMEM)] + [vmem] * 7,
        out_specs=vmem,
        scratch_shapes=[
            pltpu.VMEM((heads, seq, HD), BF),
            pltpu.VMEM((heads, seq, HD), F32),
            pltpu.VMEM((heads, seq, HD), F32),
            pltpu.VMEM((heads, seq, HD), F32),
        ],
        compiler_params=pltpu.CompilerParams(vmem_limit_bytes=56 << 20),
        cost_estimate=pl.CostEstimate(
            flops=10 * heads * seq * seq * HD, transcendentals=heads * seq * seq, bytes_accessed=20 << 20
        ),
    )(length, grad_context, q_heads, k_heads, v_heads, level, cosine, sine)


def tables(seq):
    frequency = jnp.power(10000.0, -2.0 * jnp.arange(HD // 2, dtype=F32) / HD)
    angle = jnp.arange(seq, dtype=F32)[:, None] * frequency[None, :]
    cosine, sine = jnp.cos(angle), jnp.sin(angle)
    return jnp.tile(cosine, (1, 4)), jnp.concatenate([-sine, sine, -sine, sine], axis=1)


MESH = pl.DeviceIdType.MESH


def greet(count):
    barrier = pltpu.get_barrier_semaphore()
    z, c, t = lax.axis_index("fsdp"), lax.axis_index("cp"), lax.axis_index("tp")

    def hello(**place):
        pl.semaphore_signal(barrier, inc=1, device_id=place, device_id_type=MESH)

    hello(cp=1 - c)
    hello(tp=t + 1 - 2 * (t % 2))
    hello(tp=(t + 2) % 4)
    pl.when(z > 0)(lambda: hello(fsdp=z - 1))
    pl.when(z < count - 1)(lambda: hello(fsdp=z + 1))
    peers = 3 + jnp.minimum(z, 1) + jnp.minimum(count - 1 - z, 1)
    pl.semaphore_wait(barrier, peers)


class Mail:
    def __init__(self, send, recv):
        self.send, self.recv, self.used, self.open = send, recv, 0, []

    def slot(self):
        self.used += 1
        return self.used - 1

    def copy(self, slot, source, target, **place):
        return pltpu.make_async_remote_copy(
            src_ref=source,
            dst_ref=target,
            send_sem=self.send.at[slot],
            recv_sem=self.recv.at[slot],
            device_id=place,
            device_id_type=MESH,
        )

    def start(self, slot, source, target, when=None, **place):
        made = self.copy(slot, source, target, **place)
        if when is None:
            made.start()
        else:
            pl.when(when)(made.start)
        self.open.append((made, when))

    def arrive(self, slot, target, when=None, **place):
        made = self.copy(slot, target, target, **place)
        if when is None:
            made.wait_recv()
        else:
            pl.when(when)(made.wait_recv)

    def finish(self):
        for made, when in self.open:
            if when is None:
                made.wait_send()
            else:
                pl.when(when)(made.wait_send)


class Line:
    def __init__(self, mail, count, own, at, low=None, high=None):
        self.mail, self.count, self.own, self.at = mail, count, own, at
        self.low, self.high = low, high
        self.z = lax.axis_index("fsdp")
        self.up = [mail.slot() for _ in range(count)]
        self.down = [mail.slot() for _ in range(count)]

    def has_low(self, hop):
        return self.z >= hop

    def has_high(self, hop):
        return self.z <= self.count - 1 - hop

    def send(self, hop):
        z, count, mail = self.z, self.count, self.mail
        low, high = jnp.maximum(z - hop + 1, 0), jnp.minimum(z + hop - 1, count - 1)
        from_low = from_high = self.own
        if hop > 1:
            ready = hop == 2 and self.low is not None
            from_low = self.low if ready else self.at(low)
            from_high = self.high if ready else self.at(high)
        mail.start(
            self.up[hop], from_low, self.at(low),
            when=(z >= hop - 1) & (z < count - 1), fsdp=jnp.minimum(z + 1, count - 1),
        )
        mail.start(
            self.down[hop], from_high, self.at(high),
            when=(z <= count - hop) & (z > 0), fsdp=jnp.maximum(z - 1, 0),
        )

    def arrive(self, hop):
        z, count = self.z, self.count
        self.mail.arrive(
            self.up[hop], self.at(jnp.maximum(z - hop, 0)), when=self.has_low(hop), fsdp=z
        )
        self.mail.arrive(
            self.down[hop], self.at(jnp.minimum(z + hop, count - 1)), when=self.has_high(hop), fsdp=z
        )


class Across:
    def __init__(self, line, own, mine_at, other_at):
        self.line, self.own, self.mine_at, self.other_at = line, own, mine_at, other_at
        self.c = lax.axis_index("cp")
        self.low = [line.mail.slot() for _ in range(line.count)]
        self.high = [line.mail.slot() for _ in range(line.count)]

    def send(self, hop):
        line, mail = self.line, self.line.mail
        z, count, other = line.z, line.count, 1 - self.c
        if hop == 0:
            mail.start(self.low[0], self.own, self.mine_at(z), cp=other)
            return
        low, high = jnp.maximum(z - hop, 0), jnp.minimum(z + hop, count - 1)
        mail.start(self.low[hop], self.mine_at(low), self.mine_at(low), when=line.has_low(hop), cp=other)
        mail.start(self.high[hop], self.mine_at(high), self.mine_at(high), when=line.has_high(hop), cp=other)

    def arrive(self, hop):
        line, mail = self.line, self.line.mail
        z, count, other = line.z, line.count, 1 - self.c
        if hop == 0:
            mail.arrive(self.low[0], self.other_at(z), cp=other)
            return
        low, high = jnp.maximum(z - hop, 0), jnp.minimum(z + hop, count - 1)
        mail.arrive(self.low[hop], self.other_at(low), when=line.has_low(hop), cp=other)
        mail.arrive(self.high[hop], self.other_at(high), when=line.has_high(hop), cp=other)


def first_gather_kernel(
    count, normed, qkv, turned_out, wide, normed_full, qkv_full, out_half, low, high,
    send, recv, local,
):
    z, c, t = lax.axis_index("fsdp"), lax.axis_index("cp"), lax.axis_index("tp")
    beside, yonder = t + 1 - 2 * (t % 2), (t + 2) % 4
    mail = Mail(send, recv)
    greet(count)
    kept = [
        pltpu.make_async_copy(qkv, qkv_full.at[z, c], local.at[0]),
        pltpu.make_async_copy(turned_out, out_half.at[z], local.at[1]),
        pltpu.make_async_copy(normed.at[c], normed_full.at[t, c], local.at[2]),
    ]
    for copy in kept:
        copy.start()

    heads = Line(mail, count, qkv, lambda j: qkv_full.at[j, c])
    heads_across = Across(
        heads, qkv, lambda j: qkv_full.at[j, c], lambda j: qkv_full.at[j, 1 - c]
    )
    outs = Line(mail, count, turned_out, lambda j: out_half.at[j])
    wide_up, wide_down = mail.slot(), mail.slot()
    rows_x = mail.slot()
    rows_y = [mail.slot() for _ in range(2)]
    rows_core = [mail.slot() for _ in range(4)]

    mail.start(rows_x, normed.at[1 - c], normed_full.at[t, c], cp=1 - c)
    heads.send(1)
    heads_across.send(0)
    mail.start(rows_y[0], normed.at[c], normed_full.at[t, c], tp=yonder)
    mail.start(rows_core[0], normed.at[c], normed_full.at[t, c], tp=beside)
    mail.arrive(rows_x, normed_full.at[t, 1 - c], cp=1 - c)
    mail.start(rows_y[1], normed_full.at[t, 1 - c], normed_full.at[t, 1 - c], tp=yonder)
    mail.start(rows_core[1], normed_full.at[t, 1 - c], normed_full.at[t, 1 - c], tp=beside)

    def rows_on(k, half):
        mail.arrive(rows_y[k], normed_full.at[yonder, half], tp=yonder)
        mail.start(
            rows_core[2 + k], normed_full.at[yonder, half], normed_full.at[yonder, half], tp=beside
        )

    for hop in range(1, count):
        heads.arrive(hop)
        if hop + 1 < count:
            heads.send(hop + 1)
        if hop > 1:
            outs.arrive(hop - 1)
        outs.send(hop)
        heads_across.send(hop)
        if hop == 1:
            rows_on(0, c)
            rows_on(1, 1 - c)
    mail.start(wide_up, wide, low, when=z < count - 1, fsdp=jnp.minimum(z + 1, count - 1))
    mail.start(wide_down, wide, high, when=z > 0, fsdp=jnp.maximum(z - 1, 0))
    if count > 1:
        outs.arrive(count - 1)
    for hop in range(count):
        heads_across.arrive(hop)
    mail.arrive(rows_core[0], normed_full.at[beside, c], tp=beside)
    mail.arrive(rows_core[1], normed_full.at[beside, 1 - c], tp=beside)
    far = (beside + 2) % 4
    mail.arrive(rows_core[2], normed_full.at[far, c], tp=beside)
    mail.arrive(rows_core[3], normed_full.at[far, 1 - c], tp=beside)
    mail.arrive(wide_up, low, when=z > 0, fsdp=z)
    mail.arrive(wide_down, high, when=z < count - 1, fsdp=z)
    for copy in kept:
        copy.wait()
    mail.finish()


def first_gather(count, normed, qkv, turned_out, wide):
    slots = 6 * count + 9
    anywhere = pl.BlockSpec(memory_space=pl.ANY)
    share = qkv.shape[0]
    return pl.pallas_call(
        functools.partial(first_gather_kernel, count),
        out_shape=(
            jax.ShapeDtypeStruct((4,) + normed.shape, BF),
            jax.ShapeDtypeStruct((count, 2) + qkv.shape, BF),
            jax.ShapeDtypeStruct((count,) + turned_out.shape, BF),
            jax.ShapeDtypeStruct(wide.shape, BF),
            jax.ShapeDtypeStruct(wide.shape, BF),
        ),
        in_specs=[anywhere] * 4,
        out_specs=(anywhere,) * 5,
        scratch_shapes=[
            pltpu.SemaphoreType.DMA((slots,)),
            pltpu.SemaphoreType.DMA((slots,)),
            pltpu.SemaphoreType.DMA((3,)),
        ],
        compiler_params=pltpu.CompilerParams(collective_id=1, has_side_effects=True),
    )(normed, qkv, turned_out, wide)


def in_pieces(rows, body, size=16):
    if rows % size:
        body(pl.ds(0, rows))
        return
    lax.fori_loop(0, rows // size, lambda i, carry: (body(pl.ds(i * size, size)), carry)[1], 0)


class Spread:
    def __init__(self, mail, own, at):
        self.mail, self.own, self.at = mail, own, at
        self.c, self.t = lax.axis_index("cp"), lax.axis_index("tp")
        self.beside, self.yonder = self.t + 1 - 2 * (self.t % 2), (self.t + 2) % 4
        self.x = [mail.slot() for _ in range(3)]
        self.y = [mail.slot() for _ in range(3)]
        self.core = {}

    def to_core(self, c_is_own, t_is_own, piece):
        slot = self.core[c_is_own, t_is_own, piece] = self.mail.slot()
        c = self.c if c_is_own else 1 - self.c
        t = self.t if t_is_own else self.yonder
        source = self.own(piece) if c_is_own and t_is_own else self.at(c, t, piece)
        self.mail.start(slot, source, self.at(c, t, piece), tp=self.beside)

    def begin(self, piece):
        c, t = self.c, self.t
        if piece == 0:
            self.mail.start(self.x[0], self.own(0), self.at(c, t, 0), cp=1 - c)
        else:
            self.mail.start(self.y[0], self.own(1), self.at(c, t, 1), tp=self.yonder)
            self.mail.start(self.x[1], self.own(1), self.at(c, t, 1), cp=1 - c)
            self.mail.start(self.y[1], self.own(0), self.at(c, t, 0), tp=self.yonder)
        self.to_core(True, True, piece)

    def turn(self):
        c, t, mail, yonder = self.c, self.t, self.mail, self.yonder
        mail.arrive(self.x[0], self.at(1 - c, t, 0), cp=1 - c)
        mail.start(self.y[2], self.at(1 - c, t, 0), self.at(1 - c, t, 0), tp=yonder)
        self.to_core(False, True, 0)
        mail.arrive(self.y[0], self.at(c, yonder, 1), tp=yonder)
        mail.start(self.x[2], self.at(c, yonder, 1), self.at(c, yonder, 1), cp=1 - c)
        self.to_core(True, False, 1)

    def end(self):
        c, t, mail, yonder = self.c, self.t, self.mail, self.yonder
        mail.arrive(self.x[1], self.at(1 - c, t, 1), cp=1 - c)
        self.to_core(False, True, 1)
        mail.arrive(self.y[1], self.at(c, yonder, 0), tp=yonder)
        self.to_core(True, False, 0)
        mail.arrive(self.x[2], self.at(1 - c, yonder, 1), cp=1 - c)
        self.to_core(False, False, 1)
        mail.arrive(self.y[2], self.at(1 - c, yonder, 0), tp=yonder)
        self.to_core(False, False, 0)
        far = (self.beside + 2) % 4
        for (c_is_own, t_is_own, piece), slot in self.core.items():
            place = self.at(
                c if c_is_own else 1 - c, self.beside if t_is_own else far, piece
            )
            mail.arrive(slot, place, tp=self.beside)


def second_gather_kernel(
    count, part, tokens, gain, wide, wide_low, wide_high, wide_other,
    middle, normed_full, wide_full,
    own, from_core, to_yonder, from_yonder, normed,
    send, recv, local,
):
    z, c, t = lax.axis_index("fsdp"), lax.axis_index("cp"), lax.axis_index("tp")
    beside, yonder = t + 1 - 2 * (t % 2), (t + 2) % 4
    far = (beside + 2) % 4
    rows = tokens.shape[0]
    half = rows // 2
    mail = Mail(send, recv)
    greet(count)

    mine = Line(mail, count, None, lambda j: wide_full.at[:, j, c], wide_low, wide_high)
    other = Line(mail, count, wide_other, lambda j: wide_full.at[:, j, 1 - c])
    core = [mail.slot() for _ in range(2)]
    across = [mail.slot() for _ in range(2)]
    spread = Spread(
        mail, lambda piece: normed.at[piece], lambda c, t, piece: normed_full.at[c, t, piece]
    )

    mail.start(core[1], part.at[far], from_core.at[1], tp=beside)
    mail.start(core[0], part.at[beside], from_core.at[0], tp=beside)
    kept = [
        (pltpu.make_async_copy(part.at[yonder], own.at[1], local.at[0]), None),
        (pltpu.make_async_copy(part.at[t], own.at[0], local.at[1]), None),
        (pltpu.make_async_copy(wide, wide_full.at[:, z, c], local.at[2]), None),
        (pltpu.make_async_copy(wide_other, wide_full.at[:, z, 1 - c], local.at[3]), None),
        (
            pltpu.make_async_copy(
                wide_low, wide_full.at[:, jnp.maximum(z - 1, 0), c], local.at[4]
            ),
            z > 0,
        ),
        (
            pltpu.make_async_copy(
                wide_high, wide_full.at[:, jnp.minimum(z + 1, count - 1), c], local.at[5]
            ),
            z < count - 1,
        ),
    ]
    for copy, when in kept:
        copy.start() if when is None else pl.when(when)(copy.start)
    if count > 2:
        mine.send(2)
    if count > 1:
        other.send(1)

    kept[0][0].wait()
    mail.arrive(core[1], from_core.at[1], tp=beside)
    for piece in range(2):

        def add(place, piece=piece):
            place = pl.ds(place.start + piece * half, place.size)
            to_yonder[place, :] = (
                own[1, place, :].astype(F32) + from_core[1, place, :].astype(F32)
            ).astype(BF)

        in_pieces(half, add)
        block = pl.ds(piece * half, half)
        mail.start(across[piece], to_yonder.at[block], from_yonder.at[block], tp=yonder)

    kept[1][0].wait()
    mail.arrive(core[0], from_core.at[0], tp=beside)
    for piece in range(2):
        block = pl.ds(piece * half, half)
        mail.arrive(across[piece], from_yonder.at[block], tp=yonder)

        def norm(place, piece=piece):
            row = pl.ds(place.start + piece * half, place.size)
            attended = (
                own[0, row, :].astype(F32)
                + from_core[0, row, :].astype(F32)
                + from_yonder[row, :].astype(F32)
            )
            values = tokens[row, :].astype(F32) + BRANCH * attended
            middle[row, :] = values
            normed[piece, place, :] = (normalize(values) * gain[...]).astype(BF)

        in_pieces(half, norm)
        spread.begin(piece)
    keep_normed = pltpu.make_async_copy(normed, normed_full.at[c, t], local.at[0])
    keep_normed.start()
    spread.turn()

    for hop in range(1, count):
        if hop + 1 < count:
            mine.arrive(hop + 1)
            if hop + 2 < count:
                mine.send(hop + 2)
        other.arrive(hop)
        if hop + 1 < count:
            other.send(hop + 1)
        if hop == 1:
            spread.end()
    if count == 1:
        spread.end()
    keep_normed.wait()
    for copy, when in kept[2:]:
        copy.wait() if when is None else pl.when(when)(copy.wait)
    mail.finish()


def second_gather(count, part, tokens, gain, wide, wide_low, wide_high, wide_other):
    slots = 4 * count + 20
    rows, width = tokens.shape
    anywhere = pl.BlockSpec(memory_space=pl.ANY)
    vmem = pl.BlockSpec(memory_space=pltpu.VMEM)
    return pl.pallas_call(
        functools.partial(second_gather_kernel, count),
        out_shape=(
            jax.ShapeDtypeStruct((rows, width), F32),
            jax.ShapeDtypeStruct((2, 4, 2, rows // 2, width), BF),
            jax.ShapeDtypeStruct((3, count, 2) + wide.shape[1:], BF),
        ),
        in_specs=[anywhere, vmem, vmem] + [anywhere] * 4,
        out_specs=(vmem, anywhere, anywhere),
        scratch_shapes=[
            pltpu.VMEM((2, rows, width), BF),
            pltpu.VMEM((2, rows, width), BF),
            pltpu.VMEM((rows, width), BF),
            pltpu.VMEM((rows, width), BF),
            pltpu.VMEM((2, rows // 2, width), BF),
            pltpu.SemaphoreType.DMA((slots,)),
            pltpu.SemaphoreType.DMA((slots,)),
            pltpu.SemaphoreType.DMA((6,)),
        ],
        compiler_params=pltpu.CompilerParams(
            collective_id=2, has_side_effects=True, vmem_limit_bytes=40 << 20
        ),
    )(part, tokens, gain, wide, wide_low, wide_high, wide_other)


class TensorSum:
    def __init__(self, mail, part, own, from_core, to_yonder, from_yonder, local):
        self.mail, self.part, self.own, self.from_core = mail, part, own, from_core
        self.to_yonder, self.from_yonder, self.local = to_yonder, from_yonder, local
        self.t = t = lax.axis_index("tp")
        self.beside, self.yonder = t + 1 - 2 * (t % 2), (t + 2) % 4
        self.core = [mail.slot() for _ in range(2)]
        self.across = [mail.slot() for _ in range(2)]
        self.half = from_yonder.shape[0] // 2

    def begin(self):
        part, far = self.part, (self.beside + 2) % 4
        self.mail.start(self.core[1], part.at[far], self.from_core.at[1], tp=self.beside)
        self.mail.start(self.core[0], part.at[self.beside], self.from_core.at[0], tp=self.beside)
        self.kept = [
            pltpu.make_async_copy(part.at[self.yonder], self.own.at[1], self.local.at[0]),
            pltpu.make_async_copy(part.at[self.t], self.own.at[0], self.local.at[1]),
        ]
        for copy in self.kept:
            copy.start()

    def turn(self):
        own, from_core = self.own, self.from_core
        self.kept[0].wait()
        self.mail.arrive(self.core[1], from_core.at[1], tp=self.beside)
        for piece in range(2):

            def add(place, piece=piece):
                place = pl.ds(place.start + piece * self.half, place.size)
                self.to_yonder[place, :] = (
                    own[1, place, :].astype(F32) + from_core[1, place, :].astype(F32)
                ).astype(BF)

            in_pieces(self.half, add)
            block = pl.ds(piece * self.half, self.half)
            self.mail.start(
                self.across[piece], self.to_yonder.at[block], self.from_yonder.at[block],
                tp=self.yonder,
            )
        self.kept[1].wait()
        self.mail.arrive(self.core[0], from_core.at[0], tp=self.beside)

    def arrive(self, piece):
        block = pl.ds(piece * self.half, self.half)
        self.mail.arrive(self.across[piece], self.from_yonder.at[block], tp=self.yonder)

    def rows(self, row):
        return (
            self.own[0, row, :].astype(F32)
            + self.from_core[0, row, :].astype(F32)
            + self.from_yonder[row, :].astype(F32)
        )


class Drain:
    def __init__(self, mail, count, fill, total, landed):
        self.mail, self.count, self.fill, self.total, self.landed = mail, count, fill, total, landed
        self.z = lax.axis_index("fsdp")
        self.slots = [[mail.slot() for _ in range(count)] for _ in range(2)]

    def sends(self, hop, up):
        z, count = self.z, self.count
        return (z <= hop - 1) & (z < count - 1) if up else (z >= count - hop) & (z > 0)

    def gets(self, hop, up):
        z, count = self.z, self.count
        return (z >= 1) & (z <= hop) if up else (z <= count - 2) & (z >= count - 1 - hop)

    def block(self, hop, up):
        z, count = self.z, self.count
        return jnp.minimum(z + count - hop, count - 1) if up else jnp.maximum(z - count + hop, 0)

    def arrive(self, hop):
        for side, up in enumerate((True, False)):
            self.mail.arrive(
                self.slots[side][hop], self.landed(side, hop), when=self.gets(hop, up), fsdp=self.z
            )

    def gather(self, hop):
        for side, up in enumerate((True, False)):
            target = self.total(side, hop)

            def work(side=side, up=up, target=target):
                self.fill(hop, up, self.block(hop, up), target)
                if hop > 1:

                    def add():
                        landed = self.landed(side, hop - 1)

                        def one(place):
                            target[place, :] = (
                                target[place, :].astype(F32) + landed[place, :].astype(F32)
                            ).astype(BF)

                        in_pieces(target.shape[0], one)

                    pl.when(self.gets(hop - 1, up))(add)

            pl.when(self.sends(hop, up))(work)

    def send(self, hop):
        z, count = self.z, self.count
        for side, up in enumerate((True, False)):
            to = jnp.minimum(z + 1, count - 1) if up else jnp.maximum(z - 1, 0)
            self.mail.start(
                self.slots[side][hop], self.total(side, hop), self.landed(side, hop),
                when=self.sends(hop, up), fsdp=to,
            )


def norm_back(values, gain, upstream):
    scale = lax.rsqrt(jnp.mean(values * values, axis=-1, keepdims=True) + EPSILON)
    norm = values * scale
    scaled = upstream * gain
    mean = jnp.mean(scaled * norm, axis=-1, keepdims=True)
    return scale * (scaled - norm * mean), upstream * norm


def first_sum_kernel(
    count, part, gate_grad, up_grad, down_grad, middle, cotangent, gain,
    grad_middle, attention_full, gain_rows, leaving,
    own, from_core, first, second, grad_attention, totals, landed,
    send, recv, local,
):
    z, c, t = lax.axis_index("fsdp"), lax.axis_index("cp"), lax.axis_index("tp")
    beside, yonder = t + 1 - 2 * (t % 2), (t + 2) % 4
    far = (beside + 2) % 4
    half = middle.shape[0] // 2
    width = middle.shape[1]
    mail = Mail(send, recv)
    greet(count)
    last = count - 1

    def fill_from(which):
        def fill(hop, up, j, target):
            copy = pltpu.make_async_copy((gate_grad, up_grad, down_grad)[which].at[j], target, local.at[4])
            copy.start()
            copy.wait()

        return fill

    drains = [
        Drain(
            mail, count, fill_from(which),
            lambda side, hop, which=which: (
                leaving.at[side, which] if hop == last else totals.at[side, hop - 1, which]
            ),
            lambda side, hop, which=which: landed.at[side, hop - 1, which],
        )
        for which in range(3)
    ]

    core = {}
    mine = {}
    order = ((1, 0), (0, 0), (0, 1), (1, 1))
    for index, (c_own, t_own) in enumerate(order):
        block_c = c if c_own else 1 - c
        core[c_own, t_own] = mail.slot()
        mail.start(
            core[c_own, t_own], part.at[block_c, beside if t_own else far],
            from_core.at[c_own, t_own], tp=beside,
        )
        mine[c_own, t_own] = pltpu.make_async_copy(
            part.at[block_c, t if t_own else yonder], own.at[c_own, t_own], local.at[index]
        )
        mine[c_own, t_own].start()
    if last > 1:
        for drain in drains:
            drain.gather(1)
            drain.send(1)
    for c_own, t_own in order:
        mine[c_own, t_own].wait()
        mail.arrive(core[c_own, t_own], from_core.at[c_own, t_own], tp=beside)

        def add(place, c_own=c_own, t_own=t_own):
            own[c_own, t_own, place, :] = (
                own[c_own, t_own, place, :].astype(F32)
                + from_core[c_own, t_own, place, :].astype(F32)
            ).astype(BF)

        in_pieces(2 * half, add)

    top, low = pl.ds(0, half), pl.ds(half, half)
    y_first = [mail.slot() for _ in range(2)]
    x_first = [mail.slot() for _ in range(2)]
    x_second, y_second = mail.slot(), mail.slot()
    for c_own in (0, 1):
        mail.start(y_first[c_own], own.at[c_own, 0, top], first.at[0, c_own], tp=yonder)
    for t_own in (0, 1):
        mail.start(x_first[t_own], own.at[0, t_own, low], first.at[1, t_own], cp=1 - c)

    def add_first(side, index, c_own, t_own):
        def one(place):
            row = pl.ds(place.start + side * half, place.size)
            own[c_own, t_own, row, :] = (
                own[c_own, t_own, row, :].astype(F32) + first[side, index, place, :].astype(F32)
            ).astype(BF)

        in_pieces(half, one)

    mail.arrive(y_first[0], first.at[0, 0], tp=yonder)
    add_first(0, 0, 0, 1)
    mail.start(x_second, own.at[0, 1, top], second.at[0], cp=1 - c)
    mail.arrive(x_first[0], first.at[1, 0], cp=1 - c)
    add_first(1, 0, 1, 0)
    mail.start(y_second, own.at[1, 0, low], second.at[1], tp=yonder)
    mail.arrive(y_first[1], first.at[0, 1], tp=yonder)
    add_first(0, 1, 1, 1)
    mail.arrive(x_first[1], first.at[1, 1], cp=1 - c)
    add_first(1, 1, 1, 1)

    gain_rows[...] = jnp.zeros_like(gain_rows)
    ring_y = [mail.slot() for _ in range(2)]
    ring_core = [mail.slot() for _ in range(4)]
    keep = []
    for piece in range(2):
        if piece == 0:
            mail.arrive(x_second, second.at[0], cp=1 - c)
        else:
            mail.arrive(y_second, second.at[1], tp=yonder)

        def back(place, piece=piece):
            row = pl.ds(place.start + piece * half, place.size)
            summed = own[1, 1, row, :].astype(F32) + second[piece, place, :].astype(F32)
            grad, rows = norm_back(middle[row, :], gain[...], summed)
            grad = cotangent[row, :].astype(F32) + grad
            grad_middle[row, :] = grad
            grad_attention[piece, place, :] = (BRANCH * grad).astype(BF)
            gain_rows[...] += jnp.sum(rows, axis=0, keepdims=True)

        in_pieces(half, back)
        mail.start(ring_y[piece], grad_attention.at[piece], attention_full.at[t, piece], tp=yonder)
        mail.start(
            ring_core[piece], grad_attention.at[piece], attention_full.at[t, piece], tp=beside
        )
    keep = pltpu.make_async_copy(grad_attention, attention_full.at[t], local.at[0])
    keep.start()
    for hop in range(2, last):
        for drain in drains:
            drain.arrive(hop - 1)
            drain.gather(hop)
            drain.send(hop)
    for piece in range(2):
        mail.arrive(ring_y[piece], attention_full.at[yonder, piece], tp=yonder)
        mail.start(
            ring_core[2 + piece], attention_full.at[yonder, piece],
            attention_full.at[yonder, piece], tp=beside,
        )
    for piece in range(2):
        mail.arrive(ring_core[piece], attention_full.at[beside, piece], tp=beside)
        mail.arrive(ring_core[2 + piece], attention_full.at[far, piece], tp=beside)
    for drain in drains:
        if last > 1:
            drain.arrive(last - 1)
        if last > 0:
            drain.gather(last)
    keep.wait()
    mail.finish()


def first_sum(count, part, gate_grad, up_grad, down_grad, middle, cotangent, gain):
    slots = 6 * count + 24
    rows, width = middle.shape
    block = gate_grad.shape[1:]
    anywhere = pl.BlockSpec(memory_space=pl.ANY)
    vmem = pl.BlockSpec(memory_space=pltpu.VMEM)
    hops = max(count - 2, 1)
    return pl.pallas_call(
        functools.partial(first_sum_kernel, count),
        out_shape=(
            jax.ShapeDtypeStruct((rows, width), F32),
            jax.ShapeDtypeStruct((4, 2, rows // 2, width), BF),
            jax.ShapeDtypeStruct((1, width), F32),
            jax.ShapeDtypeStruct((2, 3) + block, BF),
        ),
        in_specs=[anywhere] * 4 + [vmem] * 3,
        out_specs=(vmem, anywhere, vmem, vmem),
        scratch_shapes=[
            pltpu.VMEM((2, 2, rows, width), BF),
            pltpu.VMEM((2, 2, rows, width), BF),
            pltpu.VMEM((2, 2, rows // 2, width), BF),
            pltpu.VMEM((2, rows // 2, width), BF),
            pltpu.VMEM((2, rows // 2, width), BF),
            pltpu.VMEM((2, hops, 3) + block, BF),
            pltpu.VMEM((2, hops, 3) + block, BF),
            pltpu.SemaphoreType.DMA((slots,)),
            pltpu.SemaphoreType.DMA((slots,)),
            pltpu.SemaphoreType.DMA((5,)),
        ],
        compiler_params=pltpu.CompilerParams(
            collective_id=3, has_side_effects=True, vmem_limit_bytes=60 << 20
        ),
    )(part, gate_grad, up_grad, down_grad, middle, cotangent, gain)


def last_sum_kernel(
    count, part, qkv_grad, out_grad, tokens, grad_middle, gain, gain_rows,
    qkv_total, out_total, grad_tokens, gain_sums,
    own, from_core, to_yonder, from_yonder, pieces,
    from_x, heads_sum, heads_landed, outs_sum, outs_landed, final_out, gains, gain_line,
    send, recv, local,
):
    z, c, t = lax.axis_index("fsdp"), lax.axis_index("cp"), lax.axis_index("tp")
    beside, yonder = t + 1 - 2 * (t % 2), (t + 2) % 4
    half = tokens.shape[0] // 2
    last = count - 1
    mail = Mail(send, recv)
    greet(count)

    summed = TensorSum(mail, part, own, from_core, to_yonder, from_yonder, local)

    cross = [[mail.slot() for _ in range(count)] for _ in range(2)]
    cross_own = mail.slot()

    def fill_heads(hop, up, j, target):
        side = 0 if up else 1
        copy = pltpu.make_async_copy(qkv_grad.at[j, c], target, local.at[2])
        copy.start()
        mail.arrive(cross[side][hop], from_x.at[side, hop - 1], cp=1 - c)
        copy.wait()

        def one(place):
            target[place, :] = (
                target[place, :].astype(F32) + from_x[side, hop - 1, place, :].astype(F32)
            ).astype(BF)

        in_pieces(target.shape[0], one)

    heads = Drain(
        mail, count, fill_heads,
        lambda side, hop: heads_sum.at[side, hop - 1],
        lambda side, hop: heads_landed.at[side, hop - 1],
    )

    def fill_outs(hop, up, j, target):
        copy = pltpu.make_async_copy(out_grad.at[j], target, local.at[3])
        copy.start()
        copy.wait()

    outs = Drain(
        mail, count, fill_outs,
        lambda side, hop: outs_sum.at[side, hop - 1],
        lambda side, hop: outs_landed.at[side, hop - 1],
    )

    def cross_send(hop):
        if hop == count:
            mail.start(cross_own, qkv_grad.at[z, 1 - c], from_x.at[0, last], cp=1 - c)
        elif hop < count:
            for side, up in enumerate((True, False)):
                mail.start(
                    cross[side][hop], qkv_grad.at[heads.block(hop, up), 1 - c],
                    from_x.at[side, hop - 1], when=heads.sends(hop, up), cp=1 - c,
                )

    cross_send(1)
    cross_send(2)
    summed.begin()
    outs.gather(1)
    outs.send(1)
    summed.turn()

    keep = pltpu.make_async_copy(pieces.at[c], grad_tokens.at[c], local.at[0])
    home = mail.slot()
    gain_x, gain_y, gain_core = mail.slot(), mail.slot(), mail.slot()
    line = Line(mail, count, gain_line.at[z], lambda j: gain_line.at[j])

    def finish_rows():
        gains[0, 0:1, :] = jnp.zeros_like(gain_rows)
        gains[0, 1:2, :] = gain_rows[...]
        for piece in range(2):
            summed.arrive(piece)

            def back(place, piece=piece):
                row = pl.ds(place.start + piece * half, place.size)
                grad, rows = norm_back(tokens[row, :].astype(F32), gain[...], summed.rows(row))
                pieces[piece, place, :] = (grad_middle[row, :] + grad).astype(BF)
                gains[0, 0:1, :] += jnp.sum(rows, axis=0, keepdims=True)

            in_pieces(half, back)
        mail.start(home, pieces.at[1 - c], grad_tokens.at[c], cp=1 - c)
        keep.start()
        mail.start(gain_core, gains.at[0], gains.at[1], tp=beside)

    def gain_step(k):
        if k == 0:
            mail.arrive(gain_core, gains.at[1], tp=beside)
            gains[2] = gains[0] + gains[1]
            mail.start(gain_y, gains.at[2], gains.at[3], tp=yonder)
        elif k == 1:
            mail.arrive(gain_y, gains.at[3], tp=yonder)
            gains[4] = gains[2] + gains[3]
            mail.start(gain_x, gains.at[4], gains.at[5], cp=1 - c)
        elif k == 2:
            mail.arrive(gain_x, gains.at[5], cp=1 - c)
            gain_line[z] = gains[4] + gains[5]
            if count > 1:
                line.send(1)
        else:
            hop = k - 2
            line.arrive(hop)
            if hop + 1 < count:
                line.send(hop + 1)

    for hop in range(1, count):
        if hop > 1:
            heads.arrive(hop - 1)
        heads.gather(hop)
        heads.send(hop)
        cross_send(hop + 2)
        if hop > 1:
            outs.arrive(hop - 1)
            outs.gather(hop)
            outs.send(hop)
        if hop == 1:
            finish_rows()
        if hop == 2:
            gain_step(0)
            gain_step(1)
    if count == 1:
        finish_rows()
    if count <= 2:
        gain_step(0)
        gain_step(1)
    gain_step(2)

    own_copy = pltpu.make_async_copy(qkv_grad.at[z, c], from_x.at[1, last], local.at[2])
    own_copy.start()
    out_copy = pltpu.make_async_copy(out_grad.at[z], final_out, local.at[3])
    out_copy.start()
    mail.arrive(cross_own, from_x.at[0, last], cp=1 - c)
    own_copy.wait()
    out_copy.wait()

    def start_heads(place):
        qkv_total[place, :] = from_x[0, last, place, :].astype(F32) + from_x[
            1, last, place, :
        ].astype(F32)

    in_pieces(qkv_total.shape[0], start_heads)

    def start_outs(place):
        out_total[place, :] = final_out[place, :].astype(F32)

    in_pieces(out_total.shape[0], start_outs)
    for hop in range(1, count):
        gain_step(2 + hop)
    if count > 1:
        outs.arrive(last)
        heads.arrive(last)
        for drain, total in ((outs, out_total), (heads, qkv_total)):
            for side, up in enumerate((True, False)):

                def more(drain=drain, total=total, side=side):
                    landed = drain.landed(side, last)

                    def one(place):
                        total[place, :] += landed[place, :].astype(F32)

                    in_pieces(total.shape[0], one)

                pl.when(drain.gets(last, up))(more)
    gain_sums[...] = jnp.sum(gain_line[...], axis=0)
    mail.arrive(home, grad_tokens.at[1 - c], cp=1 - c)
    keep.wait()
    mail.finish()


def last_sum(count, part, qkv_grad, out_grad, tokens, grad_middle, gain, gain_rows):
    slots = 8 * count + 16
    rows, width = tokens.shape
    hops = max(count - 1, 1)
    block, out_block = qkv_grad.shape[2:], out_grad.shape[1:]
    anywhere = pl.BlockSpec(memory_space=pl.ANY)
    vmem = pl.BlockSpec(memory_space=pltpu.VMEM)
    return pl.pallas_call(
        functools.partial(last_sum_kernel, count),
        out_shape=(
            jax.ShapeDtypeStruct(block, F32),
            jax.ShapeDtypeStruct(out_block, F32),
            jax.ShapeDtypeStruct((2, rows // 2, width), BF),
            jax.ShapeDtypeStruct((2, width), F32),
        ),
        in_specs=[anywhere] * 3 + [vmem] * 4,
        out_specs=(vmem, vmem, anywhere, vmem),
        scratch_shapes=[
            pltpu.VMEM((2, rows, width), BF),
            pltpu.VMEM((2, rows, width), BF),
            pltpu.VMEM((rows, width), BF),
            pltpu.VMEM((rows, width), BF),
            pltpu.VMEM((2, rows // 2, width), BF),
            pltpu.VMEM((2, count) + block, BF),
            pltpu.VMEM((2, hops) + block, BF),
            pltpu.VMEM((2, hops) + block, BF),
            pltpu.VMEM((2, hops) + out_block, BF),
            pltpu.VMEM((2, hops) + out_block, BF),
            pltpu.VMEM(out_block, BF),
            pltpu.VMEM((6, 2, width), F32),
            pltpu.VMEM((count, 2, width), F32),
            pltpu.SemaphoreType.DMA((slots,)),
            pltpu.SemaphoreType.DMA((slots,)),
            pltpu.SemaphoreType.DMA((4,)),
        ],
        compiler_params=pltpu.CompilerParams(
            collective_id=4, has_side_effects=True, vmem_limit_bytes=60 << 20
        ),
    )(part, qkv_grad, out_grad, tokens, grad_middle, gain, gain_rows)


def normalize(values):
    return values * lax.rsqrt(jnp.mean(values * values, axis=-1, keepdims=True) + EPSILON)


def silu_product(gate_pre, up_pre):
    return gate_pre / (1.0 + jnp.exp(-gate_pre)) * up_pre


def matmul(left, right):
    return jnp.dot(left, right, preferred_element_type=F32)


def rows_inner(left, right):
    return lax.dot_general(left, right, (((0,), (0,)), ((), ())), preferred_element_type=F32)


def cols_inner(left, right):
    return lax.dot_general(left, right, (((1,), (1,)), ((), ())), preferred_element_type=F32)


def after(value, *earlier):
    return lax.optimization_barrier((value, *earlier))[0]


def swap(value):
    return lax.ppermute(value, "cp", [(0, 1), (1, 0)])


def in_order(place, mine, other, axis):
    return jnp.where(
        place == 0,
        jnp.concatenate([mine, other], axis=axis),
        jnp.concatenate([other, mine], axis=axis),
    )


def on_device(
    tokens,
    seq_lengths,
    attention_gain,
    query_weight,
    key_weight,
    value_weight,
    out_weight,
    feedforward_gain,
    gate_weight,
    up_weight,
    down_weight,
    cotangent,
):
    c = lax.axis_index("cp")
    z = lax.axis_index("fsdp")
    sets = lax.axis_size("cp")
    count = lax.axis_size("fsdp")
    lanes = lax.axis_size("tp")
    slots, local, width = tokens.shape
    share = query_weight.shape[0]
    heads_width = query_weight.shape[1]
    head_count = heads_width // HD
    hidden_width = gate_weight.shape[1] // sets
    rows = sets * local
    seq = rows * lanes
    blocks = row_blocks(seq, sets, local)
    everyone = ("cp", "tp")

    def pick(value, which, axis=0):
        return lax.dynamic_index_in_dim(value, which, axis, keepdims=False)

    def to_sequence(value):
        mine = pick(value, c)
        other = swap(pick(value, 1 - c))
        return in_order(c, mine, other, 0)

    def from_sequence(value):
        value = value.reshape(sets, local, width)
        mine = pick(value, c)
        other = swap(pick(value, 1 - c))
        return in_order(c, mine[None], other[None], 0)

    token_rows = to_sequence(tokens)
    cotangent_rows = to_sequence(cotangent)
    upstream = cotangent_rows.astype(F32)
    length = pick(seq_lengths, c)[None]
    gain_one = attention_gain.astype(F32)
    gain_two = feedforward_gain.astype(F32)

    def normed_rows(values):
        return (normalize(values.astype(F32)) * gain_one).astype(BF)

    qkv = jnp.concatenate([query_weight, key_weight, value_weight], axis=1)
    wide = jnp.stack([gate_weight, up_weight, down_weight.T]).reshape(3, share, sets, hidden_width)
    own_wide = pick(wide, c, 2)
    normed_one, full_qkv, out_half, wide_low, wide_high = first_gather(
        count, normed_rows(tokens), qkv, out_weight.T, own_wide
    )
    normed_one = normed_one.reshape(seq, width)
    full_qkv = full_qkv.reshape(width, 3 * heads_width)
    out_other, wide_other = after((out_half, pick(wide, 1 - c, 2)), full_qkv)
    wide_other = swap(wide_other)
    full_out = in_order(c, out_half[:, None], swap(out_other)[:, None], 1)
    full_out = full_out.reshape(width, heads_width)

    cosine_table, sine_table = tables(seq)
    projected = matmul(normed_one, full_qkv)
    context, q_heads, k_heads, v_heads, level = attention(
        blocks, head_count, length, projected, cosine_table, sine_table
    )
    part = cols_inner(context, full_out).astype(BF)

    middle, normed_two, full_wide = second_gather(
        count, part.reshape(lanes, rows, width), token_rows, gain_two[None], own_wide,
        wide_low, wide_high, wide_other,
    )
    normed_two = normed_two.reshape(sets * seq, width)
    full_gate, full_up, full_down = full_wide.reshape(3, width, hidden_width)
    grad_branch = lax.all_gather((BRANCH * upstream).astype(BF), everyone, axis=0, tiled=True)
    gate_pre = matmul(normed_two, full_gate)
    up_pre = matmul(normed_two, full_up)
    hidden_exact, silu_back = jax.vjp(silu_product, gate_pre, up_pre)
    hidden = hidden_exact.astype(BF)

    def blocks_of(gradient):
        return gradient.astype(BF).reshape(count, width // count, hidden_width)

    down_blocks = blocks_of(rows_inner(grad_branch, hidden))
    grad_hidden = matmul(grad_branch, full_down)
    grad_gate_exact, grad_up_exact = silu_back(grad_hidden)
    grad_gate_pre = grad_gate_exact.astype(BF)
    grad_up_pre = grad_up_exact.astype(BF)
    grad_normed_two = cols_inner(grad_gate_pre, full_gate) + cols_inner(grad_up_pre, full_up)
    gate_blocks = blocks_of(rows_inner(normed_two, grad_gate_pre))
    up_blocks = blocks_of(rows_inner(normed_two, grad_up_pre))
    grad_middle, grad_attention, gain_two_rows, leaving = first_sum(
        count, grad_normed_two.astype(BF).reshape(sets, lanes, rows, width),
        gate_blocks, up_blocks, down_blocks, middle, cotangent_rows, gain_two[None],
    )
    grad_attention = grad_attention.reshape(seq, width)

    low = lax.ppermute(leaving[0], "fsdp", [(i, i + 1) for i in range(count - 1)])
    high = lax.ppermute(leaving[1], "fsdp", [(i, i - 1) for i in range(1, count)])

    def own_share(which, gradient):
        total = pick(gradient, z).astype(F32)
        if count > 1:
            total = total + low[which].astype(F32) + high[which].astype(F32)
        return total.reshape(sets, share, hidden_width)

    shares = [
        own_share(which, gradient)
        for which, gradient in enumerate((gate_blocks, up_blocks, down_blocks))
    ]
    others = swap(jnp.stack([pick(total, 1 - c).astype(BF) for total in shares]))
    grad_gate, grad_up, grad_down = (
        in_order(c, pick(total, c), others[which].astype(F32), 1)
        for which, total in enumerate(shares)
    )
    grad_down = grad_down.T

    out_pieces = rows_inner(grad_attention, context).astype(BF)
    out_pieces = out_pieces.reshape(count, sets, share, heads_width)
    out_pieces = (
        pick(out_pieces, c, 1).astype(F32) + swap(pick(out_pieces, 1 - c, 1)).astype(F32)
    ).astype(BF)
    grad_context = matmul(grad_attention, full_out).astype(BF)
    feedforward = lax.psum_scatter(
        cols_inner(after(hidden, grad_attention), full_down).astype(BF),
        everyone, scatter_dimension=0, tiled=True,
    )
    output = from_sequence((middle + BRANCH * feedforward.astype(F32)).astype(BF))
    grad_projected = attention_back(
        blocks, head_count, length, grad_context, q_heads, k_heads, v_heads, level,
        cosine_table, sine_table,
    )
    grad_qkv = rows_inner(normed_one, grad_projected).astype(BF)
    grad_qkv, grad_out, grad_tokens, gain_sums = last_sum(
        count, cols_inner(grad_projected, full_qkv).astype(BF).reshape(lanes, rows, width),
        grad_qkv.reshape(count, sets, share, 3 * heads_width), out_pieces,
        token_rows, grad_middle, gain_one[None], gain_two_rows,
    )
    return (
        output,
        grad_tokens,
        grad_qkv[:, :heads_width],
        grad_qkv[:, heads_width : 2 * heads_width],
        grad_qkv[:, 2 * heads_width :],
        grad_out.T,
        gain_sums[0],
        grad_gate,
        grad_up,
        grad_down,
        gain_sums[1],
    )


def solution(mesh):
    in_specs = (
        P("fsdp", ("cp", "tp"), None),
        P("fsdp"),
        P(),
        P(("fsdp", "cp"), "tp"),
        P(("fsdp", "cp"), "tp"),
        P(("fsdp", "cp"), "tp"),
        P("tp", ("fsdp", "cp")),
        P(),
        P(("fsdp", "cp"), "tp"),
        P(("fsdp", "cp"), "tp"),
        P("tp", ("fsdp", "cp")),
        P("fsdp", ("cp", "tp"), None),
    )
    out_specs = (
        P("fsdp", ("cp", "tp"), None),
        P("fsdp", ("cp", "tp"), None),
        P(("fsdp", "cp"), "tp"),
        P(("fsdp", "cp"), "tp"),
        P(("fsdp", "cp"), "tp"),
        P("tp", ("fsdp", "cp")),
        P(),
        P(("fsdp", "cp"), "tp"),
        P(("fsdp", "cp"), "tp"),
        P("tp", ("fsdp", "cp")),
        P(),
    )
    return jax.shard_map(
        on_device, mesh=mesh, in_specs=in_specs, out_specs=out_specs, check_vma=False
    )
```

```python
import functools
import math

import jax
import jax.numpy as jnp
import numpy as np
from jax import lax
from jax.experimental import pallas as pl
from jax.experimental.layout import Layout, with_layout_constraint
from jax.experimental.pallas import tpu as pltpu
from jax.sharding import PartitionSpec as P

HD = 64
EPSILON = 1e-05
BRANCH = 1.4 / math.sqrt(40.0)
BF = jnp.bfloat16
F32 = jnp.float32
TILE = 128
QUERY_ROWS = 256


def turned(values, cosine, sine):
    lane = lax.broadcasted_iota(jnp.int32, values.shape, 1)
    partner = jnp.where(
        lane % HD < HD // 2,
        pltpu.roll(values, TILE - HD // 2, 1),
        pltpu.roll(values, HD // 2, 1),
    )
    return values * cosine + partner * sine


def row_blocks(seq, sets, local):
    lanes = seq // sets // local
    return [
        ((t * sets + h) * local, (h * lanes + t) * local)
        for t in range(lanes)
        for h in range(sets)
    ]


def key_mask(length, first, rows, columns):
    place = first + lax.broadcasted_iota(jnp.int32, (rows, columns), 0)
    return place < length


def scores_of(keys, queries, length, first_query):
    raw = lax.dot_general(keys, queries, (((1,), (1,)), ((), ())), preferred_element_type=F32)
    key_place = lax.broadcasted_iota(jnp.int32, raw.shape, 0)
    query_place = first_query + lax.broadcasted_iota(jnp.int32, raw.shape, 1)
    return jnp.where((key_place <= query_place) & (key_place < length), raw, -1e30)


def attention_kernel(
    blocks, length_ref, projected, cosine, sine, context, q_heads, k_heads, v_heads, level, kept
):
    heads, seq, _ = q_heads.shape
    local = seq // len(blocks)
    length = length_ref[0]
    for gathered, ordered in blocks:
        source, target = pl.ds(gathered, local), pl.ds(ordered, local)
        for tile in range(-(-3 * heads // 2)):
            width = min(TILE, 3 * heads * HD - tile * TILE)
            values = projected[source, tile * TILE : tile * TILE + width]
            if tile * 2 < 2 * heads:
                values = turned(values, cosine[target, :], sine[target, :])
            for which in range(width // HD):
                index = tile * 2 + which
                piece = values[:, which * HD : (which + 1) * HD]
                if index < heads:
                    q_heads[index, target, :] = (piece * (1.0 / math.sqrt(HD))).astype(BF)
                elif index < 2 * heads:
                    k_heads[index - heads, target, :] = piece.astype(BF)
                else:
                    v_heads[index - 2 * heads, target, :] = piece.astype(BF)

    def one_head(head, carry):
        for first in range(0, seq, QUERY_ROWS):
            most = first + QUERY_ROWS
            queries = q_heads[head, first:most, :]
            keys = k_heads[head, :most, :]
            values = v_heads[head, :most, :]
            scores = scores_of(keys, queries, length, first)
            top = jnp.max(scores, axis=0, keepdims=True)
            exponent = jnp.exp(scores - top)
            total = jnp.sum(exponent, axis=0, keepdims=True)
            probabilities = (exponent * (1.0 / total)).astype(BF)
            level[head, :, first:most] = top + jnp.log(total)
            mixed = lax.dot_general(
                values, probabilities, (((0,), (0,)), ((), ())), preferred_element_type=F32
            )
            kept[head, first:most, :] = mixed.T.astype(BF)
        return carry

    lax.fori_loop(0, heads, one_head, 0)
    for gathered, ordered in blocks:
        source, target = pl.ds(ordered, local), pl.ds(gathered, local)
        for head in range(0, heads, 2):
            parts = [kept[index, source, :] for index in range(head, min(head + 2, heads))]
            joined = parts[0] if len(parts) == 1 else jnp.concatenate(parts, axis=1)
            context[target, head * HD : head * HD + joined.shape[1]] = joined


def attention(blocks, heads, length, projected, cosine, sine):
    seq = projected.shape[0]
    per_head = jax.ShapeDtypeStruct((heads, seq, HD), BF)
    vmem = pl.BlockSpec(memory_space=pltpu.VMEM)
    return pl.pallas_call(
        functools.partial(attention_kernel, blocks),
        out_shape=(
            jax.ShapeDtypeStruct((seq, heads * HD), BF),
            per_head,
            per_head,
            per_head,
            jax.ShapeDtypeStruct((heads, 1, seq), F32),
        ),
        in_specs=[pl.BlockSpec(memory_space=pltpu.SMEM), vmem, vmem, vmem],
        out_specs=(vmem,) * 5,
        scratch_shapes=[pltpu.VMEM((heads, seq, HD), BF)],
        compiler_params=pltpu.CompilerParams(vmem_limit_bytes=48 << 20),
        cost_estimate=pl.CostEstimate(
            flops=4 * heads * seq * seq * HD, transcendentals=heads * seq * seq, bytes_accessed=20 << 20
        ),
    )(length, projected, cosine, sine)


def attention_back_kernel(
    blocks, length_ref, grad_context, q_heads, k_heads, v_heads, level, cosine, sine,
    grad_projected, g_heads, dq, dk, dv,
):
    heads, seq, _ = q_heads.shape
    local = seq // len(blocks)
    length = length_ref[0]
    for gathered, ordered in blocks:
        source, target = pl.ds(gathered, local), pl.ds(ordered, local)
        for head in range(heads):
            g_heads[head, target, :] = grad_context[source, head * HD : (head + 1) * HD]

    def one_head(head, carry):
        keys_turned = k_heads[head].T
        for first in reversed(range(0, seq, QUERY_ROWS)):
            most = first + QUERY_ROWS
            queries = q_heads[head, first:most, :]
            upstream = g_heads[head, first:most, :]
            keys = k_heads[head, :most, :]
            values = v_heads[head, :most, :]
            scores = scores_of(keys, queries, length, first)
            probabilities = jnp.exp(scores - level[head, :, first:most])
            grad_probabilities = lax.dot_general(
                values, upstream, (((1,), (1,)), ((), ())), preferred_element_type=F32
            )
            weighted = probabilities * grad_probabilities
            balance = jnp.sum(weighted, axis=0, keepdims=True)
            grad_scores = (weighted - probabilities * balance).astype(BF)
            grad_keys = jnp.dot(grad_scores, queries, preferred_element_type=F32)
            grad_values = jnp.dot(
                probabilities.astype(BF), upstream, preferred_element_type=F32
            )
            if most == seq:
                dk[head, :, :] = grad_keys
                dv[head, :, :] = grad_values
            else:
                dk[head, :most, :] += grad_keys
                dv[head, :most, :] += grad_values
            grad_queries = jnp.dot(
                keys_turned[:, :most], grad_scores, preferred_element_type=F32
            )
            dq[head, first:most, :] = grad_queries.T * (1.0 / math.sqrt(HD))
        return carry

    lax.fori_loop(0, heads, one_head, 0)
    sources = [dq] * heads + [dk] * heads + [dv] * heads
    for gathered, ordered in blocks:
        source, target = pl.ds(ordered, local), pl.ds(gathered, local)
        for tile in range(-(-3 * heads // 2)):
            indices = range(tile * 2, min(tile * 2 + 2, 3 * heads))
            parts = [sources[index][index % heads, source, :] for index in indices]
            joined = parts[0] if len(parts) == 1 else jnp.concatenate(parts, axis=1)
            if tile * 2 < 2 * heads:
                joined = turned(joined, cosine[source, :], -sine[source, :])
            grad_projected[target, tile * TILE : tile * TILE + joined.shape[1]] = joined.astype(BF)


def attention_back(blocks, heads, length, grad_context, q_heads, k_heads, v_heads, level, cosine, sine):
    seq = grad_context.shape[0]
    vmem = pl.BlockSpec(memory_space=pltpu.VMEM)
    return pl.pallas_call(
        functools.partial(attention_back_kernel, blocks),
        out_shape=jax.ShapeDtypeStruct((seq, 3 * heads * HD), BF),
        in_specs=[pl.BlockSpec(memory_space=pltpu.SMEM)] + [vmem] * 7,
        out_specs=vmem,
        scratch_shapes=[
            pltpu.VMEM((heads, seq, HD), BF),
            pltpu.VMEM((heads, seq, HD), F32),
            pltpu.VMEM((heads, seq, HD), F32),
            pltpu.VMEM((heads, seq, HD), F32),
        ],
        compiler_params=pltpu.CompilerParams(vmem_limit_bytes=56 << 20),
        cost_estimate=pl.CostEstimate(
            flops=10 * heads * seq * seq * HD, transcendentals=heads * seq * seq, bytes_accessed=20 << 20
        ),
    )(length, grad_context, q_heads, k_heads, v_heads, level, cosine, sine)


def tables(seq):
    step = np.arange(HD // 2, dtype=np.float32)
    frequency = np.power(np.float32(10000.0), np.float32(-2.0) * step / np.float32(HD))
    angle = np.arange(seq, dtype=np.float32)[:, None] * frequency[None, :]
    cosine, sine = np.cos(angle), np.sin(angle)
    signed = np.concatenate([-sine, sine, -sine, sine], axis=1)
    return jnp.asarray(np.tile(cosine, (1, 4))), jnp.asarray(signed)


MESH = pl.DeviceIdType.MESH


def greet(count):
    barrier = pltpu.get_barrier_semaphore()
    z, c, t = lax.axis_index("fsdp"), lax.axis_index("cp"), lax.axis_index("tp")

    def hello(**place):
        pl.semaphore_signal(barrier, inc=1, device_id=place, device_id_type=MESH)

    hello(cp=1 - c)
    hello(tp=t + 1 - 2 * (t % 2))
    hello(tp=(t + 2) % 4)
    pl.when(z > 0)(lambda: hello(fsdp=z - 1))
    pl.when(z < count - 1)(lambda: hello(fsdp=z + 1))
    peers = 3 + jnp.minimum(z, 1) + jnp.minimum(count - 1 - z, 1)
    pl.semaphore_wait(barrier, peers)


class Mail:
    def __init__(self, send, recv):
        self.send, self.recv, self.used, self.open = send, recv, 0, []

    def slot(self):
        self.used += 1
        return self.used - 1

    def copy(self, slot, source, target, **place):
        return pltpu.make_async_remote_copy(
            src_ref=source,
            dst_ref=target,
            send_sem=self.send.at[slot],
            recv_sem=self.recv.at[slot],
            device_id=place,
            device_id_type=MESH,
        )

    def start(self, slot, source, target, when=None, **place):
        made = self.copy(slot, source, target, **place)
        if when is None:
            made.start()
        else:
            pl.when(when)(made.start)
        self.open.append((made, when))

    def arrive(self, slot, target, when=None, **place):
        made = self.copy(slot, target, target, **place)
        if when is None:
            made.wait_recv()
        else:
            pl.when(when)(made.wait_recv)

    def finish(self):
        for made, when in self.open:
            if when is None:
                made.wait_send()
            else:
                pl.when(when)(made.wait_send)


class Line:
    def __init__(self, mail, count, own, at, ready=()):
        self.mail, self.count, self.own, self.at = mail, count, own, at
        self.ready = ready
        self.z = lax.axis_index("fsdp")
        self.up = [mail.slot() for _ in range(count)]
        self.down = [mail.slot() for _ in range(count)]

    def has_low(self, hop):
        return self.z >= hop

    def has_high(self, hop):
        return self.z <= self.count - 1 - hop

    def send(self, hop):
        z, count, mail = self.z, self.count, self.mail
        low, high = jnp.maximum(z - hop + 1, 0), jnp.minimum(z + hop - 1, count - 1)
        from_low = from_high = self.own
        if hop > 1:
            from_low, from_high = self.at(low), self.at(high)
        if 0 < hop - 1 <= len(self.ready):
            from_low, from_high = self.ready[hop - 2]
        mail.start(
            self.up[hop], from_low, self.at(low),
            when=(z >= hop - 1) & (z < count - 1), fsdp=jnp.minimum(z + 1, count - 1),
        )
        mail.start(
            self.down[hop], from_high, self.at(high),
            when=(z <= count - hop) & (z > 0), fsdp=jnp.maximum(z - 1, 0),
        )

    def arrive(self, hop):
        z, count = self.z, self.count
        self.mail.arrive(
            self.up[hop], self.at(jnp.maximum(z - hop, 0)), when=self.has_low(hop), fsdp=z
        )
        self.mail.arrive(
            self.down[hop], self.at(jnp.minimum(z + hop, count - 1)), when=self.has_high(hop), fsdp=z
        )


    def keep(self, local, first):
        z, count = self.z, self.count
        made = [(pltpu.make_async_copy(self.own, self.at(z), local.at[first]), None)]
        for index, (low, high) in enumerate(self.ready):
            hop, place = index + 1, first + 2 * index + 1
            to_low, to_high = jnp.maximum(z - hop, 0), jnp.minimum(z + hop, count - 1)
            made.append(
                (pltpu.make_async_copy(low, self.at(to_low), local.at[place]), self.has_low(hop))
            )
            made.append(
                (
                    pltpu.make_async_copy(high, self.at(to_high), local.at[place + 1]),
                    self.has_high(hop),
                )
            )
        return made


class Across:
    def __init__(self, line, own, mine_at, other_at):
        self.line, self.own, self.mine_at, self.other_at = line, own, mine_at, other_at
        self.c = lax.axis_index("cp")
        self.low = [line.mail.slot() for _ in range(line.count)]
        self.high = [line.mail.slot() for _ in range(line.count)]

    def send(self, hop):
        line, mail = self.line, self.line.mail
        z, count, other = line.z, line.count, 1 - self.c
        if hop == 0:
            mail.start(self.low[0], self.own, self.mine_at(z), cp=other)
            return
        low, high = jnp.maximum(z - hop, 0), jnp.minimum(z + hop, count - 1)
        mail.start(self.low[hop], self.mine_at(low), self.mine_at(low), when=line.has_low(hop), cp=other)
        mail.start(self.high[hop], self.mine_at(high), self.mine_at(high), when=line.has_high(hop), cp=other)

    def arrive(self, hop):
        line, mail = self.line, self.line.mail
        z, count, other = line.z, line.count, 1 - self.c
        if hop == 0:
            mail.arrive(self.low[0], self.other_at(z), cp=other)
            return
        low, high = jnp.maximum(z - hop, 0), jnp.minimum(z + hop, count - 1)
        mail.arrive(self.low[hop], self.other_at(low), when=line.has_low(hop), cp=other)
        mail.arrive(self.high[hop], self.other_at(high), when=line.has_high(hop), cp=other)


def first_gather_kernel(
    count, tokens, tokens_away, gain, qkv, turned_out, wide, wide_away,
    token_rows, normed_full, qkv_full, out_half, low_pair, high_pair,
    landed, normed, send, recv, local,
):
    z, c, t = lax.axis_index("fsdp"), lax.axis_index("cp"), lax.axis_index("tp")
    beside, yonder = t + 1 - 2 * (t % 2), (t + 2) % 4
    low, high, wide_other = low_pair.at[0], high_pair.at[0], low_pair.at[1]
    mail = Mail(send, recv)
    greet(count)
    kept = [
        pltpu.make_async_copy(qkv, qkv_full.at[z, c], local.at[0]),
        pltpu.make_async_copy(turned_out, out_half.at[z], local.at[1]),
    ]
    for copy in kept:
        copy.start()

    heads = Line(mail, count, qkv, lambda j: qkv_full.at[j, c])
    heads_across = Across(
        heads, qkv, lambda j: qkv_full.at[j, c], lambda j: qkv_full.at[j, 1 - c]
    )
    outs = Line(mail, count, turned_out, lambda j: out_half.at[j])
    wide_up, wide_down = mail.slot(), mail.slot()
    rows_x, wide_x = mail.slot(), mail.slot()
    rows_y = [mail.slot() for _ in range(2)]
    rows_core = [mail.slot() for _ in range(4)]

    mail.start(rows_x, tokens_away, landed, cp=1 - c)
    heads.send(1)
    heads_across.send(0)

    def rows_out(source, side, half):
        def one(place):
            rows = source[place, :]
            token_rows[half, place, :] = rows
            normed[half, place, :] = (normalize(rows.astype(F32)) * gain[...]).astype(BF)

        in_pieces(source.shape[0], one)
        mail.start(rows_y[side], normed.at[half], normed_full.at[t, half], tp=yonder)
        mail.start(rows_core[side], normed.at[half], normed_full.at[t, half], tp=beside)

    rows_out(tokens, 0, c)
    mail.arrive(rows_x, landed, cp=1 - c)
    rows_out(landed, 1, 1 - c)
    kept.append(pltpu.make_async_copy(normed, normed_full.at[t], local.at[2]))
    kept[-1].start()

    def rows_on(k, half):
        mail.arrive(rows_y[k], normed_full.at[yonder, half], tp=yonder)
        mail.start(
            rows_core[2 + k], normed_full.at[yonder, half], normed_full.at[yonder, half], tp=beside
        )

    for hop in range(1, count):
        heads.arrive(hop)
        if hop + 1 < count:
            heads.send(hop + 1)
        if hop > 1:
            outs.arrive(hop - 1)
        outs.send(hop)
        heads_across.send(hop)
        if hop == min(2, count - 1):
            mail.start(wide_x, wide_away, wide_other, cp=1 - c)
        if hop == 1:
            rows_on(0, c)
            rows_on(1, 1 - c)
    mail.start(wide_up, wide, low, when=z < count - 1, fsdp=jnp.minimum(z + 1, count - 1))
    mail.start(wide_down, wide, high, when=z > 0, fsdp=jnp.maximum(z - 1, 0))
    if count > 1:
        outs.arrive(count - 1)
    for hop in range(count):
        heads_across.arrive(hop)
    mail.arrive(rows_core[0], normed_full.at[beside, c], tp=beside)
    mail.arrive(rows_core[1], normed_full.at[beside, 1 - c], tp=beside)
    far = (beside + 2) % 4
    mail.arrive(rows_core[2], normed_full.at[far, c], tp=beside)
    mail.arrive(rows_core[3], normed_full.at[far, 1 - c], tp=beside)
    mail.arrive(wide_x, wide_other, cp=1 - c)
    kept.append(pltpu.make_async_copy(wide_other, high_pair.at[1], local.at[3]))
    kept[-1].start()
    mail.arrive(wide_up, low, when=z > 0, fsdp=z)
    mail.arrive(wide_down, high, when=z < count - 1, fsdp=z)
    for copy in kept:
        copy.wait()
    mail.finish()


def first_gather(count, tokens, tokens_away, gain, qkv, turned_out, wide, wide_away):
    slots = 6 * count + 10
    anywhere = pl.BlockSpec(memory_space=pl.ANY)
    vmem = pl.BlockSpec(memory_space=pltpu.VMEM)
    pair = (2,) + tokens.shape
    return pl.pallas_call(
        functools.partial(first_gather_kernel, count),
        out_shape=(
            jax.ShapeDtypeStruct(pair, BF),
            jax.ShapeDtypeStruct((4,) + pair, BF),
            jax.ShapeDtypeStruct((count, 2) + qkv.shape, BF),
            jax.ShapeDtypeStruct((count,) + turned_out.shape, BF),
            jax.ShapeDtypeStruct((2,) + wide.shape, BF),
            jax.ShapeDtypeStruct((2,) + wide.shape, BF),
        ),
        in_specs=[vmem, anywhere, vmem] + [anywhere] * 4,
        out_specs=(vmem,) + (anywhere,) * 5,
        scratch_shapes=[
            pltpu.VMEM(tokens.shape, BF),
            pltpu.VMEM(pair, BF),
            pltpu.SemaphoreType.DMA((slots,)),
            pltpu.SemaphoreType.DMA((slots,)),
            pltpu.SemaphoreType.DMA((4,)),
        ],
        compiler_params=pltpu.CompilerParams(collective_id=1, has_side_effects=True),
    )(tokens, tokens_away, gain, qkv, turned_out, wide, wide_away)


def in_pieces(rows, body, size=16):
    if rows % size:
        body(pl.ds(0, rows))
        return
    lax.fori_loop(0, rows // size, lambda i, carry: (body(pl.ds(i * size, size)), carry)[1], 0)


class Spread:
    def __init__(self, mail, own, at):
        self.mail, self.own, self.at = mail, own, at
        self.c, self.t = lax.axis_index("cp"), lax.axis_index("tp")
        self.beside, self.yonder = self.t + 1 - 2 * (self.t % 2), (self.t + 2) % 4
        self.x = [mail.slot() for _ in range(3)]
        self.y = [mail.slot() for _ in range(3)]
        self.core = {}

    def to_core(self, c_is_own, t_is_own, piece):
        slot = self.core[c_is_own, t_is_own, piece] = self.mail.slot()
        c = self.c if c_is_own else 1 - self.c
        t = self.t if t_is_own else self.yonder
        source = self.own(piece) if c_is_own and t_is_own else self.at(c, t, piece)
        self.mail.start(slot, source, self.at(c, t, piece), tp=self.beside)

    def begin(self, piece):
        c, t = self.c, self.t
        if piece == 0:
            self.mail.start(self.x[0], self.own(0), self.at(c, t, 0), cp=1 - c)
        else:
            self.mail.start(self.y[0], self.own(1), self.at(c, t, 1), tp=self.yonder)
            self.mail.start(self.x[1], self.own(1), self.at(c, t, 1), cp=1 - c)
            self.mail.start(self.y[1], self.own(0), self.at(c, t, 0), tp=self.yonder)
        self.to_core(True, True, piece)

    def turn(self):
        c, t, mail, yonder = self.c, self.t, self.mail, self.yonder
        mail.arrive(self.x[0], self.at(1 - c, t, 0), cp=1 - c)
        mail.start(self.y[2], self.at(1 - c, t, 0), self.at(1 - c, t, 0), tp=yonder)
        self.to_core(False, True, 0)
        mail.arrive(self.y[0], self.at(c, yonder, 1), tp=yonder)
        mail.start(self.x[2], self.at(c, yonder, 1), self.at(c, yonder, 1), cp=1 - c)
        self.to_core(True, False, 1)

    def end(self):
        c, t, mail, yonder = self.c, self.t, self.mail, self.yonder
        mail.arrive(self.x[1], self.at(1 - c, t, 1), cp=1 - c)
        self.to_core(False, True, 1)
        mail.arrive(self.y[1], self.at(c, yonder, 0), tp=yonder)
        self.to_core(True, False, 0)
        mail.arrive(self.x[2], self.at(1 - c, yonder, 1), cp=1 - c)
        self.to_core(False, False, 1)
        mail.arrive(self.y[2], self.at(1 - c, yonder, 0), tp=yonder)
        self.to_core(False, False, 0)
        far = (self.beside + 2) % 4
        for (c_is_own, t_is_own, piece), slot in self.core.items():
            place = self.at(
                c if c_is_own else 1 - c, self.beside if t_is_own else far, piece
            )
            mail.arrive(slot, place, tp=self.beside)


def second_gather_kernel(
    count, part, tokens, gain, wide, first_low, first_high, second_low, second_high, *refs
):
    hops_mine, hops_other = min(2, count - 1), 1
    wide_other = first_low.at[1]
    ready_mine = [first_low.at[0], first_high.at[0], second_low.at[0], second_high.at[0]]
    ready_mine = ready_mine[: 2 * hops_mine]
    ready_other = [second_low.at[1], second_high.at[1]]
    middle, normed_full, gate_full, up_full, down_full = refs[:5]
    own, from_core, to_yonder, from_yonder, normed, send, recv, local, local_line = refs[5:]
    c, t = lax.axis_index("cp"), lax.axis_index("tp")
    rows = tokens.shape[0]
    half = rows // 2
    mail = Mail(send, recv)
    greet(count)

    mine, other = [], []
    for which, full in enumerate((gate_full, up_full, down_full)):
        for lines, side, piece, ready in (
            (mine, c, wide, ready_mine), (other, 1 - c, wide_other, ready_other),
        ):
            arrived = [
                (ready[2 * hop].at[which], ready[2 * hop + 1].at[which])
                for hop in range(len(ready) // 2)
            ]
            lines.append(
                Line(
                    mail, count, piece.at[which],
                    lambda j, full=full, side=side: full.at[j, side], arrived,
                )
            )
    summed = TensorSum(mail, part, own, from_core, to_yonder, from_yonder, local)
    spread = Spread(
        mail, lambda piece: normed.at[piece], lambda c, t, piece: normed_full.at[piece, t, c]
    )

    summed.begin()
    kept = []
    for lines, hops in ((mine, hops_mine), (other, hops_other)):
        for line in lines:
            kept += line.keep(local_line, len(kept))
    for copy, when in kept:
        copy.start() if when is None else pl.when(when)(copy.start)

    def send_hop(lines, hop):
        for line in lines:
            if hop < count:
                line.send(hop)

    def arrive_hop(lines, hop):
        for line in lines:
            if hop < count:
                line.arrive(hop)

    send_hop(other, hops_other + 1)
    send_hop(mine, hops_mine + 1)
    summed.turn()
    for piece in range(2):
        summed.arrive(piece)

        def norm(place, piece=piece):
            row = pl.ds(place.start + piece * half, place.size)
            values = tokens[row, :].astype(F32) + BRANCH * summed.rows(row)
            middle[row, :] = values
            normed[piece, place, :] = (normalize(values) * gain[...]).astype(BF)

        in_pieces(half, norm)
        spread.begin(piece)
    keep_normed = pltpu.make_async_copy(normed, normed_full.at[:, t, c], local.at[0])
    keep_normed.start()
    spread.turn()
    for step in range(1, count):
        hop = hops_other + step
        if hop < count:
            for line_other, line_mine in zip(other, mine):
                line_other.arrive(hop)
                if hop + 1 < count:
                    line_other.send(hop + 1)
                if hops_mine + step < count:
                    line_mine.arrive(hops_mine + step)
                    if hops_mine + step + 1 < count:
                        line_mine.send(hops_mine + step + 1)
        if step == 1:
            spread.end()
    if count == 1:
        spread.end()
    keep_normed.wait()
    for copy, when in kept:
        copy.wait() if when is None else pl.when(when)(copy.wait)
    mail.finish()


def second_gather(count, part, tokens, gain, wide, first_low, first_high, second_low, second_high):
    slots = 12 * count + 20
    rows, width = tokens.shape
    anywhere = pl.BlockSpec(memory_space=pl.ANY)
    vmem = pl.BlockSpec(memory_space=pltpu.VMEM)
    full = jax.ShapeDtypeStruct((count, 2) + wide.shape[1:], BF)
    return pl.pallas_call(
        functools.partial(second_gather_kernel, count),
        out_shape=(
            jax.ShapeDtypeStruct((rows, width), F32),
            jax.ShapeDtypeStruct((2, 4, 2, rows // 2, width), BF),
            full,
            full,
            full,
        ),
        in_specs=[anywhere, vmem, vmem] + [anywhere] * 5,
        out_specs=(vmem,) + (anywhere,) * 4,
        scratch_shapes=[
            pltpu.VMEM((2, rows, width), BF),
            pltpu.VMEM((2, rows, width), BF),
            pltpu.VMEM((rows, width), BF),
            pltpu.VMEM((rows, width), BF),
            pltpu.VMEM((2, rows // 2, width), BF),
            pltpu.SemaphoreType.DMA((slots,)),
            pltpu.SemaphoreType.DMA((slots,)),
            pltpu.SemaphoreType.DMA((2,)),
            pltpu.SemaphoreType.DMA((24,)),
        ],
        compiler_params=pltpu.CompilerParams(
            collective_id=2, has_side_effects=True, vmem_limit_bytes=40 << 20
        ),
    )(part, tokens, gain, wide, first_low, first_high, second_low, second_high)


class TensorSum:
    def __init__(self, mail, part, own, from_core, to_yonder, from_yonder, local):
        self.mail, self.part, self.own, self.from_core = mail, part, own, from_core
        self.to_yonder, self.from_yonder, self.local = to_yonder, from_yonder, local
        self.t = t = lax.axis_index("tp")
        self.beside, self.yonder = t + 1 - 2 * (t % 2), (t + 2) % 4
        self.core = [mail.slot() for _ in range(2)]
        self.across = [mail.slot() for _ in range(2)]
        self.half = from_yonder.shape[0] // 2

    def begin(self):
        part, far = self.part, (self.beside + 2) % 4
        self.mail.start(self.core[1], part.at[far], self.from_core.at[1], tp=self.beside)
        self.mail.start(self.core[0], part.at[self.beside], self.from_core.at[0], tp=self.beside)
        self.kept = [
            pltpu.make_async_copy(part.at[self.yonder], self.own.at[1], self.local.at[0]),
            pltpu.make_async_copy(part.at[self.t], self.own.at[0], self.local.at[1]),
        ]
        for copy in self.kept:
            copy.start()

    def turn(self):
        own, from_core = self.own, self.from_core
        self.kept[0].wait()
        self.mail.arrive(self.core[1], from_core.at[1], tp=self.beside)
        for piece in range(2):

            def add(place, piece=piece):
                place = pl.ds(place.start + piece * self.half, place.size)
                self.to_yonder[place, :] = (
                    own[1, place, :].astype(F32) + from_core[1, place, :].astype(F32)
                ).astype(BF)

            in_pieces(self.half, add)
            block = pl.ds(piece * self.half, self.half)
            self.mail.start(
                self.across[piece], self.to_yonder.at[block], self.from_yonder.at[block],
                tp=self.yonder,
            )
        self.kept[1].wait()
        self.mail.arrive(self.core[0], from_core.at[0], tp=self.beside)

    def arrive(self, piece):
        block = pl.ds(piece * self.half, self.half)
        self.mail.arrive(self.across[piece], self.from_yonder.at[block], tp=self.yonder)

    def rows(self, row):
        return (
            self.own[0, row, :].astype(F32)
            + self.from_core[0, row, :].astype(F32)
            + self.from_yonder[row, :].astype(F32)
        )


class Drain:
    def __init__(self, mail, count, fill, total, landed):
        self.mail, self.count, self.fill, self.total, self.landed = mail, count, fill, total, landed
        self.z = lax.axis_index("fsdp")
        self.slots = [[mail.slot() for _ in range(count)] for _ in range(2)]

    def sends(self, hop, up):
        z, count = self.z, self.count
        return (z <= hop - 1) & (z < count - 1) if up else (z >= count - hop) & (z > 0)

    def gets(self, hop, up):
        z, count = self.z, self.count
        return (z >= 1) & (z <= hop) if up else (z <= count - 2) & (z >= count - 1 - hop)

    def block(self, hop, up):
        z, count = self.z, self.count
        return jnp.minimum(z + count - hop, count - 1) if up else jnp.maximum(z - count + hop, 0)

    def arrive(self, hop):
        for side, up in enumerate((True, False)):
            self.mail.arrive(
                self.slots[side][hop], self.landed(side, hop), when=self.gets(hop, up), fsdp=self.z
            )

    def gather(self, hop):
        for side, up in enumerate((True, False)):
            target = self.total(side, hop)

            def work(side=side, up=up, target=target):
                self.fill(hop, up, self.block(hop, up), target)
                if hop > 1:

                    def add():
                        landed = self.landed(side, hop - 1)

                        def one(place):
                            target[place, :] = (
                                target[place, :].astype(F32) + landed[place, :].astype(F32)
                            ).astype(BF)

                        in_pieces(target.shape[0], one)

                    pl.when(self.gets(hop - 1, up))(add)

            pl.when(self.sends(hop, up))(work)

    def send(self, hop):
        z, count = self.z, self.count
        for side, up in enumerate((True, False)):
            to = jnp.minimum(z + 1, count - 1) if up else jnp.maximum(z - 1, 0)
            self.mail.start(
                self.slots[side][hop], self.total(side, hop), self.landed(side, hop),
                when=self.sends(hop, up), fsdp=to,
            )


def norm_back(values, gain, upstream):
    scale = lax.rsqrt(jnp.mean(values * values, axis=-1, keepdims=True) + EPSILON)
    norm = values * scale
    scaled = upstream * gain
    mean = jnp.mean(scaled * norm, axis=-1, keepdims=True)
    return scale * (scaled - norm * mean), upstream * norm


def first_sum_kernel(
    count, part, gate_grad, up_grad, middle, cotangent, gain,
    grad_middle, attention_full, gain_rows, leaving_up, leaving_down,
    own, from_core, first, second, grad_attention, totals, landed,
    send, recv, local,
):
    z, c, t = lax.axis_index("fsdp"), lax.axis_index("cp"), lax.axis_index("tp")
    beside, yonder = t + 1 - 2 * (t % 2), (t + 2) % 4
    far = (beside + 2) % 4
    half = middle.shape[0] // 2
    width = middle.shape[1]
    mail = Mail(send, recv)
    greet(count)
    last = count - 1

    def fill_from(which):
        def fill(hop, up, j, target):
            copy = pltpu.make_async_copy((gate_grad, up_grad)[which].at[j], target, local.at[4])
            copy.start()
            copy.wait()

        return fill

    drains = [
        Drain(
            mail, count, fill_from(which),
            lambda side, hop, which=which: (
                (leaving_up, leaving_down)[side].at[which] if hop == last else totals.at[side, hop - 1, which]
            ),
            lambda side, hop, which=which: landed.at[side, hop - 1, which],
        )
        for which in range(2)
    ]

    core = {}
    mine = {}
    order = ((1, 0), (0, 0), (0, 1), (1, 1))
    for index, (c_own, t_own) in enumerate(order):
        block_c = c if c_own else 1 - c
        core[c_own, t_own] = mail.slot()
        mail.start(
            core[c_own, t_own], part.at[:, beside if t_own else far, block_c],
            from_core.at[c_own, t_own], tp=beside,
        )
        mine[c_own, t_own] = pltpu.make_async_copy(
            part.at[:, t if t_own else yonder, block_c], own.at[c_own, t_own], local.at[index]
        )
        mine[c_own, t_own].start()
    if last > 1:
        for drain in drains:
            drain.gather(1)
            drain.send(1)
    for c_own, t_own in order:
        mine[c_own, t_own].wait()
        mail.arrive(core[c_own, t_own], from_core.at[c_own, t_own], tp=beside)
        for piece in range(2):

            def add(place, c_own=c_own, t_own=t_own, piece=piece):
                own[c_own, t_own, piece, place, :] = (
                    own[c_own, t_own, piece, place, :].astype(F32)
                    + from_core[c_own, t_own, piece, place, :].astype(F32)
                ).astype(BF)

            in_pieces(half, add)

    y_first = [mail.slot() for _ in range(2)]
    x_first = [mail.slot() for _ in range(2)]
    x_second, y_second = mail.slot(), mail.slot()
    for c_own in (0, 1):
        mail.start(y_first[c_own], own.at[c_own, 0, 0], first.at[0, c_own], tp=yonder)
    for t_own in (0, 1):
        mail.start(x_first[t_own], own.at[0, t_own, 1], first.at[1, t_own], cp=1 - c)

    def add_first(side, index, c_own, t_own):
        def one(place):
            own[c_own, t_own, side, place, :] = (
                own[c_own, t_own, side, place, :].astype(F32)
                + first[side, index, place, :].astype(F32)
            ).astype(BF)

        in_pieces(half, one)

    mail.arrive(y_first[0], first.at[0, 0], tp=yonder)
    add_first(0, 0, 0, 1)
    mail.start(x_second, own.at[0, 1, 0], second.at[0], cp=1 - c)
    mail.arrive(x_first[0], first.at[1, 0], cp=1 - c)
    add_first(1, 0, 1, 0)
    mail.start(y_second, own.at[1, 0, 1], second.at[1], tp=yonder)
    mail.arrive(y_first[1], first.at[0, 1], tp=yonder)
    add_first(0, 1, 1, 1)
    mail.arrive(x_first[1], first.at[1, 1], cp=1 - c)
    add_first(1, 1, 1, 1)

    gain_rows[...] = jnp.zeros_like(gain_rows)
    ring_y = [mail.slot() for _ in range(2)]
    ring_core = [mail.slot() for _ in range(4)]
    keep = []
    for piece in range(2):
        if piece == 0:
            mail.arrive(x_second, second.at[0], cp=1 - c)
        else:
            mail.arrive(y_second, second.at[1], tp=yonder)

        def back(place, piece=piece):
            row = pl.ds(place.start + piece * half, place.size)
            summed = own[1, 1, piece, place, :].astype(F32) + second[piece, place, :].astype(F32)
            grad, rows = norm_back(middle[row, :], gain[...], summed)
            grad = cotangent[row, :].astype(F32) + grad
            grad_middle[row, :] = grad
            grad_attention[piece, place, :] = (BRANCH * grad).astype(BF)
            gain_rows[...] += jnp.sum(rows, axis=0, keepdims=True)

        in_pieces(half, back)
        mail.start(ring_y[piece], grad_attention.at[piece], attention_full.at[t, piece], tp=yonder)
        mail.start(
            ring_core[piece], grad_attention.at[piece], attention_full.at[t, piece], tp=beside
        )
    keep = pltpu.make_async_copy(grad_attention, attention_full.at[t], local.at[0])
    keep.start()
    for hop in range(2, last):
        for drain in drains:
            drain.arrive(hop - 1)
            drain.gather(hop)
            drain.send(hop)
    for piece in range(2):
        mail.arrive(ring_y[piece], attention_full.at[yonder, piece], tp=yonder)
        mail.start(
            ring_core[2 + piece], attention_full.at[yonder, piece],
            attention_full.at[yonder, piece], tp=beside,
        )
    for piece in range(2):
        mail.arrive(ring_core[piece], attention_full.at[beside, piece], tp=beside)
        mail.arrive(ring_core[2 + piece], attention_full.at[far, piece], tp=beside)
    for drain in drains:
        if last > 1:
            drain.arrive(last - 1)
        if last > 0:
            drain.gather(last)
    keep.wait()
    mail.finish()


def first_sum(count, part, gate_grad, up_grad, middle, cotangent, gain):
    slots = 6 * count + 24
    rows, width = middle.shape
    block = gate_grad.shape[1:]
    anywhere = pl.BlockSpec(memory_space=pl.ANY)
    vmem = pl.BlockSpec(memory_space=pltpu.VMEM)
    hops = max(count - 2, 1)
    return pl.pallas_call(
        functools.partial(first_sum_kernel, count),
        out_shape=(
            jax.ShapeDtypeStruct((rows, width), F32),
            jax.ShapeDtypeStruct((4, 2, rows // 2, width), BF),
            jax.ShapeDtypeStruct((1, width), F32),
            jax.ShapeDtypeStruct((2,) + block, BF),
            jax.ShapeDtypeStruct((2,) + block, BF),
        ),
        in_specs=[anywhere] * 3 + [vmem] * 3,
        out_specs=(vmem, anywhere, vmem, vmem, vmem),
        scratch_shapes=[
            pltpu.VMEM((2, 2, 2, rows // 2, width), BF),
            pltpu.VMEM((2, 2, 2, rows // 2, width), BF),
            pltpu.VMEM((2, 2, rows // 2, width), BF),
            pltpu.VMEM((2, rows // 2, width), BF),
            pltpu.VMEM((2, rows // 2, width), BF),
            pltpu.VMEM((2, hops, 2) + block, BF),
            pltpu.VMEM((2, hops, 2) + block, BF),
            pltpu.SemaphoreType.DMA((slots,)),
            pltpu.SemaphoreType.DMA((slots,)),
            pltpu.SemaphoreType.DMA((5,)),
        ],
        compiler_params=pltpu.CompilerParams(
            collective_id=3, has_side_effects=True, vmem_limit_bytes=60 << 20
        ),
    )(part, gate_grad, up_grad, middle, cotangent, gain)


def last_sum_kernel(
    count, part, qkv_grad, out_grad, tokens, grad_middle, gain, gain_rows,
    qkv_total, out_total, grad_tokens, gain_sums,
    own, from_core, to_yonder, from_yonder, pieces,
    from_x, heads_sum, heads_landed, outs_sum, outs_landed, final_out, gains, gain_line,
    send, recv, local,
):
    z, c, t = lax.axis_index("fsdp"), lax.axis_index("cp"), lax.axis_index("tp")
    beside, yonder = t + 1 - 2 * (t % 2), (t + 2) % 4
    half = tokens.shape[0] // 2
    last = count - 1
    mail = Mail(send, recv)
    greet(count)

    summed = TensorSum(mail, part, own, from_core, to_yonder, from_yonder, local)

    cross = [[mail.slot() for _ in range(count)] for _ in range(2)]
    cross_own = mail.slot()

    def fill_heads(hop, up, j, target):
        side = 0 if up else 1
        copy = pltpu.make_async_copy(qkv_grad.at[j, c], target, local.at[2])
        copy.start()
        mail.arrive(cross[side][hop], from_x.at[side, hop - 1], cp=1 - c)
        copy.wait()

        def one(place):
            target[place, :] = (
                target[place, :].astype(F32) + from_x[side, hop - 1, place, :].astype(F32)
            ).astype(BF)

        in_pieces(target.shape[0], one)

    heads = Drain(
        mail, count, fill_heads,
        lambda side, hop: heads_sum.at[side, hop - 1],
        lambda side, hop: heads_landed.at[side, hop - 1],
    )

    def fill_outs(hop, up, j, target):
        copy = pltpu.make_async_copy(out_grad.at[j], target, local.at[3])
        copy.start()
        copy.wait()

    outs = Drain(
        mail, count, fill_outs,
        lambda side, hop: outs_sum.at[side, hop - 1],
        lambda side, hop: outs_landed.at[side, hop - 1],
    )

    def cross_send(hop):
        if hop == count:
            mail.start(cross_own, qkv_grad.at[z, 1 - c], from_x.at[0, last], cp=1 - c)
        elif hop < count:
            for side, up in enumerate((True, False)):
                mail.start(
                    cross[side][hop], qkv_grad.at[heads.block(hop, up), 1 - c],
                    from_x.at[side, hop - 1], when=heads.sends(hop, up), cp=1 - c,
                )

    cross_send(1)
    cross_send(2)
    summed.begin()
    outs.gather(1)
    outs.send(1)
    summed.turn()

    keep = pltpu.make_async_copy(pieces.at[c], grad_tokens.at[c], local.at[0])
    home = mail.slot()
    gain_x, gain_y, gain_core = mail.slot(), mail.slot(), mail.slot()
    line = Line(mail, count, gain_line.at[z], lambda j: gain_line.at[j])

    def finish_rows():
        gains[0, 0:1, :] = jnp.zeros_like(gain_rows)
        gains[0, 1:2, :] = gain_rows[...]
        for piece in range(2):
            summed.arrive(piece)

            def back(place, piece=piece):
                row = pl.ds(place.start + piece * half, place.size)
                grad, rows = norm_back(tokens[row, :].astype(F32), gain[...], summed.rows(row))
                pieces[piece, place, :] = (grad_middle[row, :] + grad).astype(BF)
                gains[0, 0:1, :] += jnp.sum(rows, axis=0, keepdims=True)

            in_pieces(half, back)
        mail.start(home, pieces.at[1 - c], grad_tokens.at[c], cp=1 - c)
        keep.start()
        mail.start(gain_core, gains.at[0], gains.at[1], tp=beside)

    def gain_step(k):
        if k == 0:
            mail.arrive(gain_core, gains.at[1], tp=beside)
            gains[2] = gains[0] + gains[1]
            mail.start(gain_y, gains.at[2], gains.at[3], tp=yonder)
        elif k == 1:
            mail.arrive(gain_y, gains.at[3], tp=yonder)
            gains[4] = gains[2] + gains[3]
            mail.start(gain_x, gains.at[4], gains.at[5], cp=1 - c)
        elif k == 2:
            mail.arrive(gain_x, gains.at[5], cp=1 - c)
            gain_line[z] = gains[4] + gains[5]
            if count > 1:
                line.send(1)
        else:
            hop = k - 2
            line.arrive(hop)
            if hop + 1 < count:
                line.send(hop + 1)

    for hop in range(1, count):
        if hop > 1:
            heads.arrive(hop - 1)
        heads.gather(hop)
        heads.send(hop)
        cross_send(hop + 2)
        if hop > 1:
            outs.arrive(hop - 1)
            outs.gather(hop)
            outs.send(hop)
        if hop == 1:
            finish_rows()
        if hop == 2:
            gain_step(0)
            gain_step(1)
    if count == 1:
        finish_rows()
    if count <= 2:
        gain_step(0)
        gain_step(1)
    gain_step(2)

    own_copy = pltpu.make_async_copy(qkv_grad.at[z, c], from_x.at[1, last], local.at[2])
    own_copy.start()
    out_copy = pltpu.make_async_copy(out_grad.at[z], final_out, local.at[3])
    out_copy.start()
    mail.arrive(cross_own, from_x.at[0, last], cp=1 - c)
    own_copy.wait()
    out_copy.wait()

    def start_heads(place):
        qkv_total[place, :] = from_x[0, last, place, :].astype(F32) + from_x[
            1, last, place, :
        ].astype(F32)

    in_pieces(qkv_total.shape[0], start_heads)

    def start_outs(place):
        out_total[place, :] = final_out[place, :].astype(F32)

    in_pieces(out_total.shape[0], start_outs)
    for hop in range(1, count):
        gain_step(2 + hop)
    if count > 1:
        outs.arrive(last)
        heads.arrive(last)
        for drain, total in ((outs, out_total), (heads, qkv_total)):
            for side, up in enumerate((True, False)):

                def more(drain=drain, total=total, side=side):
                    landed = drain.landed(side, last)

                    def one(place):
                        total[place, :] += landed[place, :].astype(F32)

                    in_pieces(total.shape[0], one)

                pl.when(drain.gets(last, up))(more)
    gain_sums[...] = jnp.sum(gain_line[...], axis=0)
    mail.arrive(home, grad_tokens.at[1 - c], cp=1 - c)
    keep.wait()
    mail.finish()


def last_sum(count, part, qkv_grad, out_grad, tokens, grad_middle, gain, gain_rows):
    slots = 8 * count + 16
    rows, width = tokens.shape
    hops = max(count - 1, 1)
    block, out_block = qkv_grad.shape[2:], out_grad.shape[1:]
    anywhere = pl.BlockSpec(memory_space=pl.ANY)
    vmem = pl.BlockSpec(memory_space=pltpu.VMEM)
    return pl.pallas_call(
        functools.partial(last_sum_kernel, count),
        out_shape=(
            jax.ShapeDtypeStruct(block, F32),
            jax.ShapeDtypeStruct(out_block, F32),
            jax.ShapeDtypeStruct((2, rows // 2, width), BF),
            jax.ShapeDtypeStruct((2, width), F32),
        ),
        in_specs=[anywhere] * 3 + [vmem] * 4,
        out_specs=(vmem, vmem, anywhere, vmem),
        scratch_shapes=[
            pltpu.VMEM((2, rows, width), BF),
            pltpu.VMEM((2, rows, width), BF),
            pltpu.VMEM((rows, width), BF),
            pltpu.VMEM((rows, width), BF),
            pltpu.VMEM((2, rows // 2, width), BF),
            pltpu.VMEM((2, count) + block, BF),
            pltpu.VMEM((2, hops) + block, BF),
            pltpu.VMEM((2, hops) + block, BF),
            pltpu.VMEM((2, hops) + out_block, BF),
            pltpu.VMEM((2, hops) + out_block, BF),
            pltpu.VMEM(out_block, BF),
            pltpu.VMEM((6, 2, width), F32),
            pltpu.VMEM((count, 2, width), F32),
            pltpu.SemaphoreType.DMA((slots,)),
            pltpu.SemaphoreType.DMA((slots,)),
            pltpu.SemaphoreType.DMA((4,)),
        ],
        compiler_params=pltpu.CompilerParams(
            collective_id=4, has_side_effects=True, vmem_limit_bytes=60 << 20
        ),
    )(part, qkv_grad, out_grad, tokens, grad_middle, gain, gain_rows)


def normalize(values):
    return values * lax.rsqrt(jnp.mean(values * values, axis=-1, keepdims=True) + EPSILON)


def silu_product(gate_pre, up_pre):
    return gate_pre / (1.0 + jnp.exp(-gate_pre)) * up_pre


def matmul(left, right):
    return jnp.dot(left, right, preferred_element_type=F32)


def rows_inner(left, right):
    return lax.dot_general(left, right, (((0,), (0,)), ((), ())), preferred_element_type=F32)


def cols_inner(left, right):
    return lax.dot_general(left, right, (((1,), (1,)), ((), ())), preferred_element_type=F32)


def row_major(value):
    return with_layout_constraint(value, Layout(major_to_minor=(0, 1)))


def after(value, *earlier):
    return lax.optimization_barrier((value, *earlier))[0]


def swap(value):
    return lax.ppermute(value, "cp", [(0, 1), (1, 0)])


def in_order(place, mine, other, axis):
    return jnp.where(
        place == 0,
        jnp.concatenate([mine, other], axis=axis),
        jnp.concatenate([other, mine], axis=axis),
    )


def on_device(
    tokens,
    seq_lengths,
    attention_gain,
    query_weight,
    key_weight,
    value_weight,
    out_weight,
    feedforward_gain,
    gate_weight,
    up_weight,
    down_weight,
    cotangent,
):
    c = lax.axis_index("cp")
    z = lax.axis_index("fsdp")
    sets = lax.axis_size("cp")
    count = lax.axis_size("fsdp")
    lanes = lax.axis_size("tp")
    slots, local, width = tokens.shape
    share = query_weight.shape[0]
    heads_width = query_weight.shape[1]
    head_count = heads_width // HD
    hidden_width = gate_weight.shape[1] // sets
    rows = sets * local
    seq = rows * lanes
    blocks = row_blocks(seq, sets, local)
    everyone = ("cp", "tp")

    def pick(value, which, axis=0):
        return lax.dynamic_index_in_dim(value, which, axis, keepdims=False)

    def from_sequence(value):
        value = value.reshape(sets, local, width)
        mine = pick(value, c)
        other = swap(pick(value, 1 - c))
        return in_order(c, mine[None], other[None], 0)

    length = pick(seq_lengths, c)[None]
    gain_one = attention_gain.astype(F32)
    gain_two = feedforward_gain.astype(F32)

    qkv = jnp.concatenate([query_weight, key_weight, value_weight], axis=1)

    def halves(weight):
        return weight[:, :hidden_width], weight[:, hidden_width:]

    parts = [halves(weight) for weight in (gate_weight, up_weight, down_weight.T)]
    own_wide = jnp.stack([jnp.where(c == 0, low, high) for low, high in parts])
    wide_away = jnp.stack([jnp.where(c == 0, high, low) for low, high in parts])
    token_rows, normed_one, full_qkv, out_half, first_low, first_high = first_gather(
        count, pick(tokens, c), pick(tokens, 1 - c), gain_one[None], qkv, out_weight.T,
        own_wide, wide_away,
    )
    token_rows = token_rows.reshape(rows, width)
    normed_one = normed_one.reshape(seq, width)
    full_qkv = full_qkv.reshape(width, 3 * heads_width)

    out_half, cotangent = after((out_half, cotangent), full_qkv)
    cotangents = lax.all_gather(cotangent, everyone, axis=0).reshape(
        sets, lanes, slots, local, width
    )
    full_out = in_order(c, out_half[:, None], swap(out_half)[:, None], 1)
    full_out = full_out.reshape(width, heads_width)
    up_hop = [(i, i + 1) for i in range(count - 1)]
    down_hop = [(i, i - 1) for i in range(1, count)]
    second_low = lax.ppermute(first_low, "fsdp", up_hop)
    second_high = lax.ppermute(first_high, "fsdp", down_hop)
    cosine_table, sine_table = tables(seq)
    projected = matmul(normed_one, full_qkv)
    context, q_heads, k_heads, v_heads, level = attention(
        blocks, head_count, length, projected, cosine_table, sine_table
    )
    part = cols_inner(context, full_out).astype(BF)

    middle, normed_two, full_gate, full_up, full_down = second_gather(
        count, part.reshape(lanes, rows, width), token_rows, gain_two[None], own_wide,
        first_low, first_high, second_low, second_high,
    )
    normed_two = normed_two.reshape(sets * seq, width)
    full_gate, full_up, full_down = (
        full.reshape(width, hidden_width) for full in (full_gate, full_up, full_down)
    )
    t = lax.axis_index("tp")
    grad_branch = (BRANCH * cotangents.astype(F32)).astype(BF).reshape(sets * seq, width)
    middle_home = from_sequence(middle)
    cotangent_rows = pick(pick(cotangents, t, 1), c, 1).reshape(rows, width)
    gate_pre = matmul(normed_two, full_gate)
    up_pre = matmul(normed_two, full_up)
    hidden_exact, silu_back = jax.vjp(silu_product, gate_pre, up_pre)
    hidden = hidden_exact.astype(BF)

    def blocks_of(gradient):
        gradient = row_major(gradient.astype(BF))
        return gradient.reshape(count, width // count, hidden_width)

    down_blocks = blocks_of(rows_inner(grad_branch, hidden))
    low = high = None
    for hop in range(1, count):
        leaving_up = pick(down_blocks, jnp.minimum(z + count - hop, count - 1))
        leaving_down = pick(down_blocks, jnp.maximum(z - count + hop, 0))
        if hop > 1:
            leaving_up = (leaving_up.astype(F32) + low.astype(F32)).astype(BF)
            leaving_down = (leaving_down.astype(F32) + high.astype(F32)).astype(BF)
        if hop < count - 1:
            low = lax.ppermute(leaving_up, "fsdp", up_hop[:hop])
            high = lax.ppermute(leaving_down, "fsdp", down_hop[count - 1 - hop :])
    grad_hidden = matmul(grad_branch, full_down)
    grad_gate_exact, grad_up_exact = silu_back(grad_hidden)
    grad_gate_pre = grad_gate_exact.astype(BF)
    grad_up_pre = grad_up_exact.astype(BF)
    grad_normed_two = cols_inner(grad_gate_pre, full_gate) + cols_inner(grad_up_pre, full_up)
    gate_blocks = blocks_of(rows_inner(normed_two, grad_gate_pre))
    up_blocks = blocks_of(rows_inner(normed_two, grad_up_pre))
    part = grad_normed_two.astype(BF).reshape(sets, lanes, slots, local, width)
    if count > 1:
        part, leaving_up, leaving_down = lax.optimization_barrier((part, leaving_up, leaving_down))
    part, middle_home = lax.optimization_barrier((part, middle_home))
    grad_middle, grad_attention, gain_two_rows, pair_up, pair_down = first_sum(
        count, part, gate_blocks, up_blocks, middle, cotangent_rows, gain_two[None],
    )
    grad_attention = grad_attention.reshape(seq, width)

    if count > 1:
        leaving_up, leaving_down = after((leaving_up, leaving_down), grad_attention)
        low = [lax.ppermute(pair_up, "fsdp", up_hop), lax.ppermute(leaving_up, "fsdp", up_hop)]
        high = [
            lax.ppermute(pair_down, "fsdp", down_hop), lax.ppermute(leaving_down, "fsdp", down_hop),
        ]
        low = [low[0][0], low[0][1], low[1]]
        high = [high[0][0], high[0][1], high[1]]

    def own_share(which, gradient):
        total = pick(gradient, z).astype(F32)
        if count > 1:
            total = total + low[which].astype(F32) + high[which].astype(F32)
        return total.reshape(sets, share, hidden_width)

    shares = [
        own_share(which, gradient)
        for which, gradient in enumerate((gate_blocks, up_blocks, down_blocks))
    ]
    others = swap(jnp.stack([pick(total, 1 - c).astype(BF) for total in shares]))
    grad_gate, grad_up, grad_down = (
        in_order(c, pick(total, c), others[which].astype(F32), 1)
        for which, total in enumerate(shares)
    )
    grad_down = grad_down.T

    out_pieces = row_major(rows_inner(grad_attention, context).astype(BF))
    out_pieces = out_pieces.reshape(count, sets, share, heads_width)
    out_other = swap(pick(out_pieces, 1 - c, 1))
    out_pieces = (pick(out_pieces, c, 1).astype(F32) + out_other.astype(F32)).astype(BF)
    grad_context = row_major(matmul(grad_attention, full_out).astype(BF))
    feedforward = lax.psum_scatter(
        cols_inner(after(hidden, grad_attention), full_down).astype(BF),
        everyone, scatter_dimension=0, tiled=True,
    )
    feedforward = feedforward.reshape(slots, local, width)
    output = (middle_home + BRANCH * feedforward.astype(F32)).astype(BF)
    grad_projected = attention_back(
        blocks, head_count, length, grad_context, q_heads, k_heads, v_heads, level,
        cosine_table, sine_table,
    )
    grad_projected = after(grad_projected, out_other, low[2], high[2])
    grad_qkv = row_major(rows_inner(normed_one, grad_projected).astype(BF))
    grad_qkv, grad_out, grad_tokens, gain_sums = last_sum(
        count, cols_inner(grad_projected, full_qkv).astype(BF).reshape(lanes, rows, width),
        grad_qkv.reshape(count, sets, share, 3 * heads_width), out_pieces,
        token_rows, grad_middle, gain_one[None], gain_two_rows,
    )
    return (
        output,
        grad_tokens,
        grad_qkv[:, :heads_width],
        grad_qkv[:, heads_width : 2 * heads_width],
        grad_qkv[:, 2 * heads_width :],
        grad_out.T,
        gain_sums[0],
        grad_gate,
        grad_up,
        grad_down,
        gain_sums[1],
    )


def solution(mesh):
    in_specs = (
        P("fsdp", ("cp", "tp"), None),
        P("fsdp"),
        P(),
        P(("fsdp", "cp"), "tp"),
        P(("fsdp", "cp"), "tp"),
        P(("fsdp", "cp"), "tp"),
        P("tp", ("fsdp", "cp")),
        P(),
        P(("fsdp", "cp"), "tp"),
        P(("fsdp", "cp"), "tp"),
        P("tp", ("fsdp", "cp")),
        P("fsdp", ("cp", "tp"), None),
    )
    out_specs = (
        P("fsdp", ("cp", "tp"), None),
        P("fsdp", ("cp", "tp"), None),
        P(("fsdp", "cp"), "tp"),
        P(("fsdp", "cp"), "tp"),
        P(("fsdp", "cp"), "tp"),
        P("tp", ("fsdp", "cp")),
        P(),
        P(("fsdp", "cp"), "tp"),
        P(("fsdp", "cp"), "tp"),
        P("tp", ("fsdp", "cp")),
        P(),
    )
    return jax.shard_map(
        on_device, mesh=mesh, in_specs=in_specs, out_specs=out_specs, check_vma=False
    )
```

```python
import functools
import math

import jax
import jax.numpy as jnp
import numpy as np
from jax import lax
from jax.experimental import pallas as pl
from jax.experimental.layout import Layout, with_layout_constraint
from jax.experimental.pallas import tpu as pltpu
from jax.sharding import PartitionSpec as P

HD = 64
EPSILON = 1e-05
BRANCH = 1.4 / math.sqrt(40.0)
BF = jnp.bfloat16
F32 = jnp.float32
TILE = 128
QUERY_ROWS = 256


def turned(values, cosine, sine):
    lane = lax.broadcasted_iota(jnp.int32, values.shape, 1)
    partner = jnp.where(
        lane % HD < HD // 2,
        pltpu.roll(values, TILE - HD // 2, 1),
        pltpu.roll(values, HD // 2, 1),
    )
    return values * cosine + partner * sine


def row_blocks(seq, sets, local):
    lanes = seq // sets // local
    return [
        ((t * sets + h) * local, (h * lanes + t) * local)
        for t in range(lanes)
        for h in range(sets)
    ]


def key_mask(length, first, rows, columns):
    place = first + lax.broadcasted_iota(jnp.int32, (rows, columns), 0)
    return place < length


def scores_of(keys, queries, length, first_query):
    raw = lax.dot_general(keys, queries, (((1,), (1,)), ((), ())), preferred_element_type=F32)
    key_place = lax.broadcasted_iota(jnp.int32, raw.shape, 0)
    query_place = first_query + lax.broadcasted_iota(jnp.int32, raw.shape, 1)
    return jnp.where((key_place <= query_place) & (key_place < length), raw, -1e30)


def attention_kernel(
    blocks, length_ref, projected, cosine, sine, context, q_heads, k_heads, v_heads, level, kept
):
    heads, seq, _ = q_heads.shape
    local = seq // len(blocks)
    length = length_ref[0]
    for gathered, ordered in blocks:
        source, target = pl.ds(gathered, local), pl.ds(ordered, local)
        for tile in range(-(-3 * heads // 2)):
            width = min(TILE, 3 * heads * HD - tile * TILE)
            values = projected[source, tile * TILE : tile * TILE + width]
            if tile * 2 < 2 * heads:
                values = turned(values, cosine[target, :], sine[target, :])
            for which in range(width // HD):
                index = tile * 2 + which
                piece = values[:, which * HD : (which + 1) * HD]
                if index < heads:
                    q_heads[index, target, :] = (piece * (1.0 / math.sqrt(HD))).astype(BF)
                elif index < 2 * heads:
                    k_heads[index - heads, target, :] = piece.astype(BF)
                else:
                    v_heads[index - 2 * heads, target, :] = piece.astype(BF)

    def one_head(head, carry):
        for first in range(0, seq, QUERY_ROWS):
            most = first + QUERY_ROWS
            queries = q_heads[head, first:most, :]
            keys = k_heads[head, :most, :]
            values = v_heads[head, :most, :]
            scores = scores_of(keys, queries, length, first)
            top = jnp.max(scores, axis=0, keepdims=True)
            exponent = jnp.exp(scores - top)
            total = jnp.sum(exponent, axis=0, keepdims=True)
            probabilities = (exponent * (1.0 / total)).astype(BF)
            level[head, :, first:most] = top + jnp.log(total)
            mixed = lax.dot_general(
                values, probabilities, (((0,), (0,)), ((), ())), preferred_element_type=F32
            )
            kept[head, first:most, :] = mixed.T.astype(BF)
        return carry

    lax.fori_loop(0, heads, one_head, 0)
    for gathered, ordered in blocks:
        source, target = pl.ds(ordered, local), pl.ds(gathered, local)
        for head in range(0, heads, 2):
            parts = [kept[index, source, :] for index in range(head, min(head + 2, heads))]
            joined = parts[0] if len(parts) == 1 else jnp.concatenate(parts, axis=1)
            context[target, head * HD : head * HD + joined.shape[1]] = joined


def attention(blocks, heads, length, projected, cosine, sine):
    seq = projected.shape[0]
    per_head = jax.ShapeDtypeStruct((heads, seq, HD), BF)
    vmem = pl.BlockSpec(memory_space=pltpu.VMEM)
    return pl.pallas_call(
        functools.partial(attention_kernel, blocks),
        out_shape=(
            jax.ShapeDtypeStruct((seq, heads * HD), BF),
            per_head,
            per_head,
            per_head,
            jax.ShapeDtypeStruct((heads, 1, seq), F32),
        ),
        in_specs=[pl.BlockSpec(memory_space=pltpu.SMEM), vmem, vmem, vmem],
        out_specs=(vmem,) * 5,
        scratch_shapes=[pltpu.VMEM((heads, seq, HD), BF)],
        compiler_params=pltpu.CompilerParams(vmem_limit_bytes=48 << 20),
        cost_estimate=pl.CostEstimate(
            flops=4 * heads * seq * seq * HD, transcendentals=heads * seq * seq, bytes_accessed=20 << 20
        ),
    )(length, projected, cosine, sine)


def attention_back_kernel(
    blocks, length_ref, grad_context, q_heads, k_heads, v_heads, level, cosine, sine,
    grad_projected, g_heads, dq, dk, dv,
):
    heads, seq, _ = q_heads.shape
    local = seq // len(blocks)
    length = length_ref[0]
    for gathered, ordered in blocks:
        source, target = pl.ds(gathered, local), pl.ds(ordered, local)
        for head in range(heads):
            g_heads[head, target, :] = grad_context[source, head * HD : (head + 1) * HD]

    def one_head(head, carry):
        keys_turned = k_heads[head].T
        for first in reversed(range(0, seq, QUERY_ROWS)):
            most = first + QUERY_ROWS
            queries = q_heads[head, first:most, :]
            upstream = g_heads[head, first:most, :]
            keys = k_heads[head, :most, :]
            values = v_heads[head, :most, :]
            scores = scores_of(keys, queries, length, first)
            probabilities = jnp.exp(scores - level[head, :, first:most])
            grad_probabilities = lax.dot_general(
                values, upstream, (((1,), (1,)), ((), ())), preferred_element_type=F32
            )
            weighted = probabilities * grad_probabilities
            balance = jnp.sum(weighted, axis=0, keepdims=True)
            grad_scores = (weighted - probabilities * balance).astype(BF)
            grad_keys = jnp.dot(grad_scores, queries, preferred_element_type=F32)
            grad_values = jnp.dot(
                probabilities.astype(BF), upstream, preferred_element_type=F32
            )
            if most == seq:
                dk[head, :, :] = grad_keys
                dv[head, :, :] = grad_values
            else:
                dk[head, :most, :] += grad_keys
                dv[head, :most, :] += grad_values
            grad_queries = jnp.dot(
                keys_turned[:, :most], grad_scores, preferred_element_type=F32
            )
            dq[head, first:most, :] = grad_queries.T * (1.0 / math.sqrt(HD))
        return carry

    lax.fori_loop(0, heads, one_head, 0)
    sources = [dq] * heads + [dk] * heads + [dv] * heads
    for gathered, ordered in blocks:
        source, target = pl.ds(ordered, local), pl.ds(gathered, local)
        for tile in range(-(-3 * heads // 2)):
            indices = range(tile * 2, min(tile * 2 + 2, 3 * heads))
            parts = [sources[index][index % heads, source, :] for index in indices]
            joined = parts[0] if len(parts) == 1 else jnp.concatenate(parts, axis=1)
            if tile * 2 < 2 * heads:
                joined = turned(joined, cosine[source, :], -sine[source, :])
            grad_projected[target, tile * TILE : tile * TILE + joined.shape[1]] = joined.astype(BF)


def attention_back(blocks, heads, length, grad_context, q_heads, k_heads, v_heads, level, cosine, sine):
    seq = grad_context.shape[0]
    vmem = pl.BlockSpec(memory_space=pltpu.VMEM)
    return pl.pallas_call(
        functools.partial(attention_back_kernel, blocks),
        out_shape=jax.ShapeDtypeStruct((seq, 3 * heads * HD), BF),
        in_specs=[pl.BlockSpec(memory_space=pltpu.SMEM)] + [vmem] * 7,
        out_specs=vmem,
        scratch_shapes=[
            pltpu.VMEM((heads, seq, HD), BF),
            pltpu.VMEM((heads, seq, HD), F32),
            pltpu.VMEM((heads, seq, HD), F32),
            pltpu.VMEM((heads, seq, HD), F32),
        ],
        compiler_params=pltpu.CompilerParams(vmem_limit_bytes=56 << 20),
        cost_estimate=pl.CostEstimate(
            flops=10 * heads * seq * seq * HD, transcendentals=heads * seq * seq, bytes_accessed=20 << 20
        ),
    )(length, grad_context, q_heads, k_heads, v_heads, level, cosine, sine)


def tables(seq):
    step = np.arange(HD // 2, dtype=np.float32)
    frequency = np.power(np.float32(10000.0), np.float32(-2.0) * step / np.float32(HD))
    angle = np.arange(seq, dtype=np.float32)[:, None] * frequency[None, :]
    cosine, sine = np.cos(angle), np.sin(angle)
    signed = np.concatenate([-sine, sine, -sine, sine], axis=1)
    return jnp.asarray(np.tile(cosine, (1, 4))), jnp.asarray(signed)


MESH = pl.DeviceIdType.MESH


def greet(count):
    barrier = pltpu.get_barrier_semaphore()
    z, c, t = lax.axis_index("fsdp"), lax.axis_index("cp"), lax.axis_index("tp")

    def hello(**place):
        pl.semaphore_signal(barrier, inc=1, device_id=place, device_id_type=MESH)

    hello(cp=1 - c)
    hello(tp=t + 1 - 2 * (t % 2))
    hello(tp=(t + 2) % 4)
    pl.when(z > 0)(lambda: hello(fsdp=z - 1))
    pl.when(z < count - 1)(lambda: hello(fsdp=z + 1))
    peers = 3 + jnp.minimum(z, 1) + jnp.minimum(count - 1 - z, 1)
    pl.semaphore_wait(barrier, peers)


class Mail:
    def __init__(self, send, recv):
        self.send, self.recv, self.used, self.open = send, recv, 0, []

    def slot(self):
        self.used += 1
        return self.used - 1

    def copy(self, slot, source, target, **place):
        return pltpu.make_async_remote_copy(
            src_ref=source,
            dst_ref=target,
            send_sem=self.send.at[slot],
            recv_sem=self.recv.at[slot],
            device_id=place,
            device_id_type=MESH,
        )

    def start(self, slot, source, target, when=None, **place):
        made = self.copy(slot, source, target, **place)
        if when is None:
            made.start()
        else:
            pl.when(when)(made.start)
        self.open.append((made, when))

    def arrive(self, slot, target, when=None, **place):
        made = self.copy(slot, target, target, **place)
        if when is None:
            made.wait_recv()
        else:
            pl.when(when)(made.wait_recv)

    def finish(self):
        for made, when in self.open:
            if when is None:
                made.wait_send()
            else:
                pl.when(when)(made.wait_send)


class Stage:
    def __init__(self, pieces, stage, sems):
        self.made = []
        for k, (source, target, when) in enumerate(pieces):
            self.made.append(
                (
                    pltpu.make_async_copy(source, stage.at[k], sems.at[0, k]),
                    pltpu.make_async_copy(stage.at[k], target, sems.at[1, k]),
                    when,
                )
            )

    def begin(self):
        for copy, _, when in self.made:
            copy.start() if when is None else pl.when(when)(copy.start)

    def turn(self):
        for first, second, when in self.made:

            def on(first=first, second=second):
                first.wait()
                second.start()

            on() if when is None else pl.when(when)(on)

    def end(self):
        for _, copy, when in self.made:
            copy.wait() if when is None else pl.when(when)(copy.wait)


class Line:
    def __init__(self, mail, count, own, at, ready=()):
        self.mail, self.count, self.own, self.at = mail, count, own, at
        self.ready = ready
        self.z = lax.axis_index("fsdp")
        self.up = [mail.slot() for _ in range(count)]
        self.down = [mail.slot() for _ in range(count)]

    def has_low(self, hop):
        return self.z >= hop

    def has_high(self, hop):
        return self.z <= self.count - 1 - hop

    def send(self, hop):
        z, count, mail = self.z, self.count, self.mail
        low, high = jnp.maximum(z - hop + 1, 0), jnp.minimum(z + hop - 1, count - 1)
        from_low = from_high = self.own
        if hop > 1:
            from_low, from_high = self.at(low), self.at(high)
        if 0 < hop - 1 <= len(self.ready):
            from_low, from_high = self.ready[hop - 2]
        mail.start(
            self.up[hop], from_low, self.at(low),
            when=(z >= hop - 1) & (z < count - 1), fsdp=jnp.minimum(z + 1, count - 1),
        )
        mail.start(
            self.down[hop], from_high, self.at(high),
            when=(z <= count - hop) & (z > 0), fsdp=jnp.maximum(z - 1, 0),
        )

    def arrive(self, hop):
        z, count = self.z, self.count
        self.mail.arrive(
            self.up[hop], self.at(jnp.maximum(z - hop, 0)), when=self.has_low(hop), fsdp=z
        )
        self.mail.arrive(
            self.down[hop], self.at(jnp.minimum(z + hop, count - 1)), when=self.has_high(hop), fsdp=z
        )


    def keep(self):
        z, count = self.z, self.count
        made = [(self.own, self.at(z), None)]
        for index, (low, high) in enumerate(self.ready):
            hop = index + 1
            made.append((low, self.at(jnp.maximum(z - hop, 0)), self.has_low(hop)))
            made.append((high, self.at(jnp.minimum(z + hop, count - 1)), self.has_high(hop)))
        return made


class Across:
    def __init__(self, line, own, mine_at, other_at):
        self.line, self.own, self.mine_at, self.other_at = line, own, mine_at, other_at
        self.c = lax.axis_index("cp")
        self.low = [line.mail.slot() for _ in range(line.count)]
        self.high = [line.mail.slot() for _ in range(line.count)]

    def send(self, hop):
        line, mail = self.line, self.line.mail
        z, count, other = line.z, line.count, 1 - self.c
        if hop == 0:
            mail.start(self.low[0], self.own, self.mine_at(z), cp=other)
            return
        low, high = jnp.maximum(z - hop, 0), jnp.minimum(z + hop, count - 1)
        mail.start(self.low[hop], self.mine_at(low), self.mine_at(low), when=line.has_low(hop), cp=other)
        mail.start(self.high[hop], self.mine_at(high), self.mine_at(high), when=line.has_high(hop), cp=other)

    def arrive(self, hop):
        line, mail = self.line, self.line.mail
        z, count, other = line.z, line.count, 1 - self.c
        if hop == 0:
            mail.arrive(self.low[0], self.other_at(z), cp=other)
            return
        low, high = jnp.maximum(z - hop, 0), jnp.minimum(z + hop, count - 1)
        mail.arrive(self.low[hop], self.other_at(low), when=line.has_low(hop), cp=other)
        mail.arrive(self.high[hop], self.other_at(high), when=line.has_high(hop), cp=other)


def first_gather_kernel(
    count, tokens, tokens_away, gain, qkv, turned_out, wide, wide_away,
    token_rows, normed_full, qkv_full, out_half, low_pair, high_pair,
    landed, normed, wide_landed, qkv_stage, out_stage,
    send, recv, local, qkv_local, out_local,
):
    z, c, t = lax.axis_index("fsdp"), lax.axis_index("cp"), lax.axis_index("tp")
    beside, yonder = t + 1 - 2 * (t % 2), (t + 2) % 4
    low, high = low_pair.at[0], high_pair.at[0]
    mail = Mail(send, recv)
    greet(count)
    stage_qkv = Stage([(qkv, qkv_full.at[z, c], None)], qkv_stage, qkv_local)
    stage_out = Stage([(turned_out, out_half.at[z], None)], out_stage, out_local)
    kept = []

    heads = Line(mail, count, qkv, lambda j: qkv_full.at[j, c])
    heads_across = Across(
        heads, qkv, lambda j: qkv_full.at[j, c], lambda j: qkv_full.at[j, 1 - c]
    )
    outs = Line(mail, count, turned_out, lambda j: out_half.at[j])
    wide_up, wide_down = mail.slot(), mail.slot()
    rows_x, wide_x = mail.slot(), mail.slot()
    rows_y = [mail.slot() for _ in range(2)]
    rows_core = [mail.slot() for _ in range(4)]

    mail.start(rows_x, tokens_away, landed, cp=1 - c)
    heads.send(1)

    def rows_out(source, side, half):
        def one(place):
            rows = source[place, :]
            token_rows[half, place, :] = rows
            normed[half, place, :] = (normalize(rows.astype(F32)) * gain[...]).astype(BF)

        in_pieces(source.shape[0], one)
        mail.start(rows_y[side], normed.at[half], normed_full.at[t, half], tp=yonder)
        mail.start(rows_core[side], normed.at[half], normed_full.at[t, half], tp=beside)

    stage_qkv.begin()
    stage_out.begin()
    rows_out(tokens, 0, c)
    stage_qkv.turn()
    stage_out.turn()
    mail.arrive(rows_x, landed, cp=1 - c)
    heads_across.send(0)
    rows_out(landed, 1, 1 - c)
    kept.append(pltpu.make_async_copy(normed, normed_full.at[t], local.at[2]))
    kept[-1].start()

    def rows_on(k, half):
        mail.arrive(rows_y[k], normed_full.at[yonder, half], tp=yonder)
        mail.start(
            rows_core[2 + k], normed_full.at[yonder, half], normed_full.at[yonder, half], tp=beside
        )

    for hop in range(1, count):
        heads.arrive(hop)
        if hop + 1 < count:
            heads.send(hop + 1)
        heads_across.send(hop)
        if hop == 1:
            rows_on(0, c)
            rows_on(1, 1 - c)
            outs.send(1)
        if hop == min(2, count - 1):
            mail.start(wide_up, wide, low, when=z < count - 1, fsdp=jnp.minimum(z + 1, count - 1))
            mail.start(wide_down, wide, high, when=z > 0, fsdp=jnp.maximum(z - 1, 0))
    mail.start(wide_x, wide_away, wide_landed, cp=1 - c)
    for hop in range(1, count):
        outs.arrive(hop)
        if hop + 1 < count:
            outs.send(hop + 1)
    for hop in range(count):
        heads_across.arrive(hop)
    mail.arrive(rows_core[0], normed_full.at[beside, c], tp=beside)
    mail.arrive(rows_core[1], normed_full.at[beside, 1 - c], tp=beside)
    far = (beside + 2) % 4
    mail.arrive(rows_core[2], normed_full.at[far, c], tp=beside)
    mail.arrive(rows_core[3], normed_full.at[far, 1 - c], tp=beside)
    mail.arrive(wide_x, wide_landed, cp=1 - c)
    for pair, place in ((low_pair, 1), (high_pair, 3)):
        kept.append(pltpu.make_async_copy(wide_landed, pair.at[1], local.at[place]))
        kept[-1].start()
    mail.arrive(wide_up, low, when=z > 0, fsdp=z)
    mail.arrive(wide_down, high, when=z < count - 1, fsdp=z)
    for copy in kept:
        copy.wait()
    stage_qkv.end()
    stage_out.end()
    mail.finish()


def first_gather(count, tokens, tokens_away, gain, qkv, turned_out, wide, wide_away):
    slots = 6 * count + 10
    anywhere = pl.BlockSpec(memory_space=pl.ANY)
    vmem = pl.BlockSpec(memory_space=pltpu.VMEM)
    pair = (2,) + tokens.shape
    return pl.pallas_call(
        functools.partial(first_gather_kernel, count),
        out_shape=(
            jax.ShapeDtypeStruct(pair, BF),
            jax.ShapeDtypeStruct((4,) + pair, BF),
            jax.ShapeDtypeStruct((count, 2) + qkv.shape, BF),
            jax.ShapeDtypeStruct((count,) + turned_out.shape, BF),
            jax.ShapeDtypeStruct((2,) + wide.shape, BF),
            jax.ShapeDtypeStruct((2,) + wide.shape, BF),
        ),
        in_specs=[vmem, anywhere, vmem] + [anywhere] * 4,
        out_specs=(vmem,) + (anywhere,) * 5,
        scratch_shapes=[
            pltpu.VMEM(tokens.shape, BF),
            pltpu.VMEM(pair, BF),
            pltpu.VMEM(wide.shape, BF),
            pltpu.VMEM((1,) + qkv.shape, BF),
            pltpu.VMEM((1,) + turned_out.shape, BF),
            pltpu.SemaphoreType.DMA((slots,)),
            pltpu.SemaphoreType.DMA((slots,)),
            pltpu.SemaphoreType.DMA((4,)),
            pltpu.SemaphoreType.DMA((2, 1)),
            pltpu.SemaphoreType.DMA((2, 1)),
        ],
        compiler_params=pltpu.CompilerParams(
            collective_id=1, has_side_effects=True, vmem_limit_bytes=32 << 20
        ),
    )(tokens, tokens_away, gain, qkv, turned_out, wide, wide_away)


def in_pieces(rows, body, size=16):
    if rows % size:
        body(pl.ds(0, rows))
        return
    lax.fori_loop(0, rows // size, lambda i, carry: (body(pl.ds(i * size, size)), carry)[1], 0)


class Spread:
    def __init__(self, mail, own, at):
        self.mail, self.own, self.at = mail, own, at
        self.c, self.t = lax.axis_index("cp"), lax.axis_index("tp")
        self.beside, self.yonder = self.t + 1 - 2 * (self.t % 2), (self.t + 2) % 4
        self.x = [mail.slot() for _ in range(3)]
        self.y = [mail.slot() for _ in range(3)]
        self.core = {}

    def to_core(self, c_is_own, t_is_own, piece):
        slot = self.core[c_is_own, t_is_own, piece] = self.mail.slot()
        c = self.c if c_is_own else 1 - self.c
        t = self.t if t_is_own else self.yonder
        source = self.own(piece) if c_is_own and t_is_own else self.at(c, t, piece)
        self.mail.start(slot, source, self.at(c, t, piece), tp=self.beside)

    def begin(self, piece):
        c, t = self.c, self.t
        if piece == 0:
            self.mail.start(self.x[0], self.own(0), self.at(c, t, 0), cp=1 - c)
        else:
            self.mail.start(self.y[0], self.own(1), self.at(c, t, 1), tp=self.yonder)
            self.mail.start(self.x[1], self.own(1), self.at(c, t, 1), cp=1 - c)
            self.mail.start(self.y[1], self.own(0), self.at(c, t, 0), tp=self.yonder)
        self.to_core(True, True, piece)

    def turn(self):
        c, t, mail, yonder = self.c, self.t, self.mail, self.yonder
        mail.arrive(self.x[0], self.at(1 - c, t, 0), cp=1 - c)
        mail.start(self.y[2], self.at(1 - c, t, 0), self.at(1 - c, t, 0), tp=yonder)
        self.to_core(False, True, 0)
        mail.arrive(self.y[0], self.at(c, yonder, 1), tp=yonder)
        mail.start(self.x[2], self.at(c, yonder, 1), self.at(c, yonder, 1), cp=1 - c)
        self.to_core(True, False, 1)

    def end(self):
        c, t, mail, yonder = self.c, self.t, self.mail, self.yonder
        mail.arrive(self.x[1], self.at(1 - c, t, 1), cp=1 - c)
        self.to_core(False, True, 1)
        mail.arrive(self.y[1], self.at(c, yonder, 0), tp=yonder)
        self.to_core(True, False, 0)
        mail.arrive(self.x[2], self.at(1 - c, yonder, 1), cp=1 - c)
        self.to_core(False, False, 1)
        mail.arrive(self.y[2], self.at(1 - c, yonder, 0), tp=yonder)
        self.to_core(False, False, 0)
        far = (self.beside + 2) % 4
        for (c_is_own, t_is_own, piece), slot in self.core.items():
            place = self.at(
                c if c_is_own else 1 - c, self.beside if t_is_own else far, piece
            )
            mail.arrive(slot, place, tp=self.beside)


def second_gather_kernel(
    count, part, tokens, gain, wide, first_low, first_high, second_low, second_high, *refs
):
    hops_mine, hops_other = min(2, count - 1), 1
    wide_other = first_low.at[1]
    ready_mine = [first_low.at[0], first_high.at[0], second_low.at[0], second_high.at[0]]
    ready_mine = ready_mine[: 2 * hops_mine]
    ready_other = [second_low.at[1], second_high.at[1]]
    middle, middle_home, normed_full, gate_full, up_full, down_full = refs[:6]
    own, from_core, to_yonder, from_yonder, normed, stage, send, recv, local, local_line = refs[6:]
    c, t = lax.axis_index("cp"), lax.axis_index("tp")
    rows = tokens.shape[0]
    half = rows // 2
    mail = Mail(send, recv)
    greet(count)

    mine, other = [], []
    for which, full in enumerate((gate_full, up_full, down_full)):
        for lines, side, piece, ready in (
            (mine, c, wide, ready_mine), (other, 1 - c, wide_other, ready_other),
        ):
            arrived = [
                (ready[2 * hop].at[which], ready[2 * hop + 1].at[which])
                for hop in range(len(ready) // 2)
            ]
            lines.append(
                Line(
                    mail, count, piece.at[which],
                    lambda j, full=full, side=side: full.at[j, side], arrived,
                )
            )
    summed = TensorSum(mail, part, own, from_core, to_yonder, from_yonder, local)
    spread = Spread(
        mail, lambda piece: normed.at[piece], lambda c, t, piece: normed_full.at[piece, t, c]
    )

    summed.begin()
    placing = Stage([piece for line in mine + other for piece in line.keep()], stage, local_line)
    placing.begin()

    def send_hop(lines, hop):
        for line in lines:
            if hop < count:
                line.send(hop)

    def arrive_hop(lines, hop):
        for line in lines:
            if hop < count:
                line.arrive(hop)

    send_hop(other, hops_other + 1)
    send_hop(mine, hops_mine + 1)
    summed.turn()
    placing.turn()
    for piece in range(2):
        summed.arrive(piece)

        def norm(place, piece=piece):
            row = pl.ds(place.start + piece * half, place.size)
            values = tokens[row, :].astype(F32) + BRANCH * summed.rows(row)
            middle[row, :] = values
            normed[piece, place, :] = (normalize(values) * gain[...]).astype(BF)

        in_pieces(half, norm)
        spread.begin(piece)
    keep_normed = pltpu.make_async_copy(normed, normed_full.at[:, t, c], local.at[0])
    keep_normed.start()
    home = mail.slot()
    stay, go = pl.ds(c * half, half), pl.ds((1 - c) * half, half)
    keep_home = pltpu.make_async_copy(middle.at[stay], middle_home.at[c], local.at[1])
    keep_home.start()
    spread.turn()
    mail.start(home, middle.at[go], middle_home.at[c], cp=1 - c)
    for step in range(1, count):
        hop = hops_other + step
        if hop < count:
            for line_other, line_mine in zip(other, mine):
                line_other.arrive(hop)
                if hop + 1 < count:
                    line_other.send(hop + 1)
                if hops_mine + step < count:
                    line_mine.arrive(hops_mine + step)
                    if hops_mine + step + 1 < count:
                        line_mine.send(hops_mine + step + 1)
        if step == 1:
            spread.end()
    if count == 1:
        spread.end()
    mail.arrive(home, middle_home.at[1 - c], cp=1 - c)
    keep_home.wait()
    keep_normed.wait()
    placing.end()
    mail.finish()


def second_gather(count, part, tokens, gain, wide, first_low, first_high, second_low, second_high):
    slots = 12 * count + 24
    rows, width = tokens.shape
    anywhere = pl.BlockSpec(memory_space=pl.ANY)
    vmem = pl.BlockSpec(memory_space=pltpu.VMEM)
    full = jax.ShapeDtypeStruct((count, 2) + wide.shape[1:], BF)
    return pl.pallas_call(
        functools.partial(second_gather_kernel, count),
        out_shape=(
            jax.ShapeDtypeStruct((rows, width), F32),
            jax.ShapeDtypeStruct((2, rows // 2, width), F32),
            jax.ShapeDtypeStruct((2, 4, 2, rows // 2, width), BF),
            full,
            full,
            full,
        ),
        in_specs=[anywhere, vmem, vmem] + [anywhere] * 5,
        out_specs=(vmem,) + (anywhere,) * 5,
        scratch_shapes=[
            pltpu.VMEM((2, rows, width), BF),
            pltpu.VMEM((2, rows, width), BF),
            pltpu.VMEM((rows, width), BF),
            pltpu.VMEM((rows, width), BF),
            pltpu.VMEM((2, rows // 2, width), BF),
            pltpu.VMEM((24,) + wide.shape[1:], BF),
            pltpu.SemaphoreType.DMA((slots,)),
            pltpu.SemaphoreType.DMA((slots,)),
            pltpu.SemaphoreType.DMA((2,)),
            pltpu.SemaphoreType.DMA((2, 24)),
        ],
        compiler_params=pltpu.CompilerParams(
            collective_id=2, has_side_effects=True, vmem_limit_bytes=40 << 20
        ),
    )(part, tokens, gain, wide, first_low, first_high, second_low, second_high)


class TensorSum:
    def __init__(self, mail, part, own, from_core, to_yonder, from_yonder, local):
        self.mail, self.part, self.own, self.from_core = mail, part, own, from_core
        self.to_yonder, self.from_yonder, self.local = to_yonder, from_yonder, local
        self.t = t = lax.axis_index("tp")
        self.beside, self.yonder = t + 1 - 2 * (t % 2), (t + 2) % 4
        self.core = [mail.slot() for _ in range(2)]
        self.across = [mail.slot() for _ in range(2)]
        self.half = from_yonder.shape[0] // 2

    def begin(self):
        part, far = self.part, (self.beside + 2) % 4
        self.mail.start(self.core[1], part.at[far], self.from_core.at[1], tp=self.beside)
        self.mail.start(self.core[0], part.at[self.beside], self.from_core.at[0], tp=self.beside)
        self.kept = [
            pltpu.make_async_copy(part.at[self.yonder], self.own.at[1], self.local.at[0]),
            pltpu.make_async_copy(part.at[self.t], self.own.at[0], self.local.at[1]),
        ]
        for copy in self.kept:
            copy.start()

    def turn(self):
        own, from_core = self.own, self.from_core
        self.kept[0].wait()
        self.mail.arrive(self.core[1], from_core.at[1], tp=self.beside)
        for piece in range(2):

            def add(place, piece=piece):
                place = pl.ds(place.start + piece * self.half, place.size)
                self.to_yonder[place, :] = (
                    own[1, place, :].astype(F32) + from_core[1, place, :].astype(F32)
                ).astype(BF)

            in_pieces(self.half, add)
            block = pl.ds(piece * self.half, self.half)
            self.mail.start(
                self.across[piece], self.to_yonder.at[block], self.from_yonder.at[block],
                tp=self.yonder,
            )
        self.kept[1].wait()
        self.mail.arrive(self.core[0], from_core.at[0], tp=self.beside)

    def arrive(self, piece):
        block = pl.ds(piece * self.half, self.half)
        self.mail.arrive(self.across[piece], self.from_yonder.at[block], tp=self.yonder)

    def rows(self, row):
        return (
            self.own[0, row, :].astype(F32)
            + self.from_core[0, row, :].astype(F32)
            + self.from_yonder[row, :].astype(F32)
        )


class Drain:
    def __init__(self, mail, count, fill, total, landed):
        self.mail, self.count, self.fill, self.total, self.landed = mail, count, fill, total, landed
        self.z = lax.axis_index("fsdp")
        self.slots = [[mail.slot() for _ in range(count)] for _ in range(2)]

    def sends(self, hop, up):
        z, count = self.z, self.count
        return (z <= hop - 1) & (z < count - 1) if up else (z >= count - hop) & (z > 0)

    def gets(self, hop, up):
        z, count = self.z, self.count
        return (z >= 1) & (z <= hop) if up else (z <= count - 2) & (z >= count - 1 - hop)

    def block(self, hop, up):
        z, count = self.z, self.count
        return jnp.minimum(z + count - hop, count - 1) if up else jnp.maximum(z - count + hop, 0)

    def arrive(self, hop):
        for side, up in enumerate((True, False)):
            self.mail.arrive(
                self.slots[side][hop], self.landed(side, hop), when=self.gets(hop, up), fsdp=self.z
            )

    def gather(self, hop):
        for side, up in enumerate((True, False)):
            target = self.total(side, hop)

            def work(side=side, up=up, target=target):
                self.fill(hop, up, self.block(hop, up), target)
                if hop > 1:

                    def add():
                        landed = self.landed(side, hop - 1)

                        def one(place):
                            target[place, :] = (
                                target[place, :].astype(F32) + landed[place, :].astype(F32)
                            ).astype(BF)

                        in_pieces(target.shape[0], one)

                    pl.when(self.gets(hop - 1, up))(add)

            pl.when(self.sends(hop, up))(work)

    def send(self, hop):
        z, count = self.z, self.count
        for side, up in enumerate((True, False)):
            to = jnp.minimum(z + 1, count - 1) if up else jnp.maximum(z - 1, 0)
            self.mail.start(
                self.slots[side][hop], self.total(side, hop), self.landed(side, hop),
                when=self.sends(hop, up), fsdp=to,
            )


def norm_back(values, gain, upstream):
    scale = lax.rsqrt(jnp.mean(values * values, axis=-1, keepdims=True) + EPSILON)
    norm = values * scale
    scaled = upstream * gain
    mean = jnp.mean(scaled * norm, axis=-1, keepdims=True)
    return scale * (scaled - norm * mean), upstream * norm


def first_sum_kernel(
    count, part, gate_grad, up_grad, middle, cotangent, gain,
    grad_middle, attention_full, gain_rows, leaving_up, leaving_down,
    own, from_core, first, second, grad_attention, totals, landed,
    send, recv, local,
):
    z, c, t = lax.axis_index("fsdp"), lax.axis_index("cp"), lax.axis_index("tp")
    beside, yonder = t + 1 - 2 * (t % 2), (t + 2) % 4
    far = (beside + 2) % 4
    half = middle.shape[0] // 2
    width = middle.shape[1]
    mail = Mail(send, recv)
    greet(count)
    last = count - 1

    def fill_from(which):
        def fill(hop, up, j, target):
            copy = pltpu.make_async_copy((gate_grad, up_grad)[which].at[j], target, local.at[4])
            copy.start()
            copy.wait()

        return fill

    drains = [
        Drain(
            mail, count, fill_from(which),
            lambda side, hop, which=which: (
                (leaving_up, leaving_down)[side].at[which] if hop == last else totals.at[side, hop - 1, which]
            ),
            lambda side, hop, which=which: landed.at[side, hop - 1, which],
        )
        for which in range(2)
    ]

    core = {}
    mine = {}
    order = ((0, 0), (0, 1), (1, 0), (1, 1))
    for index, (c_own, t_own) in enumerate(order):
        block_c = c if c_own else 1 - c
        core[c_own, t_own] = mail.slot()
        mail.start(
            core[c_own, t_own], part.at[:, beside if t_own else far, block_c],
            from_core.at[c_own, t_own], tp=beside,
        )
        mine[c_own, t_own] = pltpu.make_async_copy(
            part.at[:, t if t_own else yonder, block_c], own.at[c_own, t_own], local.at[index]
        )
        mine[c_own, t_own].start()
    if last > 1:
        for drain in drains:
            drain.gather(1)
            drain.send(1)

    quarter = half // 2
    quarters = [(piece, pl.ds(side * quarter, quarter)) for piece in range(2) for side in range(2)]
    x_first = [[mail.slot() for _ in range(2)] for _ in quarters]
    y_second = [mail.slot() for _ in quarters]
    ring_y = [mail.slot() for _ in quarters]
    ring_core = [mail.slot() for _ in quarters]
    ring_far = [mail.slot() for _ in quarters]

    def core_add(c_own, t_own, piece, rows):
        def one(place):
            row = pl.ds(rows.start + place.start, place.size)
            own[c_own, t_own, piece, row, :] = (
                own[c_own, t_own, piece, row, :].astype(F32)
                + from_core[c_own, t_own, piece, row, :].astype(F32)
            ).astype(BF)

        in_pieces(quarter, one)

    for t_own in (0, 1):
        mine[0, t_own].wait()
        mail.arrive(core[0, t_own], from_core.at[0, t_own], tp=beside)
    for k, (piece, rows) in enumerate(quarters):
        for t_own in (0, 1):
            core_add(0, t_own, piece, rows)
            mail.start(
                x_first[k][t_own], own.at[0, t_own, piece, rows], first.at[k, t_own], cp=1 - c
            )
    for t_own in (0, 1):
        mine[1, t_own].wait()
        mail.arrive(core[1, t_own], from_core.at[1, t_own], tp=beside)

    def add_first(k, t_own):
        piece, rows = quarters[k]

        def one(place):
            row = pl.ds(rows.start + place.start, place.size)
            own[1, t_own, piece, row, :] = (
                own[1, t_own, piece, row, :].astype(F32)
                + from_core[1, t_own, piece, row, :].astype(F32)
                + first[k, t_own, place, :].astype(F32)
            ).astype(BF)

        in_pieces(quarter, one)

    gain_rows[...] = jnp.zeros_like(gain_rows)

    def finish(k):
        piece, rows = quarters[k]
        mail.arrive(y_second[k], second.at[k], tp=yonder)

        def back(place):
            local_row = pl.ds(rows.start + place.start, place.size)
            row = pl.ds(piece * half + rows.start + place.start, place.size)
            summed = own[1, 1, piece, local_row, :].astype(F32) + second[k, place, :].astype(F32)
            grad, products = norm_back(middle[row, :], gain[...], summed)
            grad = cotangent[row, :].astype(F32) + grad
            grad_middle[row, :] = grad
            grad_attention[piece, local_row, :] = (BRANCH * grad).astype(BF)
            gain_rows[...] += jnp.sum(products, axis=0, keepdims=True)

        in_pieces(quarter, back)
        source = grad_attention.at[piece, rows]
        mail.start(ring_y[k], source, attention_full.at[t, piece, rows], tp=yonder)
        mail.start(ring_core[k], source, attention_full.at[t, piece, rows], tp=beside)

    def z_hop(hop):
        for drain in drains:
            drain.arrive(hop - 1)
            drain.gather(hop)
            drain.send(hop)

    for k, (piece, rows) in enumerate(quarters):
        mail.arrive(x_first[k][0], first.at[k, 0], cp=1 - c)
        add_first(k, 0)
        mail.start(y_second[k], own.at[1, 0, piece, rows], second.at[k], tp=yonder)
        mail.arrive(x_first[k][1], first.at[k, 1], cp=1 - c)
        add_first(k, 1)
        if k > 0:
            finish(k - 1)
        if k == 2 and last > 2:
            z_hop(2)
    finish(len(quarters) - 1)
    keep = pltpu.make_async_copy(grad_attention, attention_full.at[t], local.at[0])
    keep.start()
    for hop in range(3, last):
        z_hop(hop)
    for k, (piece, rows) in enumerate(quarters):
        arrived = attention_full.at[yonder, piece, rows]
        mail.arrive(ring_y[k], arrived, tp=yonder)
        mail.start(ring_far[k], arrived, arrived, tp=beside)
    for k, (piece, rows) in enumerate(quarters):
        mail.arrive(ring_core[k], attention_full.at[beside, piece, rows], tp=beside)
        mail.arrive(ring_far[k], attention_full.at[far, piece, rows], tp=beside)
    for drain in drains:
        if last > 1:
            drain.arrive(last - 1)
        if last > 0:
            drain.gather(last)
    keep.wait()
    mail.finish()


def first_sum(count, part, gate_grad, up_grad, middle, cotangent, gain):
    slots = 6 * count + 32
    rows, width = middle.shape
    block = gate_grad.shape[1:]
    anywhere = pl.BlockSpec(memory_space=pl.ANY)
    vmem = pl.BlockSpec(memory_space=pltpu.VMEM)
    hops = max(count - 2, 1)
    return pl.pallas_call(
        functools.partial(first_sum_kernel, count),
        out_shape=(
            jax.ShapeDtypeStruct((rows, width), F32),
            jax.ShapeDtypeStruct((4, 2, rows // 2, width), BF),
            jax.ShapeDtypeStruct((1, width), F32),
            jax.ShapeDtypeStruct((2,) + block, BF),
            jax.ShapeDtypeStruct((2,) + block, BF),
        ),
        in_specs=[anywhere] * 3 + [vmem] * 3,
        out_specs=(vmem, anywhere, vmem, vmem, vmem),
        scratch_shapes=[
            pltpu.VMEM((2, 2, 2, rows // 2, width), BF),
            pltpu.VMEM((2, 2, 2, rows // 2, width), BF),
            pltpu.VMEM((4, 2, rows // 4, width), BF),
            pltpu.VMEM((4, rows // 4, width), BF),
            pltpu.VMEM((2, rows // 2, width), BF),
            pltpu.VMEM((2, hops, 2) + block, BF),
            pltpu.VMEM((2, hops, 2) + block, BF),
            pltpu.SemaphoreType.DMA((slots,)),
            pltpu.SemaphoreType.DMA((slots,)),
            pltpu.SemaphoreType.DMA((5,)),
        ],
        compiler_params=pltpu.CompilerParams(
            collective_id=3, has_side_effects=True, vmem_limit_bytes=60 << 20
        ),
    )(part, gate_grad, up_grad, middle, cotangent, gain)


AHEAD = 4


def last_sum_kernel(
    count, part, qkv_grad, out_grad, tokens, grad_middle, gain, gain_rows,
    qkv_total, out_total, grad_tokens, gain_sums,
    own, from_core, to_yonder, from_yonder, pieces,
    from_x, heads_sum, heads_landed, outs_sum, outs_landed, final_out, gains, gain_line,
    send, recv, local,
):
    z, c, t = lax.axis_index("fsdp"), lax.axis_index("cp"), lax.axis_index("tp")
    beside, yonder = t + 1 - 2 * (t % 2), (t + 2) % 4
    half = tokens.shape[0] // 2
    last = count - 1
    mail = Mail(send, recv)
    greet(count)

    summed = TensorSum(mail, part, own, from_core, to_yonder, from_yonder, local)

    columns = qkv_total.shape[1]
    split = -(-columns // (2 * TILE)) * TILE
    parts = [pl.ds(0, split), pl.ds(split, columns - split)]
    cross = [[[mail.slot() for _ in range(count)] for _ in range(2)] for _ in parts]
    cross_own = [mail.slot() for _ in parts]

    def head_drain(lanes):
        def fill(hop, up, j, target):
            side = 0 if up else 1
            copy = pltpu.make_async_copy(qkv_grad.at[j, c, :, lanes], target, local.at[2])
            copy.start()
            copy.wait()
            arrived = from_x.at[side, hop - 1, :, lanes]

            def one(place):
                target[place, :] = (
                    target[place, :].astype(F32) + arrived[place, :].astype(F32)
                ).astype(BF)

            in_pieces(target.shape[0], one)

        return Drain(
            mail, count, fill,
            lambda side, hop: heads_sum.at[side, hop - 1, :, lanes],
            lambda side, hop: heads_landed.at[side, hop - 1, :, lanes],
        )

    heads = [head_drain(lanes) for lanes in parts]

    def fill_outs(hop, up, j, target):
        copy = pltpu.make_async_copy(out_grad.at[j], target, local.at[3])
        copy.start()
        copy.wait()

    outs = Drain(
        mail, count, fill_outs,
        lambda side, hop: outs_sum.at[side, hop - 1],
        lambda side, hop: outs_landed.at[side, hop - 1],
    )

    steps = [(hop, k) for hop in range(1, count + 1) for k in range(2)]

    def cross_send(step):
        if step >= len(steps):
            return
        hop, k = steps[step]
        lanes = parts[k]
        if hop == count:
            mail.start(
                cross_own[k], qkv_grad.at[z, 1 - c, :, lanes], from_x.at[0, last, :, lanes], cp=1 - c
            )
            return
        for side, up in enumerate((True, False)):
            mail.start(
                cross[k][side][hop], qkv_grad.at[heads[k].block(hop, up), 1 - c, :, lanes],
                from_x.at[side, hop - 1, :, lanes], when=heads[k].sends(hop, up), cp=1 - c,
            )

    def cross_arrive(hop, k):
        for side, up in enumerate((True, False)):
            mail.arrive(
                cross[k][side][hop], from_x.at[side, hop - 1, :, parts[k]],
                when=heads[k].sends(hop, up), cp=1 - c,
            )

    for step in range(AHEAD):
        cross_send(step)
    summed.begin()
    if count > 1:
        outs.gather(1)
        outs.send(1)
    summed.turn()

    keep = pltpu.make_async_copy(pieces.at[c], grad_tokens.at[c], local.at[0])
    home = mail.slot()
    gain_x, gain_y, gain_core = mail.slot(), mail.slot(), mail.slot()
    line = Line(mail, count, gain_line.at[z], lambda j: gain_line.at[j])

    def finish_rows():
        gains[0, 0:1, :] = jnp.zeros_like(gain_rows)
        gains[0, 1:2, :] = gain_rows[...]
        for piece in range(2):
            summed.arrive(piece)

            def back(place, piece=piece):
                row = pl.ds(place.start + piece * half, place.size)
                grad, rows = norm_back(tokens[row, :].astype(F32), gain[...], summed.rows(row))
                pieces[piece, place, :] = (grad_middle[row, :] + grad).astype(BF)
                gains[0, 0:1, :] += jnp.sum(rows, axis=0, keepdims=True)

            in_pieces(half, back)
        mail.start(home, pieces.at[1 - c], grad_tokens.at[c], cp=1 - c)
        keep.start()
        mail.start(gain_core, gains.at[0], gains.at[1], tp=beside)

    def gain_step(k):
        if k == 0:
            mail.arrive(gain_core, gains.at[1], tp=beside)
            gains[2] = gains[0] + gains[1]
            mail.start(gain_y, gains.at[2], gains.at[3], tp=yonder)
        elif k == 1:
            mail.arrive(gain_y, gains.at[3], tp=yonder)
            gains[4] = gains[2] + gains[3]
            mail.start(gain_x, gains.at[4], gains.at[5], cp=1 - c)
        elif k == 2:
            mail.arrive(gain_x, gains.at[5], cp=1 - c)
            gain_line[z] = gains[4] + gains[5]
            if count > 1:
                line.send(1)
        else:
            hop = k - 2
            line.arrive(hop)
            if hop + 1 < count:
                line.send(hop + 1)

    def outs_hop(hop):
        outs.arrive(hop - 1)
        outs.gather(hop)
        outs.send(hop)

    early = min(3, count)
    for hop in range(2, early + 1):
        if hop < count:
            outs_hop(hop)
    for step, (hop, k) in enumerate(steps[:-2]):
        cross_arrive(hop, k)
        cross_send(step + AHEAD)
        if hop > 1:
            heads[k].arrive(hop - 1)
        heads[k].gather(hop)
        heads[k].send(hop)
        if k == 1 and hop > early:
            outs_hop(hop)
        if step == 2 or step == 1 and count == 2:
            finish_rows()
        if step == 4:
            gain_step(0)
        if step == 5:
            gain_step(1)
    if count == 1:
        finish_rows()
    if count <= 2:
        gain_step(0)
        gain_step(1)
    gain_step(2)

    own_copy = pltpu.make_async_copy(qkv_grad.at[z, c], from_x.at[1, last], local.at[2])
    own_copy.start()
    out_copy = pltpu.make_async_copy(out_grad.at[z], final_out, local.at[3])
    out_copy.start()
    for k, lanes in enumerate(parts):
        mail.arrive(cross_own[k], from_x.at[0, last, :, lanes], cp=1 - c)
    own_copy.wait()
    out_copy.wait()

    def start_heads(place):
        qkv_total[place, :] = from_x[0, last, place, :].astype(F32) + from_x[
            1, last, place, :
        ].astype(F32)

    in_pieces(qkv_total.shape[0], start_heads)

    def start_outs(place):
        out_total[place, :] = final_out[place, :].astype(F32)

    in_pieces(out_total.shape[0], start_outs)
    for hop in range(1, count):
        gain_step(2 + hop)
    if count > 1:
        chains = [(outs, pl.ds(0, out_total.shape[1]), out_total)]
        chains += [(heads[k], lanes, qkv_total) for k, lanes in enumerate(parts)]
        for drain, lanes, total in chains:
            drain.arrive(last)
            for side, up in enumerate((True, False)):

                def more(drain=drain, total=total, side=side, lanes=lanes):
                    landed = drain.landed(side, last)

                    def one(place):
                        total[place, lanes] += landed[place, :].astype(F32)

                    in_pieces(total.shape[0], one)

                pl.when(drain.gets(last, up))(more)
    gain_sums[...] = jnp.sum(gain_line[...], axis=0)
    mail.arrive(home, grad_tokens.at[1 - c], cp=1 - c)
    keep.wait()
    mail.finish()


def last_sum(count, part, qkv_grad, out_grad, tokens, grad_middle, gain, gain_rows):
    slots = 13 * count + 16
    rows, width = tokens.shape
    hops = max(count - 1, 1)
    block, out_block = qkv_grad.shape[2:], out_grad.shape[1:]
    anywhere = pl.BlockSpec(memory_space=pl.ANY)
    vmem = pl.BlockSpec(memory_space=pltpu.VMEM)
    return pl.pallas_call(
        functools.partial(last_sum_kernel, count),
        out_shape=(
            jax.ShapeDtypeStruct(block, F32),
            jax.ShapeDtypeStruct(out_block, F32),
            jax.ShapeDtypeStruct((2, rows // 2, width), BF),
            jax.ShapeDtypeStruct((2, width), F32),
        ),
        in_specs=[anywhere] * 3 + [vmem] * 4,
        out_specs=(vmem, vmem, anywhere, vmem),
        scratch_shapes=[
            pltpu.VMEM((2, rows, width), BF),
            pltpu.VMEM((2, rows, width), BF),
            pltpu.VMEM((rows, width), BF),
            pltpu.VMEM((rows, width), BF),
            pltpu.VMEM((2, rows // 2, width), BF),
            pltpu.VMEM((2, count) + block, BF),
            pltpu.VMEM((2, hops) + block, BF),
            pltpu.VMEM((2, hops) + block, BF),
            pltpu.VMEM((2, hops) + out_block, BF),
            pltpu.VMEM((2, hops) + out_block, BF),
            pltpu.VMEM(out_block, BF),
            pltpu.VMEM((6, 2, width), F32),
            pltpu.VMEM((count, 2, width), F32),
            pltpu.SemaphoreType.DMA((slots,)),
            pltpu.SemaphoreType.DMA((slots,)),
            pltpu.SemaphoreType.DMA((4,)),
        ],
        compiler_params=pltpu.CompilerParams(
            collective_id=4, has_side_effects=True, vmem_limit_bytes=60 << 20
        ),
    )(part, qkv_grad, out_grad, tokens, grad_middle, gain, gain_rows)


def normalize(values):
    return values * lax.rsqrt(jnp.mean(values * values, axis=-1, keepdims=True) + EPSILON)


def silu_product(gate_pre, up_pre):
    return gate_pre / (1.0 + jnp.exp(-gate_pre)) * up_pre


def matmul(left, right):
    return jnp.dot(left, right, preferred_element_type=F32)


def rows_inner(left, right):
    return lax.dot_general(left, right, (((0,), (0,)), ((), ())), preferred_element_type=F32)


def cols_inner(left, right):
    return lax.dot_general(left, right, (((1,), (1,)), ((), ())), preferred_element_type=F32)


def row_major(value):
    return with_layout_constraint(value, Layout(major_to_minor=(0, 1)))


def after(value, *earlier):
    return lax.optimization_barrier((value, *earlier))[0]


def swap(value):
    return lax.ppermute(value, "cp", [(0, 1), (1, 0)])


def in_order(place, mine, other, axis):
    return jnp.where(
        place == 0,
        jnp.concatenate([mine, other], axis=axis),
        jnp.concatenate([other, mine], axis=axis),
    )


def on_device(
    tokens,
    seq_lengths,
    attention_gain,
    query_weight,
    key_weight,
    value_weight,
    out_weight,
    feedforward_gain,
    gate_weight,
    up_weight,
    down_weight,
    cotangent,
):
    c = lax.axis_index("cp")
    z = lax.axis_index("fsdp")
    sets = lax.axis_size("cp")
    count = lax.axis_size("fsdp")
    lanes = lax.axis_size("tp")
    slots, local, width = tokens.shape
    share = query_weight.shape[0]
    heads_width = query_weight.shape[1]
    head_count = heads_width // HD
    hidden_width = gate_weight.shape[1] // sets
    rows = sets * local
    seq = rows * lanes
    blocks = row_blocks(seq, sets, local)
    everyone = ("cp", "tp")

    def pick(value, which, axis=0):
        return lax.dynamic_index_in_dim(value, which, axis, keepdims=False)

    length = pick(seq_lengths, c)[None]
    gain_one = attention_gain.astype(F32)
    gain_two = feedforward_gain.astype(F32)

    qkv = jnp.concatenate([query_weight, key_weight, value_weight], axis=1)

    def halves(weight):
        return weight[:, :hidden_width], weight[:, hidden_width:]

    parts = [halves(weight) for weight in (gate_weight, up_weight, down_weight.T)]
    own_wide = jnp.stack([jnp.where(c == 0, low, high) for low, high in parts])
    wide_away = jnp.stack([jnp.where(c == 0, high, low) for low, high in parts])
    token_rows, normed_one, full_qkv, out_half, first_low, first_high = first_gather(
        count, pick(tokens, c), pick(tokens, 1 - c), gain_one[None], qkv, out_weight.T,
        own_wide, wide_away,
    )
    token_rows = token_rows.reshape(rows, width)
    normed_one = normed_one.reshape(seq, width)
    full_qkv = full_qkv.reshape(width, 3 * heads_width)

    out_half, cotangent = after((out_half, cotangent), full_qkv)
    cotangents = lax.all_gather(cotangent, everyone, axis=0).reshape(
        sets, lanes, slots, local, width
    )
    full_out = in_order(c, out_half[:, None], swap(out_half)[:, None], 1)
    full_out = full_out.reshape(width, heads_width)
    up_hop = [(i, i + 1) for i in range(count - 1)]
    down_hop = [(i, i - 1) for i in range(1, count)]
    second_low = lax.ppermute(first_low, "fsdp", up_hop)
    second_high = lax.ppermute(first_high, "fsdp", down_hop)
    cosine_table, sine_table = tables(seq)
    projected = matmul(normed_one, full_qkv)
    context, q_heads, k_heads, v_heads, level = attention(
        blocks, head_count, length, projected, cosine_table, sine_table
    )
    part = cols_inner(context, full_out).astype(BF)

    middle, middle_home, normed_two, full_gate, full_up, full_down = second_gather(
        count, part.reshape(lanes, rows, width), token_rows, gain_two[None], own_wide,
        first_low, first_high, second_low, second_high,
    )
    normed_two = normed_two.reshape(sets * seq, width)
    full_gate, full_up, full_down = (
        full.reshape(width, hidden_width) for full in (full_gate, full_up, full_down)
    )
    t = lax.axis_index("tp")
    cotangents_all = cotangents.reshape(sets * seq, width)
    cotangent_rows = pick(pick(cotangents, t, 1), c, 1).reshape(rows, width)
    gate_pre = matmul(normed_two, full_gate)
    up_pre = matmul(normed_two, full_up)
    hidden_exact, silu_back = jax.vjp(silu_product, gate_pre, up_pre)
    hidden = hidden_exact.astype(BF)

    def blocks_of(gradient):
        gradient = row_major(gradient.astype(BF))
        return gradient.reshape(count, width // count, hidden_width)

    down_blocks = blocks_of(BRANCH * rows_inner(cotangents_all, hidden))
    low = high = None
    for hop in range(1, count):
        leaving_up = pick(down_blocks, jnp.minimum(z + count - hop, count - 1))
        leaving_down = pick(down_blocks, jnp.maximum(z - count + hop, 0))
        if hop > 1:
            leaving_up = (leaving_up.astype(F32) + low.astype(F32)).astype(BF)
            leaving_down = (leaving_down.astype(F32) + high.astype(F32)).astype(BF)
        if hop < count - 1:
            low = lax.ppermute(leaving_up, "fsdp", up_hop[:hop])
            high = lax.ppermute(leaving_down, "fsdp", down_hop[count - 1 - hop :])
    grad_hidden = BRANCH * matmul(cotangents_all, full_down)
    grad_gate_exact, grad_up_exact = silu_back(grad_hidden)
    grad_gate_pre = grad_gate_exact.astype(BF)
    grad_up_pre = grad_up_exact.astype(BF)
    grad_normed_two = cols_inner(grad_gate_pre, full_gate) + cols_inner(grad_up_pre, full_up)
    gate_blocks = blocks_of(rows_inner(normed_two, grad_gate_pre))
    up_blocks = blocks_of(rows_inner(normed_two, grad_up_pre))
    part = grad_normed_two.astype(BF).reshape(sets, lanes, slots, local, width)
    if count > 1:
        part, leaving_up, leaving_down = lax.optimization_barrier((part, leaving_up, leaving_down))
    grad_middle, grad_attention, gain_two_rows, pair_up, pair_down = first_sum(
        count, part, gate_blocks, up_blocks, middle, cotangent_rows, gain_two[None],
    )
    grad_attention = grad_attention.reshape(seq, width)

    if count > 1:
        leaving_up, leaving_down = after((leaving_up, leaving_down), grad_attention)
        low = [lax.ppermute(pair_up, "fsdp", up_hop), lax.ppermute(leaving_up, "fsdp", up_hop)]
        high = [
            lax.ppermute(pair_down, "fsdp", down_hop), lax.ppermute(leaving_down, "fsdp", down_hop),
        ]
        low = [low[0][0], low[0][1], low[1]]
        high = [high[0][0], high[0][1], high[1]]

    def own_share(which, gradient):
        total = pick(gradient, z).astype(F32)
        if count > 1:
            total = total + low[which].astype(F32) + high[which].astype(F32)
        return total.reshape(sets, share, hidden_width)

    shares = [
        own_share(which, gradient)
        for which, gradient in enumerate((gate_blocks, up_blocks, down_blocks))
    ]
    others = swap(jnp.stack([pick(total, 1 - c).astype(BF) for total in shares]))
    grad_gate, grad_up, grad_down = (
        in_order(c, pick(total, c), others[which].astype(F32), 1)
        for which, total in enumerate(shares)
    )
    grad_down = grad_down.T

    out_pieces = row_major(rows_inner(grad_attention, context).astype(BF))
    out_pieces = out_pieces.reshape(count, sets, share, heads_width)
    out_other = swap(pick(out_pieces, 1 - c, 1))
    out_pieces = (pick(out_pieces, c, 1).astype(F32) + out_other.astype(F32)).astype(BF)
    grad_context = row_major(matmul(grad_attention, full_out).astype(BF))
    feedforward = lax.psum_scatter(
        cols_inner(after(hidden, grad_attention), full_down).astype(BF),
        everyone, scatter_dimension=0, tiled=True,
    )
    feedforward = feedforward.reshape(slots, local, width)
    output = (middle_home + BRANCH * feedforward.astype(F32)).astype(BF)
    grad_projected = attention_back(
        blocks, head_count, length, grad_context, q_heads, k_heads, v_heads, level,
        cosine_table, sine_table,
    )
    grad_projected = after(grad_projected, out_other, low[2], high[2])
    grad_qkv = row_major(rows_inner(normed_one, grad_projected).astype(BF))
    grad_qkv, grad_out, grad_tokens, gain_sums = last_sum(
        count, cols_inner(grad_projected, full_qkv).astype(BF).reshape(lanes, rows, width),
        grad_qkv.reshape(count, sets, share, 3 * heads_width), out_pieces,
        token_rows, grad_middle, gain_one[None], gain_two_rows,
    )
    return (
        output,
        grad_tokens,
        grad_qkv[:, :heads_width],
        grad_qkv[:, heads_width : 2 * heads_width],
        grad_qkv[:, 2 * heads_width :],
        grad_out.T,
        gain_sums[0],
        grad_gate,
        grad_up,
        grad_down,
        gain_sums[1],
    )


def solution(mesh):
    in_specs = (
        P("fsdp", ("cp", "tp"), None),
        P("fsdp"),
        P(),
        P(("fsdp", "cp"), "tp"),
        P(("fsdp", "cp"), "tp"),
        P(("fsdp", "cp"), "tp"),
        P("tp", ("fsdp", "cp")),
        P(),
        P(("fsdp", "cp"), "tp"),
        P(("fsdp", "cp"), "tp"),
        P("tp", ("fsdp", "cp")),
        P("fsdp", ("cp", "tp"), None),
    )
    out_specs = (
        P("fsdp", ("cp", "tp"), None),
        P("fsdp", ("cp", "tp"), None),
        P(("fsdp", "cp"), "tp"),
        P(("fsdp", "cp"), "tp"),
        P(("fsdp", "cp"), "tp"),
        P("tp", ("fsdp", "cp")),
        P(),
        P(("fsdp", "cp"), "tp"),
        P(("fsdp", "cp"), "tp"),
        P("tp", ("fsdp", "cp")),
        P(),
    )
    return jax.shard_map(
        on_device, mesh=mesh, in_specs=in_specs, out_specs=out_specs, check_vma=False
    )
```

```python
import functools
import math

import jax
import jax.numpy as jnp
import numpy as np
from jax import lax
from jax.experimental import pallas as pl
from jax.experimental.layout import Layout, with_layout_constraint
from jax.experimental.pallas import tpu as pltpu
from jax.sharding import PartitionSpec as P

HD = 64
EPSILON = 1e-05
BRANCH = 1.4 / math.sqrt(40.0)
BF = jnp.bfloat16
F32 = jnp.float32
TILE = 128
QUERY_ROWS = 256


def turned(values, cosine, sine):
    lane = lax.broadcasted_iota(jnp.int32, values.shape, 1)
    partner = jnp.where(
        lane % HD < HD // 2,
        pltpu.roll(values, TILE - HD // 2, 1),
        pltpu.roll(values, HD // 2, 1),
    )
    return values * cosine + partner * sine


def row_blocks(seq, sets, local):
    lanes = seq // sets // local
    return [
        ((t * sets + h) * local, (h * lanes + t) * local)
        for t in range(lanes)
        for h in range(sets)
    ]


def key_mask(length, first, rows, columns):
    place = first + lax.broadcasted_iota(jnp.int32, (rows, columns), 0)
    return place < length


def scores_of(keys, queries, length, first_query):
    raw = lax.dot_general(keys, queries, (((1,), (1,)), ((), ())), preferred_element_type=F32)
    key_place = lax.broadcasted_iota(jnp.int32, raw.shape, 0)
    query_place = first_query + lax.broadcasted_iota(jnp.int32, raw.shape, 1)
    return jnp.where((key_place <= query_place) & (key_place < length), raw, -1e30)


def attention_kernel(
    blocks, length_ref, projected, cosine, sine, context, q_heads, k_heads, v_heads, level, kept
):
    heads, seq, _ = q_heads.shape
    local = seq // len(blocks)
    length = length_ref[0]
    for gathered, ordered in blocks:
        source, target = pl.ds(gathered, local), pl.ds(ordered, local)
        for tile in range(-(-3 * heads // 2)):
            width = min(TILE, 3 * heads * HD - tile * TILE)
            values = projected[source, tile * TILE : tile * TILE + width]
            if tile * 2 < 2 * heads:
                values = turned(values, cosine[target, :], sine[target, :])
            for which in range(width // HD):
                index = tile * 2 + which
                piece = values[:, which * HD : (which + 1) * HD]
                if index < heads:
                    q_heads[index, target, :] = (piece * (1.0 / math.sqrt(HD))).astype(BF)
                elif index < 2 * heads:
                    k_heads[index - heads, target, :] = piece.astype(BF)
                else:
                    v_heads[index - 2 * heads, target, :] = piece.astype(BF)

    def one_head(head, carry):
        for first in range(0, seq, QUERY_ROWS):
            most = first + QUERY_ROWS
            queries = q_heads[head, first:most, :]
            keys = k_heads[head, :most, :]
            values = v_heads[head, :most, :]
            scores = scores_of(keys, queries, length, first)
            top = jnp.max(scores, axis=0, keepdims=True)
            exponent = jnp.exp(scores - top)
            total = jnp.sum(exponent, axis=0, keepdims=True)
            probabilities = (exponent * (1.0 / total)).astype(BF)
            level[head, :, first:most] = top + jnp.log(total)
            mixed = lax.dot_general(
                values, probabilities, (((0,), (0,)), ((), ())), preferred_element_type=F32
            )
            kept[head, first:most, :] = mixed.T.astype(BF)
        return carry

    lax.fori_loop(0, heads, one_head, 0)
    for gathered, ordered in blocks:
        source, target = pl.ds(ordered, local), pl.ds(gathered, local)
        for head in range(0, heads, 2):
            parts = [kept[index, source, :] for index in range(head, min(head + 2, heads))]
            joined = parts[0] if len(parts) == 1 else jnp.concatenate(parts, axis=1)
            context[target, head * HD : head * HD + joined.shape[1]] = joined


def attention(blocks, heads, length, projected, cosine, sine):
    seq = projected.shape[0]
    per_head = jax.ShapeDtypeStruct((heads, seq, HD), BF)
    vmem = pl.BlockSpec(memory_space=pltpu.VMEM)
    return pl.pallas_call(
        functools.partial(attention_kernel, blocks),
        out_shape=(
            jax.ShapeDtypeStruct((seq, heads * HD), BF),
            per_head,
            per_head,
            per_head,
            jax.ShapeDtypeStruct((heads, 1, seq), F32),
        ),
        in_specs=[pl.BlockSpec(memory_space=pltpu.SMEM), vmem, vmem, vmem],
        out_specs=(vmem,) * 5,
        scratch_shapes=[pltpu.VMEM((heads, seq, HD), BF)],
        compiler_params=pltpu.CompilerParams(vmem_limit_bytes=48 << 20),
        cost_estimate=pl.CostEstimate(
            flops=4 * heads * seq * seq * HD, transcendentals=heads * seq * seq, bytes_accessed=20 << 20
        ),
    )(length, projected, cosine, sine)


def attention_back_kernel(
    blocks, length_ref, grad_context, q_heads, k_heads, v_heads, level, cosine, sine,
    grad_projected, g_heads, dq, dk, dv,
):
    heads, seq, _ = q_heads.shape
    local = seq // len(blocks)
    length = length_ref[0]
    for gathered, ordered in blocks:
        source, target = pl.ds(gathered, local), pl.ds(ordered, local)
        for head in range(heads):
            g_heads[head, target, :] = grad_context[source, head * HD : (head + 1) * HD]

    def one_head(head, carry):
        keys_turned = k_heads[head].T
        for first in reversed(range(0, seq, QUERY_ROWS)):
            most = first + QUERY_ROWS
            queries = q_heads[head, first:most, :]
            upstream = g_heads[head, first:most, :]
            keys = k_heads[head, :most, :]
            values = v_heads[head, :most, :]
            scores = scores_of(keys, queries, length, first)
            probabilities = jnp.exp(scores - level[head, :, first:most])
            grad_probabilities = lax.dot_general(
                values, upstream, (((1,), (1,)), ((), ())), preferred_element_type=F32
            )
            weighted = probabilities * grad_probabilities
            balance = jnp.sum(weighted, axis=0, keepdims=True)
            grad_scores = (weighted - probabilities * balance).astype(BF)
            grad_keys = jnp.dot(grad_scores, queries, preferred_element_type=F32)
            grad_values = jnp.dot(
                probabilities.astype(BF), upstream, preferred_element_type=F32
            )
            if most == seq:
                dk[head, :, :] = grad_keys
                dv[head, :, :] = grad_values
            else:
                dk[head, :most, :] += grad_keys
                dv[head, :most, :] += grad_values
            grad_queries = jnp.dot(
                keys_turned[:, :most], grad_scores, preferred_element_type=F32
            )
            dq[head, first:most, :] = grad_queries.T * (1.0 / math.sqrt(HD))
        return carry

    lax.fori_loop(0, heads, one_head, 0)
    sources = [dq] * heads + [dk] * heads + [dv] * heads
    for gathered, ordered in blocks:
        source, target = pl.ds(ordered, local), pl.ds(gathered, local)
        for tile in range(-(-3 * heads // 2)):
            indices = range(tile * 2, min(tile * 2 + 2, 3 * heads))
            parts = [sources[index][index % heads, source, :] for index in indices]
            joined = parts[0] if len(parts) == 1 else jnp.concatenate(parts, axis=1)
            if tile * 2 < 2 * heads:
                joined = turned(joined, cosine[source, :], -sine[source, :])
            grad_projected[target, tile * TILE : tile * TILE + joined.shape[1]] = joined.astype(BF)


def attention_back(blocks, heads, length, grad_context, q_heads, k_heads, v_heads, level, cosine, sine):
    seq = grad_context.shape[0]
    vmem = pl.BlockSpec(memory_space=pltpu.VMEM)
    return pl.pallas_call(
        functools.partial(attention_back_kernel, blocks),
        out_shape=jax.ShapeDtypeStruct((seq, 3 * heads * HD), BF),
        in_specs=[pl.BlockSpec(memory_space=pltpu.SMEM)] + [vmem] * 7,
        out_specs=vmem,
        scratch_shapes=[
            pltpu.VMEM((heads, seq, HD), BF),
            pltpu.VMEM((heads, seq, HD), F32),
            pltpu.VMEM((heads, seq, HD), F32),
            pltpu.VMEM((heads, seq, HD), F32),
        ],
        compiler_params=pltpu.CompilerParams(vmem_limit_bytes=56 << 20),
        cost_estimate=pl.CostEstimate(
            flops=10 * heads * seq * seq * HD, transcendentals=heads * seq * seq, bytes_accessed=20 << 20
        ),
    )(length, grad_context, q_heads, k_heads, v_heads, level, cosine, sine)


def tables(seq):
    step = np.arange(HD // 2, dtype=np.float32)
    frequency = np.power(np.float32(10000.0), np.float32(-2.0) * step / np.float32(HD))
    angle = np.arange(seq, dtype=np.float32)[:, None] * frequency[None, :]
    cosine, sine = np.cos(angle), np.sin(angle)
    signed = np.concatenate([-sine, sine, -sine, sine], axis=1)
    return jnp.asarray(np.tile(cosine, (1, 4))), jnp.asarray(signed)


MESH = pl.DeviceIdType.MESH


def greet(count):
    barrier = pltpu.get_barrier_semaphore()
    z, c, t = lax.axis_index("fsdp"), lax.axis_index("cp"), lax.axis_index("tp")

    def hello(**place):
        pl.semaphore_signal(barrier, inc=1, device_id=place, device_id_type=MESH)

    hello(cp=1 - c)
    hello(tp=t + 1 - 2 * (t % 2))
    hello(tp=(t + 2) % 4)
    pl.when(z > 0)(lambda: hello(fsdp=z - 1))
    pl.when(z < count - 1)(lambda: hello(fsdp=z + 1))
    peers = 3 + jnp.minimum(z, 1) + jnp.minimum(count - 1 - z, 1)
    pl.semaphore_wait(barrier, peers)


class Mail:
    def __init__(self, send, recv):
        self.send, self.recv, self.used, self.open = send, recv, 0, []

    def slot(self):
        self.used += 1
        return self.used - 1

    def copy(self, slot, source, target, **place):
        return pltpu.make_async_remote_copy(
            src_ref=source,
            dst_ref=target,
            send_sem=self.send.at[slot],
            recv_sem=self.recv.at[slot],
            device_id=place,
            device_id_type=MESH,
        )

    def start(self, slot, source, target, when=None, **place):
        made = self.copy(slot, source, target, **place)
        if when is None:
            made.start()
        else:
            pl.when(when)(made.start)
        self.open.append((made, when))

    def arrive(self, slot, target, when=None, **place):
        made = self.copy(slot, target, target, **place)
        if when is None:
            made.wait_recv()
        else:
            pl.when(when)(made.wait_recv)

    def finish(self):
        for made, when in self.open:
            if when is None:
                made.wait_send()
            else:
                pl.when(when)(made.wait_send)


class Stage:
    def __init__(self, pieces, stage, sems):
        self.made = []
        for k, (source, target, when) in enumerate(pieces):
            self.made.append(
                (
                    pltpu.make_async_copy(source, stage.at[k], sems.at[0, k]),
                    pltpu.make_async_copy(stage.at[k], target, sems.at[1, k]),
                    when,
                )
            )

    def begin(self):
        for copy, _, when in self.made:
            copy.start() if when is None else pl.when(when)(copy.start)

    def turn(self):
        for first, second, when in self.made:

            def on(first=first, second=second):
                first.wait()
                second.start()

            on() if when is None else pl.when(when)(on)

    def end(self):
        for _, copy, when in self.made:
            copy.wait() if when is None else pl.when(when)(copy.wait)


class Line:
    def __init__(self, mail, count, own, at, ready=()):
        self.mail, self.count, self.own, self.at = mail, count, own, at
        self.ready = ready
        self.z = lax.axis_index("fsdp")
        self.up = [mail.slot() for _ in range(count)]
        self.down = [mail.slot() for _ in range(count)]

    def has_low(self, hop):
        return self.z >= hop

    def has_high(self, hop):
        return self.z <= self.count - 1 - hop

    def send(self, hop):
        z, count, mail = self.z, self.count, self.mail
        low, high = jnp.maximum(z - hop + 1, 0), jnp.minimum(z + hop - 1, count - 1)
        from_low = from_high = self.own
        if hop > 1:
            from_low, from_high = self.at(low), self.at(high)
        if 0 < hop - 1 <= len(self.ready):
            from_low, from_high = self.ready[hop - 2]
        mail.start(
            self.up[hop], from_low, self.at(low),
            when=(z >= hop - 1) & (z < count - 1), fsdp=jnp.minimum(z + 1, count - 1),
        )
        mail.start(
            self.down[hop], from_high, self.at(high),
            when=(z <= count - hop) & (z > 0), fsdp=jnp.maximum(z - 1, 0),
        )

    def arrive(self, hop):
        z, count = self.z, self.count
        self.mail.arrive(
            self.up[hop], self.at(jnp.maximum(z - hop, 0)), when=self.has_low(hop), fsdp=z
        )
        self.mail.arrive(
            self.down[hop], self.at(jnp.minimum(z + hop, count - 1)), when=self.has_high(hop), fsdp=z
        )


    def keep(self):
        z, count = self.z, self.count
        made = [(self.own, self.at(z), None)]
        for index, (low, high) in enumerate(self.ready):
            hop = index + 1
            made.append((low, self.at(jnp.maximum(z - hop, 0)), self.has_low(hop)))
            made.append((high, self.at(jnp.minimum(z + hop, count - 1)), self.has_high(hop)))
        return made


class Across:
    def __init__(self, line, own, mine_at, other_at):
        self.line, self.own, self.mine_at, self.other_at = line, own, mine_at, other_at
        self.c = lax.axis_index("cp")
        self.low = [line.mail.slot() for _ in range(line.count)]
        self.high = [line.mail.slot() for _ in range(line.count)]

    def send(self, hop):
        line, mail = self.line, self.line.mail
        z, count, other = line.z, line.count, 1 - self.c
        if hop == 0:
            mail.start(self.low[0], self.own, self.mine_at(z), cp=other)
            return
        low, high = jnp.maximum(z - hop, 0), jnp.minimum(z + hop, count - 1)
        mail.start(self.low[hop], self.mine_at(low), self.mine_at(low), when=line.has_low(hop), cp=other)
        mail.start(self.high[hop], self.mine_at(high), self.mine_at(high), when=line.has_high(hop), cp=other)

    def arrive(self, hop):
        line, mail = self.line, self.line.mail
        z, count, other = line.z, line.count, 1 - self.c
        if hop == 0:
            mail.arrive(self.low[0], self.other_at(z), cp=other)
            return
        low, high = jnp.maximum(z - hop, 0), jnp.minimum(z + hop, count - 1)
        mail.arrive(self.low[hop], self.other_at(low), when=line.has_low(hop), cp=other)
        mail.arrive(self.high[hop], self.other_at(high), when=line.has_high(hop), cp=other)


def first_gather_kernel(
    count, tokens, tokens_away, gain, qkv, turned_out, wide, wide_away,
    token_rows, normed_full, qkv_full, out_half, low_pair, high_pair,
    landed, normed, wide_landed, qkv_stage, out_stage,
    send, recv, local, qkv_local, out_local,
):
    z, c, t = lax.axis_index("fsdp"), lax.axis_index("cp"), lax.axis_index("tp")
    beside, yonder = t + 1 - 2 * (t % 2), (t + 2) % 4
    low, high = low_pair.at[0], high_pair.at[0]
    mail = Mail(send, recv)
    greet(count)
    stage_qkv = Stage([(qkv, qkv_full.at[z, c], None)], qkv_stage, qkv_local)
    stage_out = Stage([(turned_out, out_half.at[z], None)], out_stage, out_local)
    kept = []

    heads = Line(mail, count, qkv, lambda j: qkv_full.at[j, c])
    heads_across = Across(
        heads, qkv, lambda j: qkv_full.at[j, c], lambda j: qkv_full.at[j, 1 - c]
    )
    outs = Line(mail, count, turned_out, lambda j: out_half.at[j])
    wide_up, wide_down = mail.slot(), mail.slot()
    rows_x, wide_x = mail.slot(), mail.slot()
    rows_y = [mail.slot() for _ in range(2)]
    rows_core = [mail.slot() for _ in range(4)]

    mail.start(rows_x, tokens_away, landed, cp=1 - c)
    heads.send(1)

    def rows_out(source, side, half):
        def one(place):
            rows = source[place, :]
            token_rows[half, place, :] = rows
            normed[half, place, :] = (normalize(rows.astype(F32)) * gain[...]).astype(BF)

        in_pieces(source.shape[0], one)
        mail.start(rows_y[side], normed.at[half], normed_full.at[t, half], tp=yonder)
        mail.start(rows_core[side], normed.at[half], normed_full.at[t, half], tp=beside)

    stage_qkv.begin()
    stage_out.begin()
    rows_out(tokens, 0, c)
    stage_qkv.turn()
    stage_out.turn()
    mail.arrive(rows_x, landed, cp=1 - c)
    heads_across.send(0)
    rows_out(landed, 1, 1 - c)
    kept.append(pltpu.make_async_copy(normed, normed_full.at[t], local.at[2]))
    kept[-1].start()

    def rows_on(k, half):
        mail.arrive(rows_y[k], normed_full.at[yonder, half], tp=yonder)
        mail.start(
            rows_core[2 + k], normed_full.at[yonder, half], normed_full.at[yonder, half], tp=beside
        )

    for hop in range(1, count):
        heads.arrive(hop)
        if hop + 1 < count:
            heads.send(hop + 1)
        heads_across.send(hop)
        if hop == 1:
            rows_on(0, c)
            rows_on(1, 1 - c)
            outs.send(1)
        if hop == min(2, count - 1):
            mail.start(wide_up, wide, low, when=z < count - 1, fsdp=jnp.minimum(z + 1, count - 1))
            mail.start(wide_down, wide, high, when=z > 0, fsdp=jnp.maximum(z - 1, 0))
    mail.start(wide_x, wide_away, wide_landed, cp=1 - c)
    for hop in range(1, count):
        outs.arrive(hop)
        if hop + 1 < count:
            outs.send(hop + 1)
    for hop in range(count):
        heads_across.arrive(hop)
    mail.arrive(rows_core[0], normed_full.at[beside, c], tp=beside)
    mail.arrive(rows_core[1], normed_full.at[beside, 1 - c], tp=beside)
    far = (beside + 2) % 4
    mail.arrive(rows_core[2], normed_full.at[far, c], tp=beside)
    mail.arrive(rows_core[3], normed_full.at[far, 1 - c], tp=beside)
    mail.arrive(wide_x, wide_landed, cp=1 - c)
    for pair, place in ((low_pair, 1), (high_pair, 3)):
        kept.append(pltpu.make_async_copy(wide_landed, pair.at[1], local.at[place]))
        kept[-1].start()
    mail.arrive(wide_up, low, when=z > 0, fsdp=z)
    mail.arrive(wide_down, high, when=z < count - 1, fsdp=z)
    for copy in kept:
        copy.wait()
    stage_qkv.end()
    stage_out.end()
    mail.finish()


def first_gather(count, tokens, tokens_away, gain, qkv, turned_out, wide, wide_away):
    slots = 6 * count + 10
    anywhere = pl.BlockSpec(memory_space=pl.ANY)
    vmem = pl.BlockSpec(memory_space=pltpu.VMEM)
    pair = (2,) + tokens.shape
    return pl.pallas_call(
        functools.partial(first_gather_kernel, count),
        out_shape=(
            jax.ShapeDtypeStruct(pair, BF),
            jax.ShapeDtypeStruct((4,) + pair, BF),
            jax.ShapeDtypeStruct((count, 2) + qkv.shape, BF),
            jax.ShapeDtypeStruct((count,) + turned_out.shape, BF),
            jax.ShapeDtypeStruct((2,) + wide.shape, BF),
            jax.ShapeDtypeStruct((2,) + wide.shape, BF),
        ),
        in_specs=[vmem, anywhere, vmem] + [anywhere] * 4,
        out_specs=(vmem,) + (anywhere,) * 5,
        scratch_shapes=[
            pltpu.VMEM(tokens.shape, BF),
            pltpu.VMEM(pair, BF),
            pltpu.VMEM(wide.shape, BF),
            pltpu.VMEM((1,) + qkv.shape, BF),
            pltpu.VMEM((1,) + turned_out.shape, BF),
            pltpu.SemaphoreType.DMA((slots,)),
            pltpu.SemaphoreType.DMA((slots,)),
            pltpu.SemaphoreType.DMA((4,)),
            pltpu.SemaphoreType.DMA((2, 1)),
            pltpu.SemaphoreType.DMA((2, 1)),
        ],
        compiler_params=pltpu.CompilerParams(
            collective_id=1, has_side_effects=True, vmem_limit_bytes=32 << 20
        ),
    )(tokens, tokens_away, gain, qkv, turned_out, wide, wide_away)


def in_pieces(rows, body, size=16):
    if rows % size:
        body(pl.ds(0, rows))
        return
    lax.fori_loop(0, rows // size, lambda i, carry: (body(pl.ds(i * size, size)), carry)[1], 0)


class Spread:
    def __init__(self, mail, own, at):
        self.mail, self.own, self.at = mail, own, at
        self.c, self.t = lax.axis_index("cp"), lax.axis_index("tp")
        self.beside, self.yonder = self.t + 1 - 2 * (self.t % 2), (self.t + 2) % 4
        self.x = [mail.slot() for _ in range(3)]
        self.y = [mail.slot() for _ in range(3)]
        self.core = {}

    def to_core(self, c_is_own, t_is_own, piece):
        slot = self.core[c_is_own, t_is_own, piece] = self.mail.slot()
        c = self.c if c_is_own else 1 - self.c
        t = self.t if t_is_own else self.yonder
        source = self.own(piece) if c_is_own and t_is_own else self.at(c, t, piece)
        self.mail.start(slot, source, self.at(c, t, piece), tp=self.beside)

    def begin(self, piece):
        c, t = self.c, self.t
        if piece == 0:
            self.mail.start(self.x[0], self.own(0), self.at(c, t, 0), cp=1 - c)
        else:
            self.mail.start(self.y[0], self.own(1), self.at(c, t, 1), tp=self.yonder)
            self.mail.start(self.x[1], self.own(1), self.at(c, t, 1), cp=1 - c)
            self.mail.start(self.y[1], self.own(0), self.at(c, t, 0), tp=self.yonder)
        self.to_core(True, True, piece)

    def turn(self):
        c, t, mail, yonder = self.c, self.t, self.mail, self.yonder
        mail.arrive(self.x[0], self.at(1 - c, t, 0), cp=1 - c)
        mail.start(self.y[2], self.at(1 - c, t, 0), self.at(1 - c, t, 0), tp=yonder)
        self.to_core(False, True, 0)
        mail.arrive(self.y[0], self.at(c, yonder, 1), tp=yonder)
        mail.start(self.x[2], self.at(c, yonder, 1), self.at(c, yonder, 1), cp=1 - c)
        self.to_core(True, False, 1)

    def end(self):
        c, t, mail, yonder = self.c, self.t, self.mail, self.yonder
        mail.arrive(self.x[1], self.at(1 - c, t, 1), cp=1 - c)
        self.to_core(False, True, 1)
        mail.arrive(self.y[1], self.at(c, yonder, 0), tp=yonder)
        self.to_core(True, False, 0)
        mail.arrive(self.x[2], self.at(1 - c, yonder, 1), cp=1 - c)
        self.to_core(False, False, 1)
        mail.arrive(self.y[2], self.at(1 - c, yonder, 0), tp=yonder)
        self.to_core(False, False, 0)
        far = (self.beside + 2) % 4
        for (c_is_own, t_is_own, piece), slot in self.core.items():
            place = self.at(
                c if c_is_own else 1 - c, self.beside if t_is_own else far, piece
            )
            mail.arrive(slot, place, tp=self.beside)


def second_gather_kernel(
    count, part, tokens, gain, wide, first_low, first_high, second_low, second_high, *refs
):
    hops_mine, hops_other = min(2, count - 1), 1
    wide_other = first_low.at[1]
    ready_mine = [first_low.at[0], first_high.at[0], second_low.at[0], second_high.at[0]]
    ready_mine = ready_mine[: 2 * hops_mine]
    ready_other = [second_low.at[1], second_high.at[1]]
    middle, middle_home, normed_full, gate_full, up_full, down_full = refs[:6]
    own, from_core, to_yonder, from_yonder, normed, stage, send, recv, local, local_line = refs[6:]
    c, t = lax.axis_index("cp"), lax.axis_index("tp")
    rows = tokens.shape[0]
    half = rows // 2
    mail = Mail(send, recv)
    greet(count)

    mine, other = [], []
    for which, full in enumerate((gate_full, up_full, down_full)):
        for lines, side, piece, ready in (
            (mine, c, wide, ready_mine), (other, 1 - c, wide_other, ready_other),
        ):
            arrived = [
                (ready[2 * hop].at[which], ready[2 * hop + 1].at[which])
                for hop in range(len(ready) // 2)
            ]
            lines.append(
                Line(
                    mail, count, piece.at[which],
                    lambda j, full=full, side=side: full.at[j, side], arrived,
                )
            )
    summed = TensorSum(mail, part, own, from_core, to_yonder, from_yonder, local)
    spread = Spread(
        mail, lambda piece: normed.at[piece], lambda c, t, piece: normed_full.at[piece, t, c]
    )

    summed.begin()
    placing = Stage([piece for line in mine + other for piece in line.keep()], stage, local_line)
    placing.begin()

    def send_hop(lines, hop):
        for line in lines:
            if hop < count:
                line.send(hop)

    def arrive_hop(lines, hop):
        for line in lines:
            if hop < count:
                line.arrive(hop)

    send_hop(other, hops_other + 1)
    send_hop(mine, hops_mine + 1)
    summed.turn()
    placing.turn()
    for piece in range(2):
        summed.arrive(piece)

        def norm(place, piece=piece):
            row = pl.ds(place.start + piece * half, place.size)
            values = tokens[row, :].astype(F32) + BRANCH * summed.rows(row)
            middle[row, :] = values
            normed[piece, place, :] = (normalize(values) * gain[...]).astype(BF)

        in_pieces(half, norm)
        spread.begin(piece)
    keep_normed = pltpu.make_async_copy(normed, normed_full.at[:, t, c], local.at[0])
    keep_normed.start()
    home = mail.slot()
    stay, go = pl.ds(c * half, half), pl.ds((1 - c) * half, half)
    keep_home = pltpu.make_async_copy(middle.at[stay], middle_home.at[c], local.at[1])
    keep_home.start()
    spread.turn()
    mail.start(home, middle.at[go], middle_home.at[c], cp=1 - c)
    for step in range(1, count):
        hop = hops_other + step
        if hop < count:
            for line_other, line_mine in zip(other, mine):
                line_other.arrive(hop)
                if hop + 1 < count:
                    line_other.send(hop + 1)
                if hops_mine + step < count:
                    line_mine.arrive(hops_mine + step)
                    if hops_mine + step + 1 < count:
                        line_mine.send(hops_mine + step + 1)
        if step == 1:
            spread.end()
    if count == 1:
        spread.end()
    mail.arrive(home, middle_home.at[1 - c], cp=1 - c)
    keep_home.wait()
    keep_normed.wait()
    placing.end()
    mail.finish()


def second_gather(count, part, tokens, gain, wide, first_low, first_high, second_low, second_high):
    slots = 12 * count + 24
    rows, width = tokens.shape
    anywhere = pl.BlockSpec(memory_space=pl.ANY)
    vmem = pl.BlockSpec(memory_space=pltpu.VMEM)
    full = jax.ShapeDtypeStruct((count, 2) + wide.shape[1:], BF)
    return pl.pallas_call(
        functools.partial(second_gather_kernel, count),
        out_shape=(
            jax.ShapeDtypeStruct((rows, width), F32),
            jax.ShapeDtypeStruct((2, rows // 2, width), F32),
            jax.ShapeDtypeStruct((2, 4, 2, rows // 2, width), BF),
            full,
            full,
            full,
        ),
        in_specs=[anywhere, vmem, vmem] + [anywhere] * 5,
        out_specs=(vmem,) + (anywhere,) * 5,
        scratch_shapes=[
            pltpu.VMEM((2, rows, width), BF),
            pltpu.VMEM((2, rows, width), BF),
            pltpu.VMEM((rows, width), BF),
            pltpu.VMEM((rows, width), BF),
            pltpu.VMEM((2, rows // 2, width), BF),
            pltpu.VMEM((24,) + wide.shape[1:], BF),
            pltpu.SemaphoreType.DMA((slots,)),
            pltpu.SemaphoreType.DMA((slots,)),
            pltpu.SemaphoreType.DMA((2,)),
            pltpu.SemaphoreType.DMA((2, 24)),
        ],
        compiler_params=pltpu.CompilerParams(
            collective_id=2, has_side_effects=True, vmem_limit_bytes=40 << 20
        ),
    )(part, tokens, gain, wide, first_low, first_high, second_low, second_high)


class TensorSum:
    def __init__(self, mail, part, own, from_core, to_yonder, from_yonder, local):
        self.mail, self.part, self.own, self.from_core = mail, part, own, from_core
        self.to_yonder, self.from_yonder, self.local = to_yonder, from_yonder, local
        self.t = t = lax.axis_index("tp")
        self.beside, self.yonder = t + 1 - 2 * (t % 2), (t + 2) % 4
        self.core = [mail.slot() for _ in range(2)]
        self.across = [mail.slot() for _ in range(2)]
        self.half = from_yonder.shape[0] // 2

    def begin(self):
        part, far = self.part, (self.beside + 2) % 4
        self.mail.start(self.core[1], part.at[far], self.from_core.at[1], tp=self.beside)
        self.mail.start(self.core[0], part.at[self.beside], self.from_core.at[0], tp=self.beside)
        self.kept = [
            pltpu.make_async_copy(part.at[self.yonder], self.own.at[1], self.local.at[0]),
            pltpu.make_async_copy(part.at[self.t], self.own.at[0], self.local.at[1]),
        ]
        for copy in self.kept:
            copy.start()

    def turn(self):
        own, from_core = self.own, self.from_core
        self.kept[0].wait()
        self.mail.arrive(self.core[1], from_core.at[1], tp=self.beside)
        for piece in range(2):

            def add(place, piece=piece):
                place = pl.ds(place.start + piece * self.half, place.size)
                self.to_yonder[place, :] = (
                    own[1, place, :].astype(F32) + from_core[1, place, :].astype(F32)
                ).astype(BF)

            in_pieces(self.half, add)
            block = pl.ds(piece * self.half, self.half)
            self.mail.start(
                self.across[piece], self.to_yonder.at[block], self.from_yonder.at[block],
                tp=self.yonder,
            )
        self.kept[1].wait()
        self.mail.arrive(self.core[0], from_core.at[0], tp=self.beside)

    def arrive(self, piece):
        block = pl.ds(piece * self.half, self.half)
        self.mail.arrive(self.across[piece], self.from_yonder.at[block], tp=self.yonder)

    def rows(self, row):
        return (
            self.own[0, row, :].astype(F32)
            + self.from_core[0, row, :].astype(F32)
            + self.from_yonder[row, :].astype(F32)
        )


class Drain:
    def __init__(self, mail, count, fill, total, landed):
        self.mail, self.count, self.fill, self.total, self.landed = mail, count, fill, total, landed
        self.z = lax.axis_index("fsdp")
        self.slots = [[mail.slot() for _ in range(count)] for _ in range(2)]

    def sends(self, hop, up):
        z, count = self.z, self.count
        return (z <= hop - 1) & (z < count - 1) if up else (z >= count - hop) & (z > 0)

    def gets(self, hop, up):
        z, count = self.z, self.count
        return (z >= 1) & (z <= hop) if up else (z <= count - 2) & (z >= count - 1 - hop)

    def block(self, hop, up):
        z, count = self.z, self.count
        return jnp.minimum(z + count - hop, count - 1) if up else jnp.maximum(z - count + hop, 0)

    def arrive(self, hop):
        for side, up in enumerate((True, False)):
            self.mail.arrive(
                self.slots[side][hop], self.landed(side, hop), when=self.gets(hop, up), fsdp=self.z
            )

    def gather(self, hop):
        for side, up in enumerate((True, False)):
            target = self.total(side, hop)

            def work(side=side, up=up, target=target):
                self.fill(hop, up, self.block(hop, up), target)
                if hop > 1:

                    def add():
                        landed = self.landed(side, hop - 1)

                        def one(place):
                            target[place, :] = (
                                target[place, :].astype(F32) + landed[place, :].astype(F32)
                            ).astype(BF)

                        in_pieces(target.shape[0], one)

                    pl.when(self.gets(hop - 1, up))(add)

            pl.when(self.sends(hop, up))(work)

    def send(self, hop):
        z, count = self.z, self.count
        for side, up in enumerate((True, False)):
            to = jnp.minimum(z + 1, count - 1) if up else jnp.maximum(z - 1, 0)
            self.mail.start(
                self.slots[side][hop], self.total(side, hop), self.landed(side, hop),
                when=self.sends(hop, up), fsdp=to,
            )


def norm_back(values, gain, upstream):
    scale = lax.rsqrt(jnp.mean(values * values, axis=-1, keepdims=True) + EPSILON)
    norm = values * scale
    scaled = upstream * gain
    mean = jnp.mean(scaled * norm, axis=-1, keepdims=True)
    return scale * (scaled - norm * mean), upstream * norm


def first_sum_kernel(
    count, part, gate_grad, up_grad, hidden, middle, cotangent, gain, down,
    grad_middle, attention_full, gain_rows, leaving_up, leaving_down, feedforward,
    own, from_core, first, second, grad_attention, totals, landed, hidden_rows, product,
    send, recv, local, hidden_local,
):
    z, c, t = lax.axis_index("fsdp"), lax.axis_index("cp"), lax.axis_index("tp")
    beside, yonder = t + 1 - 2 * (t % 2), (t + 2) % 4
    far = (beside + 2) % 4
    half = middle.shape[0] // 2
    width = middle.shape[1]
    mail = Mail(send, recv)
    greet(count)
    last = count - 1

    def fill_from(which):
        def fill(hop, up, j, target):
            copy = pltpu.make_async_copy((gate_grad, up_grad)[which].at[j], target, local.at[4])
            copy.start()
            copy.wait()

        return fill

    drains = [
        Drain(
            mail, count, fill_from(which),
            lambda side, hop, which=which: (
                (leaving_up, leaving_down)[side].at[which] if hop == last else totals.at[side, hop - 1, which]
            ),
            lambda side, hop, which=which: landed.at[side, hop - 1, which],
        )
        for which in range(2)
    ]

    core = {}
    mine = {}
    order = ((0, 0), (0, 1), (1, 0), (1, 1))
    for index, (c_own, t_own) in enumerate(order):
        block_c = c if c_own else 1 - c
        core[c_own, t_own] = mail.slot()
        mail.start(
            core[c_own, t_own], part.at[:, beside if t_own else far, block_c],
            from_core.at[c_own, t_own], tp=beside,
        )
        mine[c_own, t_own] = pltpu.make_async_copy(
            part.at[:, t if t_own else yonder, block_c], own.at[c_own, t_own], local.at[index]
        )
        mine[c_own, t_own].start()
    if last > 1:
        for drain in drains:
            drain.gather(1)
            drain.send(1)

    block_rows = product.shape[1]
    blocks = hidden.shape[0] // block_rows

    def hidden_copy(block):
        return pltpu.make_async_copy(
            hidden.at[pl.ds(block * block_rows, block_rows)], hidden_rows.at[block % 2],
            hidden_local.at[0, block % 2],
        )

    def product_copy(block):
        return pltpu.make_async_copy(
            product.at[block % 2], feedforward.at[pl.ds(block * block_rows, block_rows)],
            hidden_local.at[1, block % 2],
        )

    def product_block(block):
        hidden_copy(block).wait()
        if block + 1 < blocks:
            hidden_copy(block + 1).start()
        if block > 1:
            product_copy(block - 2).wait()

        def one(k, carry):
            columns = pl.ds(pl.multiple_of(k * 2 * TILE, 2 * TILE), 2 * TILE)
            value = lax.dot_general(
                hidden_rows[block % 2], down[columns, :], (((1,), (1,)), ((), ())),
                preferred_element_type=F32,
            )
            product[block % 2, :, columns] = value.astype(BF)
            return carry

        lax.fori_loop(0, width // (2 * TILE), one, 0)
        product_copy(block).start()

    hidden_copy(0).start()
    product_block(0)

    quarter = half // 2
    quarters = [(piece, pl.ds(side * quarter, quarter)) for piece in range(2) for side in range(2)]
    x_first = [[mail.slot() for _ in range(2)] for _ in quarters]
    y_second = [mail.slot() for _ in quarters]
    ring_y = [mail.slot() for _ in quarters]
    ring_core = [mail.slot() for _ in quarters]
    ring_far = [mail.slot() for _ in quarters]

    def core_add(c_own, t_own, piece, rows):
        def one(place):
            row = pl.ds(rows.start + place.start, place.size)
            own[c_own, t_own, piece, row, :] = (
                own[c_own, t_own, piece, row, :].astype(F32)
                + from_core[c_own, t_own, piece, row, :].astype(F32)
            ).astype(BF)

        in_pieces(quarter, one)

    for t_own in (0, 1):
        mine[0, t_own].wait()
        mail.arrive(core[0, t_own], from_core.at[0, t_own], tp=beside)
    for k, (piece, rows) in enumerate(quarters):
        for t_own in (0, 1):
            core_add(0, t_own, piece, rows)
            mail.start(
                x_first[k][t_own], own.at[0, t_own, piece, rows], first.at[k, t_own], cp=1 - c
            )
    for t_own in (0, 1):
        mine[1, t_own].wait()
        mail.arrive(core[1, t_own], from_core.at[1, t_own], tp=beside)

    def add_first(k, t_own):
        piece, rows = quarters[k]

        def one(place):
            row = pl.ds(rows.start + place.start, place.size)
            own[1, t_own, piece, row, :] = (
                own[1, t_own, piece, row, :].astype(F32)
                + from_core[1, t_own, piece, row, :].astype(F32)
                + first[k, t_own, place, :].astype(F32)
            ).astype(BF)

        in_pieces(quarter, one)

    gain_rows[...] = jnp.zeros_like(gain_rows)

    def finish(k):
        piece, rows = quarters[k]
        mail.arrive(y_second[k], second.at[k], tp=yonder)

        def back(place):
            local_row = pl.ds(rows.start + place.start, place.size)
            row = pl.ds(piece * half + rows.start + place.start, place.size)
            summed = own[1, 1, piece, local_row, :].astype(F32) + second[k, place, :].astype(F32)
            grad, products = norm_back(middle[row, :], gain[...], summed)
            grad = cotangent[row, :].astype(F32) + grad
            grad_middle[row, :] = grad
            grad_attention[piece, local_row, :] = (BRANCH * grad).astype(BF)
            gain_rows[...] += jnp.sum(products, axis=0, keepdims=True)

        in_pieces(quarter, back)
        source = grad_attention.at[piece, rows]
        mail.start(ring_y[k], source, attention_full.at[t, piece, rows], tp=yonder)
        mail.start(ring_core[k], source, attention_full.at[t, piece, rows], tp=beside)

    def z_hop(hop):
        for drain in drains:
            drain.arrive(hop - 1)
            drain.gather(hop)
            drain.send(hop)

    for k, (piece, rows) in enumerate(quarters):
        mail.arrive(x_first[k][0], first.at[k, 0], cp=1 - c)
        add_first(k, 0)
        mail.start(y_second[k], own.at[1, 0, piece, rows], second.at[k], tp=yonder)
        mail.arrive(x_first[k][1], first.at[k, 1], cp=1 - c)
        add_first(k, 1)
        if k > 0:
            finish(k - 1)
        if k == 2 and last > 2:
            z_hop(2)
        product_block(k + 1)
    finish(len(quarters) - 1)
    for block in range(len(quarters) + 1, blocks):
        product_block(block)
    keep = pltpu.make_async_copy(grad_attention, attention_full.at[t], local.at[0])
    keep.start()
    for hop in range(3, last):
        z_hop(hop)
    for k, (piece, rows) in enumerate(quarters):
        arrived = attention_full.at[yonder, piece, rows]
        mail.arrive(ring_y[k], arrived, tp=yonder)
        mail.start(ring_far[k], arrived, arrived, tp=beside)
    for k, (piece, rows) in enumerate(quarters):
        mail.arrive(ring_core[k], attention_full.at[beside, piece, rows], tp=beside)
        mail.arrive(ring_far[k], attention_full.at[far, piece, rows], tp=beside)
    for drain in drains:
        if last > 1:
            drain.arrive(last - 1)
        if last > 0:
            drain.gather(last)
    keep.wait()
    for block in range(blocks - 2, blocks):
        product_copy(block).wait()
    mail.finish()


def first_sum(count, part, gate_grad, up_grad, hidden, middle, cotangent, gain, down):
    slots = 6 * count + 32
    rows, width = middle.shape
    block = gate_grad.shape[1:]
    anywhere = pl.BlockSpec(memory_space=pl.ANY)
    vmem = pl.BlockSpec(memory_space=pltpu.VMEM)
    hops = max(count - 2, 1)
    return pl.pallas_call(
        functools.partial(first_sum_kernel, count),
        out_shape=(
            jax.ShapeDtypeStruct((rows, width), F32),
            jax.ShapeDtypeStruct((4, 2, rows // 2, width), BF),
            jax.ShapeDtypeStruct((1, width), F32),
            jax.ShapeDtypeStruct((2,) + block, BF),
            jax.ShapeDtypeStruct((2,) + block, BF),
            jax.ShapeDtypeStruct((hidden.shape[0], width), BF),
        ),
        in_specs=[anywhere] * 4 + [vmem] * 4,
        out_specs=(vmem, anywhere, vmem, vmem, vmem, anywhere),
        scratch_shapes=[
            pltpu.VMEM((2, 2, 2, rows // 2, width), BF),
            pltpu.VMEM((2, 2, 2, rows // 2, width), BF),
            pltpu.VMEM((4, 2, rows // 4, width), BF),
            pltpu.VMEM((4, rows // 4, width), BF),
            pltpu.VMEM((2, rows // 2, width), BF),
            pltpu.VMEM((2, hops, 2) + block, BF),
            pltpu.VMEM((2, hops, 2) + block, BF),
            pltpu.VMEM((2, hidden.shape[0] // 8, hidden.shape[1]), BF),
            pltpu.VMEM((2, hidden.shape[0] // 8, width), BF),
            pltpu.SemaphoreType.DMA((slots,)),
            pltpu.SemaphoreType.DMA((slots,)),
            pltpu.SemaphoreType.DMA((5,)),
            pltpu.SemaphoreType.DMA((2, 2)),
        ],
        compiler_params=pltpu.CompilerParams(
            collective_id=3, has_side_effects=True, vmem_limit_bytes=60 << 20
        ),
    )(part, gate_grad, up_grad, hidden, middle, cotangent, gain, down)


AHEAD = 6


def last_sum_kernel(
    count, grad_projected, qkv_full, qkv_grad, out_grad, tokens, grad_middle, gain, gain_rows,
    qkv_total, out_total, grad_tokens, gain_sums,
    own, from_core, to_yonder, from_yonder, pieces,
    from_x, heads_sum, heads_landed, outs_sum, outs_landed, final_out, gains, gain_line,
    part, weights, send, recv, local, weights_local,
):
    z, c, t = lax.axis_index("fsdp"), lax.axis_index("cp"), lax.axis_index("tp")
    beside, yonder = t + 1 - 2 * (t % 2), (t + 2) % 4
    half = tokens.shape[0] // 2
    last = count - 1
    mail = Mail(send, recv)
    greet(count)

    summed = TensorSum(mail, part, own, from_core, to_yonder, from_yonder, local)

    columns = qkv_total.shape[1]
    split = -(-columns // (2 * TILE)) * TILE
    parts = [pl.ds(0, split), pl.ds(split, columns - split)]
    cross = [[[mail.slot() for _ in range(count)] for _ in range(2)] for _ in parts]
    cross_own = [mail.slot() for _ in parts]

    def head_drain(lanes):
        def fill(hop, up, j, target):
            side = 0 if up else 1
            copy = pltpu.make_async_copy(qkv_grad.at[j, c, :, lanes], target, local.at[2])
            copy.start()
            copy.wait()
            arrived = from_x.at[side, hop - 1, :, lanes]

            def one(place):
                target[place, :] = (
                    target[place, :].astype(F32) + arrived[place, :].astype(F32)
                ).astype(BF)

            in_pieces(target.shape[0], one)

        return Drain(
            mail, count, fill,
            lambda side, hop: heads_sum.at[side, hop - 1, :, lanes],
            lambda side, hop: heads_landed.at[side, hop - 1, :, lanes],
        )

    heads = [head_drain(lanes) for lanes in parts]

    def fill_outs(hop, up, j, target):
        copy = pltpu.make_async_copy(out_grad.at[j], target, local.at[3])
        copy.start()
        copy.wait()

    outs = Drain(
        mail, count, fill_outs,
        lambda side, hop: outs_sum.at[side, hop - 1],
        lambda side, hop: outs_landed.at[side, hop - 1],
    )

    steps = [(hop, k) for hop in range(1, count + 1) for k in range(2)]

    def cross_send(step):
        if step >= len(steps):
            return
        hop, k = steps[step]
        lanes = parts[k]
        if hop == count:
            mail.start(
                cross_own[k], qkv_grad.at[z, 1 - c, :, lanes], from_x.at[0, last, :, lanes], cp=1 - c
            )
            return
        for side, up in enumerate((True, False)):
            mail.start(
                cross[k][side][hop], qkv_grad.at[heads[k].block(hop, up), 1 - c, :, lanes],
                from_x.at[side, hop - 1, :, lanes], when=heads[k].sends(hop, up), cp=1 - c,
            )

    def cross_arrive(hop, k):
        for side, up in enumerate((True, False)):
            mail.arrive(
                cross[k][side][hop], from_x.at[side, hop - 1, :, parts[k]],
                when=heads[k].sends(hop, up), cp=1 - c,
            )

    for step in range(AHEAD):
        cross_send(step)
    if count > 1:
        outs.gather(1)
        outs.send(1)

    wide_block = weights.shape[1]
    blocks = qkv_full.shape[0] // wide_block

    def weights_copy(block, slot):
        return pltpu.make_async_copy(
            qkv_full.at[pl.ds(block * wide_block, wide_block)], weights.at[slot],
            weights_local.at[slot],
        )

    def product(block, carry):
        slot = lax.rem(block, 2)
        weights_copy(block, slot).wait()
        pl.when(block + 1 < blocks)(lambda: weights_copy(block + 1, 1 - slot).start())
        columns = pl.ds(pl.multiple_of(block * wide_block, wide_block), wide_block)
        value = lax.dot_general(
            grad_projected[...], weights[slot], (((1,), (1,)), ((), ())),
            preferred_element_type=F32,
        )
        part[:, :, columns] = value.astype(BF).reshape(part.shape[:2] + (wide_block,))
        return carry

    weights_copy(0, 0).start()
    thirds = [blocks * k // 3 for k in range(4)]
    lax.fori_loop(thirds[0], thirds[1], product, 0)

    keep = pltpu.make_async_copy(pieces.at[c], grad_tokens.at[c], local.at[0])
    home = mail.slot()
    gain_x, gain_y, gain_core = mail.slot(), mail.slot(), mail.slot()
    line = Line(mail, count, gain_line.at[z], lambda j: gain_line.at[j])

    def finish_rows():
        gains[0, 0:1, :] = jnp.zeros_like(gain_rows)
        gains[0, 1:2, :] = gain_rows[...]
        for piece in range(2):
            summed.arrive(piece)

            def back(place, piece=piece):
                row = pl.ds(place.start + piece * half, place.size)
                grad, rows = norm_back(tokens[row, :].astype(F32), gain[...], summed.rows(row))
                pieces[piece, place, :] = (grad_middle[row, :] + grad).astype(BF)
                gains[0, 0:1, :] += jnp.sum(rows, axis=0, keepdims=True)

            in_pieces(half, back)
        mail.start(home, pieces.at[1 - c], grad_tokens.at[c], cp=1 - c)
        keep.start()
        mail.start(gain_core, gains.at[0], gains.at[1], tp=beside)

    def gain_step(k):
        if k == 0:
            mail.arrive(gain_core, gains.at[1], tp=beside)
            gains[2] = gains[0] + gains[1]
            mail.start(gain_y, gains.at[2], gains.at[3], tp=yonder)
        elif k == 1:
            mail.arrive(gain_y, gains.at[3], tp=yonder)
            gains[4] = gains[2] + gains[3]
            mail.start(gain_x, gains.at[4], gains.at[5], cp=1 - c)
        elif k == 2:
            mail.arrive(gain_x, gains.at[5], cp=1 - c)
            gain_line[z] = gains[4] + gains[5]
            if count > 1:
                line.send(1)
        else:
            hop = k - 2
            line.arrive(hop)
            if hop + 1 < count:
                line.send(hop + 1)

    def outs_hop(hop):
        outs.arrive(hop - 1)
        outs.gather(hop)
        outs.send(hop)

    early = min(3, count)
    for k, hop in enumerate(range(2, early + 1)):
        if hop < count:
            outs_hop(hop)
        if k == 0:
            lax.fori_loop(thirds[1], thirds[2], product, 0)
    if early < 2:
        lax.fori_loop(thirds[1], thirds[2], product, 0)
    lax.fori_loop(thirds[2], thirds[3], product, 0)
    summed.begin()
    for step, (hop, k) in enumerate(steps[:-2]):
        cross_arrive(hop, k)
        cross_send(step + AHEAD)
        if hop > 1:
            heads[k].arrive(hop - 1)
        heads[k].gather(hop)
        heads[k].send(hop)
        if k == 1 and hop > early:
            outs_hop(hop)
        if step == 0:
            summed.turn()
        if step == 3 or step == 1 and count == 2:
            finish_rows()
        if step == 5:
            gain_step(0)
            gain_step(1)
    if count == 1:
        summed.turn()
        finish_rows()
    if count <= 2:
        gain_step(0)
        gain_step(1)
    gain_step(2)

    own_copy = pltpu.make_async_copy(qkv_grad.at[z, c], from_x.at[1, last], local.at[2])
    own_copy.start()
    out_copy = pltpu.make_async_copy(out_grad.at[z], final_out, local.at[3])
    out_copy.start()
    for k, lanes in enumerate(parts):
        mail.arrive(cross_own[k], from_x.at[0, last, :, lanes], cp=1 - c)
    own_copy.wait()
    out_copy.wait()

    def start_heads(place):
        qkv_total[place, :] = from_x[0, last, place, :].astype(F32) + from_x[
            1, last, place, :
        ].astype(F32)

    in_pieces(qkv_total.shape[0], start_heads)

    def start_outs(place):
        out_total[place, :] = final_out[place, :].astype(F32)

    in_pieces(out_total.shape[0], start_outs)
    for hop in range(1, count):
        gain_step(2 + hop)
    if count > 1:
        chains = [(outs, pl.ds(0, out_total.shape[1]), out_total)]
        chains += [(heads[k], lanes, qkv_total) for k, lanes in enumerate(parts)]
        for drain, lanes, total in chains:
            drain.arrive(last)
            for side, up in enumerate((True, False)):

                def more(drain=drain, total=total, side=side, lanes=lanes):
                    landed = drain.landed(side, last)

                    def one(place):
                        total[place, lanes] += landed[place, :].astype(F32)

                    in_pieces(total.shape[0], one)

                pl.when(drain.gets(last, up))(more)
    gain_sums[...] = jnp.sum(gain_line[...], axis=0)
    mail.arrive(home, grad_tokens.at[1 - c], cp=1 - c)
    keep.wait()
    mail.finish()


def last_sum(count, grad_projected, qkv_full, qkv_grad, out_grad, tokens, grad_middle, gain, gain_rows):
    slots = 13 * count + 16
    rows, width = tokens.shape
    hops = max(count - 1, 1)
    block, out_block = qkv_grad.shape[2:], out_grad.shape[1:]
    anywhere = pl.BlockSpec(memory_space=pl.ANY)
    vmem = pl.BlockSpec(memory_space=pltpu.VMEM)
    return pl.pallas_call(
        functools.partial(last_sum_kernel, count),
        out_shape=(
            jax.ShapeDtypeStruct(block, F32),
            jax.ShapeDtypeStruct(out_block, F32),
            jax.ShapeDtypeStruct((2, rows // 2, width), BF),
            jax.ShapeDtypeStruct((2, width), F32),
        ),
        in_specs=[vmem] + [anywhere] * 3 + [vmem] * 4,
        out_specs=(vmem, vmem, anywhere, vmem),
        scratch_shapes=[
            pltpu.VMEM((2, rows, width), BF),
            pltpu.VMEM((2, rows, width), BF),
            pltpu.VMEM((rows, width), BF),
            pltpu.VMEM((rows, width), BF),
            pltpu.VMEM((2, rows // 2, width), BF),
            pltpu.VMEM((2, count) + block, BF),
            pltpu.VMEM((2, hops) + block, BF),
            pltpu.VMEM((2, hops) + block, BF),
            pltpu.VMEM((2, hops) + out_block, BF),
            pltpu.VMEM((2, hops) + out_block, BF),
            pltpu.VMEM(out_block, BF),
            pltpu.VMEM((6, 2, width), F32),
            pltpu.VMEM((count, 2, width), F32),
            pltpu.VMEM((4, rows, width), BF),
            pltpu.VMEM((2, 2 * TILE, qkv_full.shape[1]), BF),
            pltpu.SemaphoreType.DMA((slots,)),
            pltpu.SemaphoreType.DMA((slots,)),
            pltpu.SemaphoreType.DMA((4,)),
            pltpu.SemaphoreType.DMA((2,)),
        ],
        compiler_params=pltpu.CompilerParams(
            collective_id=4, has_side_effects=True, vmem_limit_bytes=60 << 20
        ),
    )(grad_projected, qkv_full, qkv_grad, out_grad, tokens, grad_middle, gain, gain_rows)


def normalize(values):
    return values * lax.rsqrt(jnp.mean(values * values, axis=-1, keepdims=True) + EPSILON)


def silu_product(gate_pre, up_pre):
    return gate_pre / (1.0 + jnp.exp(-gate_pre)) * up_pre


def matmul(left, right):
    return jnp.dot(left, right, preferred_element_type=F32)


def rows_inner(left, right):
    return lax.dot_general(left, right, (((0,), (0,)), ((), ())), preferred_element_type=F32)


def cols_inner(left, right):
    return lax.dot_general(left, right, (((1,), (1,)), ((), ())), preferred_element_type=F32)


def row_major(value):
    return with_layout_constraint(value, Layout(major_to_minor=(0, 1)))


def after(value, *earlier):
    return lax.optimization_barrier((value, *earlier))[0]


def swap(value):
    return lax.ppermute(value, "cp", [(0, 1), (1, 0)])


def in_order(place, mine, other, axis):
    return jnp.where(
        place == 0,
        jnp.concatenate([mine, other], axis=axis),
        jnp.concatenate([other, mine], axis=axis),
    )


def on_device(
    tokens,
    seq_lengths,
    attention_gain,
    query_weight,
    key_weight,
    value_weight,
    out_weight,
    feedforward_gain,
    gate_weight,
    up_weight,
    down_weight,
    cotangent,
):
    c = lax.axis_index("cp")
    z = lax.axis_index("fsdp")
    sets = lax.axis_size("cp")
    count = lax.axis_size("fsdp")
    lanes = lax.axis_size("tp")
    slots, local, width = tokens.shape
    share = query_weight.shape[0]
    heads_width = query_weight.shape[1]
    head_count = heads_width // HD
    hidden_width = gate_weight.shape[1] // sets
    rows = sets * local
    seq = rows * lanes
    blocks = row_blocks(seq, sets, local)
    everyone = ("cp", "tp")

    def pick(value, which, axis=0):
        return lax.dynamic_index_in_dim(value, which, axis, keepdims=False)

    length = pick(seq_lengths, c)[None]
    gain_one = attention_gain.astype(F32)
    gain_two = feedforward_gain.astype(F32)

    qkv = jnp.concatenate([query_weight, key_weight, value_weight], axis=1)

    def halves(weight):
        return weight[:, :hidden_width], weight[:, hidden_width:]

    parts = [halves(weight) for weight in (gate_weight, up_weight, down_weight.T)]
    own_wide = jnp.stack([jnp.where(c == 0, low, high) for low, high in parts])
    wide_away = jnp.stack([jnp.where(c == 0, high, low) for low, high in parts])
    token_rows, normed_one, full_qkv, out_half, first_low, first_high = first_gather(
        count, pick(tokens, c), pick(tokens, 1 - c), gain_one[None], qkv, out_weight.T,
        own_wide, wide_away,
    )
    token_rows = token_rows.reshape(rows, width)
    normed_one = normed_one.reshape(seq, width)
    full_qkv = full_qkv.reshape(width, 3 * heads_width)

    out_half, cotangent = after((out_half, cotangent), full_qkv)
    cotangents = lax.all_gather(cotangent, everyone, axis=0).reshape(
        sets, lanes, slots, local, width
    )
    full_out = in_order(c, out_half[:, None], swap(out_half)[:, None], 1)
    full_out = full_out.reshape(width, heads_width)
    up_hop = [(i, i + 1) for i in range(count - 1)]
    down_hop = [(i, i - 1) for i in range(1, count)]
    second_low = lax.ppermute(first_low, "fsdp", up_hop)
    second_high = lax.ppermute(first_high, "fsdp", down_hop)
    cosine_table, sine_table = tables(seq)
    projected = matmul(normed_one, full_qkv)
    context, q_heads, k_heads, v_heads, level = attention(
        blocks, head_count, length, projected, cosine_table, sine_table
    )
    part = cols_inner(context, full_out).astype(BF)

    middle, middle_home, normed_two, full_gate, full_up, full_down = second_gather(
        count, part.reshape(lanes, rows, width), token_rows, gain_two[None], own_wide,
        first_low, first_high, second_low, second_high,
    )
    normed_two = normed_two.reshape(sets * seq, width)
    full_gate, full_up, full_down = (
        full.reshape(width, hidden_width) for full in (full_gate, full_up, full_down)
    )
    t = lax.axis_index("tp")
    cotangents_all = cotangents.reshape(sets * seq, width)
    cotangent_rows = pick(pick(cotangents, t, 1), c, 1).reshape(rows, width)
    gate_pre = matmul(normed_two, full_gate)
    up_pre = matmul(normed_two, full_up)
    hidden_exact, silu_back = jax.vjp(silu_product, gate_pre, up_pre)
    hidden = hidden_exact.astype(BF)

    def blocks_of(gradient):
        gradient = row_major(gradient.astype(BF))
        return gradient.reshape(count, width // count, hidden_width)

    down_blocks = blocks_of(BRANCH * rows_inner(cotangents_all, hidden))
    low = high = None
    for hop in range(1, count):
        leaving_up = pick(down_blocks, jnp.minimum(z + count - hop, count - 1))
        leaving_down = pick(down_blocks, jnp.maximum(z - count + hop, 0))
        if hop > 1:
            leaving_up = (leaving_up.astype(F32) + low.astype(F32)).astype(BF)
            leaving_down = (leaving_down.astype(F32) + high.astype(F32)).astype(BF)
        if hop < count - 1:
            low = lax.ppermute(leaving_up, "fsdp", up_hop[:hop])
            high = lax.ppermute(leaving_down, "fsdp", down_hop[count - 1 - hop :])
    grad_hidden = BRANCH * matmul(cotangents_all, full_down)
    grad_gate_exact, grad_up_exact = silu_back(grad_hidden)
    grad_gate_pre = grad_gate_exact.astype(BF)
    grad_up_pre = grad_up_exact.astype(BF)
    gate_part = lax.optimization_barrier(cols_inner(grad_gate_pre, full_gate).astype(BF))
    grad_normed_two = gate_part.astype(F32) + cols_inner(grad_up_pre, full_up)
    gate_blocks = blocks_of(rows_inner(normed_two, grad_gate_pre))
    up_blocks = blocks_of(rows_inner(normed_two, grad_up_pre))
    part = grad_normed_two.astype(BF).reshape(sets, lanes, slots, local, width)
    if count > 1:
        part, leaving_up, leaving_down = lax.optimization_barrier((part, leaving_up, leaving_down))
    grad_middle, grad_attention, gain_two_rows, pair_up, pair_down, feedforward = first_sum(
        count, part, gate_blocks, up_blocks, hidden, middle, cotangent_rows, gain_two[None],
        full_down,
    )
    grad_attention = grad_attention.reshape(seq, width)

    if count > 1:
        leaving_up, leaving_down = after((leaving_up, leaving_down), grad_attention)
        low = [lax.ppermute(pair_up, "fsdp", up_hop), lax.ppermute(leaving_up, "fsdp", up_hop)]
        high = [
            lax.ppermute(pair_down, "fsdp", down_hop), lax.ppermute(leaving_down, "fsdp", down_hop),
        ]
        low = [low[0][0], low[0][1], low[1]]
        high = [high[0][0], high[0][1], high[1]]

    def own_share(which, gradient):
        total = pick(gradient, z).astype(F32)
        if count > 1:
            total = total + low[which].astype(F32) + high[which].astype(F32)
        return total.reshape(sets, share, hidden_width)

    shares = [
        own_share(which, gradient)
        for which, gradient in enumerate((gate_blocks, up_blocks, down_blocks))
    ]
    others = swap(jnp.stack([pick(total, 1 - c).astype(BF) for total in shares]))
    grad_gate, grad_up, grad_down = (
        in_order(c, pick(total, c), others[which].astype(F32), 1)
        for which, total in enumerate(shares)
    )
    grad_down = grad_down.T

    out_pieces = row_major(rows_inner(grad_attention, context).astype(BF))
    out_pieces = out_pieces.reshape(count, sets, share, heads_width)
    out_other = swap(pick(out_pieces, 1 - c, 1))
    out_pieces = (pick(out_pieces, c, 1).astype(F32) + out_other.astype(F32)).astype(BF)
    grad_context = row_major(matmul(grad_attention, full_out).astype(BF))
    feedforward = lax.psum_scatter(feedforward, everyone, scatter_dimension=0, tiled=True)
    feedforward = feedforward.reshape(slots, local, width)
    output = (middle_home + BRANCH * feedforward.astype(F32)).astype(BF)
    grad_projected = attention_back(
        blocks, head_count, length, grad_context, q_heads, k_heads, v_heads, level,
        cosine_table, sine_table,
    )
    grad_projected = after(grad_projected, out_other, low[2], high[2])
    grad_qkv = row_major(rows_inner(normed_one, grad_projected).astype(BF))
    grad_qkv, grad_out, grad_tokens, gain_sums = last_sum(
        count, grad_projected, full_qkv, grad_qkv.reshape(count, sets, share, 3 * heads_width), out_pieces,
        token_rows, grad_middle, gain_one[None], gain_two_rows,
    )
    return (
        output,
        grad_tokens,
        grad_qkv[:, :heads_width],
        grad_qkv[:, heads_width : 2 * heads_width],
        grad_qkv[:, 2 * heads_width :],
        grad_out.T,
        gain_sums[0],
        grad_gate,
        grad_up,
        grad_down,
        gain_sums[1],
    )


def solution(mesh):
    in_specs = (
        P("fsdp", ("cp", "tp"), None),
        P("fsdp"),
        P(),
        P(("fsdp", "cp"), "tp"),
        P(("fsdp", "cp"), "tp"),
        P(("fsdp", "cp"), "tp"),
        P("tp", ("fsdp", "cp")),
        P(),
        P(("fsdp", "cp"), "tp"),
        P(("fsdp", "cp"), "tp"),
        P("tp", ("fsdp", "cp")),
        P("fsdp", ("cp", "tp"), None),
    )
    out_specs = (
        P("fsdp", ("cp", "tp"), None),
        P("fsdp", ("cp", "tp"), None),
        P(("fsdp", "cp"), "tp"),
        P(("fsdp", "cp"), "tp"),
        P(("fsdp", "cp"), "tp"),
        P("tp", ("fsdp", "cp")),
        P(),
        P(("fsdp", "cp"), "tp"),
        P(("fsdp", "cp"), "tp"),
        P("tp", ("fsdp", "cp")),
        P(),
    )
    return jax.shard_map(
        on_device, mesh=mesh, in_specs=in_specs, out_specs=out_specs, check_vma=False
    )
```

```python
import functools
import math

import jax
import jax.numpy as jnp
import numpy as np
from jax import lax
from jax.experimental import pallas as pl
from jax.experimental.layout import Layout, with_layout_constraint
from jax.experimental.pallas import tpu as pltpu
from jax.sharding import PartitionSpec as P

HD = 64
EPSILON = 1e-05
BRANCH = 1.4 / math.sqrt(40.0)
BF = jnp.bfloat16
F32 = jnp.float32
TILE = 128
QUERY_ROWS = 512


def turned(values, cosine, sine):
    lane = lax.broadcasted_iota(jnp.int32, values.shape, 1)
    partner = jnp.where(
        lane % HD < HD // 2,
        pltpu.roll(values, TILE - HD // 2, 1),
        pltpu.roll(values, HD // 2, 1),
    )
    return values * cosine + partner * sine


def row_blocks(seq, sets, local):
    lanes = seq // sets // local
    return [
        ((t * sets + h) * local, (h * lanes + t) * local)
        for t in range(lanes)
        for h in range(sets)
    ]


def key_mask(length, first, rows, columns):
    place = first + lax.broadcasted_iota(jnp.int32, (rows, columns), 0)
    return place < length


def scores_of(keys, queries, length, first_query):
    raw = lax.dot_general(keys, queries, (((1,), (1,)), ((), ())), preferred_element_type=F32)
    key_place = lax.broadcasted_iota(jnp.int32, raw.shape, 0)
    query_place = first_query + lax.broadcasted_iota(jnp.int32, raw.shape, 1)
    return jnp.where((key_place <= query_place) & (key_place < length), raw, -1e30)


def attention_kernel(
    blocks, length_ref, projected, cosine, sine, context, q_heads, k_heads, v_heads, level, kept
):
    heads, seq, _ = q_heads.shape
    local = seq // len(blocks)
    length = length_ref[0]
    for gathered, ordered in blocks:
        source, target = pl.ds(gathered, local), pl.ds(ordered, local)
        for tile in range(-(-3 * heads // 2)):
            width = min(TILE, 3 * heads * HD - tile * TILE)
            values = projected[source, tile * TILE : tile * TILE + width]
            if tile * 2 < 2 * heads:
                values = turned(values, cosine[target, :], sine[target, :])
            for which in range(width // HD):
                index = tile * 2 + which
                piece = values[:, which * HD : (which + 1) * HD]
                if index < heads:
                    q_heads[index, target, :] = (piece * (1.0 / math.sqrt(HD))).astype(BF)
                elif index < 2 * heads:
                    k_heads[index - heads, target, :] = piece.astype(BF)
                else:
                    v_heads[index - 2 * heads, target, :] = piece.astype(BF)

    def one_head(head, carry):
        for first in range(0, seq, QUERY_ROWS):
            most = first + QUERY_ROWS
            queries = q_heads[head, first:most, :]
            keys = k_heads[head, :most, :]
            values = v_heads[head, :most, :]
            scores = scores_of(keys, queries, length, first)
            top = jnp.max(scores, axis=0, keepdims=True)
            exponent = jnp.exp(scores - top)
            total = jnp.sum(exponent, axis=0, keepdims=True)
            probabilities = exponent.astype(BF)
            level[head, :, first:most] = top + jnp.log(total)
            mixed = lax.dot_general(
                values, probabilities, (((0,), (0,)), ((), ())), preferred_element_type=F32
            )
            kept[head, first:most, :] = (mixed * (1.0 / total)).T.astype(BF)
        return carry

    lax.fori_loop(0, heads, one_head, 0, unroll=True)
    for gathered, ordered in blocks:
        source, target = pl.ds(ordered, local), pl.ds(gathered, local)
        for head in range(0, heads, 2):
            parts = [kept[index, source, :] for index in range(head, min(head + 2, heads))]
            joined = parts[0] if len(parts) == 1 else jnp.concatenate(parts, axis=1)
            context[target, head * HD : head * HD + joined.shape[1]] = joined


def attention(blocks, heads, length, projected, cosine, sine):
    seq = projected.shape[0]
    per_head = jax.ShapeDtypeStruct((heads, seq, HD), BF)
    vmem = pl.BlockSpec(memory_space=pltpu.VMEM)
    return pl.pallas_call(
        functools.partial(attention_kernel, blocks),
        out_shape=(
            jax.ShapeDtypeStruct((seq, heads * HD), BF),
            per_head,
            per_head,
            per_head,
            jax.ShapeDtypeStruct((heads, 1, seq), F32),
        ),
        in_specs=[pl.BlockSpec(memory_space=pltpu.SMEM), vmem, vmem, vmem],
        out_specs=(vmem,) * 5,
        scratch_shapes=[pltpu.VMEM((heads, seq, HD), BF)],
        compiler_params=pltpu.CompilerParams(vmem_limit_bytes=48 << 20),
        cost_estimate=pl.CostEstimate(
            flops=4 * heads * seq * seq * HD, transcendentals=heads * seq * seq, bytes_accessed=20 << 20
        ),
    )(length, projected, cosine, sine)


def attention_back_kernel(
    blocks, length_ref, grad_context, q_heads, k_heads, v_heads, level, cosine, sine,
    grad_projected, g_heads, dq, dk, dv,
):
    heads, seq, _ = q_heads.shape
    local = seq // len(blocks)
    length = length_ref[0]
    for gathered, ordered in blocks:
        source, target = pl.ds(gathered, local), pl.ds(ordered, local)
        for head in range(heads):
            g_heads[head, target, :] = grad_context[source, head * HD : (head + 1) * HD]

    def one_head(head, carry):
        keys_turned = k_heads[head].T
        for first in reversed(range(0, seq, QUERY_ROWS)):
            most = first + QUERY_ROWS
            queries = q_heads[head, first:most, :]
            upstream = g_heads[head, first:most, :]
            keys = k_heads[head, :most, :]
            values = v_heads[head, :most, :]
            scores = scores_of(keys, queries, length, first)
            probabilities = jnp.exp(scores - level[head, :, first:most])
            grad_probabilities = lax.dot_general(
                values, upstream, (((1,), (1,)), ((), ())), preferred_element_type=F32
            )
            weighted = probabilities * grad_probabilities
            balance = jnp.sum(weighted, axis=0, keepdims=True)
            grad_scores = (weighted - probabilities * balance).astype(BF)
            grad_keys = jnp.dot(grad_scores, queries, preferred_element_type=F32)
            grad_values = jnp.dot(
                probabilities.astype(BF), upstream, preferred_element_type=F32
            )
            if most == seq:
                dk[head, :, :] = grad_keys
                dv[head, :, :] = grad_values
            else:
                dk[head, :most, :] += grad_keys
                dv[head, :most, :] += grad_values
            grad_queries = jnp.dot(
                keys_turned[:, :most], grad_scores, preferred_element_type=F32
            )
            dq[head, first:most, :] = grad_queries.T * (1.0 / math.sqrt(HD))
        return carry

    lax.fori_loop(0, heads, one_head, 0, unroll=True)
    sources = [dq] * heads + [dk] * heads + [dv] * heads
    for gathered, ordered in blocks:
        source, target = pl.ds(ordered, local), pl.ds(gathered, local)
        for tile in range(-(-3 * heads // 2)):
            indices = range(tile * 2, min(tile * 2 + 2, 3 * heads))
            parts = [sources[index][index % heads, source, :] for index in indices]
            joined = parts[0] if len(parts) == 1 else jnp.concatenate(parts, axis=1)
            if tile * 2 < 2 * heads:
                joined = turned(joined, cosine[source, :], -sine[source, :])
            grad_projected[target, tile * TILE : tile * TILE + joined.shape[1]] = joined.astype(BF)


def attention_back(blocks, heads, length, grad_context, q_heads, k_heads, v_heads, level, cosine, sine):
    seq = grad_context.shape[0]
    vmem = pl.BlockSpec(memory_space=pltpu.VMEM)
    return pl.pallas_call(
        functools.partial(attention_back_kernel, blocks),
        out_shape=jax.ShapeDtypeStruct((seq, 3 * heads * HD), BF),
        in_specs=[pl.BlockSpec(memory_space=pltpu.SMEM)] + [vmem] * 7,
        out_specs=vmem,
        scratch_shapes=[
            pltpu.VMEM((heads, seq, HD), BF),
            pltpu.VMEM((heads, seq, HD), F32),
            pltpu.VMEM((heads, seq, HD), F32),
            pltpu.VMEM((heads, seq, HD), F32),
        ],
        compiler_params=pltpu.CompilerParams(vmem_limit_bytes=56 << 20),
        cost_estimate=pl.CostEstimate(
            flops=10 * heads * seq * seq * HD, transcendentals=heads * seq * seq, bytes_accessed=20 << 20
        ),
    )(length, grad_context, q_heads, k_heads, v_heads, level, cosine, sine)


def tables(seq):
    step = np.arange(HD // 2, dtype=np.float32)
    frequency = np.power(np.float32(10000.0), np.float32(-2.0) * step / np.float32(HD))
    angle = np.arange(seq, dtype=np.float32)[:, None] * frequency[None, :]
    cosine, sine = np.cos(angle), np.sin(angle)
    signed = np.concatenate([-sine, sine, -sine, sine], axis=1)
    return jnp.asarray(np.tile(cosine, (1, 4))), jnp.asarray(signed)


MESH = pl.DeviceIdType.MESH


def greet(count):
    barrier = pltpu.get_barrier_semaphore()
    z, c, t = lax.axis_index("fsdp"), lax.axis_index("cp"), lax.axis_index("tp")

    def hello(**place):
        pl.semaphore_signal(barrier, inc=1, device_id=place, device_id_type=MESH)

    hello(cp=1 - c)
    hello(tp=t + 1 - 2 * (t % 2))
    hello(tp=(t + 2) % 4)
    pl.when(z > 0)(lambda: hello(fsdp=z - 1))
    pl.when(z < count - 1)(lambda: hello(fsdp=z + 1))
    peers = 3 + jnp.minimum(z, 1) + jnp.minimum(count - 1 - z, 1)
    pl.semaphore_wait(barrier, peers)


class Mail:
    def __init__(self, send, recv):
        self.send, self.recv, self.used, self.open = send, recv, 0, []

    def slot(self):
        self.used += 1
        return self.used - 1

    def copy(self, slot, source, target, **place):
        return pltpu.make_async_remote_copy(
            src_ref=source,
            dst_ref=target,
            send_sem=self.send.at[slot],
            recv_sem=self.recv.at[slot],
            device_id=place,
            device_id_type=MESH,
        )

    def start(self, slot, source, target, when=None, **place):
        made = self.copy(slot, source, target, **place)
        if when is None:
            made.start()
        else:
            pl.when(when)(made.start)
        self.open.append((made, when))

    def arrive(self, slot, target, when=None, **place):
        made = self.copy(slot, target, target, **place)
        if when is None:
            made.wait_recv()
        else:
            pl.when(when)(made.wait_recv)

    def finish(self):
        for made, when in self.open:
            if when is None:
                made.wait_send()
            else:
                pl.when(when)(made.wait_send)


class Stage:
    def __init__(self, pieces, stage, sems):
        self.made = []
        for k, (source, target, when) in enumerate(pieces):
            self.made.append(
                (
                    pltpu.make_async_copy(source, stage.at[k], sems.at[0, k]),
                    pltpu.make_async_copy(stage.at[k], target, sems.at[1, k]),
                    when,
                )
            )

    def begin(self):
        for copy, _, when in self.made:
            copy.start() if when is None else pl.when(when)(copy.start)

    def turn(self):
        for first, second, when in self.made:

            def on(first=first, second=second):
                first.wait()
                second.start()

            on() if when is None else pl.when(when)(on)

    def end(self):
        for _, copy, when in self.made:
            copy.wait() if when is None else pl.when(when)(copy.wait)


class Line:
    def __init__(self, mail, count, own, at, ready=()):
        self.mail, self.count, self.own, self.at = mail, count, own, at
        self.ready = ready
        self.z = lax.axis_index("fsdp")
        self.up = [mail.slot() for _ in range(count)]
        self.down = [mail.slot() for _ in range(count)]

    def has_low(self, hop):
        return self.z >= hop

    def has_high(self, hop):
        return self.z <= self.count - 1 - hop

    def send(self, hop):
        z, count, mail = self.z, self.count, self.mail
        low, high = jnp.maximum(z - hop + 1, 0), jnp.minimum(z + hop - 1, count - 1)
        from_low = from_high = self.own
        if hop > 1:
            from_low, from_high = self.at(low), self.at(high)
        if 0 < hop - 1 <= len(self.ready):
            from_low, from_high = self.ready[hop - 2]
        mail.start(
            self.up[hop], from_low, self.at(low),
            when=(z >= hop - 1) & (z < count - 1), fsdp=jnp.minimum(z + 1, count - 1),
        )
        mail.start(
            self.down[hop], from_high, self.at(high),
            when=(z <= count - hop) & (z > 0), fsdp=jnp.maximum(z - 1, 0),
        )

    def arrive(self, hop):
        z, count = self.z, self.count
        self.mail.arrive(
            self.up[hop], self.at(jnp.maximum(z - hop, 0)), when=self.has_low(hop), fsdp=z
        )
        self.mail.arrive(
            self.down[hop], self.at(jnp.minimum(z + hop, count - 1)), when=self.has_high(hop), fsdp=z
        )


    def keep(self):
        z, count = self.z, self.count
        made = [(self.own, self.at(z), None)]
        for index, (low, high) in enumerate(self.ready):
            hop = index + 1
            made.append((low, self.at(jnp.maximum(z - hop, 0)), self.has_low(hop)))
            made.append((high, self.at(jnp.minimum(z + hop, count - 1)), self.has_high(hop)))
        return made


class Across:
    def __init__(self, line, own, mine_at, other_at):
        self.line, self.own, self.mine_at, self.other_at = line, own, mine_at, other_at
        self.c = lax.axis_index("cp")
        self.low = [line.mail.slot() for _ in range(line.count)]
        self.high = [line.mail.slot() for _ in range(line.count)]

    def send(self, hop):
        line, mail = self.line, self.line.mail
        z, count, other = line.z, line.count, 1 - self.c
        if hop == 0:
            mail.start(self.low[0], self.own, self.mine_at(z), cp=other)
            return
        low, high = jnp.maximum(z - hop, 0), jnp.minimum(z + hop, count - 1)
        mail.start(self.low[hop], self.mine_at(low), self.mine_at(low), when=line.has_low(hop), cp=other)
        mail.start(self.high[hop], self.mine_at(high), self.mine_at(high), when=line.has_high(hop), cp=other)

    def arrive(self, hop):
        line, mail = self.line, self.line.mail
        z, count, other = line.z, line.count, 1 - self.c
        if hop == 0:
            mail.arrive(self.low[0], self.other_at(z), cp=other)
            return
        low, high = jnp.maximum(z - hop, 0), jnp.minimum(z + hop, count - 1)
        mail.arrive(self.low[hop], self.other_at(low), when=line.has_low(hop), cp=other)
        mail.arrive(self.high[hop], self.other_at(high), when=line.has_high(hop), cp=other)


def first_gather_kernel(
    count, tokens, tokens_away, gain, qkv, turned_out, wide, wide_away,
    token_rows, normed_full, qkv_full, out_half, low_pair, high_pair,
    landed, normed, wide_landed, qkv_stage, out_stage,
    send, recv, local, qkv_local, out_local,
):
    z, c, t = lax.axis_index("fsdp"), lax.axis_index("cp"), lax.axis_index("tp")
    beside, yonder = t + 1 - 2 * (t % 2), (t + 2) % 4
    low, high = low_pair.at[0], high_pair.at[0]
    mail = Mail(send, recv)
    greet(count)
    stage_qkv = Stage([(qkv, qkv_full.at[z, c], None)], qkv_stage, qkv_local)
    stage_out = Stage([(turned_out, out_half.at[z], None)], out_stage, out_local)
    kept = []

    heads = Line(mail, count, qkv, lambda j: qkv_full.at[j, c])
    heads_across = Across(
        heads, qkv, lambda j: qkv_full.at[j, c], lambda j: qkv_full.at[j, 1 - c]
    )
    outs = Line(mail, count, turned_out, lambda j: out_half.at[j])
    wide_up, wide_down = mail.slot(), mail.slot()
    rows_x, wide_x = mail.slot(), mail.slot()
    rows_y = [mail.slot() for _ in range(2)]
    rows_core = [mail.slot() for _ in range(4)]

    mail.start(rows_x, tokens_away, landed, cp=1 - c)
    heads.send(1)

    def rows_out(source, side, half):
        def one(place):
            rows = source[place, :]
            token_rows[half, place, :] = rows
            normed[half, place, :] = (normalize(rows.astype(F32)) * gain[...]).astype(BF)

        in_pieces(source.shape[0], one)
        mail.start(rows_y[side], normed.at[half], normed_full.at[t, half], tp=yonder)
        mail.start(rows_core[side], normed.at[half], normed_full.at[t, half], tp=beside)

    stage_qkv.begin()
    stage_out.begin()
    rows_out(tokens, 0, c)
    stage_qkv.turn()
    stage_out.turn()
    mail.arrive(rows_x, landed, cp=1 - c)
    heads_across.send(0)
    rows_out(landed, 1, 1 - c)
    kept.append(pltpu.make_async_copy(normed, normed_full.at[t], local.at[2]))
    kept[-1].start()

    def rows_on(k, half):
        mail.arrive(rows_y[k], normed_full.at[yonder, half], tp=yonder)
        mail.start(
            rows_core[2 + k], normed_full.at[yonder, half], normed_full.at[yonder, half], tp=beside
        )

    for hop in range(1, count):
        heads.arrive(hop)
        if hop + 1 < count:
            heads.send(hop + 1)
        heads_across.send(hop)
        if hop == 1:
            rows_on(0, c)
            rows_on(1, 1 - c)
            outs.send(1)
        if hop == min(2, count - 1):
            mail.start(wide_up, wide, low, when=z < count - 1, fsdp=jnp.minimum(z + 1, count - 1))
            mail.start(wide_down, wide, high, when=z > 0, fsdp=jnp.maximum(z - 1, 0))
    mail.start(wide_x, wide_away, wide_landed, cp=1 - c)
    for hop in range(1, count):
        outs.arrive(hop)
        if hop + 1 < count:
            outs.send(hop + 1)
    for hop in range(count):
        heads_across.arrive(hop)
    mail.arrive(rows_core[0], normed_full.at[beside, c], tp=beside)
    mail.arrive(rows_core[1], normed_full.at[beside, 1 - c], tp=beside)
    far = (beside + 2) % 4
    mail.arrive(rows_core[2], normed_full.at[far, c], tp=beside)
    mail.arrive(rows_core[3], normed_full.at[far, 1 - c], tp=beside)
    mail.arrive(wide_x, wide_landed, cp=1 - c)
    for pair, place in ((low_pair, 1), (high_pair, 3)):
        kept.append(pltpu.make_async_copy(wide_landed, pair.at[1], local.at[place]))
        kept[-1].start()
    mail.arrive(wide_up, low, when=z > 0, fsdp=z)
    mail.arrive(wide_down, high, when=z < count - 1, fsdp=z)
    for copy in kept:
        copy.wait()
    stage_qkv.end()
    stage_out.end()
    mail.finish()


def first_gather(count, tokens, tokens_away, gain, qkv, turned_out, wide, wide_away):
    slots = 6 * count + 10
    anywhere = pl.BlockSpec(memory_space=pl.ANY)
    vmem = pl.BlockSpec(memory_space=pltpu.VMEM)
    pair = (2,) + tokens.shape
    return pl.pallas_call(
        functools.partial(first_gather_kernel, count),
        out_shape=(
            jax.ShapeDtypeStruct(pair, BF),
            jax.ShapeDtypeStruct((4,) + pair, BF),
            jax.ShapeDtypeStruct((count, 2) + qkv.shape, BF),
            jax.ShapeDtypeStruct((count,) + turned_out.shape, BF),
            jax.ShapeDtypeStruct((2,) + wide.shape, BF),
            jax.ShapeDtypeStruct((2,) + wide.shape, BF),
        ),
        in_specs=[vmem, anywhere, vmem] + [anywhere] * 4,
        out_specs=(vmem,) + (anywhere,) * 5,
        scratch_shapes=[
            pltpu.VMEM(tokens.shape, BF),
            pltpu.VMEM(pair, BF),
            pltpu.VMEM(wide.shape, BF),
            pltpu.VMEM((1,) + qkv.shape, BF),
            pltpu.VMEM((1,) + turned_out.shape, BF),
            pltpu.SemaphoreType.DMA((slots,)),
            pltpu.SemaphoreType.DMA((slots,)),
            pltpu.SemaphoreType.DMA((4,)),
            pltpu.SemaphoreType.DMA((2, 1)),
            pltpu.SemaphoreType.DMA((2, 1)),
        ],
        compiler_params=pltpu.CompilerParams(
            collective_id=1, has_side_effects=True, vmem_limit_bytes=32 << 20
        ),
    )(tokens, tokens_away, gain, qkv, turned_out, wide, wide_away)


def in_pieces(rows, body, size=16):
    if rows % size:
        body(pl.ds(0, rows))
        return
    lax.fori_loop(0, rows // size, lambda i, carry: (body(pl.ds(i * size, size)), carry)[1], 0)


class Spread:
    def __init__(self, mail, own, at):
        self.mail, self.own, self.at = mail, own, at
        self.c, self.t = lax.axis_index("cp"), lax.axis_index("tp")
        self.beside, self.yonder = self.t + 1 - 2 * (self.t % 2), (self.t + 2) % 4
        self.x = [mail.slot() for _ in range(3)]
        self.y = [mail.slot() for _ in range(3)]
        self.core = {}

    def to_core(self, c_is_own, t_is_own, piece):
        slot = self.core[c_is_own, t_is_own, piece] = self.mail.slot()
        c = self.c if c_is_own else 1 - self.c
        t = self.t if t_is_own else self.yonder
        source = self.own(piece) if c_is_own and t_is_own else self.at(c, t, piece)
        self.mail.start(slot, source, self.at(c, t, piece), tp=self.beside)

    def begin(self, piece):
        c, t = self.c, self.t
        if piece == 0:
            self.mail.start(self.x[0], self.own(0), self.at(c, t, 0), cp=1 - c)
        else:
            self.mail.start(self.y[0], self.own(1), self.at(c, t, 1), tp=self.yonder)
            self.mail.start(self.x[1], self.own(1), self.at(c, t, 1), cp=1 - c)
            self.mail.start(self.y[1], self.own(0), self.at(c, t, 0), tp=self.yonder)
        self.to_core(True, True, piece)

    def turn(self):
        c, t, mail, yonder = self.c, self.t, self.mail, self.yonder
        mail.arrive(self.x[0], self.at(1 - c, t, 0), cp=1 - c)
        mail.start(self.y[2], self.at(1 - c, t, 0), self.at(1 - c, t, 0), tp=yonder)
        self.to_core(False, True, 0)
        mail.arrive(self.y[0], self.at(c, yonder, 1), tp=yonder)
        mail.start(self.x[2], self.at(c, yonder, 1), self.at(c, yonder, 1), cp=1 - c)
        self.to_core(True, False, 1)

    def end(self):
        c, t, mail, yonder = self.c, self.t, self.mail, self.yonder
        mail.arrive(self.x[1], self.at(1 - c, t, 1), cp=1 - c)
        self.to_core(False, True, 1)
        mail.arrive(self.y[1], self.at(c, yonder, 0), tp=yonder)
        self.to_core(True, False, 0)
        mail.arrive(self.x[2], self.at(1 - c, yonder, 1), cp=1 - c)
        self.to_core(False, False, 1)
        mail.arrive(self.y[2], self.at(1 - c, yonder, 0), tp=yonder)
        self.to_core(False, False, 0)
        far = (self.beside + 2) % 4
        for (c_is_own, t_is_own, piece), slot in self.core.items():
            place = self.at(
                c if c_is_own else 1 - c, self.beside if t_is_own else far, piece
            )
            mail.arrive(slot, place, tp=self.beside)


def second_gather_kernel(
    count, part, tokens, gain, wide, first_low, first_high, second_low, second_high, *refs
):
    hops_mine, hops_other = min(2, count - 1), 1
    wide_other = first_low.at[1]
    ready_mine = [first_low.at[0], first_high.at[0], second_low.at[0], second_high.at[0]]
    ready_mine = ready_mine[: 2 * hops_mine]
    ready_other = [second_low.at[1], second_high.at[1]]
    middle, middle_home, normed_full, gate_full, up_full, down_full = refs[:6]
    own, from_core, to_yonder, from_yonder, normed, stage, send, recv, local, local_line = refs[6:]
    c, t = lax.axis_index("cp"), lax.axis_index("tp")
    rows = tokens.shape[0]
    half = rows // 2
    mail = Mail(send, recv)
    greet(count)

    mine, other = [], []
    for which, full in enumerate((gate_full, up_full, down_full)):
        for lines, side, piece, ready in (
            (mine, c, wide, ready_mine), (other, 1 - c, wide_other, ready_other),
        ):
            arrived = [
                (ready[2 * hop].at[which], ready[2 * hop + 1].at[which])
                for hop in range(len(ready) // 2)
            ]
            lines.append(
                Line(
                    mail, count, piece.at[which],
                    lambda j, full=full, side=side: full.at[j, side], arrived,
                )
            )
    summed = TensorSum(mail, part, own, from_core, to_yonder, from_yonder, local)
    spread = Spread(
        mail, lambda piece: normed.at[piece], lambda c, t, piece: normed_full.at[piece, t, c]
    )

    summed.begin()
    placing = Stage([piece for line in mine + other for piece in line.keep()], stage, local_line)
    placing.begin()

    def send_hop(lines, hop):
        for line in lines:
            if hop < count:
                line.send(hop)

    def arrive_hop(lines, hop):
        for line in lines:
            if hop < count:
                line.arrive(hop)

    send_hop(other, hops_other + 1)
    send_hop(mine, hops_mine + 1)
    summed.turn()
    placing.turn()
    for piece in range(2):
        summed.arrive(piece)

        def norm(place, piece=piece):
            row = pl.ds(place.start + piece * half, place.size)
            values = tokens[row, :].astype(F32) + BRANCH * summed.rows(row)
            middle[row, :] = values
            normed[piece, place, :] = (normalize(values) * gain[...]).astype(BF)

        in_pieces(half, norm)
        spread.begin(piece)
    keep_normed = pltpu.make_async_copy(normed, normed_full.at[:, t, c], local.at[0])
    keep_normed.start()
    home = mail.slot()
    stay, go = pl.ds(c * half, half), pl.ds((1 - c) * half, half)
    keep_home = pltpu.make_async_copy(middle.at[stay], middle_home.at[c], local.at[1])
    keep_home.start()
    spread.turn()
    mail.start(home, middle.at[go], middle_home.at[c], cp=1 - c)
    for step in range(1, count):
        hop = hops_other + step
        if hop < count:
            for line_other, line_mine in zip(other, mine):
                line_other.arrive(hop)
                if hop + 1 < count:
                    line_other.send(hop + 1)
                if hops_mine + step < count:
                    line_mine.arrive(hops_mine + step)
                    if hops_mine + step + 1 < count:
                        line_mine.send(hops_mine + step + 1)
        if step == 1:
            spread.end()
    if count == 1:
        spread.end()
    mail.arrive(home, middle_home.at[1 - c], cp=1 - c)
    keep_home.wait()
    keep_normed.wait()
    placing.end()
    mail.finish()


def second_gather(count, part, tokens, gain, wide, first_low, first_high, second_low, second_high):
    slots = 12 * count + 24
    rows, width = tokens.shape
    anywhere = pl.BlockSpec(memory_space=pl.ANY)
    vmem = pl.BlockSpec(memory_space=pltpu.VMEM)
    full = jax.ShapeDtypeStruct((count, 2) + wide.shape[1:], BF)
    return pl.pallas_call(
        functools.partial(second_gather_kernel, count),
        out_shape=(
            jax.ShapeDtypeStruct((rows, width), F32),
            jax.ShapeDtypeStruct((2, rows // 2, width), F32),
            jax.ShapeDtypeStruct((2, 4, 2, rows // 2, width), BF),
            full,
            full,
            full,
        ),
        in_specs=[anywhere, vmem, vmem] + [anywhere] * 5,
        out_specs=(vmem,) + (anywhere,) * 5,
        scratch_shapes=[
            pltpu.VMEM((2, rows, width), BF),
            pltpu.VMEM((2, rows, width), BF),
            pltpu.VMEM((rows, width), BF),
            pltpu.VMEM((rows, width), BF),
            pltpu.VMEM((2, rows // 2, width), BF),
            pltpu.VMEM((24,) + wide.shape[1:], BF),
            pltpu.SemaphoreType.DMA((slots,)),
            pltpu.SemaphoreType.DMA((slots,)),
            pltpu.SemaphoreType.DMA((2,)),
            pltpu.SemaphoreType.DMA((2, 24)),
        ],
        compiler_params=pltpu.CompilerParams(
            collective_id=2, has_side_effects=True, vmem_limit_bytes=40 << 20
        ),
    )(part, tokens, gain, wide, first_low, first_high, second_low, second_high)


class TensorSum:
    def __init__(self, mail, part, own, from_core, to_yonder, from_yonder, local):
        self.mail, self.part, self.own, self.from_core = mail, part, own, from_core
        self.to_yonder, self.from_yonder, self.local = to_yonder, from_yonder, local
        self.t = t = lax.axis_index("tp")
        self.beside, self.yonder = t + 1 - 2 * (t % 2), (t + 2) % 4
        self.core = [mail.slot() for _ in range(2)]
        self.across = [mail.slot() for _ in range(2)]
        self.half = from_yonder.shape[0] // 2

    def begin(self):
        part, far = self.part, (self.beside + 2) % 4
        self.mail.start(self.core[1], part.at[far], self.from_core.at[1], tp=self.beside)
        self.mail.start(self.core[0], part.at[self.beside], self.from_core.at[0], tp=self.beside)
        self.kept = [
            pltpu.make_async_copy(part.at[self.yonder], self.own.at[1], self.local.at[0]),
            pltpu.make_async_copy(part.at[self.t], self.own.at[0], self.local.at[1]),
        ]
        for copy in self.kept:
            copy.start()

    def turn(self):
        own, from_core = self.own, self.from_core
        self.kept[0].wait()
        self.mail.arrive(self.core[1], from_core.at[1], tp=self.beside)
        for piece in range(2):

            def add(place, piece=piece):
                place = pl.ds(place.start + piece * self.half, place.size)
                self.to_yonder[place, :] = (
                    own[1, place, :].astype(F32) + from_core[1, place, :].astype(F32)
                ).astype(BF)

            in_pieces(self.half, add)
            block = pl.ds(piece * self.half, self.half)
            self.mail.start(
                self.across[piece], self.to_yonder.at[block], self.from_yonder.at[block],
                tp=self.yonder,
            )
        self.kept[1].wait()
        self.mail.arrive(self.core[0], from_core.at[0], tp=self.beside)

    def arrive(self, piece):
        block = pl.ds(piece * self.half, self.half)
        self.mail.arrive(self.across[piece], self.from_yonder.at[block], tp=self.yonder)

    def rows(self, row):
        return (
            self.own[0, row, :].astype(F32)
            + self.from_core[0, row, :].astype(F32)
            + self.from_yonder[row, :].astype(F32)
        )


class Drain:
    def __init__(self, mail, count, fill, total, landed):
        self.mail, self.count, self.fill, self.total, self.landed = mail, count, fill, total, landed
        self.z = lax.axis_index("fsdp")
        self.slots = [[mail.slot() for _ in range(count)] for _ in range(2)]

    def sends(self, hop, up):
        z, count = self.z, self.count
        return (z <= hop - 1) & (z < count - 1) if up else (z >= count - hop) & (z > 0)

    def gets(self, hop, up):
        z, count = self.z, self.count
        return (z >= 1) & (z <= hop) if up else (z <= count - 2) & (z >= count - 1 - hop)

    def block(self, hop, up):
        z, count = self.z, self.count
        return jnp.minimum(z + count - hop, count - 1) if up else jnp.maximum(z - count + hop, 0)

    def arrive(self, hop):
        for side, up in enumerate((True, False)):
            self.mail.arrive(
                self.slots[side][hop], self.landed(side, hop), when=self.gets(hop, up), fsdp=self.z
            )

    def gather(self, hop):
        for side, up in enumerate((True, False)):
            target = self.total(side, hop)

            def work(side=side, up=up, target=target):
                self.fill(hop, up, self.block(hop, up), target)
                if hop > 1:

                    def add():
                        landed = self.landed(side, hop - 1)

                        def one(place):
                            target[place, :] = (
                                target[place, :].astype(F32) + landed[place, :].astype(F32)
                            ).astype(BF)

                        in_pieces(target.shape[0], one)

                    pl.when(self.gets(hop - 1, up))(add)

            pl.when(self.sends(hop, up))(work)

    def send(self, hop):
        z, count = self.z, self.count
        for side, up in enumerate((True, False)):
            to = jnp.minimum(z + 1, count - 1) if up else jnp.maximum(z - 1, 0)
            self.mail.start(
                self.slots[side][hop], self.total(side, hop), self.landed(side, hop),
                when=self.sends(hop, up), fsdp=to,
            )


def norm_back(values, gain, upstream):
    scale = lax.rsqrt(jnp.mean(values * values, axis=-1, keepdims=True) + EPSILON)
    norm = values * scale
    scaled = upstream * gain
    mean = jnp.mean(scaled * norm, axis=-1, keepdims=True)
    return scale * (scaled - norm * mean), upstream * norm


def first_sum_kernel(
    count, part, gate_grad, up_grad, hidden, middle, cotangent, gain, down,
    grad_middle, attention_full, gain_rows, leaving_up, leaving_down, feedforward,
    own, from_core, first, second, grad_attention, totals, landed, hidden_rows, product,
    send, recv, local, hidden_local,
):
    z, c, t = lax.axis_index("fsdp"), lax.axis_index("cp"), lax.axis_index("tp")
    beside, yonder = t + 1 - 2 * (t % 2), (t + 2) % 4
    far = (beside + 2) % 4
    half = middle.shape[0] // 2
    width = middle.shape[1]
    mail = Mail(send, recv)
    greet(count)
    last = count - 1

    def fill_from(which):
        def fill(hop, up, j, target):
            copy = pltpu.make_async_copy((gate_grad, up_grad)[which].at[j], target, local.at[4])
            copy.start()
            copy.wait()

        return fill

    drains = [
        Drain(
            mail, count, fill_from(which),
            lambda side, hop, which=which: (
                (leaving_up, leaving_down)[side].at[which] if hop == last else totals.at[side, hop - 1, which]
            ),
            lambda side, hop, which=which: landed.at[side, hop - 1, which],
        )
        for which in range(2)
    ]

    core = {}
    mine = {}
    order = ((0, 0), (0, 1), (1, 0), (1, 1))
    for index, (c_own, t_own) in enumerate(order):
        block_c = c if c_own else 1 - c
        core[c_own, t_own] = mail.slot()
        mail.start(
            core[c_own, t_own], part.at[:, beside if t_own else far, block_c],
            from_core.at[c_own, t_own], tp=beside,
        )
        mine[c_own, t_own] = pltpu.make_async_copy(
            part.at[:, t if t_own else yonder, block_c], own.at[c_own, t_own], local.at[index]
        )
        mine[c_own, t_own].start()
    if last > 1:
        for drain in drains:
            drain.gather(1)
            drain.send(1)

    block_rows = product.shape[1]
    blocks = hidden.shape[0] // block_rows

    def hidden_copy(block):
        return pltpu.make_async_copy(
            hidden.at[pl.ds(block * block_rows, block_rows)], hidden_rows.at[block % 2],
            hidden_local.at[0, block % 2],
        )

    def product_copy(block):
        return pltpu.make_async_copy(
            product.at[block % 2], feedforward.at[pl.ds(block * block_rows, block_rows)],
            hidden_local.at[1, block % 2],
        )

    def product_block(block):
        hidden_copy(block).wait()
        if block + 1 < blocks:
            hidden_copy(block + 1).start()
        if block > 1:
            product_copy(block - 2).wait()

        def one(k, carry):
            columns = pl.ds(pl.multiple_of(k * 2 * TILE, 2 * TILE), 2 * TILE)
            value = lax.dot_general(
                hidden_rows[block % 2], down[columns, :], (((1,), (1,)), ((), ())),
                preferred_element_type=F32,
            )
            product[block % 2, :, columns] = value.astype(BF)
            return carry

        lax.fori_loop(0, width // (2 * TILE), one, 0)
        product_copy(block).start()

    hidden_copy(0).start()
    product_block(0)

    quarter = half // 2
    quarters = [(piece, pl.ds(side * quarter, quarter)) for piece in range(2) for side in range(2)]
    x_first = [[mail.slot() for _ in range(2)] for _ in quarters]
    y_second = [mail.slot() for _ in quarters]
    ring_y = [mail.slot() for _ in quarters]
    ring_core = [mail.slot() for _ in quarters]
    ring_far = [mail.slot() for _ in quarters]

    def core_add(c_own, t_own, piece, rows):
        def one(place):
            row = pl.ds(rows.start + place.start, place.size)
            own[c_own, t_own, piece, row, :] = (
                own[c_own, t_own, piece, row, :].astype(F32)
                + from_core[c_own, t_own, piece, row, :].astype(F32)
            ).astype(BF)

        in_pieces(quarter, one)

    for t_own in (0, 1):
        mine[0, t_own].wait()
        mail.arrive(core[0, t_own], from_core.at[0, t_own], tp=beside)
    for k, (piece, rows) in enumerate(quarters):
        for t_own in (0, 1):
            core_add(0, t_own, piece, rows)
            mail.start(
                x_first[k][t_own], own.at[0, t_own, piece, rows], first.at[k, t_own], cp=1 - c
            )
    for t_own in (0, 1):
        mine[1, t_own].wait()
        mail.arrive(core[1, t_own], from_core.at[1, t_own], tp=beside)

    def add_first(k, t_own):
        piece, rows = quarters[k]

        def one(place):
            row = pl.ds(rows.start + place.start, place.size)
            own[1, t_own, piece, row, :] = (
                own[1, t_own, piece, row, :].astype(F32)
                + from_core[1, t_own, piece, row, :].astype(F32)
                + first[k, t_own, place, :].astype(F32)
            ).astype(BF)

        in_pieces(quarter, one)

    gain_rows[...] = jnp.zeros_like(gain_rows)

    def finish(k):
        piece, rows = quarters[k]
        mail.arrive(y_second[k], second.at[k], tp=yonder)

        def back(place):
            local_row = pl.ds(rows.start + place.start, place.size)
            row = pl.ds(piece * half + rows.start + place.start, place.size)
            summed = own[1, 1, piece, local_row, :].astype(F32) + second[k, place, :].astype(F32)
            grad, products = norm_back(middle[row, :], gain[...], summed)
            grad = cotangent[row, :].astype(F32) + grad
            grad_middle[row, :] = grad
            grad_attention[piece, local_row, :] = (BRANCH * grad).astype(BF)
            gain_rows[...] += jnp.sum(products, axis=0, keepdims=True)

        in_pieces(quarter, back)
        source = grad_attention.at[piece, rows]
        mail.start(ring_y[k], source, attention_full.at[t, piece, rows], tp=yonder)
        mail.start(ring_core[k], source, attention_full.at[t, piece, rows], tp=beside)

    def z_hop(hop):
        for drain in drains:
            drain.arrive(hop - 1)
            drain.gather(hop)
            drain.send(hop)

    for k, (piece, rows) in enumerate(quarters):
        mail.arrive(x_first[k][0], first.at[k, 0], cp=1 - c)
        add_first(k, 0)
        mail.start(y_second[k], own.at[1, 0, piece, rows], second.at[k], tp=yonder)
        mail.arrive(x_first[k][1], first.at[k, 1], cp=1 - c)
        add_first(k, 1)
        if k > 0:
            finish(k - 1)
        if k == 2 and last > 2:
            z_hop(2)
        product_block(k + 1)
    finish(len(quarters) - 1)
    for block in range(len(quarters) + 1, blocks):
        product_block(block)
    keep = pltpu.make_async_copy(grad_attention, attention_full.at[t], local.at[0])
    keep.start()
    for hop in range(3, last):
        z_hop(hop)
    for k, (piece, rows) in enumerate(quarters):
        arrived = attention_full.at[yonder, piece, rows]
        mail.arrive(ring_y[k], arrived, tp=yonder)
        mail.start(ring_far[k], arrived, arrived, tp=beside)
    for k, (piece, rows) in enumerate(quarters):
        mail.arrive(ring_core[k], attention_full.at[beside, piece, rows], tp=beside)
        mail.arrive(ring_far[k], attention_full.at[far, piece, rows], tp=beside)
    for drain in drains:
        if last > 1:
            drain.arrive(last - 1)
        if last > 0:
            drain.gather(last)
    keep.wait()
    for block in range(blocks - 2, blocks):
        product_copy(block).wait()
    mail.finish()


def first_sum(count, part, gate_grad, up_grad, hidden, middle, cotangent, gain, down):
    slots = 6 * count + 32
    rows, width = middle.shape
    block = gate_grad.shape[1:]
    anywhere = pl.BlockSpec(memory_space=pl.ANY)
    vmem = pl.BlockSpec(memory_space=pltpu.VMEM)
    hops = max(count - 2, 1)
    return pl.pallas_call(
        functools.partial(first_sum_kernel, count),
        out_shape=(
            jax.ShapeDtypeStruct((rows, width), F32),
            jax.ShapeDtypeStruct((4, 2, rows // 2, width), BF),
            jax.ShapeDtypeStruct((1, width), F32),
            jax.ShapeDtypeStruct((2,) + block, BF),
            jax.ShapeDtypeStruct((2,) + block, BF),
            jax.ShapeDtypeStruct((hidden.shape[0], width), BF),
        ),
        in_specs=[anywhere] * 4 + [vmem] * 4,
        out_specs=(vmem, anywhere, vmem, vmem, vmem, anywhere),
        scratch_shapes=[
            pltpu.VMEM((2, 2, 2, rows // 2, width), BF),
            pltpu.VMEM((2, 2, 2, rows // 2, width), BF),
            pltpu.VMEM((4, 2, rows // 4, width), BF),
            pltpu.VMEM((4, rows // 4, width), BF),
            pltpu.VMEM((2, rows // 2, width), BF),
            pltpu.VMEM((2, hops, 2) + block, BF),
            pltpu.VMEM((2, hops, 2) + block, BF),
            pltpu.VMEM((2, hidden.shape[0] // 8, hidden.shape[1]), BF),
            pltpu.VMEM((2, hidden.shape[0] // 8, width), BF),
            pltpu.SemaphoreType.DMA((slots,)),
            pltpu.SemaphoreType.DMA((slots,)),
            pltpu.SemaphoreType.DMA((5,)),
            pltpu.SemaphoreType.DMA((2, 2)),
        ],
        compiler_params=pltpu.CompilerParams(
            collective_id=3, has_side_effects=True, vmem_limit_bytes=60 << 20
        ),
    )(part, gate_grad, up_grad, hidden, middle, cotangent, gain, down)


AHEAD = 6


def last_sum_kernel(
    count, grad_projected, qkv_full, qkv_grad, out_grad, tokens, grad_middle, gain, gain_rows,
    qkv_total, out_total, grad_tokens, gain_sums,
    own, from_core, to_yonder, from_yonder, pieces,
    from_x, heads_sum, heads_landed, outs_sum, outs_landed, final_out, gains, gain_line,
    part, weights, give_sum, give_landed, give_own, give_total,
    send, recv, local, weights_local,
):
    z, c, t = lax.axis_index("fsdp"), lax.axis_index("cp"), lax.axis_index("tp")
    beside, yonder = t + 1 - 2 * (t % 2), (t + 2) % 4
    half = tokens.shape[0] // 2
    last = count - 1
    mail = Mail(send, recv)
    greet(count)

    summed = TensorSum(mail, part, own, from_core, to_yonder, from_yonder, local)

    columns = qkv_total.shape[1]
    behind = columns * 5 // 6 // TILE * TILE
    split = -(-behind // (2 * TILE)) * TILE
    parts = [pl.ds(0, split), pl.ds(split, behind - split)]
    late = pl.ds(behind, columns - behind)
    cross = [[[mail.slot() for _ in range(count)] for _ in range(2)] for _ in parts]
    cross_own = [mail.slot() for _ in parts]

    def head_drain(lanes):
        def fill(hop, up, j, target):
            side = 0 if up else 1
            copy = pltpu.make_async_copy(qkv_grad.at[j, c, :, lanes], target, local.at[2])
            copy.start()
            copy.wait()
            arrived = from_x.at[side, hop - 1, :, lanes]

            def one(place):
                target[place, :] = (
                    target[place, :].astype(F32) + arrived[place, :].astype(F32)
                ).astype(BF)

            in_pieces(target.shape[0], one)

        return Drain(
            mail, count, fill,
            lambda side, hop: heads_sum.at[side, hop - 1, :, lanes],
            lambda side, hop: heads_landed.at[side, hop - 1, :, lanes],
        )

    heads = [head_drain(lanes) for lanes in parts]

    def late_fill(side_c):
        def fill(hop, up, j, target):
            copy = pltpu.make_async_copy(qkv_grad.at[j, side_c, :, late], target, local.at[2])
            copy.start()
            copy.wait()

        return fill

    stay = Drain(
        mail, count, late_fill(c),
        lambda side, hop: heads_sum.at[side, hop - 1, :, late],
        lambda side, hop: heads_landed.at[side, hop - 1, :, late],
    )
    give = Drain(
        mail, count, late_fill(1 - c),
        lambda side, hop: give_sum.at[side, hop - 1],
        lambda side, hop: give_landed.at[side, hop - 1],
    )
    give_slot = mail.slot()

    def fill_outs(hop, up, j, target):
        copy = pltpu.make_async_copy(out_grad.at[j], target, local.at[3])
        copy.start()
        copy.wait()

    outs = Drain(
        mail, count, fill_outs,
        lambda side, hop: outs_sum.at[side, hop - 1],
        lambda side, hop: outs_landed.at[side, hop - 1],
    )

    steps = [(hop, k) for hop in range(1, count + 1) for k in range(2)]

    def cross_send(step):
        if step >= len(steps):
            return
        hop, k = steps[step]
        lanes = parts[k]
        if hop == count:
            mail.start(
                cross_own[k], qkv_grad.at[z, 1 - c, :, lanes], from_x.at[0, last, :, lanes], cp=1 - c
            )
            return
        for side, up in enumerate((True, False)):
            mail.start(
                cross[k][side][hop], qkv_grad.at[heads[k].block(hop, up), 1 - c, :, lanes],
                from_x.at[side, hop - 1, :, lanes], when=heads[k].sends(hop, up), cp=1 - c,
            )

    def cross_arrive(hop, k):
        for side, up in enumerate((True, False)):
            mail.arrive(
                cross[k][side][hop], from_x.at[side, hop - 1, :, parts[k]],
                when=heads[k].sends(hop, up), cp=1 - c,
            )

    for step in range(AHEAD):
        cross_send(step)
    early_chains = (outs, give, stay)
    if count > 1:
        for drain in early_chains:
            drain.gather(1)
            drain.send(1)

    wide_block = weights.shape[1]
    blocks = qkv_full.shape[0] // wide_block

    def weights_copy(block, slot):
        return pltpu.make_async_copy(
            qkv_full.at[pl.ds(block * wide_block, wide_block)], weights.at[slot],
            weights_local.at[slot],
        )

    def product(block, carry):
        slot = lax.rem(block, 2)
        weights_copy(block, slot).wait()
        pl.when(block + 1 < blocks)(lambda: weights_copy(block + 1, 1 - slot).start())
        columns = pl.ds(pl.multiple_of(block * wide_block, wide_block), wide_block)
        value = lax.dot_general(
            grad_projected[...], weights[slot], (((1,), (1,)), ((), ())),
            preferred_element_type=F32,
        )
        part[:, :, columns] = value.astype(BF).reshape(part.shape[:2] + (wide_block,))
        return carry

    weights_copy(0, 0).start()
    thirds = [blocks * k // 3 for k in range(4)]

    keep = pltpu.make_async_copy(pieces.at[c], grad_tokens.at[c], local.at[0])
    home = mail.slot()
    gain_x, gain_y, gain_core = mail.slot(), mail.slot(), mail.slot()
    line = Line(mail, count, gain_line.at[z], lambda j: gain_line.at[j])

    def finish_rows():
        gains[0, 0:1, :] = jnp.zeros_like(gain_rows)
        gains[0, 1:2, :] = gain_rows[...]
        for piece in range(2):
            summed.arrive(piece)

            def back(place, piece=piece):
                row = pl.ds(place.start + piece * half, place.size)
                grad, rows = norm_back(tokens[row, :].astype(F32), gain[...], summed.rows(row))
                pieces[piece, place, :] = (grad_middle[row, :] + grad).astype(BF)
                gains[0, 0:1, :] += jnp.sum(rows, axis=0, keepdims=True)

            in_pieces(half, back)
        mail.start(home, pieces.at[1 - c], grad_tokens.at[c], cp=1 - c)
        keep.start()
        mail.start(gain_core, gains.at[0], gains.at[1], tp=beside)

    def gain_step(k):
        if k == 0:
            mail.arrive(gain_core, gains.at[1], tp=beside)
            gains[2] = gains[0] + gains[1]
            mail.start(gain_y, gains.at[2], gains.at[3], tp=yonder)
        elif k == 1:
            mail.arrive(gain_y, gains.at[3], tp=yonder)
            gains[4] = gains[2] + gains[3]
            mail.start(gain_x, gains.at[4], gains.at[5], cp=1 - c)
        elif k == 2:
            mail.arrive(gain_x, gains.at[5], cp=1 - c)
            gain_line[z] = gains[4] + gains[5]
            if count > 1:
                line.send(1)
        else:
            hop = k - 2
            line.arrive(hop)
            if hop + 1 < count:
                line.send(hop + 1)

    def outs_hop(hop):
        for drain in early_chains:
            drain.arrive(hop - 1)
            drain.gather(hop)
            drain.send(hop)

    def give_away():
        copy = pltpu.make_async_copy(qkv_grad.at[z, 1 - c, :, late], give_own, local.at[3])
        copy.start()
        copy.wait()
        if count > 1:
            give.arrive(last)

        def one(place):
            total = give_own[place, :].astype(F32)
            for side, up in enumerate((True, False)):
                if count > 1:
                    landed = give.landed(side, last)[place, :].astype(F32)
                    total += jnp.where(give.gets(last, up), landed, 0.0)
            give_total[place, :] = total.astype(BF)

        in_pieces(give_own.shape[0], one)
        mail.start(give_slot, give_total, from_x.at[0, last, :, late], cp=1 - c)

    for step, (hop, k) in enumerate(steps[:-2]):
        if step < 3:
            lax.fori_loop(thirds[step], thirds[step + 1], product, 0)
        if count == 2 and step == 1:
            lax.fori_loop(thirds[2], thirds[3], product, 0)
        if step == 2 or count == 2 and step == 1:
            summed.begin()
        cross_arrive(hop, k)
        cross_send(step + AHEAD)
        if hop > 1:
            heads[k].arrive(hop - 1)
        heads[k].gather(hop)
        heads[k].send(hop)
        if k == 1 and hop + 1 < count:
            outs_hop(hop + 1)
        if step == 2 or count == 2 and step == 1:
            summed.turn()
        if step == 3 or count == 2 and step == 1:
            finish_rows()
        if step == 5 or step == 3 and count == 3:
            gain_step(0)
            gain_step(1)
    if count == 1:
        lax.fori_loop(thirds[0], thirds[3], product, 0)
        summed.begin()
        summed.turn()
        finish_rows()
    if count <= 2:
        gain_step(0)
        gain_step(1)
    gain_step(2)
    give_away()

    own_copy = pltpu.make_async_copy(qkv_grad.at[z, c], from_x.at[1, last], local.at[2])
    own_copy.start()
    out_copy = pltpu.make_async_copy(out_grad.at[z], final_out, local.at[3])
    out_copy.start()
    for k, lanes in enumerate(parts):
        mail.arrive(cross_own[k], from_x.at[0, last, :, lanes], cp=1 - c)
    mail.arrive(give_slot, from_x.at[0, last, :, late], cp=1 - c)
    own_copy.wait()
    out_copy.wait()

    def start_heads(place):
        qkv_total[place, :] = from_x[0, last, place, :].astype(F32) + from_x[
            1, last, place, :
        ].astype(F32)

    in_pieces(qkv_total.shape[0], start_heads)

    def start_outs(place):
        out_total[place, :] = final_out[place, :].astype(F32)

    in_pieces(out_total.shape[0], start_outs)
    for hop in range(1, count):
        gain_step(2 + hop)
    if count > 1:
        chains = [(outs, pl.ds(0, out_total.shape[1]), out_total)]
        chains += [(stay, late, qkv_total)]
        chains += [(heads[k], lanes, qkv_total) for k, lanes in enumerate(parts)]
        for drain, lanes, total in chains:
            drain.arrive(last)
            for side, up in enumerate((True, False)):

                def more(drain=drain, total=total, side=side, lanes=lanes):
                    landed = drain.landed(side, last)

                    def one(place):
                        total[place, lanes] += landed[place, :].astype(F32)

                    in_pieces(total.shape[0], one)

                pl.when(drain.gets(last, up))(more)
    gain_sums[...] = jnp.sum(gain_line[...], axis=0)
    mail.arrive(home, grad_tokens.at[1 - c], cp=1 - c)
    keep.wait()
    mail.finish()


def last_sum(count, grad_projected, qkv_full, qkv_grad, out_grad, tokens, grad_middle, gain, gain_rows):
    slots = 17 * count + 17
    rows, width = tokens.shape
    hops = max(count - 1, 1)
    block, out_block = qkv_grad.shape[2:], out_grad.shape[1:]
    columns = block[1]
    give_block = (block[0], columns - columns * 5 // 6 // TILE * TILE)
    anywhere = pl.BlockSpec(memory_space=pl.ANY)
    vmem = pl.BlockSpec(memory_space=pltpu.VMEM)
    return pl.pallas_call(
        functools.partial(last_sum_kernel, count),
        out_shape=(
            jax.ShapeDtypeStruct(block, F32),
            jax.ShapeDtypeStruct(out_block, F32),
            jax.ShapeDtypeStruct((2, rows // 2, width), BF),
            jax.ShapeDtypeStruct((2, width), F32),
        ),
        in_specs=[vmem] + [anywhere] * 3 + [vmem] * 4,
        out_specs=(vmem, vmem, anywhere, vmem),
        scratch_shapes=[
            pltpu.VMEM((2, rows, width), BF),
            pltpu.VMEM((2, rows, width), BF),
            pltpu.VMEM((rows, width), BF),
            pltpu.VMEM((rows, width), BF),
            pltpu.VMEM((2, rows // 2, width), BF),
            pltpu.VMEM((2, count) + block, BF),
            pltpu.VMEM((2, hops) + block, BF),
            pltpu.VMEM((2, hops) + block, BF),
            pltpu.VMEM((2, hops) + out_block, BF),
            pltpu.VMEM((2, hops) + out_block, BF),
            pltpu.VMEM(out_block, BF),
            pltpu.VMEM((6, 2, width), F32),
            pltpu.VMEM((count, 2, width), F32),
            pltpu.VMEM((4, rows, width), BF),
            pltpu.VMEM((2, 2 * TILE, qkv_full.shape[1]), BF),
            pltpu.VMEM((2, hops) + give_block, BF),
            pltpu.VMEM((2, hops) + give_block, BF),
            pltpu.VMEM(give_block, BF),
            pltpu.VMEM(give_block, BF),
            pltpu.SemaphoreType.DMA((slots,)),
            pltpu.SemaphoreType.DMA((slots,)),
            pltpu.SemaphoreType.DMA((4,)),
            pltpu.SemaphoreType.DMA((2,)),
        ],
        compiler_params=pltpu.CompilerParams(
            collective_id=4, has_side_effects=True, vmem_limit_bytes=60 << 20
        ),
    )(grad_projected, qkv_full, qkv_grad, out_grad, tokens, grad_middle, gain, gain_rows)


def normalize(values):
    return values * lax.rsqrt(jnp.mean(values * values, axis=-1, keepdims=True) + EPSILON)


def silu_product(gate_pre, up_pre):
    return gate_pre / (1.0 + jnp.exp(-gate_pre)) * up_pre


def matmul(left, right):
    return jnp.dot(left, right, preferred_element_type=F32)


def rows_inner(left, right):
    return lax.dot_general(left, right, (((0,), (0,)), ((), ())), preferred_element_type=F32)


def cols_inner(left, right):
    return lax.dot_general(left, right, (((1,), (1,)), ((), ())), preferred_element_type=F32)


def row_major(value):
    return with_layout_constraint(value, Layout(major_to_minor=(0, 1)))


def after(value, *earlier):
    return lax.optimization_barrier((value, *earlier))[0]


def swap(value):
    return lax.ppermute(value, "cp", [(0, 1), (1, 0)])


def in_order(place, mine, other, axis):
    return jnp.where(
        place == 0,
        jnp.concatenate([mine, other], axis=axis),
        jnp.concatenate([other, mine], axis=axis),
    )


def on_device(
    tokens,
    seq_lengths,
    attention_gain,
    query_weight,
    key_weight,
    value_weight,
    out_weight,
    feedforward_gain,
    gate_weight,
    up_weight,
    down_weight,
    cotangent,
):
    c = lax.axis_index("cp")
    z = lax.axis_index("fsdp")
    sets = lax.axis_size("cp")
    count = lax.axis_size("fsdp")
    lanes = lax.axis_size("tp")
    slots, local, width = tokens.shape
    share = query_weight.shape[0]
    heads_width = query_weight.shape[1]
    head_count = heads_width // HD
    hidden_width = gate_weight.shape[1] // sets
    rows = sets * local
    seq = rows * lanes
    blocks = row_blocks(seq, sets, local)
    everyone = ("cp", "tp")

    def pick(value, which, axis=0):
        return lax.dynamic_index_in_dim(value, which, axis, keepdims=False)

    length = pick(seq_lengths, c)[None]
    gain_one = attention_gain.astype(F32)
    gain_two = feedforward_gain.astype(F32)

    qkv = jnp.concatenate([query_weight, key_weight, value_weight], axis=1)

    def halves(weight):
        return weight[:, :hidden_width], weight[:, hidden_width:]

    parts = [halves(weight) for weight in (gate_weight, up_weight, down_weight.T)]
    own_wide = jnp.stack([jnp.where(c == 0, low, high) for low, high in parts])
    wide_away = jnp.stack([jnp.where(c == 0, high, low) for low, high in parts])
    token_rows, normed_one, full_qkv, out_half, first_low, first_high = first_gather(
        count, pick(tokens, c), pick(tokens, 1 - c), gain_one[None], qkv, out_weight.T,
        own_wide, wide_away,
    )
    token_rows = token_rows.reshape(rows, width)
    normed_one = normed_one.reshape(seq, width)
    full_qkv = full_qkv.reshape(width, 3 * heads_width)

    out_half, cotangent = after((out_half, cotangent), full_qkv)
    cotangents = lax.all_gather(cotangent, everyone, axis=0).reshape(
        sets, lanes, slots, local, width
    )
    full_out = in_order(c, out_half[:, None], swap(out_half)[:, None], 1)
    full_out = full_out.reshape(width, heads_width)
    up_hop = [(i, i + 1) for i in range(count - 1)]
    down_hop = [(i, i - 1) for i in range(1, count)]
    second_low = lax.ppermute(first_low, "fsdp", up_hop)
    second_high = lax.ppermute(first_high, "fsdp", down_hop)
    cosine_table, sine_table = tables(seq)
    projected = matmul(normed_one, full_qkv)
    context, q_heads, k_heads, v_heads, level = attention(
        blocks, head_count, length, projected, cosine_table, sine_table
    )
    part = cols_inner(context, full_out).astype(BF)

    middle, middle_home, normed_two, full_gate, full_up, full_down = second_gather(
        count, part.reshape(lanes, rows, width), token_rows, gain_two[None], own_wide,
        first_low, first_high, second_low, second_high,
    )
    normed_two = normed_two.reshape(sets * seq, width)
    full_gate, full_up, full_down = (
        full.reshape(width, hidden_width) for full in (full_gate, full_up, full_down)
    )
    t = lax.axis_index("tp")
    cotangents_all = cotangents.reshape(sets * seq, width)
    cotangent_rows = pick(pick(cotangents, t, 1), c, 1).reshape(rows, width)
    gate_pre = matmul(normed_two, full_gate)
    up_pre = matmul(normed_two, full_up)
    hidden_exact, silu_back = jax.vjp(silu_product, gate_pre, up_pre)
    hidden = hidden_exact.astype(BF)

    def blocks_of(gradient):
        gradient = row_major(gradient.astype(BF))
        return gradient.reshape(count, width // count, hidden_width)

    down_blocks = blocks_of(BRANCH * rows_inner(cotangents_all, hidden))
    low = high = None
    for hop in range(1, count):
        leaving_up = pick(down_blocks, jnp.minimum(z + count - hop, count - 1))
        leaving_down = pick(down_blocks, jnp.maximum(z - count + hop, 0))
        if hop > 1:
            leaving_up = (leaving_up.astype(F32) + low.astype(F32)).astype(BF)
            leaving_down = (leaving_down.astype(F32) + high.astype(F32)).astype(BF)
        if hop < count - 1:
            low = lax.ppermute(leaving_up, "fsdp", up_hop[:hop])
            high = lax.ppermute(leaving_down, "fsdp", down_hop[count - 1 - hop :])
    grad_hidden = BRANCH * matmul(cotangents_all, full_down)
    grad_gate_exact, grad_up_exact = silu_back(grad_hidden)
    grad_gate_pre = grad_gate_exact.astype(BF)
    grad_up_pre = grad_up_exact.astype(BF)
    gate_part = lax.optimization_barrier(cols_inner(grad_gate_pre, full_gate).astype(BF))
    grad_normed_two = gate_part.astype(F32) + cols_inner(grad_up_pre, full_up)
    gate_blocks = blocks_of(rows_inner(normed_two, grad_gate_pre))
    up_blocks = blocks_of(rows_inner(normed_two, grad_up_pre))
    part = grad_normed_two.astype(BF).reshape(sets, lanes, slots, local, width)
    if count > 1:
        part, leaving_up, leaving_down = lax.optimization_barrier((part, leaving_up, leaving_down))
    grad_middle, grad_attention, gain_two_rows, pair_up, pair_down, feedforward = first_sum(
        count, part, gate_blocks, up_blocks, hidden, middle, cotangent_rows, gain_two[None],
        full_down,
    )
    grad_attention = grad_attention.reshape(seq, width)

    if count > 1:
        leaving_up, leaving_down = after((leaving_up, leaving_down), grad_attention)
        low = [lax.ppermute(pair_up, "fsdp", up_hop), lax.ppermute(leaving_up, "fsdp", up_hop)]
        high = [
            lax.ppermute(pair_down, "fsdp", down_hop), lax.ppermute(leaving_down, "fsdp", down_hop),
        ]
        low = [low[0][0], low[0][1], low[1]]
        high = [high[0][0], high[0][1], high[1]]

    def own_share(which, gradient):
        total = pick(gradient, z).astype(F32)
        if count > 1:
            total = total + low[which].astype(F32) + high[which].astype(F32)
        return total.reshape(sets, share, hidden_width)

    shares = [
        own_share(which, gradient)
        for which, gradient in enumerate((gate_blocks, up_blocks, down_blocks))
    ]
    others = swap(jnp.stack([pick(total, 1 - c).astype(BF) for total in shares]))
    grad_gate, grad_up, grad_down = (
        in_order(c, pick(total, c), others[which].astype(F32), 1)
        for which, total in enumerate(shares)
    )
    grad_down = grad_down.T

    out_pieces = row_major(rows_inner(grad_attention, context).astype(BF))
    out_pieces = out_pieces.reshape(count, sets, share, heads_width)
    out_other = swap(pick(out_pieces, 1 - c, 1))
    out_pieces = (pick(out_pieces, c, 1).astype(F32) + out_other.astype(F32)).astype(BF)
    grad_context = row_major(matmul(grad_attention, full_out).astype(BF))
    feedforward = lax.psum_scatter(feedforward, everyone, scatter_dimension=0, tiled=True)
    feedforward = feedforward.reshape(slots, local, width)
    output = (middle_home + BRANCH * feedforward.astype(F32)).astype(BF)
    grad_projected = attention_back(
        blocks, head_count, length, grad_context, q_heads, k_heads, v_heads, level,
        cosine_table, sine_table,
    )
    grad_projected = after(grad_projected, out_other, low[2], high[2])
    grad_qkv = row_major(rows_inner(normed_one, grad_projected).astype(BF))
    grad_qkv, grad_out, grad_tokens, gain_sums = last_sum(
        count, grad_projected, full_qkv, grad_qkv.reshape(count, sets, share, 3 * heads_width), out_pieces,
        token_rows, grad_middle, gain_one[None], gain_two_rows,
    )
    return (
        output,
        grad_tokens,
        grad_qkv[:, :heads_width],
        grad_qkv[:, heads_width : 2 * heads_width],
        grad_qkv[:, 2 * heads_width :],
        grad_out.T,
        gain_sums[0],
        grad_gate,
        grad_up,
        grad_down,
        gain_sums[1],
    )


def solution(mesh):
    in_specs = (
        P("fsdp", ("cp", "tp"), None),
        P("fsdp"),
        P(),
        P(("fsdp", "cp"), "tp"),
        P(("fsdp", "cp"), "tp"),
        P(("fsdp", "cp"), "tp"),
        P("tp", ("fsdp", "cp")),
        P(),
        P(("fsdp", "cp"), "tp"),
        P(("fsdp", "cp"), "tp"),
        P("tp", ("fsdp", "cp")),
        P("fsdp", ("cp", "tp"), None),
    )
    out_specs = (
        P("fsdp", ("cp", "tp"), None),
        P("fsdp", ("cp", "tp"), None),
        P(("fsdp", "cp"), "tp"),
        P(("fsdp", "cp"), "tp"),
        P(("fsdp", "cp"), "tp"),
        P("tp", ("fsdp", "cp")),
        P(),
        P(("fsdp", "cp"), "tp"),
        P(("fsdp", "cp"), "tp"),
        P("tp", ("fsdp", "cp")),
        P(),
    )
    return jax.shard_map(
        on_device, mesh=mesh, in_specs=in_specs, out_specs=out_specs, check_vma=False
    )
```

```python
import functools
import math

import jax
import jax.numpy as jnp
import numpy as np
from jax import lax
from jax.experimental import pallas as pl
from jax.experimental.layout import Layout, with_layout_constraint
from jax.experimental.pallas import tpu as pltpu
from jax.sharding import PartitionSpec as P

HD = 64
EPSILON = 1e-05
BRANCH = 1.4 / math.sqrt(40.0)
BF = jnp.bfloat16
F32 = jnp.float32
TILE = 128
QUERY_ROWS = 512


def turned(values, cosine, sine):
    lane = lax.broadcasted_iota(jnp.int32, values.shape, 1)
    partner = jnp.where(
        lane % HD < HD // 2,
        pltpu.roll(values, TILE - HD // 2, 1),
        pltpu.roll(values, HD // 2, 1),
    )
    return values * cosine + partner * sine


def row_blocks(seq, sets, local):
    lanes = seq // sets // local
    return [
        ((t * sets + h) * local, (h * lanes + t) * local)
        for t in range(lanes)
        for h in range(sets)
    ]


def key_mask(length, first, rows, columns):
    place = first + lax.broadcasted_iota(jnp.int32, (rows, columns), 0)
    return place < length


def scores_of(keys, queries, length, first_query):
    raw = lax.dot_general(keys, queries, (((1,), (1,)), ((), ())), preferred_element_type=F32)
    key_place = lax.broadcasted_iota(jnp.int32, raw.shape, 0)
    query_place = first_query + lax.broadcasted_iota(jnp.int32, raw.shape, 1)
    return jnp.where((key_place <= query_place) & (key_place < length), raw, -1e30)


def attention_kernel(
    blocks, length_ref, projected, cosine, sine, context, q_heads, k_heads, v_heads, level, kept
):
    heads, seq, _ = q_heads.shape
    local = seq // len(blocks)
    length = length_ref[0]
    for gathered, ordered in blocks:
        source, target = pl.ds(gathered, local), pl.ds(ordered, local)
        for tile in range(-(-3 * heads // 2)):
            width = min(TILE, 3 * heads * HD - tile * TILE)
            values = projected[source, tile * TILE : tile * TILE + width]
            if tile * 2 < 2 * heads:
                values = turned(values, cosine[target, :], sine[target, :])
            for which in range(width // HD):
                index = tile * 2 + which
                piece = values[:, which * HD : (which + 1) * HD]
                if index < heads:
                    q_heads[index, target, :] = (piece * (1.0 / math.sqrt(HD))).astype(BF)
                elif index < 2 * heads:
                    k_heads[index - heads, target, :] = piece.astype(BF)
                else:
                    v_heads[index - 2 * heads, target, :] = piece.astype(BF)

    def one_head(head, carry):
        for first in range(0, seq, QUERY_ROWS):
            most = first + QUERY_ROWS
            queries = q_heads[head, first:most, :]
            keys = k_heads[head, :most, :]
            values = v_heads[head, :most, :]
            scores = scores_of(keys, queries, length, first)
            top = jnp.max(scores, axis=0, keepdims=True)
            exponent = jnp.exp(scores - top)
            total = jnp.sum(exponent, axis=0, keepdims=True)
            probabilities = exponent.astype(BF)
            level[head, :, first:most] = top + jnp.log(total)
            mixed = lax.dot_general(
                values, probabilities, (((0,), (0,)), ((), ())), preferred_element_type=F32
            )
            kept[head, first:most, :] = (mixed * (1.0 / total)).T.astype(BF)
        return carry

    lax.fori_loop(0, heads, one_head, 0, unroll=True)
    for gathered, ordered in blocks:
        source, target = pl.ds(ordered, local), pl.ds(gathered, local)
        for head in range(0, heads, 2):
            parts = [kept[index, source, :] for index in range(head, min(head + 2, heads))]
            joined = parts[0] if len(parts) == 1 else jnp.concatenate(parts, axis=1)
            context[target, head * HD : head * HD + joined.shape[1]] = joined


def attention(blocks, heads, length, projected, cosine, sine):
    seq = projected.shape[0]
    per_head = jax.ShapeDtypeStruct((heads, seq, HD), BF)
    vmem = pl.BlockSpec(memory_space=pltpu.VMEM)
    return pl.pallas_call(
        functools.partial(attention_kernel, blocks),
        out_shape=(
            jax.ShapeDtypeStruct((seq, heads * HD), BF),
            per_head,
            per_head,
            per_head,
            jax.ShapeDtypeStruct((heads, 1, seq), F32),
        ),
        in_specs=[pl.BlockSpec(memory_space=pltpu.SMEM), vmem, vmem, vmem],
        out_specs=(vmem,) * 5,
        scratch_shapes=[pltpu.VMEM((heads, seq, HD), BF)],
        compiler_params=pltpu.CompilerParams(vmem_limit_bytes=48 << 20),
        cost_estimate=pl.CostEstimate(
            flops=4 * heads * seq * seq * HD, transcendentals=heads * seq * seq, bytes_accessed=20 << 20
        ),
    )(length, projected, cosine, sine)


def attention_back_kernel(
    blocks, length_ref, grad_context, q_heads, k_heads, v_heads, level, cosine, sine,
    grad_projected, g_heads, dq, dk, dv,
):
    heads, seq, _ = q_heads.shape
    local = seq // len(blocks)
    length = length_ref[0]
    for gathered, ordered in blocks:
        source, target = pl.ds(gathered, local), pl.ds(ordered, local)
        for head in range(heads):
            g_heads[head, target, :] = grad_context[source, head * HD : (head + 1) * HD]

    def one_head(head, carry):
        keys_turned = k_heads[head].T
        for first in reversed(range(0, seq, QUERY_ROWS)):
            most = first + QUERY_ROWS
            queries = q_heads[head, first:most, :]
            upstream = g_heads[head, first:most, :]
            keys = k_heads[head, :most, :]
            values = v_heads[head, :most, :]
            scores = scores_of(keys, queries, length, first)
            probabilities = jnp.exp(scores - level[head, :, first:most])
            grad_probabilities = lax.dot_general(
                values, upstream, (((1,), (1,)), ((), ())), preferred_element_type=F32
            )
            weighted = probabilities * grad_probabilities
            balance = jnp.sum(weighted, axis=0, keepdims=True)
            grad_scores = (weighted - probabilities * balance).astype(BF)
            grad_keys = jnp.dot(grad_scores, queries, preferred_element_type=F32)
            grad_values = jnp.dot(
                probabilities.astype(BF), upstream, preferred_element_type=F32
            )
            if most == seq:
                dk[head, :, :] = grad_keys
                dv[head, :, :] = grad_values
            else:
                dk[head, :most, :] += grad_keys
                dv[head, :most, :] += grad_values
            grad_queries = jnp.dot(
                keys_turned[:, :most], grad_scores, preferred_element_type=F32
            )
            dq[head, first:most, :] = grad_queries.T * (1.0 / math.sqrt(HD))
        return carry

    lax.fori_loop(0, heads, one_head, 0, unroll=True)
    sources = [dq] * heads + [dk] * heads + [dv] * heads
    for gathered, ordered in blocks:
        source, target = pl.ds(ordered, local), pl.ds(gathered, local)
        for tile in range(-(-3 * heads // 2)):
            indices = range(tile * 2, min(tile * 2 + 2, 3 * heads))
            parts = [sources[index][index % heads, source, :] for index in indices]
            joined = parts[0] if len(parts) == 1 else jnp.concatenate(parts, axis=1)
            if tile * 2 < 2 * heads:
                joined = turned(joined, cosine[source, :], -sine[source, :])
            grad_projected[target, tile * TILE : tile * TILE + joined.shape[1]] = joined.astype(BF)


def attention_back(blocks, heads, length, grad_context, q_heads, k_heads, v_heads, level, cosine, sine):
    seq = grad_context.shape[0]
    vmem = pl.BlockSpec(memory_space=pltpu.VMEM)
    return pl.pallas_call(
        functools.partial(attention_back_kernel, blocks),
        out_shape=jax.ShapeDtypeStruct((seq, 3 * heads * HD), BF),
        in_specs=[pl.BlockSpec(memory_space=pltpu.SMEM)] + [vmem] * 7,
        out_specs=vmem,
        scratch_shapes=[
            pltpu.VMEM((heads, seq, HD), BF),
            pltpu.VMEM((heads, seq, HD), F32),
            pltpu.VMEM((heads, seq, HD), F32),
            pltpu.VMEM((heads, seq, HD), F32),
        ],
        compiler_params=pltpu.CompilerParams(vmem_limit_bytes=56 << 20),
        cost_estimate=pl.CostEstimate(
            flops=10 * heads * seq * seq * HD, transcendentals=heads * seq * seq, bytes_accessed=20 << 20
        ),
    )(length, grad_context, q_heads, k_heads, v_heads, level, cosine, sine)


def tables(seq):
    step = np.arange(HD // 2, dtype=np.float32)
    frequency = np.power(np.float32(10000.0), np.float32(-2.0) * step / np.float32(HD))
    angle = np.arange(seq, dtype=np.float32)[:, None] * frequency[None, :]
    cosine, sine = np.cos(angle), np.sin(angle)
    signed = np.concatenate([-sine, sine, -sine, sine], axis=1)
    return jnp.asarray(np.tile(cosine, (1, 4))), jnp.asarray(signed)


COST = pl.CostEstimate(flops=0, transcendentals=0, bytes_accessed=300 << 20)
MESH = pl.DeviceIdType.MESH


def greet(count):
    barrier = pltpu.get_barrier_semaphore()
    z, c, t = lax.axis_index("fsdp"), lax.axis_index("cp"), lax.axis_index("tp")

    def hello(**place):
        pl.semaphore_signal(barrier, inc=1, device_id=place, device_id_type=MESH)

    hello(cp=1 - c)
    hello(tp=t + 1 - 2 * (t % 2))
    hello(tp=(t + 2) % 4)
    pl.when(z > 0)(lambda: hello(fsdp=z - 1))
    pl.when(z < count - 1)(lambda: hello(fsdp=z + 1))
    peers = 3 + jnp.minimum(z, 1) + jnp.minimum(count - 1 - z, 1)
    pl.semaphore_wait(barrier, peers)


class Mail:
    def __init__(self, send, recv):
        self.send, self.recv, self.used, self.open = send, recv, 0, []

    def slot(self):
        self.used += 1
        return self.used - 1

    def copy(self, slot, source, target, **place):
        return pltpu.make_async_remote_copy(
            src_ref=source,
            dst_ref=target,
            send_sem=self.send.at[slot],
            recv_sem=self.recv.at[slot],
            device_id=place,
            device_id_type=MESH,
        )

    def start(self, slot, source, target, when=None, **place):
        made = self.copy(slot, source, target, **place)
        if when is None:
            made.start()
        else:
            pl.when(when)(made.start)
        self.open.append((made, when))

    def arrive(self, slot, target, when=None, **place):
        made = self.copy(slot, target, target, **place)
        if when is None:
            made.wait_recv()
        else:
            pl.when(when)(made.wait_recv)

    def finish(self):
        for made, when in self.open:
            if when is None:
                made.wait_send()
            else:
                pl.when(when)(made.wait_send)


class Stage:
    def __init__(self, pieces, stage, sems):
        self.made = []
        for k, (source, target, when) in enumerate(pieces):
            self.made.append(
                (
                    pltpu.make_async_copy(source, stage.at[k], sems.at[0, k]),
                    pltpu.make_async_copy(stage.at[k], target, sems.at[1, k]),
                    when,
                )
            )

    def begin(self):
        for copy, _, when in self.made:
            copy.start() if when is None else pl.when(when)(copy.start)

    def turn(self):
        for first, second, when in self.made:

            def on(first=first, second=second):
                first.wait()
                second.start()

            on() if when is None else pl.when(when)(on)

    def end(self):
        for _, copy, when in self.made:
            copy.wait() if when is None else pl.when(when)(copy.wait)


class Line:
    def __init__(self, mail, count, own, at, ready=()):
        self.mail, self.count, self.own, self.at = mail, count, own, at
        self.ready = ready
        self.z = lax.axis_index("fsdp")
        self.up = [mail.slot() for _ in range(count)]
        self.down = [mail.slot() for _ in range(count)]

    def has_low(self, hop):
        return self.z >= hop

    def has_high(self, hop):
        return self.z <= self.count - 1 - hop

    def send(self, hop):
        z, count, mail = self.z, self.count, self.mail
        low, high = jnp.maximum(z - hop + 1, 0), jnp.minimum(z + hop - 1, count - 1)
        from_low = from_high = self.own
        if hop > 1:
            from_low, from_high = self.at(low), self.at(high)
        if 0 < hop - 1 <= len(self.ready):
            from_low, from_high = self.ready[hop - 2]
        mail.start(
            self.up[hop], from_low, self.at(low),
            when=(z >= hop - 1) & (z < count - 1), fsdp=jnp.minimum(z + 1, count - 1),
        )
        mail.start(
            self.down[hop], from_high, self.at(high),
            when=(z <= count - hop) & (z > 0), fsdp=jnp.maximum(z - 1, 0),
        )

    def arrive(self, hop):
        z, count = self.z, self.count
        self.mail.arrive(
            self.up[hop], self.at(jnp.maximum(z - hop, 0)), when=self.has_low(hop), fsdp=z
        )
        self.mail.arrive(
            self.down[hop], self.at(jnp.minimum(z + hop, count - 1)), when=self.has_high(hop), fsdp=z
        )


    def keep(self):
        z, count = self.z, self.count
        made = [(self.own, self.at(z), None)]
        for index, (low, high) in enumerate(self.ready):
            hop = index + 1
            made.append((low, self.at(jnp.maximum(z - hop, 0)), self.has_low(hop)))
            made.append((high, self.at(jnp.minimum(z + hop, count - 1)), self.has_high(hop)))
        return made


class Across:
    def __init__(self, line, own, mine_at, other_at):
        self.line, self.own, self.mine_at, self.other_at = line, own, mine_at, other_at
        self.c = lax.axis_index("cp")
        self.low = [line.mail.slot() for _ in range(line.count)]
        self.high = [line.mail.slot() for _ in range(line.count)]

    def send(self, hop):
        line, mail = self.line, self.line.mail
        z, count, other = line.z, line.count, 1 - self.c
        if hop == 0:
            mail.start(self.low[0], self.own, self.mine_at(z), cp=other)
            return
        low, high = jnp.maximum(z - hop, 0), jnp.minimum(z + hop, count - 1)
        mail.start(self.low[hop], self.mine_at(low), self.mine_at(low), when=line.has_low(hop), cp=other)
        mail.start(self.high[hop], self.mine_at(high), self.mine_at(high), when=line.has_high(hop), cp=other)

    def arrive(self, hop):
        line, mail = self.line, self.line.mail
        z, count, other = line.z, line.count, 1 - self.c
        if hop == 0:
            mail.arrive(self.low[0], self.other_at(z), cp=other)
            return
        low, high = jnp.maximum(z - hop, 0), jnp.minimum(z + hop, count - 1)
        mail.arrive(self.low[hop], self.other_at(low), when=line.has_low(hop), cp=other)
        mail.arrive(self.high[hop], self.other_at(high), when=line.has_high(hop), cp=other)


def first_gather_kernel(
    count, tokens, tokens_away, gain, qkv, turned_out, wide, wide_away,
    token_rows, normed_full, qkv_full, out_half, low_pair, high_pair,
    landed, normed, wide_landed, qkv_stage, out_stage,
    send, recv, local, qkv_local, out_local,
):
    z, c, t = lax.axis_index("fsdp"), lax.axis_index("cp"), lax.axis_index("tp")
    beside, yonder = t + 1 - 2 * (t % 2), (t + 2) % 4
    low, high = low_pair.at[0], high_pair.at[0]
    mail = Mail(send, recv)
    greet(count)
    stage_qkv = Stage([(qkv, qkv_full.at[z, c], None)], qkv_stage, qkv_local)
    stage_out = Stage([(turned_out, out_half.at[z], None)], out_stage, out_local)
    kept = []

    heads = Line(mail, count, qkv, lambda j: qkv_full.at[j, c])
    heads_across = Across(
        heads, qkv, lambda j: qkv_full.at[j, c], lambda j: qkv_full.at[j, 1 - c]
    )
    outs = Line(mail, count, turned_out, lambda j: out_half.at[j])
    wide_up, wide_down = mail.slot(), mail.slot()
    rows_x, wide_x = mail.slot(), mail.slot()
    rows_y = [mail.slot() for _ in range(2)]
    rows_core = [mail.slot() for _ in range(4)]

    mail.start(rows_x, tokens_away, landed, cp=1 - c)
    heads.send(1)

    def rows_out(source, side, half):
        def one(place):
            rows = source[place, :]
            token_rows[half, place, :] = rows
            normed[half, place, :] = (normalize(rows.astype(F32)) * gain[...]).astype(BF)

        in_pieces(source.shape[0], one)
        mail.start(rows_y[side], normed.at[half], normed_full.at[t, half], tp=yonder)
        mail.start(rows_core[side], normed.at[half], normed_full.at[t, half], tp=beside)

    stage_qkv.begin()
    stage_out.begin()
    rows_out(tokens, 0, c)
    stage_qkv.turn()
    stage_out.turn()
    mail.arrive(rows_x, landed, cp=1 - c)
    heads_across.send(0)
    rows_out(landed, 1, 1 - c)
    kept.append(pltpu.make_async_copy(normed, normed_full.at[t], local.at[2]))
    kept[-1].start()

    def rows_on(k, half):
        mail.arrive(rows_y[k], normed_full.at[yonder, half], tp=yonder)
        mail.start(
            rows_core[2 + k], normed_full.at[yonder, half], normed_full.at[yonder, half], tp=beside
        )

    for hop in range(1, count):
        heads.arrive(hop)
        if hop + 1 < count:
            heads.send(hop + 1)
        heads_across.send(hop)
        if hop == 1:
            rows_on(0, c)
            rows_on(1, 1 - c)
            outs.send(1)
        if hop == min(2, count - 1):
            mail.start(wide_up, wide, low, when=z < count - 1, fsdp=jnp.minimum(z + 1, count - 1))
            mail.start(wide_down, wide, high, when=z > 0, fsdp=jnp.maximum(z - 1, 0))
    mail.start(wide_x, wide_away, wide_landed, cp=1 - c)
    for hop in range(1, count):
        outs.arrive(hop)
        if hop + 1 < count:
            outs.send(hop + 1)
    for hop in range(count):
        heads_across.arrive(hop)
    mail.arrive(rows_core[0], normed_full.at[beside, c], tp=beside)
    mail.arrive(rows_core[1], normed_full.at[beside, 1 - c], tp=beside)
    far = (beside + 2) % 4
    mail.arrive(rows_core[2], normed_full.at[far, c], tp=beside)
    mail.arrive(rows_core[3], normed_full.at[far, 1 - c], tp=beside)
    mail.arrive(wide_x, wide_landed, cp=1 - c)
    for pair, place in ((low_pair, 1), (high_pair, 3)):
        kept.append(pltpu.make_async_copy(wide_landed, pair.at[1], local.at[place]))
        kept[-1].start()
    mail.arrive(wide_up, low, when=z > 0, fsdp=z)
    mail.arrive(wide_down, high, when=z < count - 1, fsdp=z)
    for copy in kept:
        copy.wait()
    stage_qkv.end()
    stage_out.end()
    mail.finish()


def first_gather(count, tokens, tokens_away, gain, qkv, turned_out, wide, wide_away):
    slots = 6 * count + 10
    anywhere = pl.BlockSpec(memory_space=pl.ANY)
    vmem = pl.BlockSpec(memory_space=pltpu.VMEM)
    pair = (2,) + tokens.shape
    return pl.pallas_call(
        functools.partial(first_gather_kernel, count),
        out_shape=(
            jax.ShapeDtypeStruct(pair, BF),
            jax.ShapeDtypeStruct((4,) + pair, BF),
            jax.ShapeDtypeStruct((count, 2) + qkv.shape, BF),
            jax.ShapeDtypeStruct((count,) + turned_out.shape, BF),
            jax.ShapeDtypeStruct((2,) + wide.shape, BF),
            jax.ShapeDtypeStruct((2,) + wide.shape, BF),
        ),
        in_specs=[vmem, anywhere, vmem] + [anywhere] * 4,
        out_specs=(vmem,) + (anywhere,) * 5,
        scratch_shapes=[
            pltpu.VMEM(tokens.shape, BF),
            pltpu.VMEM(pair, BF),
            pltpu.VMEM(wide.shape, BF),
            pltpu.VMEM((1,) + qkv.shape, BF),
            pltpu.VMEM((1,) + turned_out.shape, BF),
            pltpu.SemaphoreType.DMA((slots,)),
            pltpu.SemaphoreType.DMA((slots,)),
            pltpu.SemaphoreType.DMA((4,)),
            pltpu.SemaphoreType.DMA((2, 1)),
            pltpu.SemaphoreType.DMA((2, 1)),
        ],
        cost_estimate=COST,
        compiler_params=pltpu.CompilerParams(
            collective_id=1, has_side_effects=True, vmem_limit_bytes=32 << 20
        ),
    )(tokens, tokens_away, gain, qkv, turned_out, wide, wide_away)


def in_pieces(rows, body, size=16):
    if rows % size:
        body(pl.ds(0, rows))
        return
    lax.fori_loop(0, rows // size, lambda i, carry: (body(pl.ds(i * size, size)), carry)[1], 0)


class Spread:
    def __init__(self, mail, own, at):
        self.mail, self.own, self.at = mail, own, at
        self.c, self.t = lax.axis_index("cp"), lax.axis_index("tp")
        self.beside, self.yonder = self.t + 1 - 2 * (self.t % 2), (self.t + 2) % 4
        self.x = [mail.slot() for _ in range(3)]
        self.y = [mail.slot() for _ in range(3)]
        self.core = {}

    def to_core(self, c_is_own, t_is_own, piece):
        slot = self.core[c_is_own, t_is_own, piece] = self.mail.slot()
        c = self.c if c_is_own else 1 - self.c
        t = self.t if t_is_own else self.yonder
        source = self.own(piece) if c_is_own and t_is_own else self.at(c, t, piece)
        self.mail.start(slot, source, self.at(c, t, piece), tp=self.beside)

    def begin(self, piece):
        c, t = self.c, self.t
        if piece == 0:
            self.mail.start(self.x[0], self.own(0), self.at(c, t, 0), cp=1 - c)
        else:
            self.mail.start(self.y[0], self.own(1), self.at(c, t, 1), tp=self.yonder)
            self.mail.start(self.x[1], self.own(1), self.at(c, t, 1), cp=1 - c)
            self.mail.start(self.y[1], self.own(0), self.at(c, t, 0), tp=self.yonder)
        self.to_core(True, True, piece)

    def turn(self):
        c, t, mail, yonder = self.c, self.t, self.mail, self.yonder
        mail.arrive(self.x[0], self.at(1 - c, t, 0), cp=1 - c)
        mail.start(self.y[2], self.at(1 - c, t, 0), self.at(1 - c, t, 0), tp=yonder)
        self.to_core(False, True, 0)
        mail.arrive(self.y[0], self.at(c, yonder, 1), tp=yonder)
        mail.start(self.x[2], self.at(c, yonder, 1), self.at(c, yonder, 1), cp=1 - c)
        self.to_core(True, False, 1)

    def end(self):
        c, t, mail, yonder = self.c, self.t, self.mail, self.yonder
        mail.arrive(self.x[1], self.at(1 - c, t, 1), cp=1 - c)
        self.to_core(False, True, 1)
        mail.arrive(self.y[1], self.at(c, yonder, 0), tp=yonder)
        self.to_core(True, False, 0)
        mail.arrive(self.x[2], self.at(1 - c, yonder, 1), cp=1 - c)
        self.to_core(False, False, 1)
        mail.arrive(self.y[2], self.at(1 - c, yonder, 0), tp=yonder)
        self.to_core(False, False, 0)
        far = (self.beside + 2) % 4
        for (c_is_own, t_is_own, piece), slot in self.core.items():
            place = self.at(
                c if c_is_own else 1 - c, self.beside if t_is_own else far, piece
            )
            mail.arrive(slot, place, tp=self.beside)


def second_gather_kernel(
    count, part, tokens, gain, wide, first_low, first_high, second_low, second_high, *refs
):
    hops_mine, hops_other = min(2, count - 1), 1
    wide_other = first_low.at[1]
    ready_mine = [first_low.at[0], first_high.at[0], second_low.at[0], second_high.at[0]]
    ready_mine = ready_mine[: 2 * hops_mine]
    ready_other = [second_low.at[1], second_high.at[1]]
    middle, middle_home, normed_full, gate_full, up_full, down_full = refs[:6]
    own, from_core, to_yonder, from_yonder, normed, stage, send, recv, local, local_line = refs[6:]
    c, t = lax.axis_index("cp"), lax.axis_index("tp")
    rows = tokens.shape[0]
    half = rows // 2
    mail = Mail(send, recv)
    greet(count)

    mine, other = [], []
    for which, full in enumerate((gate_full, up_full, down_full)):
        for lines, side, piece, ready in (
            (mine, c, wide, ready_mine), (other, 1 - c, wide_other, ready_other),
        ):
            arrived = [
                (ready[2 * hop].at[which], ready[2 * hop + 1].at[which])
                for hop in range(len(ready) // 2)
            ]
            lines.append(
                Line(
                    mail, count, piece.at[which],
                    lambda j, full=full, side=side: full.at[j, side], arrived,
                )
            )
    summed = TensorSum(mail, part, own, from_core, to_yonder, from_yonder, local)
    spread = Spread(
        mail, lambda piece: normed.at[piece], lambda c, t, piece: normed_full.at[piece, t, c]
    )

    summed.begin()
    placing = Stage([piece for line in mine + other for piece in line.keep()], stage, local_line)
    placing.begin()

    def send_hop(lines, hop):
        for line in lines:
            if hop < count:
                line.send(hop)

    def arrive_hop(lines, hop):
        for line in lines:
            if hop < count:
                line.arrive(hop)

    send_hop(other, hops_other + 1)
    send_hop(mine, hops_mine + 1)
    summed.turn()
    placing.turn()
    for piece in range(2):
        summed.arrive(piece)

        def norm(place, piece=piece):
            row = pl.ds(place.start + piece * half, place.size)
            values = tokens[row, :].astype(F32) + BRANCH * summed.rows(row)
            middle[row, :] = values
            normed[piece, place, :] = (normalize(values) * gain[...]).astype(BF)

        in_pieces(half, norm)
        spread.begin(piece)
    keep_normed = pltpu.make_async_copy(normed, normed_full.at[:, t, c], local.at[0])
    keep_normed.start()
    home = mail.slot()
    stay, go = pl.ds(c * half, half), pl.ds((1 - c) * half, half)
    keep_home = pltpu.make_async_copy(middle.at[stay], middle_home.at[c], local.at[1])
    keep_home.start()
    spread.turn()
    mail.start(home, middle.at[go], middle_home.at[c], cp=1 - c)
    for step in range(1, count):
        hop = hops_other + step
        if hop < count:
            for line_other, line_mine in zip(other, mine):
                line_other.arrive(hop)
                if hop + 1 < count:
                    line_other.send(hop + 1)
                if hops_mine + step < count:
                    line_mine.arrive(hops_mine + step)
                    if hops_mine + step + 1 < count:
                        line_mine.send(hops_mine + step + 1)
        if step == 1:
            spread.end()
    if count == 1:
        spread.end()
    mail.arrive(home, middle_home.at[1 - c], cp=1 - c)
    keep_home.wait()
    keep_normed.wait()
    placing.end()
    mail.finish()


def second_gather(count, part, tokens, gain, wide, first_low, first_high, second_low, second_high):
    slots = 12 * count + 24
    rows, width = tokens.shape
    anywhere = pl.BlockSpec(memory_space=pl.ANY)
    vmem = pl.BlockSpec(memory_space=pltpu.VMEM)
    full = jax.ShapeDtypeStruct((count, 2) + wide.shape[1:], BF)
    return pl.pallas_call(
        functools.partial(second_gather_kernel, count),
        out_shape=(
            jax.ShapeDtypeStruct((rows, width), F32),
            jax.ShapeDtypeStruct((2, rows // 2, width), F32),
            jax.ShapeDtypeStruct((2, 4, 2, rows // 2, width), BF),
            full,
            full,
            full,
        ),
        in_specs=[anywhere, vmem, vmem] + [anywhere] * 5,
        out_specs=(vmem,) + (anywhere,) * 5,
        scratch_shapes=[
            pltpu.VMEM((2, rows, width), BF),
            pltpu.VMEM((2, rows, width), BF),
            pltpu.VMEM((rows, width), BF),
            pltpu.VMEM((rows, width), BF),
            pltpu.VMEM((2, rows // 2, width), BF),
            pltpu.VMEM((24,) + wide.shape[1:], BF),
            pltpu.SemaphoreType.DMA((slots,)),
            pltpu.SemaphoreType.DMA((slots,)),
            pltpu.SemaphoreType.DMA((2,)),
            pltpu.SemaphoreType.DMA((2, 24)),
        ],
        cost_estimate=COST,
        compiler_params=pltpu.CompilerParams(
            collective_id=2, has_side_effects=True, vmem_limit_bytes=40 << 20
        ),
    )(part, tokens, gain, wide, first_low, first_high, second_low, second_high)


class TensorSum:
    def __init__(self, mail, part, own, from_core, to_yonder, from_yonder, local):
        self.mail, self.part, self.own, self.from_core = mail, part, own, from_core
        self.to_yonder, self.from_yonder, self.local = to_yonder, from_yonder, local
        self.t = t = lax.axis_index("tp")
        self.beside, self.yonder = t + 1 - 2 * (t % 2), (t + 2) % 4
        self.core = [mail.slot() for _ in range(2)]
        self.across = [mail.slot() for _ in range(2)]
        self.half = from_yonder.shape[0] // 2

    def begin(self):
        part, far = self.part, (self.beside + 2) % 4
        self.mail.start(self.core[1], part.at[far], self.from_core.at[1], tp=self.beside)
        self.mail.start(self.core[0], part.at[self.beside], self.from_core.at[0], tp=self.beside)
        self.kept = [
            pltpu.make_async_copy(part.at[self.yonder], self.own.at[1], self.local.at[0]),
            pltpu.make_async_copy(part.at[self.t], self.own.at[0], self.local.at[1]),
        ]
        for copy in self.kept:
            copy.start()

    def turn(self):
        own, from_core = self.own, self.from_core
        self.kept[0].wait()
        self.mail.arrive(self.core[1], from_core.at[1], tp=self.beside)
        for piece in range(2):

            def add(place, piece=piece):
                place = pl.ds(place.start + piece * self.half, place.size)
                self.to_yonder[place, :] = (
                    own[1, place, :].astype(F32) + from_core[1, place, :].astype(F32)
                ).astype(BF)

            in_pieces(self.half, add)
            block = pl.ds(piece * self.half, self.half)
            self.mail.start(
                self.across[piece], self.to_yonder.at[block], self.from_yonder.at[block],
                tp=self.yonder,
            )
        self.kept[1].wait()
        self.mail.arrive(self.core[0], from_core.at[0], tp=self.beside)

    def arrive(self, piece):
        block = pl.ds(piece * self.half, self.half)
        self.mail.arrive(self.across[piece], self.from_yonder.at[block], tp=self.yonder)

    def rows(self, row):
        return (
            self.own[0, row, :].astype(F32)
            + self.from_core[0, row, :].astype(F32)
            + self.from_yonder[row, :].astype(F32)
        )


class Drain:
    def __init__(self, mail, count, fill, total, landed):
        self.mail, self.count, self.fill, self.total, self.landed = mail, count, fill, total, landed
        self.z = lax.axis_index("fsdp")
        self.slots = [[mail.slot() for _ in range(count)] for _ in range(2)]

    def sends(self, hop, up):
        z, count = self.z, self.count
        return (z <= hop - 1) & (z < count - 1) if up else (z >= count - hop) & (z > 0)

    def gets(self, hop, up):
        z, count = self.z, self.count
        return (z >= 1) & (z <= hop) if up else (z <= count - 2) & (z >= count - 1 - hop)

    def block(self, hop, up):
        z, count = self.z, self.count
        return jnp.minimum(z + count - hop, count - 1) if up else jnp.maximum(z - count + hop, 0)

    def arrive(self, hop):
        for side, up in enumerate((True, False)):
            self.mail.arrive(
                self.slots[side][hop], self.landed(side, hop), when=self.gets(hop, up), fsdp=self.z
            )

    def gather(self, hop):
        for side, up in enumerate((True, False)):
            target = self.total(side, hop)

            def work(side=side, up=up, target=target):
                self.fill(hop, up, self.block(hop, up), target)
                if hop > 1:

                    def add():
                        landed = self.landed(side, hop - 1)

                        def one(place):
                            target[place, :] = (
                                target[place, :].astype(F32) + landed[place, :].astype(F32)
                            ).astype(BF)

                        in_pieces(target.shape[0], one)

                    pl.when(self.gets(hop - 1, up))(add)

            pl.when(self.sends(hop, up))(work)

    def send(self, hop):
        z, count = self.z, self.count
        for side, up in enumerate((True, False)):
            to = jnp.minimum(z + 1, count - 1) if up else jnp.maximum(z - 1, 0)
            self.mail.start(
                self.slots[side][hop], self.total(side, hop), self.landed(side, hop),
                when=self.sends(hop, up), fsdp=to,
            )


def norm_back(values, gain, upstream):
    scale = lax.rsqrt(jnp.mean(values * values, axis=-1, keepdims=True) + EPSILON)
    norm = values * scale
    scaled = upstream * gain
    mean = jnp.mean(scaled * norm, axis=-1, keepdims=True)
    return scale * (scaled - norm * mean), upstream * norm


def first_sum_kernel(
    count, part, gate_grad, up_grad, hidden, middle, cotangent, gain, down,
    grad_middle, attention_full, gain_rows, leaving_up, leaving_down, feedforward,
    own, from_core, first, second, grad_attention, totals, landed, hidden_rows, product,
    send, recv, local, hidden_local,
):
    z, c, t = lax.axis_index("fsdp"), lax.axis_index("cp"), lax.axis_index("tp")
    beside, yonder = t + 1 - 2 * (t % 2), (t + 2) % 4
    far = (beside + 2) % 4
    half = middle.shape[0] // 2
    width = middle.shape[1]
    mail = Mail(send, recv)
    greet(count)
    last = count - 1

    def fill_from(which):
        def fill(hop, up, j, target):
            copy = pltpu.make_async_copy((gate_grad, up_grad)[which].at[j], target, local.at[4])
            copy.start()
            copy.wait()

        return fill

    drains = [
        Drain(
            mail, count, fill_from(which),
            lambda side, hop, which=which: (
                (leaving_up, leaving_down)[side].at[which] if hop == last else totals.at[side, hop - 1, which]
            ),
            lambda side, hop, which=which: landed.at[side, hop - 1, which],
        )
        for which in range(2)
    ]

    core = {}
    mine = {}
    order = ((0, 0), (0, 1), (1, 0), (1, 1))
    for index, (c_own, t_own) in enumerate(order):
        block_c = c if c_own else 1 - c
        core[c_own, t_own] = mail.slot()
        mail.start(
            core[c_own, t_own], part.at[:, beside if t_own else far, block_c],
            from_core.at[c_own, t_own], tp=beside,
        )
        mine[c_own, t_own] = pltpu.make_async_copy(
            part.at[:, t if t_own else yonder, block_c], own.at[c_own, t_own], local.at[index]
        )
        mine[c_own, t_own].start()
    if last > 1:
        for drain in drains:
            drain.gather(1)
            drain.send(1)

    block_rows = product.shape[1]
    blocks = hidden.shape[0] // block_rows

    def hidden_copy(block):
        return pltpu.make_async_copy(
            hidden.at[pl.ds(block * block_rows, block_rows)], hidden_rows.at[block % 2],
            hidden_local.at[0, block % 2],
        )

    def product_copy(block):
        return pltpu.make_async_copy(
            product.at[block % 2], feedforward.at[pl.ds(block * block_rows, block_rows)],
            hidden_local.at[1, block % 2],
        )

    def product_block(block):
        hidden_copy(block).wait()
        if block + 1 < blocks:
            hidden_copy(block + 1).start()
        if block > 1:
            product_copy(block - 2).wait()

        def one(k, carry):
            columns = pl.ds(pl.multiple_of(k * 2 * TILE, 2 * TILE), 2 * TILE)
            value = lax.dot_general(
                hidden_rows[block % 2], down[columns, :], (((1,), (1,)), ((), ())),
                preferred_element_type=F32,
            )
            product[block % 2, :, columns] = value.astype(BF)
            return carry

        lax.fori_loop(0, width // (2 * TILE), one, 0)
        product_copy(block).start()

    hidden_copy(0).start()
    product_block(0)

    quarter = half // 2
    quarters = [(piece, pl.ds(side * quarter, quarter)) for piece in range(2) for side in range(2)]
    x_first = [[mail.slot() for _ in range(2)] for _ in quarters]
    y_second = [mail.slot() for _ in quarters]
    ring_y = [mail.slot() for _ in quarters]
    ring_core = [mail.slot() for _ in quarters]
    ring_far = [mail.slot() for _ in quarters]

    def core_add(c_own, t_own, piece, rows):
        def one(place):
            row = pl.ds(rows.start + place.start, place.size)
            own[c_own, t_own, piece, row, :] = (
                own[c_own, t_own, piece, row, :].astype(F32)
                + from_core[c_own, t_own, piece, row, :].astype(F32)
            ).astype(BF)

        in_pieces(quarter, one)

    for t_own in (0, 1):
        mine[0, t_own].wait()
        mail.arrive(core[0, t_own], from_core.at[0, t_own], tp=beside)
    for k, (piece, rows) in enumerate(quarters):
        for t_own in (0, 1):
            core_add(0, t_own, piece, rows)
            mail.start(
                x_first[k][t_own], own.at[0, t_own, piece, rows], first.at[k, t_own], cp=1 - c
            )
    for t_own in (0, 1):
        mine[1, t_own].wait()
        mail.arrive(core[1, t_own], from_core.at[1, t_own], tp=beside)

    def add_first(k, t_own):
        piece, rows = quarters[k]

        def one(place):
            row = pl.ds(rows.start + place.start, place.size)
            own[1, t_own, piece, row, :] = (
                own[1, t_own, piece, row, :].astype(F32)
                + from_core[1, t_own, piece, row, :].astype(F32)
                + first[k, t_own, place, :].astype(F32)
            ).astype(BF)

        in_pieces(quarter, one)

    gain_rows[...] = jnp.zeros_like(gain_rows)

    def finish(k):
        piece, rows = quarters[k]
        mail.arrive(y_second[k], second.at[k], tp=yonder)

        def back(place):
            local_row = pl.ds(rows.start + place.start, place.size)
            row = pl.ds(piece * half + rows.start + place.start, place.size)
            summed = own[1, 1, piece, local_row, :].astype(F32) + second[k, place, :].astype(F32)
            grad, products = norm_back(middle[row, :], gain[...], summed)
            grad = cotangent[row, :].astype(F32) + grad
            grad_middle[row, :] = grad
            grad_attention[piece, local_row, :] = (BRANCH * grad).astype(BF)
            gain_rows[...] += jnp.sum(products, axis=0, keepdims=True)

        in_pieces(quarter, back)
        source = grad_attention.at[piece, rows]
        mail.start(ring_y[k], source, attention_full.at[t, piece, rows], tp=yonder)
        mail.start(ring_core[k], source, attention_full.at[t, piece, rows], tp=beside)

    def z_hop(hop):
        for drain in drains:
            drain.arrive(hop - 1)
            drain.gather(hop)
            drain.send(hop)

    for k, (piece, rows) in enumerate(quarters):
        mail.arrive(x_first[k][0], first.at[k, 0], cp=1 - c)
        add_first(k, 0)
        mail.start(y_second[k], own.at[1, 0, piece, rows], second.at[k], tp=yonder)
        mail.arrive(x_first[k][1], first.at[k, 1], cp=1 - c)
        add_first(k, 1)
        if k > 0:
            finish(k - 1)
        if k == 2 and last > 2:
            z_hop(2)
        product_block(k + 1)
    finish(len(quarters) - 1)
    for block in range(len(quarters) + 1, blocks):
        product_block(block)
    keep = pltpu.make_async_copy(grad_attention, attention_full.at[t], local.at[0])
    keep.start()
    for hop in range(3, last):
        z_hop(hop)
    for k, (piece, rows) in enumerate(quarters):
        arrived = attention_full.at[yonder, piece, rows]
        mail.arrive(ring_y[k], arrived, tp=yonder)
        mail.start(ring_far[k], arrived, arrived, tp=beside)
    for k, (piece, rows) in enumerate(quarters):
        mail.arrive(ring_core[k], attention_full.at[beside, piece, rows], tp=beside)
        mail.arrive(ring_far[k], attention_full.at[far, piece, rows], tp=beside)
    for drain in drains:
        if last > 1:
            drain.arrive(last - 1)
        if last > 0:
            drain.gather(last)
    keep.wait()
    for block in range(blocks - 2, blocks):
        product_copy(block).wait()
    mail.finish()


def first_sum(count, part, gate_grad, up_grad, hidden, middle, cotangent, gain, down):
    slots = 6 * count + 32
    rows, width = middle.shape
    block = gate_grad.shape[1:]
    anywhere = pl.BlockSpec(memory_space=pl.ANY)
    vmem = pl.BlockSpec(memory_space=pltpu.VMEM)
    hops = max(count - 2, 1)
    return pl.pallas_call(
        functools.partial(first_sum_kernel, count),
        out_shape=(
            jax.ShapeDtypeStruct((rows, width), F32),
            jax.ShapeDtypeStruct((4, 2, rows // 2, width), BF),
            jax.ShapeDtypeStruct((1, width), F32),
            jax.ShapeDtypeStruct((2,) + block, BF),
            jax.ShapeDtypeStruct((2,) + block, BF),
            jax.ShapeDtypeStruct((hidden.shape[0], width), BF),
        ),
        in_specs=[anywhere] * 4 + [vmem] * 4,
        out_specs=(vmem, anywhere, vmem, vmem, vmem, anywhere),
        scratch_shapes=[
            pltpu.VMEM((2, 2, 2, rows // 2, width), BF),
            pltpu.VMEM((2, 2, 2, rows // 2, width), BF),
            pltpu.VMEM((4, 2, rows // 4, width), BF),
            pltpu.VMEM((4, rows // 4, width), BF),
            pltpu.VMEM((2, rows // 2, width), BF),
            pltpu.VMEM((2, hops, 2) + block, BF),
            pltpu.VMEM((2, hops, 2) + block, BF),
            pltpu.VMEM((2, hidden.shape[0] // 8, hidden.shape[1]), BF),
            pltpu.VMEM((2, hidden.shape[0] // 8, width), BF),
            pltpu.SemaphoreType.DMA((slots,)),
            pltpu.SemaphoreType.DMA((slots,)),
            pltpu.SemaphoreType.DMA((5,)),
            pltpu.SemaphoreType.DMA((2, 2)),
        ],
        cost_estimate=COST,
        compiler_params=pltpu.CompilerParams(
            collective_id=3, has_side_effects=True, vmem_limit_bytes=60 << 20
        ),
    )(part, gate_grad, up_grad, hidden, middle, cotangent, gain, down)


AHEAD = 6


def last_sum_kernel(
    count, grad_projected, qkv_full, qkv_grad, out_grad, tokens, grad_middle, gain, gain_rows,
    qkv_total, out_total, grad_tokens, gain_sums,
    own, from_core, to_yonder, from_yonder, pieces,
    from_x, heads_sum, heads_landed, outs_sum, outs_landed, final_out, gains, gain_line,
    part, weights, give_sum, give_landed, give_own, give_total,
    send, recv, local, weights_local,
):
    z, c, t = lax.axis_index("fsdp"), lax.axis_index("cp"), lax.axis_index("tp")
    beside, yonder = t + 1 - 2 * (t % 2), (t + 2) % 4
    half = tokens.shape[0] // 2
    last = count - 1
    mail = Mail(send, recv)
    greet(count)

    summed = TensorSum(mail, part, own, from_core, to_yonder, from_yonder, local)

    columns = qkv_total.shape[1]
    behind = columns * 5 // 6 // TILE * TILE
    split = -(-behind // (2 * TILE)) * TILE
    parts = [pl.ds(0, split), pl.ds(split, behind - split)]
    late = pl.ds(behind, columns - behind)
    cross = [[[mail.slot() for _ in range(count)] for _ in range(2)] for _ in parts]
    cross_own = [mail.slot() for _ in parts]

    def head_drain(lanes):
        def fill(hop, up, j, target):
            side = 0 if up else 1
            copy = pltpu.make_async_copy(qkv_grad.at[j, c, :, lanes], target, local.at[2])
            copy.start()
            copy.wait()
            arrived = from_x.at[side, hop - 1, :, lanes]

            def one(place):
                target[place, :] = (
                    target[place, :].astype(F32) + arrived[place, :].astype(F32)
                ).astype(BF)

            in_pieces(target.shape[0], one)

        return Drain(
            mail, count, fill,
            lambda side, hop: heads_sum.at[side, hop - 1, :, lanes],
            lambda side, hop: heads_landed.at[side, hop - 1, :, lanes],
        )

    heads = [head_drain(lanes) for lanes in parts]

    def late_fill(side_c):
        def fill(hop, up, j, target):
            copy = pltpu.make_async_copy(qkv_grad.at[j, side_c, :, late], target, local.at[2])
            copy.start()
            copy.wait()

        return fill

    stay = Drain(
        mail, count, late_fill(c),
        lambda side, hop: heads_sum.at[side, hop - 1, :, late],
        lambda side, hop: heads_landed.at[side, hop - 1, :, late],
    )
    give = Drain(
        mail, count, late_fill(1 - c),
        lambda side, hop: give_sum.at[side, hop - 1],
        lambda side, hop: give_landed.at[side, hop - 1],
    )
    give_slot = mail.slot()

    def fill_outs(hop, up, j, target):
        copy = pltpu.make_async_copy(out_grad.at[j], target, local.at[3])
        copy.start()
        copy.wait()

    outs = Drain(
        mail, count, fill_outs,
        lambda side, hop: outs_sum.at[side, hop - 1],
        lambda side, hop: outs_landed.at[side, hop - 1],
    )

    steps = [(hop, k) for hop in range(1, count + 1) for k in range(2)]

    def cross_send(step):
        if step >= len(steps):
            return
        hop, k = steps[step]
        lanes = parts[k]
        if hop == count:
            mail.start(
                cross_own[k], qkv_grad.at[z, 1 - c, :, lanes], from_x.at[0, last, :, lanes], cp=1 - c
            )
            return
        for side, up in enumerate((True, False)):
            mail.start(
                cross[k][side][hop], qkv_grad.at[heads[k].block(hop, up), 1 - c, :, lanes],
                from_x.at[side, hop - 1, :, lanes], when=heads[k].sends(hop, up), cp=1 - c,
            )

    def cross_arrive(hop, k):
        for side, up in enumerate((True, False)):
            mail.arrive(
                cross[k][side][hop], from_x.at[side, hop - 1, :, parts[k]],
                when=heads[k].sends(hop, up), cp=1 - c,
            )

    for step in range(AHEAD):
        cross_send(step)
    early_chains = (outs, give, stay)
    if count > 1:
        for drain in early_chains:
            drain.gather(1)
            drain.send(1)

    wide_block = weights.shape[1]
    blocks = qkv_full.shape[0] // wide_block

    def weights_copy(block, slot):
        return pltpu.make_async_copy(
            qkv_full.at[pl.ds(block * wide_block, wide_block)], weights.at[slot],
            weights_local.at[slot],
        )

    def product(block, carry):
        slot = lax.rem(block, 2)
        weights_copy(block, slot).wait()
        pl.when(block + 1 < blocks)(lambda: weights_copy(block + 1, 1 - slot).start())
        columns = pl.ds(pl.multiple_of(block * wide_block, wide_block), wide_block)
        value = lax.dot_general(
            grad_projected[...], weights[slot], (((1,), (1,)), ((), ())),
            preferred_element_type=F32,
        )
        part[:, :, columns] = value.astype(BF).reshape(part.shape[:2] + (wide_block,))
        return carry

    weights_copy(0, 0).start()
    thirds = [blocks * k // 3 for k in range(4)]

    keep = pltpu.make_async_copy(pieces.at[c], grad_tokens.at[c], local.at[0])
    home = mail.slot()
    gain_x, gain_y, gain_core = mail.slot(), mail.slot(), mail.slot()
    line = Line(mail, count, gain_line.at[z], lambda j: gain_line.at[j])

    def finish_rows():
        gains[0, 0:1, :] = jnp.zeros_like(gain_rows)
        gains[0, 1:2, :] = gain_rows[...]
        for piece in range(2):
            summed.arrive(piece)

            def back(place, piece=piece):
                row = pl.ds(place.start + piece * half, place.size)
                grad, rows = norm_back(tokens[row, :].astype(F32), gain[...], summed.rows(row))
                pieces[piece, place, :] = (grad_middle[row, :] + grad).astype(BF)
                gains[0, 0:1, :] += jnp.sum(rows, axis=0, keepdims=True)

            in_pieces(half, back)
        mail.start(home, pieces.at[1 - c], grad_tokens.at[c], cp=1 - c)
        keep.start()
        mail.start(gain_core, gains.at[0], gains.at[1], tp=beside)

    def gain_step(k):
        if k == 0:
            mail.arrive(gain_core, gains.at[1], tp=beside)
            gains[2] = gains[0] + gains[1]
            mail.start(gain_y, gains.at[2], gains.at[3], tp=yonder)
        elif k == 1:
            mail.arrive(gain_y, gains.at[3], tp=yonder)
            gains[4] = gains[2] + gains[3]
            mail.start(gain_x, gains.at[4], gains.at[5], cp=1 - c)
        elif k == 2:
            mail.arrive(gain_x, gains.at[5], cp=1 - c)
            gain_line[z] = gains[4] + gains[5]
            if count > 1:
                line.send(1)
        else:
            hop = k - 2
            line.arrive(hop)
            if hop + 1 < count:
                line.send(hop + 1)

    def outs_hop(hop):
        for drain in early_chains:
            drain.arrive(hop - 1)
            drain.gather(hop)
            drain.send(hop)

    def give_away():
        copy = pltpu.make_async_copy(qkv_grad.at[z, 1 - c, :, late], give_own, local.at[3])
        copy.start()
        copy.wait()
        if count > 1:
            give.arrive(last)

        def one(place):
            total = give_own[place, :].astype(F32)
            for side, up in enumerate((True, False)):
                if count > 1:
                    landed = give.landed(side, last)[place, :].astype(F32)
                    total += jnp.where(give.gets(last, up), landed, 0.0)
            give_total[place, :] = total.astype(BF)

        in_pieces(give_own.shape[0], one)
        mail.start(give_slot, give_total, from_x.at[0, last, :, late], cp=1 - c)

    for step, (hop, k) in enumerate(steps[:-2]):
        if step < 3:
            lax.fori_loop(thirds[step], thirds[step + 1], product, 0)
        if count == 2 and step == 1:
            lax.fori_loop(thirds[2], thirds[3], product, 0)
        if step == 2 or count == 2 and step == 1:
            summed.begin()
        cross_arrive(hop, k)
        cross_send(step + AHEAD)
        if hop > 1:
            heads[k].arrive(hop - 1)
        heads[k].gather(hop)
        heads[k].send(hop)
        if k == 1 and hop + 1 < count:
            outs_hop(hop + 1)
        if step == 2 or count == 2 and step == 1:
            summed.turn()
        if step == 3 or count == 2 and step == 1:
            finish_rows()
        if step == 5 or step == 3 and count == 3:
            gain_step(0)
            gain_step(1)
    if count == 1:
        lax.fori_loop(thirds[0], thirds[3], product, 0)
        summed.begin()
        summed.turn()
        finish_rows()
    if count <= 2:
        gain_step(0)
        gain_step(1)
    gain_step(2)
    give_away()

    own_copy = pltpu.make_async_copy(qkv_grad.at[z, c], from_x.at[1, last], local.at[2])
    own_copy.start()
    out_copy = pltpu.make_async_copy(out_grad.at[z], final_out, local.at[3])
    out_copy.start()
    for k, lanes in enumerate(parts):
        mail.arrive(cross_own[k], from_x.at[0, last, :, lanes], cp=1 - c)
    mail.arrive(give_slot, from_x.at[0, last, :, late], cp=1 - c)
    own_copy.wait()
    out_copy.wait()

    def start_heads(place):
        qkv_total[place, :] = from_x[0, last, place, :].astype(F32) + from_x[
            1, last, place, :
        ].astype(F32)

    in_pieces(qkv_total.shape[0], start_heads)

    def start_outs(place):
        out_total[place, :] = final_out[place, :].astype(F32)

    in_pieces(out_total.shape[0], start_outs)
    for hop in range(1, count):
        gain_step(2 + hop)
    if count > 1:
        chains = [(outs, pl.ds(0, out_total.shape[1]), out_total)]
        chains += [(stay, late, qkv_total)]
        chains += [(heads[k], lanes, qkv_total) for k, lanes in enumerate(parts)]
        for drain, lanes, total in chains:
            drain.arrive(last)
            for side, up in enumerate((True, False)):

                def more(drain=drain, total=total, side=side, lanes=lanes):
                    landed = drain.landed(side, last)

                    def one(place):
                        total[place, lanes] += landed[place, :].astype(F32)

                    in_pieces(total.shape[0], one)

                pl.when(drain.gets(last, up))(more)
    gain_sums[...] = jnp.sum(gain_line[...], axis=0)
    mail.arrive(home, grad_tokens.at[1 - c], cp=1 - c)
    keep.wait()
    mail.finish()


def last_sum(count, grad_projected, qkv_full, qkv_grad, out_grad, tokens, grad_middle, gain, gain_rows):
    slots = 17 * count + 17
    rows, width = tokens.shape
    hops = max(count - 1, 1)
    block, out_block = qkv_grad.shape[2:], out_grad.shape[1:]
    columns = block[1]
    give_block = (block[0], columns - columns * 5 // 6 // TILE * TILE)
    anywhere = pl.BlockSpec(memory_space=pl.ANY)
    vmem = pl.BlockSpec(memory_space=pltpu.VMEM)
    return pl.pallas_call(
        functools.partial(last_sum_kernel, count),
        out_shape=(
            jax.ShapeDtypeStruct(block, F32),
            jax.ShapeDtypeStruct(out_block, F32),
            jax.ShapeDtypeStruct((2, rows // 2, width), BF),
            jax.ShapeDtypeStruct((2, width), F32),
        ),
        in_specs=[vmem] + [anywhere] * 3 + [vmem] * 4,
        out_specs=(vmem, vmem, anywhere, vmem),
        scratch_shapes=[
            pltpu.VMEM((2, rows, width), BF),
            pltpu.VMEM((2, rows, width), BF),
            pltpu.VMEM((rows, width), BF),
            pltpu.VMEM((rows, width), BF),
            pltpu.VMEM((2, rows // 2, width), BF),
            pltpu.VMEM((2, count) + block, BF),
            pltpu.VMEM((2, hops) + block, BF),
            pltpu.VMEM((2, hops) + block, BF),
            pltpu.VMEM((2, hops) + out_block, BF),
            pltpu.VMEM((2, hops) + out_block, BF),
            pltpu.VMEM(out_block, BF),
            pltpu.VMEM((6, 2, width), F32),
            pltpu.VMEM((count, 2, width), F32),
            pltpu.VMEM((4, rows, width), BF),
            pltpu.VMEM((2, 2 * TILE, qkv_full.shape[1]), BF),
            pltpu.VMEM((2, hops) + give_block, BF),
            pltpu.VMEM((2, hops) + give_block, BF),
            pltpu.VMEM(give_block, BF),
            pltpu.VMEM(give_block, BF),
            pltpu.SemaphoreType.DMA((slots,)),
            pltpu.SemaphoreType.DMA((slots,)),
            pltpu.SemaphoreType.DMA((4,)),
            pltpu.SemaphoreType.DMA((2,)),
        ],
        cost_estimate=COST,
        compiler_params=pltpu.CompilerParams(
            collective_id=4, has_side_effects=True, vmem_limit_bytes=60 << 20
        ),
    )(grad_projected, qkv_full, qkv_grad, out_grad, tokens, grad_middle, gain, gain_rows)


def normalize(values):
    return values * lax.rsqrt(jnp.mean(values * values, axis=-1, keepdims=True) + EPSILON)


def silu_product(gate_pre, up_pre):
    return gate_pre / (1.0 + jnp.exp(-gate_pre)) * up_pre


def matmul(left, right):
    return jnp.dot(left, right, preferred_element_type=F32)


def rows_inner(left, right):
    return lax.dot_general(left, right, (((0,), (0,)), ((), ())), preferred_element_type=F32)


def cols_inner(left, right):
    return lax.dot_general(left, right, (((1,), (1,)), ((), ())), preferred_element_type=F32)


def row_major(value):
    return with_layout_constraint(value, Layout(major_to_minor=(0, 1)))


def after(value, *earlier):
    return lax.optimization_barrier((value, *earlier))[0]


def swap(value):
    return lax.ppermute(value, "cp", [(0, 1), (1, 0)])


def in_order(place, mine, other, axis):
    return jnp.where(
        place == 0,
        jnp.concatenate([mine, other], axis=axis),
        jnp.concatenate([other, mine], axis=axis),
    )


def on_device(
    tokens,
    seq_lengths,
    attention_gain,
    query_weight,
    key_weight,
    value_weight,
    out_weight,
    feedforward_gain,
    gate_weight,
    up_weight,
    down_weight,
    cotangent,
):
    c = lax.axis_index("cp")
    z = lax.axis_index("fsdp")
    sets = lax.axis_size("cp")
    count = lax.axis_size("fsdp")
    lanes = lax.axis_size("tp")
    slots, local, width = tokens.shape
    share = query_weight.shape[0]
    heads_width = query_weight.shape[1]
    head_count = heads_width // HD
    hidden_width = gate_weight.shape[1] // sets
    rows = sets * local
    seq = rows * lanes
    blocks = row_blocks(seq, sets, local)
    everyone = ("cp", "tp")

    def pick(value, which, axis=0):
        return lax.dynamic_index_in_dim(value, which, axis, keepdims=False)

    length = pick(seq_lengths, c)[None]
    gain_one = attention_gain.astype(F32)
    gain_two = feedforward_gain.astype(F32)

    qkv = jnp.concatenate([query_weight, key_weight, value_weight], axis=1)

    def halves(weight):
        return weight[:, :hidden_width], weight[:, hidden_width:]

    parts = [halves(weight) for weight in (gate_weight, up_weight, down_weight.T)]
    own_wide = jnp.stack([jnp.where(c == 0, low, high) for low, high in parts])
    wide_away = jnp.stack([jnp.where(c == 0, high, low) for low, high in parts])
    token_rows, normed_one, full_qkv, out_half, first_low, first_high = first_gather(
        count, pick(tokens, c), pick(tokens, 1 - c), gain_one[None], qkv, out_weight.T,
        own_wide, wide_away,
    )
    token_rows = token_rows.reshape(rows, width)
    normed_one = normed_one.reshape(seq, width)
    full_qkv = full_qkv.reshape(width, 3 * heads_width)

    out_half, cotangent = after((out_half, cotangent), full_qkv)
    cotangents = lax.all_gather(cotangent, everyone, axis=0).reshape(
        sets, lanes, slots, local, width
    )
    full_out = in_order(c, out_half[:, None], swap(out_half)[:, None], 1)
    full_out = full_out.reshape(width, heads_width)
    up_hop = [(i, i + 1) for i in range(count - 1)]
    down_hop = [(i, i - 1) for i in range(1, count)]
    second_low = lax.ppermute(first_low, "fsdp", up_hop)
    second_high = lax.ppermute(first_high, "fsdp", down_hop)
    cosine_table, sine_table = tables(seq)
    projected = matmul(normed_one, full_qkv)
    context, q_heads, k_heads, v_heads, level = attention(
        blocks, head_count, length, projected, cosine_table, sine_table
    )
    part = cols_inner(context, full_out).astype(BF)

    middle, middle_home, normed_two, full_gate, full_up, full_down = second_gather(
        count, part.reshape(lanes, rows, width), token_rows, gain_two[None], own_wide,
        first_low, first_high, second_low, second_high,
    )
    normed_two = normed_two.reshape(sets * seq, width)
    full_gate, full_up, full_down = (
        full.reshape(width, hidden_width) for full in (full_gate, full_up, full_down)
    )
    t = lax.axis_index("tp")
    cotangents_all = cotangents.reshape(sets * seq, width)
    cotangent_rows = pick(pick(cotangents, t, 1), c, 1).reshape(rows, width)
    gate_pre = matmul(normed_two, full_gate)
    up_pre = matmul(normed_two, full_up)
    hidden_exact, silu_back = jax.vjp(silu_product, gate_pre, up_pre)
    hidden = hidden_exact.astype(BF)

    def blocks_of(gradient):
        gradient = row_major(gradient.astype(BF))
        return gradient.reshape(count, width // count, hidden_width)

    down_blocks = blocks_of(BRANCH * rows_inner(cotangents_all, hidden))
    def leaving(hop, low, high):
        leaving_up = pick(down_blocks, jnp.minimum(z + count - hop, count - 1))
        leaving_down = pick(down_blocks, jnp.maximum(z - count + hop, 0))
        if hop > 1:
            leaving_up = (leaving_up.astype(F32) + low.astype(F32)).astype(BF)
            leaving_down = (leaving_down.astype(F32) + high.astype(F32)).astype(BF)
        return leaving_up, leaving_down

    def sent(hop, leaving_up, leaving_down):
        return (
            lax.ppermute(leaving_up, "fsdp", up_hop[:hop]),
            lax.ppermute(leaving_down, "fsdp", down_hop[count - 1 - hop :]),
        )

    gone = leaving(1, None, None)
    for hop in range(2, count - 1):
        gone = leaving(hop, *sent(hop - 1, *gone))
    grad_hidden = BRANCH * matmul(cotangents_all, full_down)
    grad_gate_exact, grad_up_exact = silu_back(grad_hidden)
    grad_gate_pre = grad_gate_exact.astype(BF)
    grad_up_pre = grad_up_exact.astype(BF)
    gate_part = lax.optimization_barrier(cols_inner(grad_gate_pre, full_gate).astype(BF))
    grad_normed_two = gate_part.astype(F32) + cols_inner(grad_up_pre, full_up)
    gate_blocks = blocks_of(rows_inner(normed_two, grad_gate_pre))
    up_blocks = blocks_of(rows_inner(normed_two, grad_up_pre))
    part = grad_normed_two.astype(BF).reshape(sets, lanes, slots, local, width)
    part, gone = lax.optimization_barrier((part, gone))
    grad_middle, grad_attention, gain_two_rows, pair_up, pair_down, feedforward = first_sum(
        count, part, gate_blocks, up_blocks, hidden, middle, cotangent_rows, gain_two[None],
        full_down,
    )
    grad_attention = grad_attention.reshape(seq, width)

    if count > 1:
        if count > 2:
            arrived = after(sent(count - 2, *gone), grad_attention)
            gone = leaving(count - 1, *arrived)
        leaving_up, leaving_down = after(gone, grad_attention)
        low = [lax.ppermute(pair_up, "fsdp", up_hop), lax.ppermute(leaving_up, "fsdp", up_hop)]
        high = [
            lax.ppermute(pair_down, "fsdp", down_hop), lax.ppermute(leaving_down, "fsdp", down_hop),
        ]
        low = [low[0][0], low[0][1], low[1]]
        high = [high[0][0], high[0][1], high[1]]

    def own_share(which, gradient):
        total = pick(gradient, z).astype(F32)
        if count > 1:
            total = total + low[which].astype(F32) + high[which].astype(F32)
        return total.reshape(sets, share, hidden_width)

    shares = [
        own_share(which, gradient)
        for which, gradient in enumerate((gate_blocks, up_blocks, down_blocks))
    ]
    others = swap(jnp.stack([pick(total, 1 - c).astype(BF) for total in shares]))
    grad_gate, grad_up, grad_down = (
        in_order(c, pick(total, c), others[which].astype(F32), 1)
        for which, total in enumerate(shares)
    )
    grad_down = grad_down.T

    out_pieces = row_major(rows_inner(grad_attention, context).astype(BF))
    out_pieces = out_pieces.reshape(count, sets, share, heads_width)
    out_other = swap(pick(out_pieces, 1 - c, 1))
    out_pieces = (pick(out_pieces, c, 1).astype(F32) + out_other.astype(F32)).astype(BF)
    grad_context = row_major(matmul(grad_attention, full_out).astype(BF))
    feedforward = lax.psum_scatter(feedforward, everyone, scatter_dimension=0, tiled=True)
    feedforward = feedforward.reshape(slots, local, width)
    output = (middle_home + BRANCH * feedforward.astype(F32)).astype(BF)
    grad_projected = attention_back(
        blocks, head_count, length, grad_context, q_heads, k_heads, v_heads, level,
        cosine_table, sine_table,
    )
    grad_projected = after(grad_projected, out_other, low[2], high[2])
    grad_qkv = row_major(rows_inner(normed_one, grad_projected).astype(BF))
    grad_qkv, grad_out, grad_tokens, gain_sums = last_sum(
        count, grad_projected, full_qkv, grad_qkv.reshape(count, sets, share, 3 * heads_width), out_pieces,
        token_rows, grad_middle, gain_one[None], gain_two_rows,
    )
    return (
        output,
        grad_tokens,
        grad_qkv[:, :heads_width],
        grad_qkv[:, heads_width : 2 * heads_width],
        grad_qkv[:, 2 * heads_width :],
        grad_out.T,
        gain_sums[0],
        grad_gate,
        grad_up,
        grad_down,
        gain_sums[1],
    )


def solution(mesh):
    in_specs = (
        P("fsdp", ("cp", "tp"), None),
        P("fsdp"),
        P(),
        P(("fsdp", "cp"), "tp"),
        P(("fsdp", "cp"), "tp"),
        P(("fsdp", "cp"), "tp"),
        P("tp", ("fsdp", "cp")),
        P(),
        P(("fsdp", "cp"), "tp"),
        P(("fsdp", "cp"), "tp"),
        P("tp", ("fsdp", "cp")),
        P("fsdp", ("cp", "tp"), None),
    )
    out_specs = (
        P("fsdp", ("cp", "tp"), None),
        P("fsdp", ("cp", "tp"), None),
        P(("fsdp", "cp"), "tp"),
        P(("fsdp", "cp"), "tp"),
        P(("fsdp", "cp"), "tp"),
        P("tp", ("fsdp", "cp")),
        P(),
        P(("fsdp", "cp"), "tp"),
        P(("fsdp", "cp"), "tp"),
        P("tp", ("fsdp", "cp")),
        P(),
    )
    return jax.shard_map(
        on_device, mesh=mesh, in_specs=in_specs, out_specs=out_specs, check_vma=False
    )
```

```python
import functools
import math

import jax
import jax.numpy as jnp
import numpy as np
from jax import lax
from jax.experimental import pallas as pl
from jax.experimental.layout import Layout, with_layout_constraint
from jax.experimental.pallas import tpu as pltpu
from jax.sharding import PartitionSpec as P

HD = 64
EPSILON = 1e-05
BRANCH = 1.4 / math.sqrt(40.0)
BF = jnp.bfloat16
F32 = jnp.float32
TILE = 128
QUERY_ROWS = 512


def turned(values, cosine, sine):
    lane = lax.broadcasted_iota(jnp.int32, values.shape, 1)
    partner = jnp.where(
        lane % HD < HD // 2,
        pltpu.roll(values, TILE - HD // 2, 1),
        pltpu.roll(values, HD // 2, 1),
    )
    return values * cosine + partner * sine


def row_blocks(seq, sets, local):
    lanes = seq // sets // local
    return [
        ((t * sets + h) * local, (h * lanes + t) * local)
        for t in range(lanes)
        for h in range(sets)
    ]


def key_mask(length, first, rows, columns):
    place = first + lax.broadcasted_iota(jnp.int32, (rows, columns), 0)
    return place < length


def scores_of(keys, queries, length, first_query):
    raw = lax.dot_general(keys, queries, (((1,), (1,)), ((), ())), preferred_element_type=F32)
    key_place = lax.broadcasted_iota(jnp.int32, raw.shape, 0)
    query_place = first_query + lax.broadcasted_iota(jnp.int32, raw.shape, 1)
    return jnp.where((key_place <= query_place) & (key_place < length), raw, -1e30)


def attention_kernel(
    blocks, length_ref, projected, cosine, sine, context, q_heads, k_heads, v_heads, level, kept
):
    heads, seq, _ = q_heads.shape
    local = seq // len(blocks)
    length = length_ref[0]
    for gathered, ordered in blocks:
        source, target = pl.ds(gathered, local), pl.ds(ordered, local)
        for tile in range(-(-3 * heads // 2)):
            width = min(TILE, 3 * heads * HD - tile * TILE)
            values = projected[source, tile * TILE : tile * TILE + width]
            if tile * 2 < 2 * heads:
                values = turned(values, cosine[target, :], sine[target, :])
            for which in range(width // HD):
                index = tile * 2 + which
                piece = values[:, which * HD : (which + 1) * HD]
                if index < heads:
                    q_heads[index, target, :] = (piece * (1.0 / math.sqrt(HD))).astype(BF)
                elif index < 2 * heads:
                    k_heads[index - heads, target, :] = piece.astype(BF)
                else:
                    v_heads[index - 2 * heads, target, :] = piece.astype(BF)

    def one_head(head, carry):
        for first in range(0, seq, QUERY_ROWS):
            most = first + QUERY_ROWS
            queries = q_heads[head, first:most, :]
            keys = k_heads[head, :most, :]
            values = v_heads[head, :most, :]
            scores = scores_of(keys, queries, length, first)
            top = jnp.max(scores, axis=0, keepdims=True)
            exponent = jnp.exp(scores - top)
            total = jnp.sum(exponent, axis=0, keepdims=True)
            probabilities = exponent.astype(BF)
            level[head, :, first:most] = top + jnp.log(total)
            mixed = lax.dot_general(
                values, probabilities, (((0,), (0,)), ((), ())), preferred_element_type=F32
            )
            kept[head, first:most, :] = (mixed * (1.0 / total)).T.astype(BF)
        return carry

    lax.fori_loop(0, heads, one_head, 0, unroll=True)
    for gathered, ordered in blocks:
        source, target = pl.ds(ordered, local), pl.ds(gathered, local)
        for head in range(0, heads, 2):
            parts = [kept[index, source, :] for index in range(head, min(head + 2, heads))]
            joined = parts[0] if len(parts) == 1 else jnp.concatenate(parts, axis=1)
            context[target, head * HD : head * HD + joined.shape[1]] = joined


def attention(blocks, heads, length, projected, cosine, sine):
    seq = projected.shape[0]
    per_head = jax.ShapeDtypeStruct((heads, seq, HD), BF)
    vmem = pl.BlockSpec(memory_space=pltpu.VMEM)
    return pl.pallas_call(
        functools.partial(attention_kernel, blocks),
        out_shape=(
            jax.ShapeDtypeStruct((seq, heads * HD), BF),
            per_head,
            per_head,
            per_head,
            jax.ShapeDtypeStruct((heads, 1, seq), F32),
        ),
        in_specs=[pl.BlockSpec(memory_space=pltpu.SMEM), vmem, vmem, vmem],
        out_specs=(vmem,) * 5,
        scratch_shapes=[pltpu.VMEM((heads, seq, HD), BF)],
        compiler_params=pltpu.CompilerParams(vmem_limit_bytes=48 << 20),
        cost_estimate=pl.CostEstimate(
            flops=4 * heads * seq * seq * HD, transcendentals=heads * seq * seq, bytes_accessed=20 << 20
        ),
    )(length, projected, cosine, sine)


def attention_back_kernel(
    blocks, length_ref, grad_context, q_heads, k_heads, v_heads, level, cosine, sine,
    grad_projected, g_heads, dq, dk, dv,
):
    heads, seq, _ = q_heads.shape
    local = seq // len(blocks)
    length = length_ref[0]
    for gathered, ordered in blocks:
        source, target = pl.ds(gathered, local), pl.ds(ordered, local)
        for head in range(heads):
            g_heads[head, target, :] = grad_context[source, head * HD : (head + 1) * HD]

    def one_head(head, carry):
        keys_turned = k_heads[head].T
        for first in reversed(range(0, seq, QUERY_ROWS)):
            most = first + QUERY_ROWS
            queries = q_heads[head, first:most, :]
            upstream = g_heads[head, first:most, :]
            keys = k_heads[head, :most, :]
            values = v_heads[head, :most, :]
            scores = scores_of(keys, queries, length, first)
            probabilities = jnp.exp(scores - level[head, :, first:most])
            grad_probabilities = lax.dot_general(
                values, upstream, (((1,), (1,)), ((), ())), preferred_element_type=F32
            )
            weighted = probabilities * grad_probabilities
            balance = jnp.sum(weighted, axis=0, keepdims=True)
            grad_scores = (weighted - probabilities * balance).astype(BF)
            grad_keys = jnp.dot(grad_scores, queries, preferred_element_type=F32)
            grad_values = jnp.dot(
                probabilities.astype(BF), upstream, preferred_element_type=F32
            )
            if most == seq:
                dk[head, :, :] = grad_keys
                dv[head, :, :] = grad_values
            else:
                dk[head, :most, :] += grad_keys
                dv[head, :most, :] += grad_values
            grad_queries = jnp.dot(
                keys_turned[:, :most], grad_scores, preferred_element_type=F32
            )
            dq[head, first:most, :] = grad_queries.T * (1.0 / math.sqrt(HD))
        return carry

    lax.fori_loop(0, heads, one_head, 0, unroll=True)
    sources = [dq] * heads + [dk] * heads + [dv] * heads
    for gathered, ordered in blocks:
        source, target = pl.ds(ordered, local), pl.ds(gathered, local)
        for tile in range(-(-3 * heads // 2)):
            indices = range(tile * 2, min(tile * 2 + 2, 3 * heads))
            parts = [sources[index][index % heads, source, :] for index in indices]
            joined = parts[0] if len(parts) == 1 else jnp.concatenate(parts, axis=1)
            if tile * 2 < 2 * heads:
                joined = turned(joined, cosine[source, :], -sine[source, :])
            grad_projected[target, tile * TILE : tile * TILE + joined.shape[1]] = joined.astype(BF)


def attention_back(blocks, heads, length, grad_context, q_heads, k_heads, v_heads, level, cosine, sine):
    seq = grad_context.shape[0]
    vmem = pl.BlockSpec(memory_space=pltpu.VMEM)
    return pl.pallas_call(
        functools.partial(attention_back_kernel, blocks),
        out_shape=jax.ShapeDtypeStruct((seq, 3 * heads * HD), BF),
        in_specs=[pl.BlockSpec(memory_space=pltpu.SMEM)] + [vmem] * 7,
        out_specs=vmem,
        scratch_shapes=[
            pltpu.VMEM((heads, seq, HD), BF),
            pltpu.VMEM((heads, seq, HD), F32),
            pltpu.VMEM((heads, seq, HD), F32),
            pltpu.VMEM((heads, seq, HD), F32),
        ],
        compiler_params=pltpu.CompilerParams(vmem_limit_bytes=56 << 20),
        cost_estimate=pl.CostEstimate(
            flops=10 * heads * seq * seq * HD, transcendentals=heads * seq * seq, bytes_accessed=20 << 20
        ),
    )(length, grad_context, q_heads, k_heads, v_heads, level, cosine, sine)


def tables(seq):
    step = np.arange(HD // 2, dtype=np.float32)
    frequency = np.power(np.float32(10000.0), np.float32(-2.0) * step / np.float32(HD))
    angle = np.arange(seq, dtype=np.float32)[:, None] * frequency[None, :]
    cosine, sine = np.cos(angle), np.sin(angle)
    signed = np.concatenate([-sine, sine, -sine, sine], axis=1)
    return jnp.asarray(np.tile(cosine, (1, 4))), jnp.asarray(signed)


COST = pl.CostEstimate(flops=0, transcendentals=0, bytes_accessed=300 << 20)
MESH = pl.DeviceIdType.MESH


def greet(count):
    barrier = pltpu.get_barrier_semaphore()
    z, c, t = lax.axis_index("fsdp"), lax.axis_index("cp"), lax.axis_index("tp")

    def hello(**place):
        pl.semaphore_signal(barrier, inc=1, device_id=place, device_id_type=MESH)

    hello(cp=1 - c)
    hello(tp=t + 1 - 2 * (t % 2))
    hello(tp=(t + 2) % 4)
    pl.when(z > 0)(lambda: hello(fsdp=z - 1))
    pl.when(z < count - 1)(lambda: hello(fsdp=z + 1))
    peers = 3 + jnp.minimum(z, 1) + jnp.minimum(count - 1 - z, 1)
    pl.semaphore_wait(barrier, peers)


class Mail:
    def __init__(self, send, recv):
        self.send, self.recv, self.used, self.open = send, recv, 0, []

    def slot(self):
        self.used += 1
        return self.used - 1

    def copy(self, slot, source, target, **place):
        return pltpu.make_async_remote_copy(
            src_ref=source,
            dst_ref=target,
            send_sem=self.send.at[slot],
            recv_sem=self.recv.at[slot],
            device_id=place,
            device_id_type=MESH,
        )

    def start(self, slot, source, target, when=None, **place):
        made = self.copy(slot, source, target, **place)
        if when is None:
            made.start()
        else:
            pl.when(when)(made.start)
        self.open.append((made, when))

    def arrive(self, slot, target, when=None, **place):
        made = self.copy(slot, target, target, **place)
        if when is None:
            made.wait_recv()
        else:
            pl.when(when)(made.wait_recv)

    def finish(self):
        for made, when in self.open:
            if when is None:
                made.wait_send()
            else:
                pl.when(when)(made.wait_send)


class Stage:
    def __init__(self, pieces, stage, sems):
        self.made = []
        for k, (source, target, when) in enumerate(pieces):
            self.made.append(
                (
                    pltpu.make_async_copy(source, stage.at[k], sems.at[0, k]),
                    pltpu.make_async_copy(stage.at[k], target, sems.at[1, k]),
                    when,
                )
            )

    def begin(self):
        for copy, _, when in self.made:
            copy.start() if when is None else pl.when(when)(copy.start)

    def turn(self):
        for first, second, when in self.made:

            def on(first=first, second=second):
                first.wait()
                second.start()

            on() if when is None else pl.when(when)(on)

    def end(self):
        for _, copy, when in self.made:
            copy.wait() if when is None else pl.when(when)(copy.wait)


class Line:
    def __init__(self, mail, count, own, at, ready=()):
        self.mail, self.count, self.own, self.at = mail, count, own, at
        self.ready = ready
        self.z = lax.axis_index("fsdp")
        self.up = [mail.slot() for _ in range(count)]
        self.down = [mail.slot() for _ in range(count)]

    def has_low(self, hop):
        return self.z >= hop

    def has_high(self, hop):
        return self.z <= self.count - 1 - hop

    def send(self, hop):
        z, count, mail = self.z, self.count, self.mail
        low, high = jnp.maximum(z - hop + 1, 0), jnp.minimum(z + hop - 1, count - 1)
        from_low = from_high = self.own
        if hop > 1:
            from_low, from_high = self.at(low), self.at(high)
        if 0 < hop - 1 <= len(self.ready):
            from_low, from_high = self.ready[hop - 2]
        mail.start(
            self.up[hop], from_low, self.at(low),
            when=(z >= hop - 1) & (z < count - 1), fsdp=jnp.minimum(z + 1, count - 1),
        )
        mail.start(
            self.down[hop], from_high, self.at(high),
            when=(z <= count - hop) & (z > 0), fsdp=jnp.maximum(z - 1, 0),
        )

    def arrive(self, hop):
        z, count = self.z, self.count
        self.mail.arrive(
            self.up[hop], self.at(jnp.maximum(z - hop, 0)), when=self.has_low(hop), fsdp=z
        )
        self.mail.arrive(
            self.down[hop], self.at(jnp.minimum(z + hop, count - 1)), when=self.has_high(hop), fsdp=z
        )


    def keep(self):
        z, count = self.z, self.count
        made = [(self.own, self.at(z), None)]
        for index, (low, high) in enumerate(self.ready):
            hop = index + 1
            made.append((low, self.at(jnp.maximum(z - hop, 0)), self.has_low(hop)))
            made.append((high, self.at(jnp.minimum(z + hop, count - 1)), self.has_high(hop)))
        return made


class Across:
    def __init__(self, line, own, mine_at, other_at):
        self.line, self.own, self.mine_at, self.other_at = line, own, mine_at, other_at
        self.c = lax.axis_index("cp")
        self.low = [line.mail.slot() for _ in range(line.count)]
        self.high = [line.mail.slot() for _ in range(line.count)]

    def send(self, hop):
        line, mail = self.line, self.line.mail
        z, count, other = line.z, line.count, 1 - self.c
        if hop == 0:
            mail.start(self.low[0], self.own, self.mine_at(z), cp=other)
            return
        low, high = jnp.maximum(z - hop, 0), jnp.minimum(z + hop, count - 1)
        mail.start(self.low[hop], self.mine_at(low), self.mine_at(low), when=line.has_low(hop), cp=other)
        mail.start(self.high[hop], self.mine_at(high), self.mine_at(high), when=line.has_high(hop), cp=other)

    def arrive(self, hop):
        line, mail = self.line, self.line.mail
        z, count, other = line.z, line.count, 1 - self.c
        if hop == 0:
            mail.arrive(self.low[0], self.other_at(z), cp=other)
            return
        low, high = jnp.maximum(z - hop, 0), jnp.minimum(z + hop, count - 1)
        mail.arrive(self.low[hop], self.other_at(low), when=line.has_low(hop), cp=other)
        mail.arrive(self.high[hop], self.other_at(high), when=line.has_high(hop), cp=other)


def first_gather_kernel(
    count, tokens, tokens_away, gain, qkv, turned_out,
    wide_0, wide_1, wide_2, away_0, away_1, away_2,
    token_rows, normed_full, qkv_full, out_half, low_pair, high_pair,
    landed, normed, wide_landed, qkv_stage, out_stage,
    send, recv, local, qkv_local, out_local,
):
    z, c, t = lax.axis_index("fsdp"), lax.axis_index("cp"), lax.axis_index("tp")
    beside, yonder = t + 1 - 2 * (t % 2), (t + 2) % 4
    low, high = low_pair.at[0], high_pair.at[0]
    wide, wide_away = (wide_0, wide_1, wide_2), (away_0, away_1, away_2)
    mail = Mail(send, recv)
    greet(count)
    stage_qkv = Stage([(qkv, qkv_full.at[z, c], None)], qkv_stage, qkv_local)
    stage_out = Stage([(turned_out, out_half.at[z], None)], out_stage, out_local)
    kept = []

    heads = Line(mail, count, qkv, lambda j: qkv_full.at[j, c])
    heads_across = Across(
        heads, qkv, lambda j: qkv_full.at[j, c], lambda j: qkv_full.at[j, 1 - c]
    )
    outs = Line(mail, count, turned_out, lambda j: out_half.at[j])
    wide_up, wide_down, wide_x = ([mail.slot() for _ in wide] for _ in range(3))
    rows_x = mail.slot()
    rows_y = [mail.slot() for _ in range(2)]
    rows_core = [mail.slot() for _ in range(4)]

    mail.start(rows_x, tokens_away, landed, cp=1 - c)
    heads.send(1)

    def rows_out(source, side, half):
        def one(place):
            rows = source[place, :]
            token_rows[half, place, :] = rows
            normed[half, place, :] = (normalize(rows.astype(F32)) * gain[...]).astype(BF)

        in_pieces(source.shape[0], one)
        mail.start(rows_y[side], normed.at[half], normed_full.at[t, half], tp=yonder)
        mail.start(rows_core[side], normed.at[half], normed_full.at[t, half], tp=beside)

    stage_qkv.begin()
    stage_out.begin()
    rows_out(tokens, 0, c)
    stage_qkv.turn()
    stage_out.turn()
    mail.arrive(rows_x, landed, cp=1 - c)
    heads_across.send(0)
    rows_out(landed, 1, 1 - c)
    kept.append(pltpu.make_async_copy(normed, normed_full.at[t], local.at[2]))
    kept[-1].start()

    def rows_on(k, half):
        mail.arrive(rows_y[k], normed_full.at[yonder, half], tp=yonder)
        mail.start(
            rows_core[2 + k], normed_full.at[yonder, half], normed_full.at[yonder, half], tp=beside
        )

    for hop in range(1, count):
        heads.arrive(hop)
        if hop + 1 < count:
            heads.send(hop + 1)
        heads_across.send(hop)
        if hop == 1:
            rows_on(0, c)
            rows_on(1, 1 - c)
            outs.send(1)
        if hop == min(2, count - 1):
            for k, piece in enumerate(wide):
                mail.start(
                    wide_up[k], piece, low.at[k], when=z < count - 1, fsdp=jnp.minimum(z + 1, count - 1)
                )
                mail.start(wide_down[k], piece, high.at[k], when=z > 0, fsdp=jnp.maximum(z - 1, 0))
    for k, piece in enumerate(wide_away):
        mail.start(wide_x[k], piece, wide_landed.at[k], cp=1 - c)
    for hop in range(1, count):
        outs.arrive(hop)
        if hop + 1 < count:
            outs.send(hop + 1)
    for hop in range(count):
        heads_across.arrive(hop)
    mail.arrive(rows_core[0], normed_full.at[beside, c], tp=beside)
    mail.arrive(rows_core[1], normed_full.at[beside, 1 - c], tp=beside)
    far = (beside + 2) % 4
    mail.arrive(rows_core[2], normed_full.at[far, c], tp=beside)
    mail.arrive(rows_core[3], normed_full.at[far, 1 - c], tp=beside)
    for k in range(len(wide)):
        mail.arrive(wide_x[k], wide_landed.at[k], cp=1 - c)
    for pair, place in ((low_pair, 1), (high_pair, 3)):
        kept.append(pltpu.make_async_copy(wide_landed, pair.at[1], local.at[place]))
        kept[-1].start()
    for k in range(len(wide)):
        mail.arrive(wide_up[k], low.at[k], when=z > 0, fsdp=z)
        mail.arrive(wide_down[k], high.at[k], when=z < count - 1, fsdp=z)
    for copy in kept:
        copy.wait()
    stage_qkv.end()
    stage_out.end()
    mail.finish()


def first_gather(count, tokens, tokens_away, gain, qkv, turned_out, wide, wide_away):
    slots = 6 * count + 16
    anywhere = pl.BlockSpec(memory_space=pl.ANY)
    vmem = pl.BlockSpec(memory_space=pltpu.VMEM)
    pair = (2,) + tokens.shape
    wide_shape = (3,) + wide[0].shape
    return pl.pallas_call(
        functools.partial(first_gather_kernel, count),
        out_shape=(
            jax.ShapeDtypeStruct(pair, BF),
            jax.ShapeDtypeStruct((4,) + pair, BF),
            jax.ShapeDtypeStruct((count, 2) + qkv.shape, BF),
            jax.ShapeDtypeStruct((count,) + turned_out.shape, BF),
            jax.ShapeDtypeStruct((2,) + wide_shape, BF),
            jax.ShapeDtypeStruct((2,) + wide_shape, BF),
        ),
        in_specs=[vmem, anywhere, vmem] + [anywhere] * 8,
        out_specs=(vmem,) + (anywhere,) * 5,
        scratch_shapes=[
            pltpu.VMEM(tokens.shape, BF),
            pltpu.VMEM(pair, BF),
            pltpu.VMEM(wide_shape, BF),
            pltpu.VMEM((1,) + qkv.shape, BF),
            pltpu.VMEM((1,) + turned_out.shape, BF),
            pltpu.SemaphoreType.DMA((slots,)),
            pltpu.SemaphoreType.DMA((slots,)),
            pltpu.SemaphoreType.DMA((4,)),
            pltpu.SemaphoreType.DMA((2, 1)),
            pltpu.SemaphoreType.DMA((2, 1)),
        ],
        cost_estimate=COST,
        compiler_params=pltpu.CompilerParams(
            collective_id=1, has_side_effects=True, vmem_limit_bytes=32 << 20
        ),
    )(tokens, tokens_away, gain, qkv, turned_out, *wide, *wide_away)


def in_pieces(rows, body, size=16):
    if rows % size:
        body(pl.ds(0, rows))
        return
    lax.fori_loop(0, rows // size, lambda i, carry: (body(pl.ds(i * size, size)), carry)[1], 0)


class Spread:
    def __init__(self, mail, own, at):
        self.mail, self.own, self.at = mail, own, at
        self.c, self.t = lax.axis_index("cp"), lax.axis_index("tp")
        self.beside, self.yonder = self.t + 1 - 2 * (self.t % 2), (self.t + 2) % 4
        self.x = [mail.slot() for _ in range(3)]
        self.y = [mail.slot() for _ in range(3)]
        self.core = {}

    def to_core(self, c_is_own, t_is_own, piece):
        slot = self.core[c_is_own, t_is_own, piece] = self.mail.slot()
        c = self.c if c_is_own else 1 - self.c
        t = self.t if t_is_own else self.yonder
        source = self.own(piece) if c_is_own and t_is_own else self.at(c, t, piece)
        self.mail.start(slot, source, self.at(c, t, piece), tp=self.beside)

    def begin(self, piece):
        c, t = self.c, self.t
        if piece == 0:
            self.mail.start(self.x[0], self.own(0), self.at(c, t, 0), cp=1 - c)
        else:
            self.mail.start(self.y[0], self.own(1), self.at(c, t, 1), tp=self.yonder)
            self.mail.start(self.x[1], self.own(1), self.at(c, t, 1), cp=1 - c)
            self.mail.start(self.y[1], self.own(0), self.at(c, t, 0), tp=self.yonder)
        self.to_core(True, True, piece)

    def turn(self):
        c, t, mail, yonder = self.c, self.t, self.mail, self.yonder
        mail.arrive(self.x[0], self.at(1 - c, t, 0), cp=1 - c)
        mail.start(self.y[2], self.at(1 - c, t, 0), self.at(1 - c, t, 0), tp=yonder)
        self.to_core(False, True, 0)
        mail.arrive(self.y[0], self.at(c, yonder, 1), tp=yonder)
        mail.start(self.x[2], self.at(c, yonder, 1), self.at(c, yonder, 1), cp=1 - c)
        self.to_core(True, False, 1)

    def end(self):
        c, t, mail, yonder = self.c, self.t, self.mail, self.yonder
        mail.arrive(self.x[1], self.at(1 - c, t, 1), cp=1 - c)
        self.to_core(False, True, 1)
        mail.arrive(self.y[1], self.at(c, yonder, 0), tp=yonder)
        self.to_core(True, False, 0)
        mail.arrive(self.x[2], self.at(1 - c, yonder, 1), cp=1 - c)
        self.to_core(False, False, 1)
        mail.arrive(self.y[2], self.at(1 - c, yonder, 0), tp=yonder)
        self.to_core(False, False, 0)
        far = (self.beside + 2) % 4
        for (c_is_own, t_is_own, piece), slot in self.core.items():
            place = self.at(
                c if c_is_own else 1 - c, self.beside if t_is_own else far, piece
            )
            mail.arrive(slot, place, tp=self.beside)


def second_gather_kernel(
    count, part, tokens, gain, wide_0, wide_1, wide_2,
    first_low, first_high, second_low, second_high, *refs
):
    hops_mine, hops_other = min(2, count - 1), 1
    wide = (wide_0, wide_1, wide_2)
    wide_other = [first_low.at[1, which] for which in range(3)]
    ready_mine = [first_low.at[0], first_high.at[0], second_low.at[0], second_high.at[0]]
    ready_mine = ready_mine[: 2 * hops_mine]
    ready_other = [second_low.at[1], second_high.at[1]]
    middle, middle_home, normed_full, gate_full, up_full, down_full = refs[:6]
    own, from_core, to_yonder, from_yonder, normed, stage, send, recv, local, local_line = refs[6:]
    c, t = lax.axis_index("cp"), lax.axis_index("tp")
    rows = tokens.shape[0]
    half = rows // 2
    mail = Mail(send, recv)
    greet(count)

    mine, other = [], []
    for which, full in enumerate((gate_full, up_full, down_full)):
        for lines, side, piece, ready in (
            (mine, c, wide, ready_mine), (other, 1 - c, wide_other, ready_other),
        ):
            arrived = [
                (ready[2 * hop].at[which], ready[2 * hop + 1].at[which])
                for hop in range(len(ready) // 2)
            ]
            lines.append(
                Line(
                    mail, count, piece[which],
                    lambda j, full=full, side=side: full.at[j, side], arrived,
                )
            )
    summed = TensorSum(mail, part, own, from_core, to_yonder, from_yonder, local)
    spread = Spread(
        mail, lambda piece: normed.at[piece], lambda c, t, piece: normed_full.at[piece, t, c]
    )

    summed.begin()
    placing = Stage([piece for line in mine + other for piece in line.keep()], stage, local_line)
    placing.begin()

    def send_hop(lines, hop):
        for line in lines:
            if hop < count:
                line.send(hop)

    def arrive_hop(lines, hop):
        for line in lines:
            if hop < count:
                line.arrive(hop)

    send_hop(other, hops_other + 1)
    send_hop(mine, hops_mine + 1)
    summed.turn()
    placing.turn()
    for piece in range(2):
        summed.arrive(piece)

        def norm(place, piece=piece):
            row = pl.ds(place.start + piece * half, place.size)
            values = tokens[row, :].astype(F32) + BRANCH * summed.rows(row)
            middle[row, :] = values
            normed[piece, place, :] = (normalize(values) * gain[...]).astype(BF)

        in_pieces(half, norm)
        spread.begin(piece)
    keep_normed = pltpu.make_async_copy(normed, normed_full.at[:, t, c], local.at[0])
    keep_normed.start()
    home = mail.slot()
    stay, go = pl.ds(c * half, half), pl.ds((1 - c) * half, half)
    keep_home = pltpu.make_async_copy(middle.at[stay], middle_home.at[c], local.at[1])
    keep_home.start()
    spread.turn()
    mail.start(home, middle.at[go], middle_home.at[c], cp=1 - c)
    for step in range(1, count):
        hop = hops_other + step
        if hop < count:
            for line_other, line_mine in zip(other, mine):
                line_other.arrive(hop)
                if hop + 1 < count:
                    line_other.send(hop + 1)
                if hops_mine + step < count:
                    line_mine.arrive(hops_mine + step)
                    if hops_mine + step + 1 < count:
                        line_mine.send(hops_mine + step + 1)
        if step == 1:
            spread.end()
    if count == 1:
        spread.end()
    mail.arrive(home, middle_home.at[1 - c], cp=1 - c)
    keep_home.wait()
    keep_normed.wait()
    placing.end()
    mail.finish()


def second_gather(count, part, tokens, gain, wide, first_low, first_high, second_low, second_high):
    slots = 12 * count + 24
    rows, width = tokens.shape
    anywhere = pl.BlockSpec(memory_space=pl.ANY)
    vmem = pl.BlockSpec(memory_space=pltpu.VMEM)
    full = jax.ShapeDtypeStruct((count, 2) + wide[0].shape, BF)
    return pl.pallas_call(
        functools.partial(second_gather_kernel, count),
        out_shape=(
            jax.ShapeDtypeStruct((rows, width), F32),
            jax.ShapeDtypeStruct((2, rows // 2, width), F32),
            jax.ShapeDtypeStruct((2, 4, 2, rows // 2, width), BF),
            full,
            full,
            full,
        ),
        in_specs=[anywhere, vmem, vmem] + [anywhere] * 7,
        out_specs=(vmem,) + (anywhere,) * 5,
        scratch_shapes=[
            pltpu.VMEM((2, rows, width), BF),
            pltpu.VMEM((2, rows, width), BF),
            pltpu.VMEM((rows, width), BF),
            pltpu.VMEM((rows, width), BF),
            pltpu.VMEM((2, rows // 2, width), BF),
            pltpu.VMEM((24,) + wide[0].shape, BF),
            pltpu.SemaphoreType.DMA((slots,)),
            pltpu.SemaphoreType.DMA((slots,)),
            pltpu.SemaphoreType.DMA((2,)),
            pltpu.SemaphoreType.DMA((2, 24)),
        ],
        cost_estimate=COST,
        compiler_params=pltpu.CompilerParams(
            collective_id=2, has_side_effects=True, vmem_limit_bytes=40 << 20
        ),
    )(part, tokens, gain, *wide, first_low, first_high, second_low, second_high)


class TensorSum:
    def __init__(self, mail, part, own, from_core, to_yonder, from_yonder, local):
        self.mail, self.part, self.own, self.from_core = mail, part, own, from_core
        self.to_yonder, self.from_yonder, self.local = to_yonder, from_yonder, local
        self.t = t = lax.axis_index("tp")
        self.beside, self.yonder = t + 1 - 2 * (t % 2), (t + 2) % 4
        self.core = [mail.slot() for _ in range(2)]
        self.across = [mail.slot() for _ in range(2)]
        self.half = from_yonder.shape[0] // 2

    def begin(self):
        part, far = self.part, (self.beside + 2) % 4
        self.mail.start(self.core[1], part.at[far], self.from_core.at[1], tp=self.beside)
        self.mail.start(self.core[0], part.at[self.beside], self.from_core.at[0], tp=self.beside)
        self.kept = [
            pltpu.make_async_copy(part.at[self.yonder], self.own.at[1], self.local.at[0]),
            pltpu.make_async_copy(part.at[self.t], self.own.at[0], self.local.at[1]),
        ]
        for copy in self.kept:
            copy.start()

    def turn(self):
        own, from_core = self.own, self.from_core
        self.kept[0].wait()
        self.mail.arrive(self.core[1], from_core.at[1], tp=self.beside)
        for piece in range(2):

            def add(place, piece=piece):
                place = pl.ds(place.start + piece * self.half, place.size)
                self.to_yonder[place, :] = (
                    own[1, place, :].astype(F32) + from_core[1, place, :].astype(F32)
                ).astype(BF)

            in_pieces(self.half, add)
            block = pl.ds(piece * self.half, self.half)
            self.mail.start(
                self.across[piece], self.to_yonder.at[block], self.from_yonder.at[block],
                tp=self.yonder,
            )
        self.kept[1].wait()
        self.mail.arrive(self.core[0], from_core.at[0], tp=self.beside)

    def arrive(self, piece):
        block = pl.ds(piece * self.half, self.half)
        self.mail.arrive(self.across[piece], self.from_yonder.at[block], tp=self.yonder)

    def rows(self, row):
        return (
            self.own[0, row, :].astype(F32)
            + self.from_core[0, row, :].astype(F32)
            + self.from_yonder[row, :].astype(F32)
        )


class Drain:
    def __init__(self, mail, count, fill, total, landed):
        self.mail, self.count, self.fill, self.total, self.landed = mail, count, fill, total, landed
        self.z = lax.axis_index("fsdp")
        self.slots = [[mail.slot() for _ in range(count)] for _ in range(2)]

    def sends(self, hop, up):
        z, count = self.z, self.count
        return (z <= hop - 1) & (z < count - 1) if up else (z >= count - hop) & (z > 0)

    def gets(self, hop, up):
        z, count = self.z, self.count
        return (z >= 1) & (z <= hop) if up else (z <= count - 2) & (z >= count - 1 - hop)

    def block(self, hop, up):
        z, count = self.z, self.count
        return jnp.minimum(z + count - hop, count - 1) if up else jnp.maximum(z - count + hop, 0)

    def arrive(self, hop):
        for side, up in enumerate((True, False)):
            self.mail.arrive(
                self.slots[side][hop], self.landed(side, hop), when=self.gets(hop, up), fsdp=self.z
            )

    def gather(self, hop):
        for side, up in enumerate((True, False)):
            target = self.total(side, hop)

            def work(side=side, up=up, target=target):
                self.fill(hop, up, self.block(hop, up), target)
                if hop > 1:

                    def add():
                        landed = self.landed(side, hop - 1)

                        def one(place):
                            target[place, :] = (
                                target[place, :].astype(F32) + landed[place, :].astype(F32)
                            ).astype(BF)

                        in_pieces(target.shape[0], one)

                    pl.when(self.gets(hop - 1, up))(add)

            pl.when(self.sends(hop, up))(work)

    def send(self, hop):
        z, count = self.z, self.count
        for side, up in enumerate((True, False)):
            to = jnp.minimum(z + 1, count - 1) if up else jnp.maximum(z - 1, 0)
            self.mail.start(
                self.slots[side][hop], self.total(side, hop), self.landed(side, hop),
                when=self.sends(hop, up), fsdp=to,
            )


def norm_back(values, gain, upstream):
    scale = lax.rsqrt(jnp.mean(values * values, axis=-1, keepdims=True) + EPSILON)
    norm = values * scale
    scaled = upstream * gain
    mean = jnp.mean(scaled * norm, axis=-1, keepdims=True)
    return scale * (scaled - norm * mean), upstream * norm


def first_sum_kernel(
    count, part, gate_grad, up_grad, hidden, middle_from, cotangent_from, down_from, gain,
    grad_middle, attention_full, gain_rows, leaving_up, leaving_down, feedforward,
    own, from_core, first, second, grad_attention, totals, landed, hidden_rows, product, middle, cotangent, down,
    send, recv, local, hidden_local, loads_local,
):
    z, c, t = lax.axis_index("fsdp"), lax.axis_index("cp"), lax.axis_index("tp")
    beside, yonder = t + 1 - 2 * (t % 2), (t + 2) % 4
    far = (beside + 2) % 4
    half = middle.shape[0] // 2
    width = middle.shape[1]
    loads = [
        pltpu.make_async_copy(source, target, loads_local.at[k])
        for k, (source, target) in enumerate(
            ((down_from, down), (middle_from, middle), (cotangent_from, cotangent))
        )
    ]
    mail = Mail(send, recv)
    greet(count)
    last = count - 1

    def fill_from(which):
        def fill(hop, up, j, target):
            copy = pltpu.make_async_copy((gate_grad, up_grad)[which].at[j], target, local.at[4])
            copy.start()
            copy.wait()

        return fill

    drains = [
        Drain(
            mail, count, fill_from(which),
            lambda side, hop, which=which: (
                (leaving_up, leaving_down)[side].at[which] if hop == last else totals.at[side, hop - 1, which]
            ),
            lambda side, hop, which=which: landed.at[side, hop - 1, which],
        )
        for which in range(2)
    ]

    core = {}
    mine = {}
    order = ((0, 0), (0, 1), (1, 0), (1, 1))
    for index, (c_own, t_own) in enumerate(order):
        block_c = c if c_own else 1 - c
        core[c_own, t_own] = mail.slot()
        mail.start(
            core[c_own, t_own], part.at[:, beside if t_own else far, block_c],
            from_core.at[c_own, t_own], tp=beside,
        )
        mine[c_own, t_own] = pltpu.make_async_copy(
            part.at[:, t if t_own else yonder, block_c], own.at[c_own, t_own], local.at[index]
        )
        mine[c_own, t_own].start()
    if last > 1:
        for drain in drains:
            drain.gather(1)
            drain.send(1)

    block_rows = product.shape[1]
    blocks = hidden.shape[0] // block_rows

    def hidden_copy(block):
        return pltpu.make_async_copy(
            hidden.at[pl.ds(block * block_rows, block_rows)], hidden_rows.at[block % 2],
            hidden_local.at[0, block % 2],
        )

    def product_copy(block):
        return pltpu.make_async_copy(
            product.at[block % 2], feedforward.at[pl.ds(block * block_rows, block_rows)],
            hidden_local.at[1, block % 2],
        )

    def product_block(block):
        hidden_copy(block).wait()
        if block + 1 < blocks:
            hidden_copy(block + 1).start()
        if block > 1:
            product_copy(block - 2).wait()

        def one(k, carry):
            columns = pl.ds(pl.multiple_of(k * 2 * TILE, 2 * TILE), 2 * TILE)
            value = lax.dot_general(
                hidden_rows[block % 2], down[columns, :], (((1,), (1,)), ((), ())),
                preferred_element_type=F32,
            )
            product[block % 2, :, columns] = value.astype(BF)
            return carry

        lax.fori_loop(0, width // (2 * TILE), one, 0)
        product_copy(block).start()

    hidden_copy(0).start()
    for copy in loads:
        copy.start()
    loads[0].wait()
    product_block(0)

    quarter = half // 2
    quarters = [(piece, pl.ds(side * quarter, quarter)) for piece in range(2) for side in range(2)]
    x_first = [[mail.slot() for _ in range(2)] for _ in quarters]
    y_second = [mail.slot() for _ in quarters]
    ring_y = [mail.slot() for _ in quarters]
    ring_core = [mail.slot() for _ in quarters]
    ring_far = [mail.slot() for _ in quarters]

    def core_add(c_own, t_own, piece, rows):
        def one(place):
            row = pl.ds(rows.start + place.start, place.size)
            own[c_own, t_own, piece, row, :] = (
                own[c_own, t_own, piece, row, :].astype(F32)
                + from_core[c_own, t_own, piece, row, :].astype(F32)
            ).astype(BF)

        in_pieces(quarter, one)

    for t_own in (0, 1):
        mine[0, t_own].wait()
        mail.arrive(core[0, t_own], from_core.at[0, t_own], tp=beside)
    for k, (piece, rows) in enumerate(quarters):
        for t_own in (0, 1):
            core_add(0, t_own, piece, rows)
            mail.start(
                x_first[k][t_own], own.at[0, t_own, piece, rows], first.at[k, t_own], cp=1 - c
            )
    for t_own in (0, 1):
        mine[1, t_own].wait()
        mail.arrive(core[1, t_own], from_core.at[1, t_own], tp=beside)

    def add_first(k, t_own):
        piece, rows = quarters[k]

        def one(place):
            row = pl.ds(rows.start + place.start, place.size)
            own[1, t_own, piece, row, :] = (
                own[1, t_own, piece, row, :].astype(F32)
                + from_core[1, t_own, piece, row, :].astype(F32)
                + first[k, t_own, place, :].astype(F32)
            ).astype(BF)

        in_pieces(quarter, one)

    gain_rows[...] = jnp.zeros_like(gain_rows)
    loads[1].wait()
    loads[2].wait()

    def finish(k):
        piece, rows = quarters[k]
        mail.arrive(y_second[k], second.at[k], tp=yonder)

        def back(place):
            local_row = pl.ds(rows.start + place.start, place.size)
            row = pl.ds(piece * half + rows.start + place.start, place.size)
            summed = own[1, 1, piece, local_row, :].astype(F32) + second[k, place, :].astype(F32)
            grad, products = norm_back(middle[row, :], gain[...], summed)
            grad = cotangent[row, :].astype(F32) + grad
            grad_middle[row, :] = grad
            grad_attention[piece, local_row, :] = (BRANCH * grad).astype(BF)
            gain_rows[...] += jnp.sum(products, axis=0, keepdims=True)

        in_pieces(quarter, back)
        source = grad_attention.at[piece, rows]
        mail.start(ring_y[k], source, attention_full.at[t, piece, rows], tp=yonder)
        mail.start(ring_core[k], source, attention_full.at[t, piece, rows], tp=beside)

    def z_hop(hop):
        for drain in drains:
            drain.arrive(hop - 1)
            drain.gather(hop)
            drain.send(hop)

    for k, (piece, rows) in enumerate(quarters):
        mail.arrive(x_first[k][0], first.at[k, 0], cp=1 - c)
        add_first(k, 0)
        mail.start(y_second[k], own.at[1, 0, piece, rows], second.at[k], tp=yonder)
        mail.arrive(x_first[k][1], first.at[k, 1], cp=1 - c)
        add_first(k, 1)
        if k > 0:
            finish(k - 1)
        if k == 2 and last > 2:
            z_hop(2)
        product_block(k + 1)
    finish(len(quarters) - 1)
    for block in range(len(quarters) + 1, blocks):
        product_block(block)
    keep = pltpu.make_async_copy(grad_attention, attention_full.at[t], local.at[0])
    keep.start()
    for hop in range(3, last):
        z_hop(hop)
    for k, (piece, rows) in enumerate(quarters):
        arrived = attention_full.at[yonder, piece, rows]
        mail.arrive(ring_y[k], arrived, tp=yonder)
        mail.start(ring_far[k], arrived, arrived, tp=beside)
    for k, (piece, rows) in enumerate(quarters):
        mail.arrive(ring_core[k], attention_full.at[beside, piece, rows], tp=beside)
        mail.arrive(ring_far[k], attention_full.at[far, piece, rows], tp=beside)
    for drain in drains:
        if last > 1:
            drain.arrive(last - 1)
        if last > 0:
            drain.gather(last)
    keep.wait()
    for block in range(blocks - 2, blocks):
        product_copy(block).wait()
    mail.finish()


def first_sum(count, part, gate_grad, up_grad, hidden, middle, cotangent, gain, down):
    slots = 6 * count + 32
    rows, width = middle.shape
    block = gate_grad.shape[1:]
    anywhere = pl.BlockSpec(memory_space=pl.ANY)
    vmem = pl.BlockSpec(memory_space=pltpu.VMEM)
    hops = max(count - 2, 1)
    return pl.pallas_call(
        functools.partial(first_sum_kernel, count),
        out_shape=(
            jax.ShapeDtypeStruct((rows, width), F32),
            jax.ShapeDtypeStruct((4, 2, rows // 2, width), BF),
            jax.ShapeDtypeStruct((1, width), F32),
            jax.ShapeDtypeStruct((2,) + block, BF),
            jax.ShapeDtypeStruct((2,) + block, BF),
            jax.ShapeDtypeStruct((hidden.shape[0], width), BF),
        ),
        in_specs=[anywhere] * 7 + [vmem],
        out_specs=(vmem, anywhere, vmem, vmem, vmem, anywhere),
        scratch_shapes=[
            pltpu.VMEM((2, 2, 2, rows // 2, width), BF),
            pltpu.VMEM((2, 2, 2, rows // 2, width), BF),
            pltpu.VMEM((4, 2, rows // 4, width), BF),
            pltpu.VMEM((4, rows // 4, width), BF),
            pltpu.VMEM((2, rows // 2, width), BF),
            pltpu.VMEM((2, hops, 2) + block, BF),
            pltpu.VMEM((2, hops, 2) + block, BF),
            pltpu.VMEM((2, hidden.shape[0] // 8, hidden.shape[1]), BF),
            pltpu.VMEM((2, hidden.shape[0] // 8, width), BF),
            pltpu.VMEM((rows, width), F32),
            pltpu.VMEM((rows, width), BF),
            pltpu.VMEM(down.shape, BF),
            pltpu.SemaphoreType.DMA((slots,)),
            pltpu.SemaphoreType.DMA((slots,)),
            pltpu.SemaphoreType.DMA((5,)),
            pltpu.SemaphoreType.DMA((2, 2)),
            pltpu.SemaphoreType.DMA((3,)),
        ],
        cost_estimate=COST,
        compiler_params=pltpu.CompilerParams(
            collective_id=3, has_side_effects=True, vmem_limit_bytes=60 << 20
        ),
    )(part, gate_grad, up_grad, hidden, middle, cotangent, down, gain)


AHEAD = 6


def last_sum_kernel(
    count, projected_from, qkv_full, qkv_grad, out_grad, tokens_from, middle_from, gain, gain_rows,
    qkv_total, out_total, grad_tokens, gain_sums,
    own, from_core, to_yonder, from_yonder, pieces,
    from_x, heads_sum, heads_landed, outs_sum, outs_landed, final_out, gains, gain_line,
    part, weights, give_sum, give_landed, give_own, give_total, grad_projected, tokens, grad_middle,
    send, recv, local, weights_local, loads_local,
):
    z, c, t = lax.axis_index("fsdp"), lax.axis_index("cp"), lax.axis_index("tp")
    beside, yonder = t + 1 - 2 * (t % 2), (t + 2) % 4
    half = tokens.shape[0] // 2
    last = count - 1
    mail = Mail(send, recv)
    greet(count)

    summed = TensorSum(mail, part, own, from_core, to_yonder, from_yonder, local)

    columns = qkv_total.shape[1]
    behind = columns * 5 // 6 // TILE * TILE
    split = -(-behind // (2 * TILE)) * TILE
    parts = [pl.ds(0, split), pl.ds(split, behind - split)]
    late = pl.ds(behind, columns - behind)
    cross = [[[mail.slot() for _ in range(count)] for _ in range(2)] for _ in parts]
    cross_own = [mail.slot() for _ in parts]

    def head_drain(lanes):
        def fill(hop, up, j, target):
            side = 0 if up else 1
            copy = pltpu.make_async_copy(qkv_grad.at[j, c, :, lanes], target, local.at[2])
            copy.start()
            copy.wait()
            arrived = from_x.at[side, hop - 1, :, lanes]

            def one(place):
                target[place, :] = (
                    target[place, :].astype(F32) + arrived[place, :].astype(F32)
                ).astype(BF)

            in_pieces(target.shape[0], one)

        return Drain(
            mail, count, fill,
            lambda side, hop: heads_sum.at[side, hop - 1, :, lanes],
            lambda side, hop: heads_landed.at[side, hop - 1, :, lanes],
        )

    heads = [head_drain(lanes) for lanes in parts]

    def late_fill(side_c):
        def fill(hop, up, j, target):
            copy = pltpu.make_async_copy(qkv_grad.at[j, side_c, :, late], target, local.at[2])
            copy.start()
            copy.wait()

        return fill

    stay = Drain(
        mail, count, late_fill(c),
        lambda side, hop: heads_sum.at[side, hop - 1, :, late],
        lambda side, hop: heads_landed.at[side, hop - 1, :, late],
    )
    give = Drain(
        mail, count, late_fill(1 - c),
        lambda side, hop: give_sum.at[side, hop - 1],
        lambda side, hop: give_landed.at[side, hop - 1],
    )
    give_slot = mail.slot()

    def fill_outs(hop, up, j, target):
        copy = pltpu.make_async_copy(out_grad.at[j], target, local.at[3])
        copy.start()
        copy.wait()

    outs = Drain(
        mail, count, fill_outs,
        lambda side, hop: outs_sum.at[side, hop - 1],
        lambda side, hop: outs_landed.at[side, hop - 1],
    )

    steps = [(hop, k) for hop in range(1, count + 1) for k in range(2)]

    def cross_send(step):
        if step >= len(steps):
            return
        hop, k = steps[step]
        lanes = parts[k]
        if hop == count:
            mail.start(
                cross_own[k], qkv_grad.at[z, 1 - c, :, lanes], from_x.at[0, last, :, lanes], cp=1 - c
            )
            return
        for side, up in enumerate((True, False)):
            mail.start(
                cross[k][side][hop], qkv_grad.at[heads[k].block(hop, up), 1 - c, :, lanes],
                from_x.at[side, hop - 1, :, lanes], when=heads[k].sends(hop, up), cp=1 - c,
            )

    def cross_arrive(hop, k):
        for side, up in enumerate((True, False)):
            mail.arrive(
                cross[k][side][hop], from_x.at[side, hop - 1, :, parts[k]],
                when=heads[k].sends(hop, up), cp=1 - c,
            )

    for step in range(AHEAD):
        cross_send(step)
    early_chains = (outs, give, stay)
    if count > 1:
        for drain in early_chains:
            drain.gather(1)
            drain.send(1)

    wide_block = weights.shape[1]
    blocks = qkv_full.shape[0] // wide_block

    def weights_copy(block, slot):
        return pltpu.make_async_copy(
            qkv_full.at[pl.ds(block * wide_block, wide_block)], weights.at[slot],
            weights_local.at[slot],
        )

    def product(block, carry):
        slot = lax.rem(block, 2)
        weights_copy(block, slot).wait()
        pl.when(block + 1 < blocks)(lambda: weights_copy(block + 1, 1 - slot).start())
        columns = pl.ds(pl.multiple_of(block * wide_block, wide_block), wide_block)
        value = lax.dot_general(
            grad_projected[...], weights[slot], (((1,), (1,)), ((), ())),
            preferred_element_type=F32,
        )
        part[:, :, columns] = value.astype(BF).reshape(part.shape[:2] + (wide_block,))
        return carry

    loads = [
        pltpu.make_async_copy(source, target, loads_local.at[k])
        for k, (source, target) in enumerate(
            (
                (projected_from, grad_projected),
                (tokens_from, tokens),
                (middle_from, grad_middle),
            )
        )
    ]
    weights_copy(0, 0).start()
    for copy in loads:
        copy.start()
    loads[0].wait()
    thirds = [blocks * k // 3 for k in range(4)]

    keep = pltpu.make_async_copy(pieces.at[c], grad_tokens.at[c], local.at[0])
    home = mail.slot()
    gain_x, gain_y, gain_core = mail.slot(), mail.slot(), mail.slot()
    line = Line(mail, count, gain_line.at[z], lambda j: gain_line.at[j])

    def finish_rows():
        loads[1].wait()
        loads[2].wait()
        gains[0, 0:1, :] = jnp.zeros_like(gain_rows)
        gains[0, 1:2, :] = gain_rows[...]
        for piece in range(2):
            summed.arrive(piece)

            def back(place, piece=piece):
                row = pl.ds(place.start + piece * half, place.size)
                grad, rows = norm_back(tokens[row, :].astype(F32), gain[...], summed.rows(row))
                pieces[piece, place, :] = (grad_middle[row, :] + grad).astype(BF)
                gains[0, 0:1, :] += jnp.sum(rows, axis=0, keepdims=True)

            in_pieces(half, back)
        mail.start(home, pieces.at[1 - c], grad_tokens.at[c], cp=1 - c)
        keep.start()
        mail.start(gain_core, gains.at[0], gains.at[1], tp=beside)

    def gain_step(k):
        if k == 0:
            mail.arrive(gain_core, gains.at[1], tp=beside)
            gains[2] = gains[0] + gains[1]
            mail.start(gain_y, gains.at[2], gains.at[3], tp=yonder)
        elif k == 1:
            mail.arrive(gain_y, gains.at[3], tp=yonder)
            gains[4] = gains[2] + gains[3]
            mail.start(gain_x, gains.at[4], gains.at[5], cp=1 - c)
        elif k == 2:
            mail.arrive(gain_x, gains.at[5], cp=1 - c)
            gain_line[z] = gains[4] + gains[5]
            if count > 1:
                line.send(1)
        else:
            hop = k - 2
            line.arrive(hop)
            if hop + 1 < count:
                line.send(hop + 1)

    def outs_hop(hop):
        for drain in early_chains:
            drain.arrive(hop - 1)
            drain.gather(hop)
            drain.send(hop)

    def give_away():
        copy = pltpu.make_async_copy(qkv_grad.at[z, 1 - c, :, late], give_own, local.at[3])
        copy.start()
        copy.wait()
        if count > 1:
            give.arrive(last)

        def one(place):
            total = give_own[place, :].astype(F32)
            for side, up in enumerate((True, False)):
                if count > 1:
                    landed = give.landed(side, last)[place, :].astype(F32)
                    total += jnp.where(give.gets(last, up), landed, 0.0)
            give_total[place, :] = total.astype(BF)

        in_pieces(give_own.shape[0], one)
        mail.start(give_slot, give_total, from_x.at[0, last, :, late], cp=1 - c)

    for step, (hop, k) in enumerate(steps[:-2]):
        if step < 3:
            lax.fori_loop(thirds[step], thirds[step + 1], product, 0)
        if count == 2 and step == 1:
            lax.fori_loop(thirds[2], thirds[3], product, 0)
        if step == 2 or count == 2 and step == 1:
            summed.begin()
        cross_arrive(hop, k)
        cross_send(step + AHEAD)
        if hop > 1:
            heads[k].arrive(hop - 1)
        heads[k].gather(hop)
        heads[k].send(hop)
        if k == 1 and hop + 1 < count:
            outs_hop(hop + 1)
        if step == 2 or count == 2 and step == 1:
            summed.turn()
        if step == 3 or count == 2 and step == 1:
            finish_rows()
        if step == 5 or step == 3 and count == 3:
            gain_step(0)
            gain_step(1)
    if count == 1:
        lax.fori_loop(thirds[0], thirds[3], product, 0)
        summed.begin()
        summed.turn()
        finish_rows()
    if count <= 2:
        gain_step(0)
        gain_step(1)
    gain_step(2)
    give_away()

    own_copy = pltpu.make_async_copy(qkv_grad.at[z, c], from_x.at[1, last], local.at[2])
    own_copy.start()
    out_copy = pltpu.make_async_copy(out_grad.at[z], final_out, local.at[3])
    out_copy.start()
    for k, lanes in enumerate(parts):
        mail.arrive(cross_own[k], from_x.at[0, last, :, lanes], cp=1 - c)
    mail.arrive(give_slot, from_x.at[0, last, :, late], cp=1 - c)
    own_copy.wait()
    out_copy.wait()

    def start_heads(place):
        qkv_total[place, :] = from_x[0, last, place, :].astype(F32) + from_x[
            1, last, place, :
        ].astype(F32)

    in_pieces(qkv_total.shape[0], start_heads)

    def start_outs(place):
        out_total[place, :] = final_out[place, :].astype(F32)

    in_pieces(out_total.shape[0], start_outs)
    for hop in range(1, count):
        gain_step(2 + hop)
    if count > 1:
        chains = [(outs, pl.ds(0, out_total.shape[1]), out_total)]
        chains += [(stay, late, qkv_total)]
        chains += [(heads[k], lanes, qkv_total) for k, lanes in enumerate(parts)]
        for drain, lanes, total in chains:
            drain.arrive(last)
            for side, up in enumerate((True, False)):

                def more(drain=drain, total=total, side=side, lanes=lanes):
                    landed = drain.landed(side, last)

                    def one(place):
                        total[place, lanes] += landed[place, :].astype(F32)

                    in_pieces(total.shape[0], one)

                pl.when(drain.gets(last, up))(more)
    gain_sums[...] = jnp.sum(gain_line[...], axis=0)
    mail.arrive(home, grad_tokens.at[1 - c], cp=1 - c)
    keep.wait()
    mail.finish()


def last_sum(count, grad_projected, qkv_full, qkv_grad, out_grad, tokens, grad_middle, gain, gain_rows):
    slots = 17 * count + 17
    rows, width = tokens.shape
    hops = max(count - 1, 1)
    block, out_block = qkv_grad.shape[2:], out_grad.shape[1:]
    columns = block[1]
    give_block = (block[0], columns - columns * 5 // 6 // TILE * TILE)
    anywhere = pl.BlockSpec(memory_space=pl.ANY)
    vmem = pl.BlockSpec(memory_space=pltpu.VMEM)
    return pl.pallas_call(
        functools.partial(last_sum_kernel, count),
        out_shape=(
            jax.ShapeDtypeStruct(block, F32),
            jax.ShapeDtypeStruct(out_block, F32),
            jax.ShapeDtypeStruct((2, rows // 2, width), BF),
            jax.ShapeDtypeStruct((2, width), F32),
        ),
        in_specs=[anywhere] * 6 + [vmem] * 2,
        out_specs=(vmem, vmem, anywhere, vmem),
        scratch_shapes=[
            pltpu.VMEM((2, rows, width), BF),
            pltpu.VMEM((2, rows, width), BF),
            pltpu.VMEM((rows, width), BF),
            pltpu.VMEM((rows, width), BF),
            pltpu.VMEM((2, rows // 2, width), BF),
            pltpu.VMEM((2, count) + block, BF),
            pltpu.VMEM((2, hops) + block, BF),
            pltpu.VMEM((2, hops) + block, BF),
            pltpu.VMEM((2, hops) + out_block, BF),
            pltpu.VMEM((2, hops) + out_block, BF),
            pltpu.VMEM(out_block, BF),
            pltpu.VMEM((6, 2, width), F32),
            pltpu.VMEM((count, 2, width), F32),
            pltpu.VMEM((4, rows, width), BF),
            pltpu.VMEM((2, 2 * TILE, qkv_full.shape[1]), BF),
            pltpu.VMEM((2, hops) + give_block, BF),
            pltpu.VMEM((2, hops) + give_block, BF),
            pltpu.VMEM(give_block, BF),
            pltpu.VMEM(give_block, BF),
            pltpu.VMEM(grad_projected.shape, BF),
            pltpu.VMEM(tokens.shape, BF),
            pltpu.VMEM(grad_middle.shape, F32),
            pltpu.SemaphoreType.DMA((slots,)),
            pltpu.SemaphoreType.DMA((slots,)),
            pltpu.SemaphoreType.DMA((4,)),
            pltpu.SemaphoreType.DMA((2,)),
            pltpu.SemaphoreType.DMA((3,)),
        ],
        cost_estimate=COST,
        compiler_params=pltpu.CompilerParams(
            collective_id=4, has_side_effects=True, vmem_limit_bytes=60 << 20
        ),
    )(grad_projected, qkv_full, qkv_grad, out_grad, tokens, grad_middle, gain, gain_rows)


def normalize(values):
    return values * lax.rsqrt(jnp.mean(values * values, axis=-1, keepdims=True) + EPSILON)


def silu_product(gate_pre, up_pre):
    return gate_pre / (1.0 + jnp.exp(-gate_pre)) * up_pre


def matmul(left, right):
    return jnp.dot(left, right, preferred_element_type=F32)


def rows_inner(left, right):
    return lax.dot_general(left, right, (((0,), (0,)), ((), ())), preferred_element_type=F32)


def cols_inner(left, right):
    return lax.dot_general(left, right, (((1,), (1,)), ((), ())), preferred_element_type=F32)


def row_major(value):
    return with_layout_constraint(value, Layout(major_to_minor=(0, 1)))


def after(value, *earlier):
    return lax.optimization_barrier((value, *earlier))[0]


def swap(value):
    return lax.ppermute(value, "cp", [(0, 1), (1, 0)])


def in_order(place, mine, other, axis):
    return jnp.where(
        place == 0,
        jnp.concatenate([mine, other], axis=axis),
        jnp.concatenate([other, mine], axis=axis),
    )


def on_device(
    tokens,
    seq_lengths,
    attention_gain,
    query_weight,
    key_weight,
    value_weight,
    out_weight,
    feedforward_gain,
    gate_weight,
    up_weight,
    down_weight,
    cotangent,
):
    c = lax.axis_index("cp")
    z = lax.axis_index("fsdp")
    sets = lax.axis_size("cp")
    count = lax.axis_size("fsdp")
    lanes = lax.axis_size("tp")
    slots, local, width = tokens.shape
    share = query_weight.shape[0]
    heads_width = query_weight.shape[1]
    head_count = heads_width // HD
    hidden_width = gate_weight.shape[1] // sets
    rows = sets * local
    seq = rows * lanes
    blocks = row_blocks(seq, sets, local)
    everyone = ("cp", "tp")

    def pick(value, which, axis=0):
        return lax.dynamic_index_in_dim(value, which, axis, keepdims=False)

    length = pick(seq_lengths, c)[None]
    gain_one = attention_gain.astype(F32)
    gain_two = feedforward_gain.astype(F32)

    qkv = jnp.concatenate([query_weight, key_weight, value_weight], axis=1)

    def halves(weight):
        return weight[:, :hidden_width], weight[:, hidden_width:]

    parts = [halves(weight) for weight in (gate_weight, up_weight, down_weight.T)]
    own_wide = [jnp.where(c == 0, low, high) for low, high in parts]
    wide_away = [jnp.where(c == 0, high, low) for low, high in parts]
    token_rows, normed_one, full_qkv, out_half, first_low, first_high = first_gather(
        count, pick(tokens, c), pick(tokens, 1 - c), gain_one[None], qkv, out_weight.T,
        own_wide, wide_away,
    )
    token_rows = token_rows.reshape(rows, width)
    normed_one = normed_one.reshape(seq, width)
    full_qkv = full_qkv.reshape(width, 3 * heads_width)

    out_half, cotangent = after((out_half, cotangent), full_qkv)
    cotangents = lax.all_gather(cotangent, everyone, axis=0).reshape(
        sets, lanes, slots, local, width
    )
    full_out = in_order(c, out_half[:, None], swap(out_half)[:, None], 1)
    full_out = full_out.reshape(width, heads_width)
    up_hop = [(i, i + 1) for i in range(count - 1)]
    down_hop = [(i, i - 1) for i in range(1, count)]
    second_low = lax.ppermute(first_low, "fsdp", up_hop)
    second_high = lax.ppermute(first_high, "fsdp", down_hop)
    cosine_table, sine_table = tables(seq)
    projected = matmul(normed_one, full_qkv)
    context, q_heads, k_heads, v_heads, level = attention(
        blocks, head_count, length, projected, cosine_table, sine_table
    )
    part = cols_inner(context, full_out).astype(BF)

    middle, middle_home, normed_two, full_gate, full_up, full_down = second_gather(
        count, part.reshape(lanes, rows, width), token_rows, gain_two[None], own_wide,
        first_low, first_high, second_low, second_high,
    )
    normed_two = normed_two.reshape(sets * seq, width)
    full_gate, full_up, full_down = (
        full.reshape(width, hidden_width) for full in (full_gate, full_up, full_down)
    )
    t = lax.axis_index("tp")
    cotangents_all = cotangents.reshape(sets * seq, width)
    cotangent_rows = pick(pick(cotangents, t, 1), c, 1).reshape(rows, width)
    gate_pre = matmul(normed_two, full_gate)
    up_pre = matmul(normed_two, full_up)
    hidden_exact, silu_back = jax.vjp(silu_product, gate_pre, up_pre)
    hidden = hidden_exact.astype(BF)

    def blocks_of(gradient):
        gradient = row_major(gradient.astype(BF))
        return gradient.reshape(count, width // count, hidden_width)

    down_blocks = blocks_of(BRANCH * rows_inner(cotangents_all, hidden))
    def leaving(hop, low, high):
        leaving_up = pick(down_blocks, jnp.minimum(z + count - hop, count - 1))
        leaving_down = pick(down_blocks, jnp.maximum(z - count + hop, 0))
        if hop > 1:
            leaving_up = (leaving_up.astype(F32) + low.astype(F32)).astype(BF)
            leaving_down = (leaving_down.astype(F32) + high.astype(F32)).astype(BF)
        return leaving_up, leaving_down

    def sent(hop, leaving_up, leaving_down):
        return (
            lax.ppermute(leaving_up, "fsdp", up_hop[:hop]),
            lax.ppermute(leaving_down, "fsdp", down_hop[count - 1 - hop :]),
        )

    gone = leaving(1, None, None)
    for hop in range(2, count - 1):
        gone = leaving(hop, *sent(hop - 1, *gone))
    grad_hidden = BRANCH * matmul(cotangents_all, full_down)
    grad_gate_exact, grad_up_exact = silu_back(grad_hidden)
    grad_gate_pre = grad_gate_exact.astype(BF)
    grad_up_pre = grad_up_exact.astype(BF)
    gate_part = lax.optimization_barrier(cols_inner(grad_gate_pre, full_gate).astype(BF))
    grad_normed_two = gate_part.astype(F32) + cols_inner(grad_up_pre, full_up)
    gate_blocks = blocks_of(rows_inner(normed_two, grad_gate_pre))
    up_blocks = blocks_of(rows_inner(normed_two, grad_up_pre))
    part = grad_normed_two.astype(BF).reshape(sets, lanes, slots, local, width)
    part, gone = lax.optimization_barrier((part, gone))
    grad_middle, grad_attention, gain_two_rows, pair_up, pair_down, feedforward = first_sum(
        count, part, gate_blocks, up_blocks, hidden, middle, cotangent_rows, gain_two[None],
        full_down,
    )
    grad_attention = grad_attention.reshape(seq, width)

    if count > 1:
        if count > 2:
            arrived = after(sent(count - 2, *gone), grad_attention)
            gone = leaving(count - 1, *arrived)
        leaving_up, leaving_down = after(gone, grad_attention)
        low = [lax.ppermute(pair_up, "fsdp", up_hop), lax.ppermute(leaving_up, "fsdp", up_hop)]
        high = [
            lax.ppermute(pair_down, "fsdp", down_hop), lax.ppermute(leaving_down, "fsdp", down_hop),
        ]
        low = [low[0][0], low[0][1], low[1]]
        high = [high[0][0], high[0][1], high[1]]

    def own_share(which, gradient):
        total = pick(gradient, z).astype(F32)
        if count > 1:
            total = total + low[which].astype(F32) + high[which].astype(F32)
        return total.reshape(sets, share, hidden_width)

    shares = [
        own_share(which, gradient)
        for which, gradient in enumerate((gate_blocks, up_blocks, down_blocks))
    ]
    others = swap(jnp.stack([pick(total, 1 - c).astype(BF) for total in shares]))
    grad_gate, grad_up, grad_down = (
        in_order(c, pick(total, c), others[which].astype(F32), 1)
        for which, total in enumerate(shares)
    )
    grad_down = grad_down.T

    out_pieces = row_major(rows_inner(grad_attention, context).astype(BF))
    out_pieces = out_pieces.reshape(count, sets, share, heads_width)
    out_other = swap(pick(out_pieces, 1 - c, 1))
    out_pieces = (pick(out_pieces, c, 1).astype(F32) + out_other.astype(F32)).astype(BF)
    grad_context = row_major(matmul(grad_attention, full_out).astype(BF))
    feedforward = lax.psum_scatter(feedforward, everyone, scatter_dimension=0, tiled=True)
    feedforward = feedforward.reshape(slots, local, width)
    output = (middle_home + BRANCH * feedforward.astype(F32)).astype(BF)
    grad_projected = attention_back(
        blocks, head_count, length, grad_context, q_heads, k_heads, v_heads, level,
        cosine_table, sine_table,
    )
    grad_projected = after(grad_projected, out_other, low[2], high[2])
    grad_qkv = row_major(rows_inner(normed_one, grad_projected).astype(BF))
    grad_qkv, grad_out, grad_tokens, gain_sums = last_sum(
        count, grad_projected, full_qkv, grad_qkv.reshape(count, sets, share, 3 * heads_width), out_pieces,
        token_rows, grad_middle, gain_one[None], gain_two_rows,
    )
    return (
        output,
        grad_tokens,
        grad_qkv[:, :heads_width],
        grad_qkv[:, heads_width : 2 * heads_width],
        grad_qkv[:, 2 * heads_width :],
        grad_out.T,
        gain_sums[0],
        grad_gate,
        grad_up,
        grad_down,
        gain_sums[1],
    )


def solution(mesh):
    in_specs = (
        P("fsdp", ("cp", "tp"), None),
        P("fsdp"),
        P(),
        P(("fsdp", "cp"), "tp"),
        P(("fsdp", "cp"), "tp"),
        P(("fsdp", "cp"), "tp"),
        P("tp", ("fsdp", "cp")),
        P(),
        P(("fsdp", "cp"), "tp"),
        P(("fsdp", "cp"), "tp"),
        P("tp", ("fsdp", "cp")),
        P("fsdp", ("cp", "tp"), None),
    )
    out_specs = (
        P("fsdp", ("cp", "tp"), None),
        P("fsdp", ("cp", "tp"), None),
        P(("fsdp", "cp"), "tp"),
        P(("fsdp", "cp"), "tp"),
        P(("fsdp", "cp"), "tp"),
        P("tp", ("fsdp", "cp")),
        P(),
        P(("fsdp", "cp"), "tp"),
        P(("fsdp", "cp"), "tp"),
        P("tp", ("fsdp", "cp")),
        P(),
    )
    return jax.shard_map(
        on_device, mesh=mesh, in_specs=in_specs, out_specs=out_specs, check_vma=False
    )
```

```python
import functools
import math

import jax
import jax.numpy as jnp
import numpy as np
from jax import lax
from jax.experimental import pallas as pl
from jax.experimental.layout import Layout, with_layout_constraint
from jax.experimental.pallas import tpu as pltpu
from jax.sharding import PartitionSpec as P

HD = 64
EPSILON = 1e-05
BRANCH = 1.4 / math.sqrt(40.0)
BF = jnp.bfloat16
F32 = jnp.float32
TILE = 128
QUERY_ROWS = 512


def turned(values, cosine, sine):
    lane = lax.broadcasted_iota(jnp.int32, values.shape, 1)
    partner = jnp.where(
        lane % HD < HD // 2,
        pltpu.roll(values, TILE - HD // 2, 1),
        pltpu.roll(values, HD // 2, 1),
    )
    return values * cosine + partner * sine


def row_blocks(seq, sets, local):
    lanes = seq // sets // local
    return [
        ((t * sets + h) * local, (h * lanes + t) * local)
        for t in range(lanes)
        for h in range(sets)
    ]


def key_mask(length, first, rows, columns):
    place = first + lax.broadcasted_iota(jnp.int32, (rows, columns), 0)
    return place < length


def scores_of(keys, queries, length, first_query):
    raw = lax.dot_general(keys, queries, (((1,), (1,)), ((), ())), preferred_element_type=F32)
    key_place = lax.broadcasted_iota(jnp.int32, raw.shape, 0)
    query_place = first_query + lax.broadcasted_iota(jnp.int32, raw.shape, 1)
    return jnp.where((key_place <= query_place) & (key_place < length), raw, -1e30)


def attention_kernel(
    blocks, length_ref, projected, cosine, sine, context, q_heads, k_heads, v_heads, level, kept
):
    heads, seq, _ = q_heads.shape
    local = seq // len(blocks)
    length = length_ref[0]
    for gathered, ordered in blocks:
        source, target = pl.ds(gathered, local), pl.ds(ordered, local)
        for tile in range(-(-3 * heads // 2)):
            width = min(TILE, 3 * heads * HD - tile * TILE)
            values = projected[source, tile * TILE : tile * TILE + width]
            if tile * 2 < 2 * heads:
                values = turned(values, cosine[target, :], sine[target, :])
            for which in range(width // HD):
                index = tile * 2 + which
                piece = values[:, which * HD : (which + 1) * HD]
                if index < heads:
                    q_heads[index, target, :] = (piece * (1.0 / math.sqrt(HD))).astype(BF)
                elif index < 2 * heads:
                    k_heads[index - heads, target, :] = piece.astype(BF)
                else:
                    v_heads[index - 2 * heads, target, :] = piece.astype(BF)

    def one_head(head, carry):
        for first in range(0, seq, QUERY_ROWS):
            most = first + QUERY_ROWS
            queries = q_heads[head, first:most, :]
            keys = k_heads[head, :most, :]
            values = v_heads[head, :most, :]
            scores = scores_of(keys, queries, length, first)
            top = jnp.max(scores, axis=0, keepdims=True)
            exponent = jnp.exp(scores - top)
            total = jnp.sum(exponent, axis=0, keepdims=True)
            probabilities = exponent.astype(BF)
            level[head, :, first:most] = top + jnp.log(total)
            mixed = lax.dot_general(
                values, probabilities, (((0,), (0,)), ((), ())), preferred_element_type=F32
            )
            kept[head, first:most, :] = (mixed * (1.0 / total)).T.astype(BF)
        return carry

    lax.fori_loop(0, heads, one_head, 0, unroll=True)
    for gathered, ordered in blocks:
        source, target = pl.ds(ordered, local), pl.ds(gathered, local)
        for head in range(0, heads, 2):
            parts = [kept[index, source, :] for index in range(head, min(head + 2, heads))]
            joined = parts[0] if len(parts) == 1 else jnp.concatenate(parts, axis=1)
            context[target, head * HD : head * HD + joined.shape[1]] = joined


def attention(blocks, heads, length, projected, cosine, sine):
    seq = projected.shape[0]
    per_head = jax.ShapeDtypeStruct((heads, seq, HD), BF)
    vmem = pl.BlockSpec(memory_space=pltpu.VMEM)
    return pl.pallas_call(
        functools.partial(attention_kernel, blocks),
        out_shape=(
            jax.ShapeDtypeStruct((seq, heads * HD), BF),
            per_head,
            per_head,
            per_head,
            jax.ShapeDtypeStruct((heads, 1, seq), F32),
        ),
        in_specs=[pl.BlockSpec(memory_space=pltpu.SMEM), vmem, vmem, vmem],
        out_specs=(vmem,) * 5,
        scratch_shapes=[pltpu.VMEM((heads, seq, HD), BF)],
        compiler_params=pltpu.CompilerParams(vmem_limit_bytes=48 << 20),
        cost_estimate=pl.CostEstimate(
            flops=4 * heads * seq * seq * HD, transcendentals=heads * seq * seq, bytes_accessed=20 << 20
        ),
    )(length, projected, cosine, sine)


def attention_back_kernel(
    blocks, length_ref, grad_context, q_heads, k_heads, v_heads, level, cosine, sine,
    grad_projected, g_heads, dq, dk, dv,
):
    heads, seq, _ = q_heads.shape
    local = seq // len(blocks)
    length = length_ref[0]
    for gathered, ordered in blocks:
        source, target = pl.ds(gathered, local), pl.ds(ordered, local)
        for head in range(heads):
            g_heads[head, target, :] = grad_context[source, head * HD : (head + 1) * HD]

    def one_head(head, carry):
        keys_turned = k_heads[head].T
        for first in reversed(range(0, seq, QUERY_ROWS)):
            most = first + QUERY_ROWS
            queries = q_heads[head, first:most, :]
            upstream = g_heads[head, first:most, :]
            keys = k_heads[head, :most, :]
            values = v_heads[head, :most, :]
            scores = scores_of(keys, queries, length, first)
            probabilities = jnp.exp(scores - level[head, :, first:most])
            grad_probabilities = lax.dot_general(
                values, upstream, (((1,), (1,)), ((), ())), preferred_element_type=F32
            )
            weighted = probabilities * grad_probabilities
            balance = jnp.sum(weighted, axis=0, keepdims=True)
            grad_scores = (weighted - probabilities * balance).astype(BF)
            grad_keys = jnp.dot(grad_scores, queries, preferred_element_type=F32)
            grad_values = jnp.dot(
                probabilities.astype(BF), upstream, preferred_element_type=F32
            )
            if most == seq:
                dk[head, :, :] = grad_keys
                dv[head, :, :] = grad_values
            else:
                dk[head, :most, :] += grad_keys
                dv[head, :most, :] += grad_values
            grad_queries = jnp.dot(
                keys_turned[:, :most], grad_scores, preferred_element_type=F32
            )
            dq[head, first:most, :] = grad_queries.T * (1.0 / math.sqrt(HD))
        return carry

    lax.fori_loop(0, heads, one_head, 0, unroll=True)
    sources = [dq] * heads + [dk] * heads + [dv] * heads
    for gathered, ordered in blocks:
        source, target = pl.ds(ordered, local), pl.ds(gathered, local)
        for tile in range(-(-3 * heads // 2)):
            indices = range(tile * 2, min(tile * 2 + 2, 3 * heads))
            parts = [sources[index][index % heads, source, :] for index in indices]
            joined = parts[0] if len(parts) == 1 else jnp.concatenate(parts, axis=1)
            if tile * 2 < 2 * heads:
                joined = turned(joined, cosine[source, :], -sine[source, :])
            grad_projected[target, tile * TILE : tile * TILE + joined.shape[1]] = joined.astype(BF)


def attention_back(blocks, heads, length, grad_context, q_heads, k_heads, v_heads, level, cosine, sine):
    seq = grad_context.shape[0]
    vmem = pl.BlockSpec(memory_space=pltpu.VMEM)
    return pl.pallas_call(
        functools.partial(attention_back_kernel, blocks),
        out_shape=jax.ShapeDtypeStruct((seq, 3 * heads * HD), BF),
        in_specs=[pl.BlockSpec(memory_space=pltpu.SMEM)] + [vmem] * 7,
        out_specs=vmem,
        scratch_shapes=[
            pltpu.VMEM((heads, seq, HD), BF),
            pltpu.VMEM((heads, seq, HD), F32),
            pltpu.VMEM((heads, seq, HD), F32),
            pltpu.VMEM((heads, seq, HD), F32),
        ],
        compiler_params=pltpu.CompilerParams(vmem_limit_bytes=56 << 20),
        cost_estimate=pl.CostEstimate(
            flops=10 * heads * seq * seq * HD, transcendentals=heads * seq * seq, bytes_accessed=20 << 20
        ),
    )(length, grad_context, q_heads, k_heads, v_heads, level, cosine, sine)


def tables(seq):
    step = np.arange(HD // 2, dtype=np.float32)
    frequency = np.power(np.float32(10000.0), np.float32(-2.0) * step / np.float32(HD))
    angle = np.arange(seq, dtype=np.float32)[:, None] * frequency[None, :]
    cosine, sine = np.cos(angle), np.sin(angle)
    signed = np.concatenate([-sine, sine, -sine, sine], axis=1)
    return jnp.asarray(np.tile(cosine, (1, 4))), jnp.asarray(signed)


COST = pl.CostEstimate(flops=0, transcendentals=0, bytes_accessed=300 << 20)
MESH = pl.DeviceIdType.MESH


def greet(count):
    barrier = pltpu.get_barrier_semaphore()
    z, c, t = lax.axis_index("fsdp"), lax.axis_index("cp"), lax.axis_index("tp")

    def hello(**place):
        pl.semaphore_signal(barrier, inc=1, device_id=place, device_id_type=MESH)

    hello(cp=1 - c)
    hello(tp=t + 1 - 2 * (t % 2))
    hello(tp=(t + 2) % 4)
    pl.when(z > 0)(lambda: hello(fsdp=z - 1))
    pl.when(z < count - 1)(lambda: hello(fsdp=z + 1))
    peers = 3 + jnp.minimum(z, 1) + jnp.minimum(count - 1 - z, 1)
    pl.semaphore_wait(barrier, peers)


class Mail:
    def __init__(self, send, recv):
        self.send, self.recv, self.used, self.open = send, recv, 0, []

    def slot(self):
        self.used += 1
        return self.used - 1

    def copy(self, slot, source, target, **place):
        return pltpu.make_async_remote_copy(
            src_ref=source,
            dst_ref=target,
            send_sem=self.send.at[slot],
            recv_sem=self.recv.at[slot],
            device_id=place,
            device_id_type=MESH,
        )

    def start(self, slot, source, target, when=None, **place):
        made = self.copy(slot, source, target, **place)
        if when is None:
            made.start()
        else:
            pl.when(when)(made.start)
        self.open.append((made, when))

    def arrive(self, slot, target, when=None, **place):
        made = self.copy(slot, target, target, **place)
        if when is None:
            made.wait_recv()
        else:
            pl.when(when)(made.wait_recv)

    def finish(self):
        for made, when in self.open:
            if when is None:
                made.wait_send()
            else:
                pl.when(when)(made.wait_send)


class Stage:
    def __init__(self, pieces, stage, sems):
        self.made = []
        for k, (source, target, when) in enumerate(pieces):
            self.made.append(
                (
                    pltpu.make_async_copy(source, stage.at[k], sems.at[0, k]),
                    pltpu.make_async_copy(stage.at[k], target, sems.at[1, k]),
                    when,
                )
            )

    def begin(self):
        for copy, _, when in self.made:
            copy.start() if when is None else pl.when(when)(copy.start)

    def turn(self):
        for first, second, when in self.made:

            def on(first=first, second=second):
                first.wait()
                second.start()

            on() if when is None else pl.when(when)(on)

    def end(self):
        for _, copy, when in self.made:
            copy.wait() if when is None else pl.when(when)(copy.wait)


class Line:
    def __init__(self, mail, count, own, at, ready=()):
        self.mail, self.count, self.own, self.at = mail, count, own, at
        self.ready = ready
        self.z = lax.axis_index("fsdp")
        self.up = [mail.slot() for _ in range(count)]
        self.down = [mail.slot() for _ in range(count)]

    def has_low(self, hop):
        return self.z >= hop

    def has_high(self, hop):
        return self.z <= self.count - 1 - hop

    def send(self, hop):
        z, count, mail = self.z, self.count, self.mail
        low, high = jnp.maximum(z - hop + 1, 0), jnp.minimum(z + hop - 1, count - 1)
        from_low = from_high = self.own
        if hop > 1:
            from_low, from_high = self.at(low), self.at(high)
        if 0 < hop - 1 <= len(self.ready):
            from_low, from_high = self.ready[hop - 2]
        mail.start(
            self.up[hop], from_low, self.at(low),
            when=(z >= hop - 1) & (z < count - 1), fsdp=jnp.minimum(z + 1, count - 1),
        )
        mail.start(
            self.down[hop], from_high, self.at(high),
            when=(z <= count - hop) & (z > 0), fsdp=jnp.maximum(z - 1, 0),
        )

    def arrive(self, hop):
        z, count = self.z, self.count
        self.mail.arrive(
            self.up[hop], self.at(jnp.maximum(z - hop, 0)), when=self.has_low(hop), fsdp=z
        )
        self.mail.arrive(
            self.down[hop], self.at(jnp.minimum(z + hop, count - 1)), when=self.has_high(hop), fsdp=z
        )


    def keep(self):
        z, count = self.z, self.count
        made = [(self.own, self.at(z), None)]
        for index, (low, high) in enumerate(self.ready):
            hop = index + 1
            made.append((low, self.at(jnp.maximum(z - hop, 0)), self.has_low(hop)))
            made.append((high, self.at(jnp.minimum(z + hop, count - 1)), self.has_high(hop)))
        return made


class Across:
    def __init__(self, line, own, mine_at, other_at):
        self.line, self.own, self.mine_at, self.other_at = line, own, mine_at, other_at
        self.c = lax.axis_index("cp")
        self.low = [line.mail.slot() for _ in range(line.count)]
        self.high = [line.mail.slot() for _ in range(line.count)]

    def send(self, hop):
        line, mail = self.line, self.line.mail
        z, count, other = line.z, line.count, 1 - self.c
        if hop == 0:
            mail.start(self.low[0], self.own, self.mine_at(z), cp=other)
            return
        low, high = jnp.maximum(z - hop, 0), jnp.minimum(z + hop, count - 1)
        mail.start(self.low[hop], self.mine_at(low), self.mine_at(low), when=line.has_low(hop), cp=other)
        mail.start(self.high[hop], self.mine_at(high), self.mine_at(high), when=line.has_high(hop), cp=other)

    def arrive(self, hop):
        line, mail = self.line, self.line.mail
        z, count, other = line.z, line.count, 1 - self.c
        if hop == 0:
            mail.arrive(self.low[0], self.other_at(z), cp=other)
            return
        low, high = jnp.maximum(z - hop, 0), jnp.minimum(z + hop, count - 1)
        mail.arrive(self.low[hop], self.other_at(low), when=line.has_low(hop), cp=other)
        mail.arrive(self.high[hop], self.other_at(high), when=line.has_high(hop), cp=other)


def first_gather_kernel(
    count, tokens, tokens_away, gain, qkv, turned_out,
    wide_0, wide_1, wide_2, away_0, away_1, away_2,
    token_rows, normed_full, qkv_full, out_half, low_pair, high_pair,
    landed, normed, wide_landed, qkv_stage, out_stage,
    send, recv, local, qkv_local, out_local,
):
    z, c, t = lax.axis_index("fsdp"), lax.axis_index("cp"), lax.axis_index("tp")
    beside, yonder = t + 1 - 2 * (t % 2), (t + 2) % 4
    low, high = low_pair.at[0], high_pair.at[0]
    wide, wide_away = (wide_0, wide_1, wide_2), (away_0, away_1, away_2)
    mail = Mail(send, recv)
    greet(count)
    stage_qkv = Stage([(qkv, qkv_full.at[z, c], None)], qkv_stage, qkv_local)
    stage_out = Stage([(turned_out, out_half.at[z], None)], out_stage, out_local)
    kept = []

    heads = Line(mail, count, qkv, lambda j: qkv_full.at[j, c])
    heads_across = Across(
        heads, qkv, lambda j: qkv_full.at[j, c], lambda j: qkv_full.at[j, 1 - c]
    )
    outs = Line(mail, count, turned_out, lambda j: out_half.at[j])
    wide_up, wide_down, wide_x = ([mail.slot() for _ in wide] for _ in range(3))
    rows_x = mail.slot()
    rows_y = [mail.slot() for _ in range(2)]
    rows_core = [mail.slot() for _ in range(4)]

    mail.start(rows_x, tokens_away, landed, cp=1 - c)
    heads.send(1)

    def rows_out(source, side, half):
        def one(place):
            rows = source[place, :]
            token_rows[half, place, :] = rows
            normed[half, place, :] = (normalize(rows.astype(F32)) * gain[...]).astype(BF)

        in_pieces(source.shape[0], one)
        mail.start(rows_y[side], normed.at[half], normed_full.at[t, half], tp=yonder)
        mail.start(rows_core[side], normed.at[half], normed_full.at[t, half], tp=beside)

    stage_qkv.begin()
    stage_out.begin()
    rows_out(tokens, 0, c)
    stage_qkv.turn()
    stage_out.turn()
    mail.arrive(rows_x, landed, cp=1 - c)
    heads_across.send(0)
    rows_out(landed, 1, 1 - c)
    kept.append(pltpu.make_async_copy(normed, normed_full.at[t], local.at[2]))
    kept[-1].start()

    def rows_on(k, half):
        mail.arrive(rows_y[k], normed_full.at[yonder, half], tp=yonder)
        mail.start(
            rows_core[2 + k], normed_full.at[yonder, half], normed_full.at[yonder, half], tp=beside
        )

    for hop in range(1, count):
        heads.arrive(hop)
        if hop + 1 < count:
            heads.send(hop + 1)
        heads_across.send(hop)
        if hop == 1:
            rows_on(0, c)
            rows_on(1, 1 - c)
            outs.send(1)
        if hop == min(2, count - 1):
            for k, piece in enumerate(wide):
                mail.start(
                    wide_up[k], piece, low.at[k], when=z < count - 1, fsdp=jnp.minimum(z + 1, count - 1)
                )
                mail.start(wide_down[k], piece, high.at[k], when=z > 0, fsdp=jnp.maximum(z - 1, 0))
    for k, piece in enumerate(wide_away):
        mail.start(wide_x[k], piece, wide_landed.at[k], cp=1 - c)
    for hop in range(1, count):
        outs.arrive(hop)
        if hop + 1 < count:
            outs.send(hop + 1)
    for hop in range(count):
        heads_across.arrive(hop)
    mail.arrive(rows_core[0], normed_full.at[beside, c], tp=beside)
    mail.arrive(rows_core[1], normed_full.at[beside, 1 - c], tp=beside)
    far = (beside + 2) % 4
    mail.arrive(rows_core[2], normed_full.at[far, c], tp=beside)
    mail.arrive(rows_core[3], normed_full.at[far, 1 - c], tp=beside)
    for k in range(len(wide)):
        mail.arrive(wide_x[k], wide_landed.at[k], cp=1 - c)
    for pair, place in ((low_pair, 1), (high_pair, 3)):
        kept.append(pltpu.make_async_copy(wide_landed, pair.at[1], local.at[place]))
        kept[-1].start()
    for k in range(len(wide)):
        mail.arrive(wide_up[k], low.at[k], when=z > 0, fsdp=z)
        mail.arrive(wide_down[k], high.at[k], when=z < count - 1, fsdp=z)
    for copy in kept:
        copy.wait()
    stage_qkv.end()
    stage_out.end()
    mail.finish()


def first_gather(count, tokens, tokens_away, gain, qkv, turned_out, wide, wide_away):
    slots = 6 * count + 16
    anywhere = pl.BlockSpec(memory_space=pl.ANY)
    vmem = pl.BlockSpec(memory_space=pltpu.VMEM)
    pair = (2,) + tokens.shape
    wide_shape = (3,) + wide[0].shape
    return pl.pallas_call(
        functools.partial(first_gather_kernel, count),
        out_shape=(
            jax.ShapeDtypeStruct(pair, BF),
            jax.ShapeDtypeStruct((4,) + pair, BF),
            jax.ShapeDtypeStruct((count, 2) + qkv.shape, BF),
            jax.ShapeDtypeStruct((count,) + turned_out.shape, BF),
            jax.ShapeDtypeStruct((2,) + wide_shape, BF),
            jax.ShapeDtypeStruct((2,) + wide_shape, BF),
        ),
        in_specs=[vmem, anywhere, vmem] + [anywhere] * 8,
        out_specs=(vmem,) + (anywhere,) * 5,
        scratch_shapes=[
            pltpu.VMEM(tokens.shape, BF),
            pltpu.VMEM(pair, BF),
            pltpu.VMEM(wide_shape, BF),
            pltpu.VMEM((1,) + qkv.shape, BF),
            pltpu.VMEM((1,) + turned_out.shape, BF),
            pltpu.SemaphoreType.DMA((slots,)),
            pltpu.SemaphoreType.DMA((slots,)),
            pltpu.SemaphoreType.DMA((4,)),
            pltpu.SemaphoreType.DMA((2, 1)),
            pltpu.SemaphoreType.DMA((2, 1)),
        ],
        cost_estimate=COST,
        compiler_params=pltpu.CompilerParams(
            collective_id=1, has_side_effects=True, vmem_limit_bytes=32 << 20
        ),
    )(tokens, tokens_away, gain, qkv, turned_out, *wide, *wide_away)


def in_pieces(rows, body, size=16):
    if rows % size:
        body(pl.ds(0, rows))
        return
    lax.fori_loop(0, rows // size, lambda i, carry: (body(pl.ds(i * size, size)), carry)[1], 0)


class Spread:
    def __init__(self, mail, own, at):
        self.mail, self.own, self.at = mail, own, at
        self.c, self.t = lax.axis_index("cp"), lax.axis_index("tp")
        self.beside, self.yonder = self.t + 1 - 2 * (self.t % 2), (self.t + 2) % 4
        self.x = [mail.slot() for _ in range(3)]
        self.y = [mail.slot() for _ in range(3)]
        self.core = {}

    def to_core(self, c_is_own, t_is_own, piece):
        slot = self.core[c_is_own, t_is_own, piece] = self.mail.slot()
        c = self.c if c_is_own else 1 - self.c
        t = self.t if t_is_own else self.yonder
        source = self.own(piece) if c_is_own and t_is_own else self.at(c, t, piece)
        self.mail.start(slot, source, self.at(c, t, piece), tp=self.beside)

    def begin(self, piece):
        c, t = self.c, self.t
        if piece == 0:
            self.mail.start(self.x[0], self.own(0), self.at(c, t, 0), cp=1 - c)
        else:
            self.mail.start(self.y[0], self.own(1), self.at(c, t, 1), tp=self.yonder)
            self.mail.start(self.x[1], self.own(1), self.at(c, t, 1), cp=1 - c)
            self.mail.start(self.y[1], self.own(0), self.at(c, t, 0), tp=self.yonder)
        self.to_core(True, True, piece)

    def turn(self):
        c, t, mail, yonder = self.c, self.t, self.mail, self.yonder
        mail.arrive(self.x[0], self.at(1 - c, t, 0), cp=1 - c)
        mail.start(self.y[2], self.at(1 - c, t, 0), self.at(1 - c, t, 0), tp=yonder)
        self.to_core(False, True, 0)
        mail.arrive(self.y[0], self.at(c, yonder, 1), tp=yonder)
        mail.start(self.x[2], self.at(c, yonder, 1), self.at(c, yonder, 1), cp=1 - c)
        self.to_core(True, False, 1)

    def end(self):
        c, t, mail, yonder = self.c, self.t, self.mail, self.yonder
        mail.arrive(self.x[1], self.at(1 - c, t, 1), cp=1 - c)
        self.to_core(False, True, 1)
        mail.arrive(self.y[1], self.at(c, yonder, 0), tp=yonder)
        self.to_core(True, False, 0)
        mail.arrive(self.x[2], self.at(1 - c, yonder, 1), cp=1 - c)
        self.to_core(False, False, 1)
        mail.arrive(self.y[2], self.at(1 - c, yonder, 0), tp=yonder)
        self.to_core(False, False, 0)
        far = (self.beside + 2) % 4
        for (c_is_own, t_is_own, piece), slot in self.core.items():
            place = self.at(
                c if c_is_own else 1 - c, self.beside if t_is_own else far, piece
            )
            mail.arrive(slot, place, tp=self.beside)


def second_gather_kernel(
    count, part, tokens, gain, wide_0, wide_1, wide_2,
    first_low, first_high, second_low, second_high, *refs
):
    hops_mine, hops_other = min(2, count - 1), 1
    wide = (wide_0, wide_1, wide_2)
    wide_other = [first_low.at[1, which] for which in range(3)]
    ready_mine = [first_low.at[0], first_high.at[0], second_low.at[0], second_high.at[0]]
    ready_mine = ready_mine[: 2 * hops_mine]
    ready_other = [second_low.at[1], second_high.at[1]]
    middle, middle_home, normed_full, gate_full, up_full, down_full = refs[:6]
    own, from_core, to_yonder, from_yonder, normed, stage, send, recv, local, local_line = refs[6:]
    c, t = lax.axis_index("cp"), lax.axis_index("tp")
    rows = tokens.shape[0]
    half = rows // 2
    mail = Mail(send, recv)
    greet(count)

    mine, other = [], []
    for which, full in enumerate((gate_full, up_full, down_full)):
        for lines, side, piece, ready in (
            (mine, c, wide, ready_mine), (other, 1 - c, wide_other, ready_other),
        ):
            arrived = [
                (ready[2 * hop].at[which], ready[2 * hop + 1].at[which])
                for hop in range(len(ready) // 2)
            ]
            lines.append(
                Line(
                    mail, count, piece[which],
                    lambda j, full=full, side=side: full.at[j, side], arrived,
                )
            )
    summed = TensorSum(mail, part, own, from_core, to_yonder, from_yonder, local)
    spread = Spread(
        mail, lambda piece: normed.at[piece], lambda c, t, piece: normed_full.at[piece, t, c]
    )

    summed.begin()
    placing = Stage([piece for line in mine + other for piece in line.keep()], stage, local_line)
    placing.begin()

    def send_hop(lines, hop):
        for line in lines:
            if hop < count:
                line.send(hop)

    def arrive_hop(lines, hop):
        for line in lines:
            if hop < count:
                line.arrive(hop)

    send_hop(other, hops_other + 1)
    send_hop(mine, hops_mine + 1)
    summed.turn()
    placing.turn()
    for piece in range(2):
        summed.arrive(piece)

        def norm(place, piece=piece):
            row = pl.ds(place.start + piece * half, place.size)
            values = tokens[row, :].astype(F32) + BRANCH * summed.rows(row)
            middle[row, :] = values
            normed[piece, place, :] = (normalize(values) * gain[...]).astype(BF)

        in_pieces(half, norm)
        spread.begin(piece)
    keep_normed = pltpu.make_async_copy(normed, normed_full.at[:, t, c], local.at[0])
    keep_normed.start()
    home = mail.slot()
    stay, go = pl.ds(c * half, half), pl.ds((1 - c) * half, half)
    keep_home = pltpu.make_async_copy(middle.at[stay], middle_home.at[c], local.at[1])
    keep_home.start()
    spread.turn()
    mail.start(home, middle.at[go], middle_home.at[c], cp=1 - c)
    for step in range(1, count):
        hop = hops_other + step
        if hop < count:
            for line_other, line_mine in zip(other, mine):
                line_other.arrive(hop)
                if hop + 1 < count:
                    line_other.send(hop + 1)
                if hops_mine + step < count:
                    line_mine.arrive(hops_mine + step)
                    if hops_mine + step + 1 < count:
                        line_mine.send(hops_mine + step + 1)
        if step == 1:
            spread.end()
    if count == 1:
        spread.end()
    mail.arrive(home, middle_home.at[1 - c], cp=1 - c)
    keep_home.wait()
    keep_normed.wait()
    placing.end()
    mail.finish()


def second_gather(count, part, tokens, gain, wide, first_low, first_high, second_low, second_high):
    slots = 12 * count + 24
    rows, width = tokens.shape
    anywhere = pl.BlockSpec(memory_space=pl.ANY)
    vmem = pl.BlockSpec(memory_space=pltpu.VMEM)
    full = jax.ShapeDtypeStruct((count, 2) + wide[0].shape, BF)
    return pl.pallas_call(
        functools.partial(second_gather_kernel, count),
        out_shape=(
            jax.ShapeDtypeStruct((rows, width), F32),
            jax.ShapeDtypeStruct((2, rows // 2, width), F32),
            jax.ShapeDtypeStruct((2, 4, 2, rows // 2, width), BF),
            full,
            full,
            full,
        ),
        in_specs=[anywhere, vmem, vmem] + [anywhere] * 7,
        out_specs=(vmem,) + (anywhere,) * 5,
        scratch_shapes=[
            pltpu.VMEM((2, rows, width), BF),
            pltpu.VMEM((2, rows, width), BF),
            pltpu.VMEM((rows, width), BF),
            pltpu.VMEM((rows, width), BF),
            pltpu.VMEM((2, rows // 2, width), BF),
            pltpu.VMEM((24,) + wide[0].shape, BF),
            pltpu.SemaphoreType.DMA((slots,)),
            pltpu.SemaphoreType.DMA((slots,)),
            pltpu.SemaphoreType.DMA((2,)),
            pltpu.SemaphoreType.DMA((2, 24)),
        ],
        cost_estimate=COST,
        compiler_params=pltpu.CompilerParams(
            collective_id=2, has_side_effects=True, vmem_limit_bytes=40 << 20
        ),
    )(part, tokens, gain, *wide, first_low, first_high, second_low, second_high)


class TensorSum:
    def __init__(self, mail, part, own, from_core, to_yonder, from_yonder, local):
        self.mail, self.part, self.own, self.from_core = mail, part, own, from_core
        self.to_yonder, self.from_yonder, self.local = to_yonder, from_yonder, local
        self.t = t = lax.axis_index("tp")
        self.beside, self.yonder = t + 1 - 2 * (t % 2), (t + 2) % 4
        self.core = [mail.slot() for _ in range(2)]
        self.across = [mail.slot() for _ in range(2)]
        self.half = from_yonder.shape[0] // 2

    def begin(self):
        part, far = self.part, (self.beside + 2) % 4
        self.mail.start(self.core[1], part.at[far], self.from_core.at[1], tp=self.beside)
        self.mail.start(self.core[0], part.at[self.beside], self.from_core.at[0], tp=self.beside)
        self.kept = [
            pltpu.make_async_copy(part.at[self.yonder], self.own.at[1], self.local.at[0]),
            pltpu.make_async_copy(part.at[self.t], self.own.at[0], self.local.at[1]),
        ]
        for copy in self.kept:
            copy.start()

    def turn(self):
        own, from_core = self.own, self.from_core
        self.kept[0].wait()
        self.mail.arrive(self.core[1], from_core.at[1], tp=self.beside)
        for piece in range(2):

            def add(place, piece=piece):
                place = pl.ds(place.start + piece * self.half, place.size)
                self.to_yonder[place, :] = (
                    own[1, place, :].astype(F32) + from_core[1, place, :].astype(F32)
                ).astype(BF)

            in_pieces(self.half, add)
            block = pl.ds(piece * self.half, self.half)
            self.mail.start(
                self.across[piece], self.to_yonder.at[block], self.from_yonder.at[block],
                tp=self.yonder,
            )
        self.kept[1].wait()
        self.mail.arrive(self.core[0], from_core.at[0], tp=self.beside)

    def arrive(self, piece):
        block = pl.ds(piece * self.half, self.half)
        self.mail.arrive(self.across[piece], self.from_yonder.at[block], tp=self.yonder)

    def rows(self, row):
        return (
            self.own[0, row, :].astype(F32)
            + self.from_core[0, row, :].astype(F32)
            + self.from_yonder[row, :].astype(F32)
        )


class Drain:
    def __init__(self, mail, count, fill, total, landed):
        self.mail, self.count, self.fill, self.total, self.landed = mail, count, fill, total, landed
        self.z = lax.axis_index("fsdp")
        self.slots = [[mail.slot() for _ in range(count)] for _ in range(2)]

    def sends(self, hop, up):
        z, count = self.z, self.count
        return (z <= hop - 1) & (z < count - 1) if up else (z >= count - hop) & (z > 0)

    def gets(self, hop, up):
        z, count = self.z, self.count
        return (z >= 1) & (z <= hop) if up else (z <= count - 2) & (z >= count - 1 - hop)

    def block(self, hop, up):
        z, count = self.z, self.count
        return jnp.minimum(z + count - hop, count - 1) if up else jnp.maximum(z - count + hop, 0)

    def arrive(self, hop):
        for side, up in enumerate((True, False)):
            self.mail.arrive(
                self.slots[side][hop], self.landed(side, hop), when=self.gets(hop, up), fsdp=self.z
            )

    def gather(self, hop):
        for side, up in enumerate((True, False)):
            target = self.total(side, hop)

            def work(side=side, up=up, target=target):
                self.fill(hop, up, self.block(hop, up), target)
                if hop > 1:

                    def add():
                        landed = self.landed(side, hop - 1)

                        def one(place):
                            target[place, :] = (
                                target[place, :].astype(F32) + landed[place, :].astype(F32)
                            ).astype(BF)

                        in_pieces(target.shape[0], one)

                    pl.when(self.gets(hop - 1, up))(add)

            pl.when(self.sends(hop, up))(work)

    def send(self, hop):
        z, count = self.z, self.count
        for side, up in enumerate((True, False)):
            to = jnp.minimum(z + 1, count - 1) if up else jnp.maximum(z - 1, 0)
            self.mail.start(
                self.slots[side][hop], self.total(side, hop), self.landed(side, hop),
                when=self.sends(hop, up), fsdp=to,
            )


def norm_back(values, gain, upstream):
    scale = lax.rsqrt(jnp.mean(values * values, axis=-1, keepdims=True) + EPSILON)
    norm = values * scale
    scaled = upstream * gain
    mean = jnp.mean(scaled * norm, axis=-1, keepdims=True)
    return scale * (scaled - norm * mean), upstream * norm


def first_sum_kernel(
    count, part, gate_grad, up_grad, hidden, middle_from, cotangent_from, down_from, gain,
    grad_middle, attention_full, gain_rows, leaving_up, leaving_down, feedforward,
    own, from_core, first, second, grad_attention, totals, landed, hidden_rows, product, middle, cotangent, down,
    send, recv, local, hidden_local, loads_local,
):
    z, c, t = lax.axis_index("fsdp"), lax.axis_index("cp"), lax.axis_index("tp")
    beside, yonder = t + 1 - 2 * (t % 2), (t + 2) % 4
    far = (beside + 2) % 4
    half = middle.shape[0] // 2
    width = middle.shape[1]
    loads = [
        pltpu.make_async_copy(source, target, loads_local.at[k])
        for k, (source, target) in enumerate(
            ((down_from, down), (middle_from, middle), (cotangent_from, cotangent))
        )
    ]
    mail = Mail(send, recv)
    greet(count)
    last = count - 1

    def fill_from(which):
        def fill(hop, up, j, target):
            copy = pltpu.make_async_copy((gate_grad, up_grad)[which].at[j], target, local.at[4])
            copy.start()
            copy.wait()

        return fill

    drains = [
        Drain(
            mail, count, fill_from(which),
            lambda side, hop, which=which: (
                (leaving_up, leaving_down)[side].at[which] if hop == last else totals.at[side, hop - 1, which]
            ),
            lambda side, hop, which=which: landed.at[side, hop - 1, which],
        )
        for which in range(2)
    ]

    core = {}
    mine = {}
    order = ((0, 0), (0, 1), (1, 0), (1, 1))
    for index, (c_own, t_own) in enumerate(order):
        block_c = c if c_own else 1 - c
        core[c_own, t_own] = mail.slot()
        mail.start(
            core[c_own, t_own], part.at[:, beside if t_own else far, block_c],
            from_core.at[c_own, t_own], tp=beside,
        )
        mine[c_own, t_own] = pltpu.make_async_copy(
            part.at[:, t if t_own else yonder, block_c], own.at[c_own, t_own], local.at[index]
        )
        mine[c_own, t_own].start()
    if last > 1:
        for drain in drains:
            drain.gather(1)
            drain.send(1)

    block_rows = product.shape[1]
    blocks = hidden.shape[0] // block_rows

    def hidden_copy(block):
        return pltpu.make_async_copy(
            hidden.at[pl.ds(block * block_rows, block_rows)], hidden_rows.at[block % 2],
            hidden_local.at[0, block % 2],
        )

    def product_copy(block):
        return pltpu.make_async_copy(
            product.at[block % 2], feedforward.at[pl.ds(block * block_rows, block_rows)],
            hidden_local.at[1, block % 2],
        )

    def product_block(block):
        hidden_copy(block).wait()
        if block + 1 < blocks:
            hidden_copy(block + 1).start()
        if block > 1:
            product_copy(block - 2).wait()

        def one(k, carry):
            columns = pl.ds(pl.multiple_of(k * 2 * TILE, 2 * TILE), 2 * TILE)
            value = lax.dot_general(
                hidden_rows[block % 2], down[columns, :], (((1,), (1,)), ((), ())),
                preferred_element_type=F32,
            )
            product[block % 2, :, columns] = value.astype(BF)
            return carry

        lax.fori_loop(0, width // (2 * TILE), one, 0)
        product_copy(block).start()

    hidden_copy(0).start()
    for copy in loads:
        copy.start()
    loads[0].wait()
    product_block(0)

    quarter = half // 2
    quarters = [(piece, pl.ds(side * quarter, quarter)) for piece in range(2) for side in range(2)]
    x_first = [[mail.slot() for _ in range(2)] for _ in quarters]
    y_second = [mail.slot() for _ in quarters]
    ring_y = [mail.slot() for _ in quarters]
    ring_core = [mail.slot() for _ in quarters]
    ring_far = [mail.slot() for _ in quarters]

    def core_add(c_own, t_own, piece, rows):
        def one(place):
            row = pl.ds(rows.start + place.start, place.size)
            own[c_own, t_own, piece, row, :] = (
                own[c_own, t_own, piece, row, :].astype(F32)
                + from_core[c_own, t_own, piece, row, :].astype(F32)
            ).astype(BF)

        in_pieces(quarter, one)

    for t_own in (0, 1):
        mine[0, t_own].wait()
        mail.arrive(core[0, t_own], from_core.at[0, t_own], tp=beside)
    for k, (piece, rows) in enumerate(quarters):
        for t_own in (0, 1):
            core_add(0, t_own, piece, rows)
            mail.start(
                x_first[k][t_own], own.at[0, t_own, piece, rows], first.at[k, t_own], cp=1 - c
            )
    for t_own in (0, 1):
        mine[1, t_own].wait()
        mail.arrive(core[1, t_own], from_core.at[1, t_own], tp=beside)

    def add_first(k, t_own):
        piece, rows = quarters[k]

        def one(place):
            row = pl.ds(rows.start + place.start, place.size)
            own[1, t_own, piece, row, :] = (
                own[1, t_own, piece, row, :].astype(F32)
                + from_core[1, t_own, piece, row, :].astype(F32)
                + first[k, t_own, place, :].astype(F32)
            ).astype(BF)

        in_pieces(quarter, one)

    gain_rows[...] = jnp.zeros_like(gain_rows)
    loads[1].wait()
    loads[2].wait()

    def finish(k):
        piece, rows = quarters[k]
        mail.arrive(y_second[k], second.at[k], tp=yonder)

        def back(place):
            local_row = pl.ds(rows.start + place.start, place.size)
            row = pl.ds(piece * half + rows.start + place.start, place.size)
            summed = own[1, 1, piece, local_row, :].astype(F32) + second[k, place, :].astype(F32)
            grad, products = norm_back(middle[row, :], gain[...], summed)
            grad = cotangent[row, :].astype(F32) + grad
            grad_middle[row, :] = grad
            grad_attention[piece, local_row, :] = (BRANCH * grad).astype(BF)
            gain_rows[...] += jnp.sum(products, axis=0, keepdims=True)

        in_pieces(quarter, back)
        source = grad_attention.at[piece, rows]
        mail.start(ring_y[k], source, attention_full.at[t, piece, rows], tp=yonder)
        mail.start(ring_core[k], source, attention_full.at[t, piece, rows], tp=beside)

    def z_hop(hop):
        for drain in drains:
            drain.arrive(hop - 1)
            drain.gather(hop)
            drain.send(hop)

    for k, (piece, rows) in enumerate(quarters):
        mail.arrive(x_first[k][0], first.at[k, 0], cp=1 - c)
        add_first(k, 0)
        mail.start(y_second[k], own.at[1, 0, piece, rows], second.at[k], tp=yonder)
        mail.arrive(x_first[k][1], first.at[k, 1], cp=1 - c)
        add_first(k, 1)
        if k > 0:
            finish(k - 1)
        if k == 2 and last > 2:
            z_hop(2)
        product_block(k + 1)
    finish(len(quarters) - 1)
    for block in range(len(quarters) + 1, blocks):
        product_block(block)
    keep = pltpu.make_async_copy(grad_attention, attention_full.at[t], local.at[0])
    keep.start()
    for hop in range(3, last):
        z_hop(hop)
    for k, (piece, rows) in enumerate(quarters):
        arrived = attention_full.at[yonder, piece, rows]
        mail.arrive(ring_y[k], arrived, tp=yonder)
        mail.start(ring_far[k], arrived, arrived, tp=beside)
    for k, (piece, rows) in enumerate(quarters):
        mail.arrive(ring_core[k], attention_full.at[beside, piece, rows], tp=beside)
        mail.arrive(ring_far[k], attention_full.at[far, piece, rows], tp=beside)
    for drain in drains:
        if last > 1:
            drain.arrive(last - 1)
        if last > 0:
            drain.gather(last)
    keep.wait()
    for block in range(blocks - 2, blocks):
        product_copy(block).wait()
    mail.finish()


def first_sum(count, part, gate_grad, up_grad, hidden, middle, cotangent, gain, down):
    slots = 6 * count + 32
    rows, width = middle.shape
    block = gate_grad.shape[1:]
    anywhere = pl.BlockSpec(memory_space=pl.ANY)
    vmem = pl.BlockSpec(memory_space=pltpu.VMEM)
    hops = max(count - 2, 1)
    return pl.pallas_call(
        functools.partial(first_sum_kernel, count),
        out_shape=(
            jax.ShapeDtypeStruct((rows, width), F32),
            jax.ShapeDtypeStruct((4, 2, rows // 2, width), BF),
            jax.ShapeDtypeStruct((1, width), F32),
            jax.ShapeDtypeStruct((2,) + block, BF),
            jax.ShapeDtypeStruct((2,) + block, BF),
            jax.ShapeDtypeStruct((hidden.shape[0], width), BF),
        ),
        in_specs=[anywhere] * 7 + [vmem],
        out_specs=(vmem, anywhere, vmem, vmem, vmem, anywhere),
        scratch_shapes=[
            pltpu.VMEM((2, 2, 2, rows // 2, width), BF),
            pltpu.VMEM((2, 2, 2, rows // 2, width), BF),
            pltpu.VMEM((4, 2, rows // 4, width), BF),
            pltpu.VMEM((4, rows // 4, width), BF),
            pltpu.VMEM((2, rows // 2, width), BF),
            pltpu.VMEM((2, hops, 2) + block, BF),
            pltpu.VMEM((2, hops, 2) + block, BF),
            pltpu.VMEM((2, hidden.shape[0] // 8, hidden.shape[1]), BF),
            pltpu.VMEM((2, hidden.shape[0] // 8, width), BF),
            pltpu.VMEM((rows, width), F32),
            pltpu.VMEM((rows, width), BF),
            pltpu.VMEM(down.shape, BF),
            pltpu.SemaphoreType.DMA((slots,)),
            pltpu.SemaphoreType.DMA((slots,)),
            pltpu.SemaphoreType.DMA((5,)),
            pltpu.SemaphoreType.DMA((2, 2)),
            pltpu.SemaphoreType.DMA((3,)),
        ],
        cost_estimate=COST,
        compiler_params=pltpu.CompilerParams(
            collective_id=3, has_side_effects=True, vmem_limit_bytes=60 << 20
        ),
    )(part, gate_grad, up_grad, hidden, middle, cotangent, down, gain)


AHEAD = 6


def last_sum_kernel(
    count, projected_from, qkv_full, qkv_grad, out_grad, tokens_from, middle_from, gain, gain_rows,
    qkv_total, out_total, grad_tokens, gain_sums,
    own, from_core, to_yonder, from_yonder, pieces,
    from_x, heads_sum, heads_landed, outs_sum, outs_landed, final_out, gains, gain_line,
    part, weights, give_sum, give_landed, give_own, give_total, grad_projected, tokens, grad_middle,
    send, recv, local, weights_local, loads_local,
):
    z, c, t = lax.axis_index("fsdp"), lax.axis_index("cp"), lax.axis_index("tp")
    beside, yonder = t + 1 - 2 * (t % 2), (t + 2) % 4
    half = tokens.shape[0] // 2
    last = count - 1
    mail = Mail(send, recv)
    greet(count)

    summed = TensorSum(mail, part, own, from_core, to_yonder, from_yonder, local)

    columns = qkv_total.shape[1]
    behind = columns * 5 // 6 // TILE * TILE
    split = -(-behind // (2 * TILE)) * TILE
    parts = [pl.ds(0, split), pl.ds(split, behind - split)]
    late = pl.ds(behind, columns - behind)
    cross = [[[mail.slot() for _ in range(count)] for _ in range(2)] for _ in parts]
    cross_own = [mail.slot() for _ in parts]

    def head_drain(lanes):
        def fill(hop, up, j, target):
            side = 0 if up else 1
            copy = pltpu.make_async_copy(qkv_grad.at[j, c, :, lanes], target, local.at[2])
            copy.start()
            copy.wait()
            arrived = from_x.at[side, hop - 1, :, lanes]

            def one(place):
                target[place, :] = (
                    target[place, :].astype(F32) + arrived[place, :].astype(F32)
                ).astype(BF)

            in_pieces(target.shape[0], one)

        return Drain(
            mail, count, fill,
            lambda side, hop: heads_sum.at[side, hop - 1, :, lanes],
            lambda side, hop: heads_landed.at[side, hop - 1, :, lanes],
        )

    heads = [head_drain(lanes) for lanes in parts]

    def late_fill(side_c):
        def fill(hop, up, j, target):
            copy = pltpu.make_async_copy(qkv_grad.at[j, side_c, :, late], target, local.at[2])
            copy.start()
            copy.wait()

        return fill

    stay = Drain(
        mail, count, late_fill(c),
        lambda side, hop: heads_sum.at[side, hop - 1, :, late],
        lambda side, hop: heads_landed.at[side, hop - 1, :, late],
    )
    give = Drain(
        mail, count, late_fill(1 - c),
        lambda side, hop: give_sum.at[side, hop - 1],
        lambda side, hop: give_landed.at[side, hop - 1],
    )
    give_slot = mail.slot()

    def fill_outs(hop, up, j, target):
        copy = pltpu.make_async_copy(out_grad.at[j], target, local.at[3])
        copy.start()
        copy.wait()

    outs = Drain(
        mail, count, fill_outs,
        lambda side, hop: outs_sum.at[side, hop - 1],
        lambda side, hop: outs_landed.at[side, hop - 1],
    )

    steps = [(hop, k) for hop in range(1, count + 1) for k in range(2)]

    def cross_send(step):
        if step >= len(steps):
            return
        hop, k = steps[step]
        lanes = parts[k]
        if hop == count:
            mail.start(
                cross_own[k], qkv_grad.at[z, 1 - c, :, lanes], from_x.at[0, last, :, lanes], cp=1 - c
            )
            return
        for side, up in enumerate((True, False)):
            mail.start(
                cross[k][side][hop], qkv_grad.at[heads[k].block(hop, up), 1 - c, :, lanes],
                from_x.at[side, hop - 1, :, lanes], when=heads[k].sends(hop, up), cp=1 - c,
            )

    def cross_arrive(hop, k):
        for side, up in enumerate((True, False)):
            mail.arrive(
                cross[k][side][hop], from_x.at[side, hop - 1, :, parts[k]],
                when=heads[k].sends(hop, up), cp=1 - c,
            )

    for step in range(AHEAD):
        cross_send(step)
    early_chains = (outs, give, stay)
    if count > 1:
        for drain in early_chains:
            drain.gather(1)
            drain.send(1)

    wide_block = weights.shape[1]
    blocks = qkv_full.shape[0] // wide_block

    def weights_copy(block, slot):
        return pltpu.make_async_copy(
            qkv_full.at[pl.ds(block * wide_block, wide_block)], weights.at[slot],
            weights_local.at[slot],
        )

    def product(block, carry):
        slot = lax.rem(block, 2)
        weights_copy(block, slot).wait()
        pl.when(block + 1 < blocks)(lambda: weights_copy(block + 1, 1 - slot).start())
        columns = pl.ds(pl.multiple_of(block * wide_block, wide_block), wide_block)
        value = lax.dot_general(
            grad_projected[...], weights[slot], (((1,), (1,)), ((), ())),
            preferred_element_type=F32,
        )
        part[:, :, columns] = value.astype(BF).reshape(part.shape[:2] + (wide_block,))
        return carry

    loads = [
        pltpu.make_async_copy(source, target, loads_local.at[k])
        for k, (source, target) in enumerate(
            (
                (projected_from, grad_projected),
                (tokens_from, tokens),
                (middle_from, grad_middle),
            )
        )
    ]
    weights_copy(0, 0).start()
    for copy in loads:
        copy.start()
    loads[0].wait()
    thirds = [blocks * k // 3 for k in range(4)]

    keep = pltpu.make_async_copy(pieces.at[c], grad_tokens.at[c], local.at[0])
    home = mail.slot()
    gain_x, gain_y, gain_core = mail.slot(), mail.slot(), mail.slot()
    line = Line(mail, count, gain_line.at[z], lambda j: gain_line.at[j])

    def finish_rows():
        loads[1].wait()
        loads[2].wait()
        gains[0, 0:1, :] = jnp.zeros_like(gain_rows)
        gains[0, 1:2, :] = gain_rows[...]
        for piece in range(2):
            summed.arrive(piece)

            def back(place, piece=piece):
                row = pl.ds(place.start + piece * half, place.size)
                grad, rows = norm_back(tokens[row, :].astype(F32), gain[...], summed.rows(row))
                pieces[piece, place, :] = (grad_middle[row, :] + grad).astype(BF)
                gains[0, 0:1, :] += jnp.sum(rows, axis=0, keepdims=True)

            in_pieces(half, back)
        mail.start(home, pieces.at[1 - c], grad_tokens.at[c], cp=1 - c)
        keep.start()
        mail.start(gain_core, gains.at[0], gains.at[1], tp=beside)

    def gain_step(k):
        if k == 0:
            mail.arrive(gain_core, gains.at[1], tp=beside)
            gains[2] = gains[0] + gains[1]
            mail.start(gain_y, gains.at[2], gains.at[3], tp=yonder)
        elif k == 1:
            mail.arrive(gain_y, gains.at[3], tp=yonder)
            gains[4] = gains[2] + gains[3]
            mail.start(gain_x, gains.at[4], gains.at[5], cp=1 - c)
        elif k == 2:
            mail.arrive(gain_x, gains.at[5], cp=1 - c)
            gain_line[z] = gains[4] + gains[5]
            if count > 1:
                line.send(1)
        else:
            hop = k - 2
            line.arrive(hop)
            if hop + 1 < count:
                line.send(hop + 1)

    def outs_hop(hop):
        for drain in early_chains:
            drain.arrive(hop - 1)
            drain.gather(hop)
            drain.send(hop)

    def give_away():
        copy = pltpu.make_async_copy(qkv_grad.at[z, 1 - c, :, late], give_own, local.at[3])
        copy.start()
        copy.wait()
        if count > 1:
            give.arrive(last)

        def one(place):
            total = give_own[place, :].astype(F32)
            for side, up in enumerate((True, False)):
                if count > 1:
                    landed = give.landed(side, last)[place, :].astype(F32)
                    total += jnp.where(give.gets(last, up), landed, 0.0)
            give_total[place, :] = total.astype(BF)

        in_pieces(give_own.shape[0], one)
        mail.start(give_slot, give_total, from_x.at[0, last, :, late], cp=1 - c)

    for step, (hop, k) in enumerate(steps[:-2]):
        if step < 3:
            lax.fori_loop(thirds[step], thirds[step + 1], product, 0)
        if count == 2 and step == 1:
            lax.fori_loop(thirds[2], thirds[3], product, 0)
        if step == 2 or count == 2 and step == 1:
            summed.begin()
        cross_arrive(hop, k)
        cross_send(step + AHEAD)
        if hop > 1:
            heads[k].arrive(hop - 1)
        heads[k].gather(hop)
        heads[k].send(hop)
        if k == 1 and hop + 1 < count:
            outs_hop(hop + 1)
        if step == 2 or count == 2 and step == 1:
            summed.turn()
        if step == 3 or count == 2 and step == 1:
            finish_rows()
        if step == 5 or step == 3 and count == 3:
            gain_step(0)
            gain_step(1)
    if count == 1:
        lax.fori_loop(thirds[0], thirds[3], product, 0)
        summed.begin()
        summed.turn()
        finish_rows()
    if count <= 2:
        gain_step(0)
        gain_step(1)
    gain_step(2)
    give_away()

    own_copy = pltpu.make_async_copy(qkv_grad.at[z, c], from_x.at[1, last], local.at[2])
    own_copy.start()
    out_copy = pltpu.make_async_copy(out_grad.at[z], final_out, local.at[3])
    out_copy.start()
    for k, lanes in enumerate(parts):
        mail.arrive(cross_own[k], from_x.at[0, last, :, lanes], cp=1 - c)
    mail.arrive(give_slot, from_x.at[0, last, :, late], cp=1 - c)
    own_copy.wait()
    out_copy.wait()

    def start_heads(place):
        qkv_total[place, :] = from_x[0, last, place, :].astype(F32) + from_x[
            1, last, place, :
        ].astype(F32)

    in_pieces(qkv_total.shape[0], start_heads)

    def start_outs(place):
        out_total[place, :] = final_out[place, :].astype(F32)

    in_pieces(out_total.shape[0], start_outs)
    for hop in range(1, count):
        gain_step(2 + hop)
    if count > 1:
        chains = [(outs, pl.ds(0, out_total.shape[1]), out_total)]
        chains += [(stay, late, qkv_total)]
        chains += [(heads[k], lanes, qkv_total) for k, lanes in enumerate(parts)]
        for drain, lanes, total in chains:
            drain.arrive(last)
            for side, up in enumerate((True, False)):

                def more(drain=drain, total=total, side=side, lanes=lanes):
                    landed = drain.landed(side, last)

                    def one(place):
                        total[place, lanes] += landed[place, :].astype(F32)

                    in_pieces(total.shape[0], one)

                pl.when(drain.gets(last, up))(more)
    gain_sums[...] = jnp.sum(gain_line[...], axis=0)
    mail.arrive(home, grad_tokens.at[1 - c], cp=1 - c)
    keep.wait()
    mail.finish()


def last_sum(count, grad_projected, qkv_full, qkv_grad, out_grad, tokens, grad_middle, gain, gain_rows):
    slots = 17 * count + 17
    rows, width = tokens.shape
    hops = max(count - 1, 1)
    block, out_block = qkv_grad.shape[2:], out_grad.shape[1:]
    columns = block[1]
    give_block = (block[0], columns - columns * 5 // 6 // TILE * TILE)
    anywhere = pl.BlockSpec(memory_space=pl.ANY)
    vmem = pl.BlockSpec(memory_space=pltpu.VMEM)
    return pl.pallas_call(
        functools.partial(last_sum_kernel, count),
        out_shape=(
            jax.ShapeDtypeStruct(block, F32),
            jax.ShapeDtypeStruct(out_block, F32),
            jax.ShapeDtypeStruct((2, rows // 2, width), BF),
            jax.ShapeDtypeStruct((2, width), F32),
        ),
        in_specs=[anywhere] * 6 + [vmem] * 2,
        out_specs=(vmem, vmem, anywhere, vmem),
        scratch_shapes=[
            pltpu.VMEM((2, rows, width), BF),
            pltpu.VMEM((2, rows, width), BF),
            pltpu.VMEM((rows, width), BF),
            pltpu.VMEM((rows, width), BF),
            pltpu.VMEM((2, rows // 2, width), BF),
            pltpu.VMEM((2, count) + block, BF),
            pltpu.VMEM((2, hops) + block, BF),
            pltpu.VMEM((2, hops) + block, BF),
            pltpu.VMEM((2, hops) + out_block, BF),
            pltpu.VMEM((2, hops) + out_block, BF),
            pltpu.VMEM(out_block, BF),
            pltpu.VMEM((6, 2, width), F32),
            pltpu.VMEM((count, 2, width), F32),
            pltpu.VMEM((4, rows, width), BF),
            pltpu.VMEM((2, 2 * TILE, qkv_full.shape[1]), BF),
            pltpu.VMEM((2, hops) + give_block, BF),
            pltpu.VMEM((2, hops) + give_block, BF),
            pltpu.VMEM(give_block, BF),
            pltpu.VMEM(give_block, BF),
            pltpu.VMEM(grad_projected.shape, BF),
            pltpu.VMEM(tokens.shape, BF),
            pltpu.VMEM(grad_middle.shape, F32),
            pltpu.SemaphoreType.DMA((slots,)),
            pltpu.SemaphoreType.DMA((slots,)),
            pltpu.SemaphoreType.DMA((4,)),
            pltpu.SemaphoreType.DMA((2,)),
            pltpu.SemaphoreType.DMA((3,)),
        ],
        cost_estimate=COST,
        compiler_params=pltpu.CompilerParams(
            collective_id=4, has_side_effects=True, vmem_limit_bytes=60 << 20
        ),
    )(grad_projected, qkv_full, qkv_grad, out_grad, tokens, grad_middle, gain, gain_rows)


def normalize(values):
    return values * lax.rsqrt(jnp.mean(values * values, axis=-1, keepdims=True) + EPSILON)


def silu_product(gate_pre, up_pre):
    return gate_pre / (1.0 + jnp.exp(-gate_pre)) * up_pre


def matmul(left, right):
    return jnp.dot(left, right, preferred_element_type=F32)


def rows_inner(left, right):
    return lax.dot_general(left, right, (((0,), (0,)), ((), ())), preferred_element_type=F32)


def cols_inner(left, right):
    return lax.dot_general(left, right, (((1,), (1,)), ((), ())), preferred_element_type=F32)


def row_major(value):
    return with_layout_constraint(value, Layout(major_to_minor=(0, 1)))


def after(value, *earlier):
    return lax.optimization_barrier((value, *earlier))[0]


def swap(value):
    return lax.ppermute(value, "cp", [(0, 1), (1, 0)])


def in_order(place, mine, other, axis):
    return jnp.where(
        place == 0,
        jnp.concatenate([mine, other], axis=axis),
        jnp.concatenate([other, mine], axis=axis),
    )


def on_device(
    tokens,
    seq_lengths,
    attention_gain,
    query_weight,
    key_weight,
    value_weight,
    out_weight,
    feedforward_gain,
    gate_weight,
    up_weight,
    down_weight,
    cotangent,
):
    c = lax.axis_index("cp")
    z = lax.axis_index("fsdp")
    sets = lax.axis_size("cp")
    count = lax.axis_size("fsdp")
    lanes = lax.axis_size("tp")
    slots, local, width = tokens.shape
    share = query_weight.shape[0]
    heads_width = query_weight.shape[1]
    head_count = heads_width // HD
    hidden_width = gate_weight.shape[1] // sets
    rows = sets * local
    seq = rows * lanes
    blocks = row_blocks(seq, sets, local)
    everyone = ("cp", "tp")

    def pick(value, which, axis=0):
        return lax.dynamic_index_in_dim(value, which, axis, keepdims=False)

    length = pick(seq_lengths, c)[None]
    gain_one = attention_gain.astype(F32)
    gain_two = feedforward_gain.astype(F32)

    qkv = jnp.concatenate([query_weight, key_weight, value_weight], axis=1)

    def halves(weight):
        return weight[:, :hidden_width], weight[:, hidden_width:]

    parts = [halves(weight) for weight in (gate_weight, up_weight, down_weight.T)]
    own_wide = [jnp.where(c == 0, low, high) for low, high in parts]
    wide_away = [jnp.where(c == 0, high, low) for low, high in parts]
    token_rows, normed_one, full_qkv, out_half, first_low, first_high = first_gather(
        count, pick(tokens, c), pick(tokens, 1 - c), gain_one[None], qkv, out_weight.T,
        own_wide, wide_away,
    )
    token_rows = token_rows.reshape(rows, width)
    normed_one = normed_one.reshape(seq, width)
    full_qkv = full_qkv.reshape(width, 3 * heads_width)

    out_half, cotangent = after((out_half, cotangent), full_qkv)
    cotangents = lax.all_gather(cotangent, everyone, axis=0).reshape(
        sets, lanes, slots, local, width
    )
    full_out = in_order(c, out_half[:, None], swap(out_half)[:, None], 1)
    full_out = full_out.reshape(width, heads_width)
    up_hop = [(i, i + 1) for i in range(count - 1)]
    down_hop = [(i, i - 1) for i in range(1, count)]
    second_low = lax.ppermute(first_low, "fsdp", up_hop)
    second_high = lax.ppermute(first_high, "fsdp", down_hop)
    cosine_table, sine_table = tables(seq)
    projected = matmul(normed_one, full_qkv)
    context, q_heads, k_heads, v_heads, level = attention(
        blocks, head_count, length, projected, cosine_table, sine_table
    )
    part = cols_inner(context, full_out).astype(BF)

    middle, middle_home, normed_two, full_gate, full_up, full_down = second_gather(
        count, part.reshape(lanes, rows, width), token_rows, gain_two[None], own_wide,
        first_low, first_high, second_low, second_high,
    )
    normed_two = normed_two.reshape(sets * seq, width)
    full_gate, full_up, full_down = (
        full.reshape(width, hidden_width) for full in (full_gate, full_up, full_down)
    )
    t = lax.axis_index("tp")
    cotangents_all = cotangents.reshape(sets * seq, width)
    cotangent_rows = pick(pick(cotangents, t, 1), c, 1).reshape(rows, width)
    gate_pre = matmul(normed_two, full_gate)
    up_pre = matmul(normed_two, full_up)
    hidden_exact, silu_back = jax.vjp(silu_product, gate_pre, up_pre)
    hidden = hidden_exact.astype(BF)

    def blocks_of(gradient):
        gradient = row_major(gradient.astype(BF))
        return gradient.reshape(count, width // count, hidden_width)

    down_blocks = blocks_of(BRANCH * rows_inner(cotangents_all, hidden))
    def leaving(hop, low, high):
        leaving_up = pick(down_blocks, jnp.minimum(z + count - hop, count - 1))
        leaving_down = pick(down_blocks, jnp.maximum(z - count + hop, 0))
        if hop > 1:
            leaving_up = (leaving_up.astype(F32) + low.astype(F32)).astype(BF)
            leaving_down = (leaving_down.astype(F32) + high.astype(F32)).astype(BF)
        return leaving_up, leaving_down

    def sent(hop, leaving_up, leaving_down):
        return (
            lax.ppermute(leaving_up, "fsdp", up_hop[:hop]),
            lax.ppermute(leaving_down, "fsdp", down_hop[count - 1 - hop :]),
        )

    gone = leaving(1, None, None)
    for hop in range(2, count - 1):
        gone = leaving(hop, *sent(hop - 1, *gone))
    grad_hidden = BRANCH * matmul(cotangents_all, full_down)
    grad_gate_exact, grad_up_exact = silu_back(grad_hidden)
    grad_gate_pre = grad_gate_exact.astype(BF)
    grad_up_pre = grad_up_exact.astype(BF)
    gate_part = lax.optimization_barrier(cols_inner(grad_gate_pre, full_gate).astype(BF))
    grad_normed_two = gate_part.astype(F32) + cols_inner(grad_up_pre, full_up)
    gate_blocks = blocks_of(rows_inner(normed_two, grad_gate_pre))
    up_blocks = blocks_of(rows_inner(normed_two, grad_up_pre))
    part = grad_normed_two.astype(BF).reshape(sets, lanes, slots, local, width)
    part, gone = lax.optimization_barrier((part, gone))
    grad_middle, grad_attention, gain_two_rows, pair_up, pair_down, feedforward = first_sum(
        count, part, gate_blocks, up_blocks, hidden, middle, cotangent_rows, gain_two[None],
        full_down,
    )
    grad_attention = grad_attention.reshape(seq, width)

    if count > 1:
        if count > 2:
            arrived = after(sent(count - 2, *gone), grad_attention)
            gone = leaving(count - 1, *arrived)
        leaving_up, leaving_down = after(gone, grad_attention)
        low = [lax.ppermute(pair_up, "fsdp", up_hop), lax.ppermute(leaving_up, "fsdp", up_hop)]
        high = [
            lax.ppermute(pair_down, "fsdp", down_hop), lax.ppermute(leaving_down, "fsdp", down_hop),
        ]
        low = [low[0][0], low[0][1], low[1]]
        high = [high[0][0], high[0][1], high[1]]

    def own_share(which, gradient):
        total = pick(gradient, z).astype(F32)
        if count > 1:
            total = total + low[which].astype(F32) + high[which].astype(F32)
        return total.reshape(sets, share, hidden_width)

    def halved(total):
        return pick(total, c), pick(total, 1 - c).astype(BF)

    gate_kept, gate_given = halved(own_share(0, gate_blocks))
    up_kept, up_given = halved(own_share(1, up_blocks))
    pair_given = jnp.stack([gate_given, up_given])
    pair_got = swap(pair_given).astype(F32)
    grad_gate = in_order(c, gate_kept, pair_got[0], 1)
    grad_up = in_order(c, up_kept, pair_got[1], 1)

    out_pieces = row_major(rows_inner(grad_attention, context).astype(BF))
    out_pieces = out_pieces.reshape(count, sets, share, heads_width)
    out_other = swap(pick(out_pieces, 1 - c, 1))
    out_pieces = (pick(out_pieces, c, 1).astype(F32) + out_other.astype(F32)).astype(BF)
    grad_context = row_major(matmul(grad_attention, full_out).astype(BF))
    feedforward = lax.psum_scatter(feedforward, everyone, scatter_dimension=0, tiled=True)
    feedforward = feedforward.reshape(slots, local, width)
    output = (middle_home + BRANCH * feedforward.astype(F32)).astype(BF)
    grad_projected = attention_back(
        blocks, head_count, length, grad_context, q_heads, k_heads, v_heads, level,
        cosine_table, sine_table,
    )
    grad_projected = after(grad_projected, out_other, pair_given)
    grad_qkv = row_major(rows_inner(normed_one, grad_projected).astype(BF))
    if count > 1:
        low[2], high[2] = after((low[2], high[2]), grad_qkv)
    down_kept, down_given = halved(own_share(2, down_blocks))
    grad_qkv, down_given = lax.optimization_barrier((grad_qkv, down_given))
    grad_down = in_order(c, down_kept, swap(down_given).astype(F32), 1).T
    grad_qkv, grad_out, grad_tokens, gain_sums = last_sum(
        count, grad_projected, full_qkv, grad_qkv.reshape(count, sets, share, 3 * heads_width), out_pieces,
        token_rows, grad_middle, gain_one[None], gain_two_rows,
    )
    return (
        output,
        grad_tokens,
        grad_qkv[:, :heads_width],
        grad_qkv[:, heads_width : 2 * heads_width],
        grad_qkv[:, 2 * heads_width :],
        grad_out.T,
        gain_sums[0],
        grad_gate,
        grad_up,
        grad_down,
        gain_sums[1],
    )


def solution(mesh):
    in_specs = (
        P("fsdp", ("cp", "tp"), None),
        P("fsdp"),
        P(),
        P(("fsdp", "cp"), "tp"),
        P(("fsdp", "cp"), "tp"),
        P(("fsdp", "cp"), "tp"),
        P("tp", ("fsdp", "cp")),
        P(),
        P(("fsdp", "cp"), "tp"),
        P(("fsdp", "cp"), "tp"),
        P("tp", ("fsdp", "cp")),
        P("fsdp", ("cp", "tp"), None),
    )
    out_specs = (
        P("fsdp", ("cp", "tp"), None),
        P("fsdp", ("cp", "tp"), None),
        P(("fsdp", "cp"), "tp"),
        P(("fsdp", "cp"), "tp"),
        P(("fsdp", "cp"), "tp"),
        P("tp", ("fsdp", "cp")),
        P(),
        P(("fsdp", "cp"), "tp"),
        P(("fsdp", "cp"), "tp"),
        P("tp", ("fsdp", "cp")),
        P(),
    )
    return jax.shard_map(
        on_device, mesh=mesh, in_specs=in_specs, out_specs=out_specs, check_vma=False
    )
```

```python
import functools
import math

import jax
import jax.numpy as jnp
import numpy as np
from jax import lax
from jax.experimental import pallas as pl
from jax.experimental.layout import Layout, with_layout_constraint
from jax.experimental.pallas import tpu as pltpu
from jax.sharding import PartitionSpec as P

HD = 64
EPSILON = 1e-05
BRANCH = 1.4 / math.sqrt(40.0)
BF = jnp.bfloat16
F32 = jnp.float32
TILE = 128
QUERY_ROWS = 512


def turned(values, cosine, sine):
    lane = lax.broadcasted_iota(jnp.int32, values.shape, 1)
    partner = jnp.where(
        lane % HD < HD // 2,
        pltpu.roll(values, TILE - HD // 2, 1),
        pltpu.roll(values, HD // 2, 1),
    )
    return values * cosine + partner * sine


def row_blocks(seq, sets, local):
    lanes = seq // sets // local
    return [
        ((t * sets + h) * local, (h * lanes + t) * local)
        for t in range(lanes)
        for h in range(sets)
    ]


def key_mask(length, first, rows, columns):
    place = first + lax.broadcasted_iota(jnp.int32, (rows, columns), 0)
    return place < length


def scores_of(keys, queries, length, first_query):
    raw = lax.dot_general(keys, queries, (((1,), (1,)), ((), ())), preferred_element_type=F32)
    key_place = lax.broadcasted_iota(jnp.int32, raw.shape, 0)
    query_place = first_query + lax.broadcasted_iota(jnp.int32, raw.shape, 1)
    return jnp.where((key_place <= query_place) & (key_place < length), raw, -1e30)


def attention_kernel(
    blocks, length_ref, projected, cosine, sine, context, q_heads, k_heads, v_heads, level, kept
):
    heads, seq, _ = q_heads.shape
    local = seq // len(blocks)
    length = length_ref[0]
    for gathered, ordered in blocks:
        source, target = pl.ds(gathered, local), pl.ds(ordered, local)
        for tile in range(-(-3 * heads // 2)):
            width = min(TILE, 3 * heads * HD - tile * TILE)
            values = projected[source, tile * TILE : tile * TILE + width]
            if tile * 2 < 2 * heads:
                values = turned(values, cosine[target, :], sine[target, :])
            for which in range(width // HD):
                index = tile * 2 + which
                piece = values[:, which * HD : (which + 1) * HD]
                if index < heads:
                    q_heads[index, target, :] = (piece * (1.0 / math.sqrt(HD))).astype(BF)
                elif index < 2 * heads:
                    k_heads[index - heads, target, :] = piece.astype(BF)
                else:
                    v_heads[index - 2 * heads, target, :] = piece.astype(BF)

    def one_head(head, carry):
        for first in range(0, seq, QUERY_ROWS):
            most = first + QUERY_ROWS
            queries = q_heads[head, first:most, :]
            keys = k_heads[head, :most, :]
            values = v_heads[head, :most, :]
            scores = scores_of(keys, queries, length, first)
            top = jnp.max(scores, axis=0, keepdims=True)
            exponent = jnp.exp(scores - top)
            total = jnp.sum(exponent, axis=0, keepdims=True)
            probabilities = exponent.astype(BF)
            level[head, :, first:most] = top + jnp.log(total)
            mixed = lax.dot_general(
                values, probabilities, (((0,), (0,)), ((), ())), preferred_element_type=F32
            )
            kept[head, first:most, :] = (mixed * (1.0 / total)).T.astype(BF)
        return carry

    lax.fori_loop(0, heads, one_head, 0, unroll=True)
    for gathered, ordered in blocks:
        source, target = pl.ds(ordered, local), pl.ds(gathered, local)
        for head in range(0, heads, 2):
            parts = [kept[index, source, :] for index in range(head, min(head + 2, heads))]
            joined = parts[0] if len(parts) == 1 else jnp.concatenate(parts, axis=1)
            context[target, head * HD : head * HD + joined.shape[1]] = joined


def attention(blocks, heads, length, projected, cosine, sine):
    seq = projected.shape[0]
    per_head = jax.ShapeDtypeStruct((heads, seq, HD), BF)
    vmem = pl.BlockSpec(memory_space=pltpu.VMEM)
    return pl.pallas_call(
        functools.partial(attention_kernel, blocks),
        out_shape=(
            jax.ShapeDtypeStruct((seq, heads * HD), BF),
            per_head,
            per_head,
            per_head,
            jax.ShapeDtypeStruct((heads, 1, seq), F32),
        ),
        in_specs=[pl.BlockSpec(memory_space=pltpu.SMEM), vmem, vmem, vmem],
        out_specs=(vmem,) * 5,
        scratch_shapes=[pltpu.VMEM((heads, seq, HD), BF)],
        compiler_params=pltpu.CompilerParams(vmem_limit_bytes=48 << 20),
        cost_estimate=pl.CostEstimate(
            flops=4 * heads * seq * seq * HD, transcendentals=heads * seq * seq, bytes_accessed=20 << 20
        ),
    )(length, projected, cosine, sine)


def attention_back_kernel(
    blocks, length_ref, grad_context, q_heads, k_heads, v_heads, level, cosine, sine,
    grad_projected, g_heads, dq, dk, dv,
):
    heads, seq, _ = q_heads.shape
    local = seq // len(blocks)
    length = length_ref[0]
    for gathered, ordered in blocks:
        source, target = pl.ds(gathered, local), pl.ds(ordered, local)
        for head in range(heads):
            g_heads[head, target, :] = grad_context[source, head * HD : (head + 1) * HD]

    def one_head(head, carry):
        keys_turned = k_heads[head].T
        for first in reversed(range(0, seq, QUERY_ROWS)):
            most = first + QUERY_ROWS
            queries = q_heads[head, first:most, :]
            upstream = g_heads[head, first:most, :]
            keys = k_heads[head, :most, :]
            values = v_heads[head, :most, :]
            scores = scores_of(keys, queries, length, first)
            probabilities = jnp.exp(scores - level[head, :, first:most])
            grad_probabilities = lax.dot_general(
                values, upstream, (((1,), (1,)), ((), ())), preferred_element_type=F32
            )
            weighted = probabilities * grad_probabilities
            balance = jnp.sum(weighted, axis=0, keepdims=True)
            grad_scores = (weighted - probabilities * balance).astype(BF)
            grad_keys = jnp.dot(grad_scores, queries, preferred_element_type=F32)
            grad_values = jnp.dot(
                probabilities.astype(BF), upstream, preferred_element_type=F32
            )
            if most == seq:
                dk[head, :, :] = grad_keys
                dv[head, :, :] = grad_values
            else:
                dk[head, :most, :] += grad_keys
                dv[head, :most, :] += grad_values
            grad_queries = jnp.dot(
                keys_turned[:, :most], grad_scores, preferred_element_type=F32
            )
            dq[head, first:most, :] = grad_queries.T * (1.0 / math.sqrt(HD))
        return carry

    lax.fori_loop(0, heads, one_head, 0, unroll=True)
    sources = [dq] * heads + [dk] * heads + [dv] * heads
    for gathered, ordered in blocks:
        source, target = pl.ds(ordered, local), pl.ds(gathered, local)
        for tile in range(-(-3 * heads // 2)):
            indices = range(tile * 2, min(tile * 2 + 2, 3 * heads))
            parts = [sources[index][index % heads, source, :] for index in indices]
            joined = parts[0] if len(parts) == 1 else jnp.concatenate(parts, axis=1)
            if tile * 2 < 2 * heads:
                joined = turned(joined, cosine[source, :], -sine[source, :])
            grad_projected[target, tile * TILE : tile * TILE + joined.shape[1]] = joined.astype(BF)


def attention_back(blocks, heads, length, grad_context, q_heads, k_heads, v_heads, level, cosine, sine):
    seq = grad_context.shape[0]
    vmem = pl.BlockSpec(memory_space=pltpu.VMEM)
    return pl.pallas_call(
        functools.partial(attention_back_kernel, blocks),
        out_shape=jax.ShapeDtypeStruct((seq, 3 * heads * HD), BF),
        in_specs=[pl.BlockSpec(memory_space=pltpu.SMEM)] + [vmem] * 7,
        out_specs=vmem,
        scratch_shapes=[
            pltpu.VMEM((heads, seq, HD), BF),
            pltpu.VMEM((heads, seq, HD), F32),
            pltpu.VMEM((heads, seq, HD), F32),
            pltpu.VMEM((heads, seq, HD), F32),
        ],
        compiler_params=pltpu.CompilerParams(vmem_limit_bytes=56 << 20),
        cost_estimate=pl.CostEstimate(
            flops=10 * heads * seq * seq * HD, transcendentals=heads * seq * seq, bytes_accessed=20 << 20
        ),
    )(length, grad_context, q_heads, k_heads, v_heads, level, cosine, sine)


def tables(seq):
    step = np.arange(HD // 2, dtype=np.float32)
    frequency = np.power(np.float32(10000.0), np.float32(-2.0) * step / np.float32(HD))
    angle = np.arange(seq, dtype=np.float32)[:, None] * frequency[None, :]
    cosine, sine = np.cos(angle), np.sin(angle)
    signed = np.concatenate([-sine, sine, -sine, sine], axis=1)
    return jnp.asarray(np.tile(cosine, (1, 4))), jnp.asarray(signed)


COST = pl.CostEstimate(flops=0, transcendentals=0, bytes_accessed=300 << 20)
MESH = pl.DeviceIdType.MESH


def greet(count):
    barrier = pltpu.get_barrier_semaphore()
    z, c, t = lax.axis_index("fsdp"), lax.axis_index("cp"), lax.axis_index("tp")

    def hello(**place):
        pl.semaphore_signal(barrier, inc=1, device_id=place, device_id_type=MESH)

    hello(cp=1 - c)
    hello(tp=t + 1 - 2 * (t % 2))
    hello(tp=(t + 2) % 4)
    pl.when(z > 0)(lambda: hello(fsdp=z - 1))
    pl.when(z < count - 1)(lambda: hello(fsdp=z + 1))
    peers = 3 + jnp.minimum(z, 1) + jnp.minimum(count - 1 - z, 1)
    pl.semaphore_wait(barrier, peers)


class Mail:
    def __init__(self, send, recv):
        self.send, self.recv, self.used, self.open = send, recv, 0, []

    def slot(self):
        self.used += 1
        return self.used - 1

    def copy(self, slot, source, target, **place):
        return pltpu.make_async_remote_copy(
            src_ref=source,
            dst_ref=target,
            send_sem=self.send.at[slot],
            recv_sem=self.recv.at[slot],
            device_id=place,
            device_id_type=MESH,
        )

    def start(self, slot, source, target, when=None, **place):
        made = self.copy(slot, source, target, **place)
        if when is None:
            made.start()
        else:
            pl.when(when)(made.start)
        self.open.append((made, when))

    def arrive(self, slot, target, when=None, **place):
        made = self.copy(slot, target, target, **place)
        if when is None:
            made.wait_recv()
        else:
            pl.when(when)(made.wait_recv)

    def finish(self):
        for made, when in self.open:
            if when is None:
                made.wait_send()
            else:
                pl.when(when)(made.wait_send)


class Stage:
    def __init__(self, pieces, stage, sems):
        self.made = []
        for k, (source, target, when) in enumerate(pieces):
            self.made.append(
                (
                    pltpu.make_async_copy(source, stage.at[k], sems.at[0, k]),
                    pltpu.make_async_copy(stage.at[k], target, sems.at[1, k]),
                    when,
                )
            )

    def begin(self):
        for copy, _, when in self.made:
            copy.start() if when is None else pl.when(when)(copy.start)

    def turn(self):
        for first, second, when in self.made:

            def on(first=first, second=second):
                first.wait()
                second.start()

            on() if when is None else pl.when(when)(on)

    def end(self):
        for _, copy, when in self.made:
            copy.wait() if when is None else pl.when(when)(copy.wait)


class Line:
    def __init__(self, mail, count, own, at, ready=()):
        self.mail, self.count, self.own, self.at = mail, count, own, at
        self.ready = ready
        self.z = lax.axis_index("fsdp")
        self.up = [mail.slot() for _ in range(count)]
        self.down = [mail.slot() for _ in range(count)]

    def has_low(self, hop):
        return self.z >= hop

    def has_high(self, hop):
        return self.z <= self.count - 1 - hop

    def send(self, hop):
        z, count, mail = self.z, self.count, self.mail
        low, high = jnp.maximum(z - hop + 1, 0), jnp.minimum(z + hop - 1, count - 1)
        from_low = from_high = self.own
        if hop > 1:
            from_low, from_high = self.at(low), self.at(high)
        if 0 < hop - 1 <= len(self.ready):
            from_low, from_high = self.ready[hop - 2]
        mail.start(
            self.up[hop], from_low, self.at(low),
            when=(z >= hop - 1) & (z < count - 1), fsdp=jnp.minimum(z + 1, count - 1),
        )
        mail.start(
            self.down[hop], from_high, self.at(high),
            when=(z <= count - hop) & (z > 0), fsdp=jnp.maximum(z - 1, 0),
        )

    def arrive(self, hop):
        z, count = self.z, self.count
        self.mail.arrive(
            self.up[hop], self.at(jnp.maximum(z - hop, 0)), when=self.has_low(hop), fsdp=z
        )
        self.mail.arrive(
            self.down[hop], self.at(jnp.minimum(z + hop, count - 1)), when=self.has_high(hop), fsdp=z
        )


    def keep(self):
        z, count = self.z, self.count
        made = [(self.own, self.at(z), None)]
        for index, (low, high) in enumerate(self.ready):
            hop = index + 1
            made.append((low, self.at(jnp.maximum(z - hop, 0)), self.has_low(hop)))
            made.append((high, self.at(jnp.minimum(z + hop, count - 1)), self.has_high(hop)))
        return made


class Across:
    def __init__(self, line, own, mine_at, other_at):
        self.line, self.own, self.mine_at, self.other_at = line, own, mine_at, other_at
        self.c = lax.axis_index("cp")
        self.low = [line.mail.slot() for _ in range(line.count)]
        self.high = [line.mail.slot() for _ in range(line.count)]

    def send(self, hop):
        line, mail = self.line, self.line.mail
        z, count, other = line.z, line.count, 1 - self.c
        if hop == 0:
            mail.start(self.low[0], self.own, self.mine_at(z), cp=other)
            return
        low, high = jnp.maximum(z - hop, 0), jnp.minimum(z + hop, count - 1)
        mail.start(self.low[hop], self.mine_at(low), self.mine_at(low), when=line.has_low(hop), cp=other)
        mail.start(self.high[hop], self.mine_at(high), self.mine_at(high), when=line.has_high(hop), cp=other)

    def arrive(self, hop):
        line, mail = self.line, self.line.mail
        z, count, other = line.z, line.count, 1 - self.c
        if hop == 0:
            mail.arrive(self.low[0], self.other_at(z), cp=other)
            return
        low, high = jnp.maximum(z - hop, 0), jnp.minimum(z + hop, count - 1)
        mail.arrive(self.low[hop], self.other_at(low), when=line.has_low(hop), cp=other)
        mail.arrive(self.high[hop], self.other_at(high), when=line.has_high(hop), cp=other)


def first_gather_kernel(
    count, tokens, tokens_away, gain, qkv, turned_out,
    wide_0, wide_1, wide_2, away_0, away_1, away_2,
    token_rows, normed_full, qkv_full, out_half, low_pair, high_pair,
    landed, normed, wide_landed, qkv_stage, out_stage,
    send, recv, local, qkv_local, out_local,
):
    z, c, t = lax.axis_index("fsdp"), lax.axis_index("cp"), lax.axis_index("tp")
    beside, yonder = t + 1 - 2 * (t % 2), (t + 2) % 4
    low, high = low_pair.at[0], high_pair.at[0]
    wide, wide_away = (wide_0, wide_1, wide_2), (away_0, away_1, away_2)
    mail = Mail(send, recv)
    greet(count)
    stage_qkv = Stage([(qkv, qkv_full.at[z, c], None)], qkv_stage, qkv_local)
    stage_out = Stage([(turned_out, out_half.at[z], None)], out_stage, out_local)
    kept = []

    heads = Line(mail, count, qkv, lambda j: qkv_full.at[j, c])
    heads_across = Across(
        heads, qkv, lambda j: qkv_full.at[j, c], lambda j: qkv_full.at[j, 1 - c]
    )
    outs = Line(mail, count, turned_out, lambda j: out_half.at[j])
    wide_up, wide_down, wide_x = ([mail.slot() for _ in wide] for _ in range(3))
    rows_x = mail.slot()
    rows_y = [mail.slot() for _ in range(2)]
    rows_core = [mail.slot() for _ in range(4)]

    mail.start(rows_x, tokens_away, landed, cp=1 - c)
    heads.send(1)

    def rows_out(source, side, half):
        def one(place):
            rows = source[place, :]
            token_rows[half, place, :] = rows
            normed[half, place, :] = (normalize(rows.astype(F32)) * gain[...]).astype(BF)

        in_pieces(source.shape[0], one)
        mail.start(rows_y[side], normed.at[half], normed_full.at[t, half], tp=yonder)
        mail.start(rows_core[side], normed.at[half], normed_full.at[t, half], tp=beside)

    stage_qkv.begin()
    stage_out.begin()
    rows_out(tokens, 0, c)
    stage_qkv.turn()
    stage_out.turn()
    mail.arrive(rows_x, landed, cp=1 - c)
    heads_across.send(0)
    rows_out(landed, 1, 1 - c)
    kept.append(pltpu.make_async_copy(normed, normed_full.at[t], local.at[2]))
    kept[-1].start()

    def rows_on(k, half):
        mail.arrive(rows_y[k], normed_full.at[yonder, half], tp=yonder)
        mail.start(
            rows_core[2 + k], normed_full.at[yonder, half], normed_full.at[yonder, half], tp=beside
        )

    for hop in range(1, count):
        heads.arrive(hop)
        if hop + 1 < count:
            heads.send(hop + 1)
        heads_across.send(hop)
        if hop == 1:
            rows_on(0, c)
            rows_on(1, 1 - c)
            outs.send(1)
        if hop == min(2, count - 1):
            for k, piece in enumerate(wide):
                mail.start(
                    wide_up[k], piece, low.at[k], when=z < count - 1, fsdp=jnp.minimum(z + 1, count - 1)
                )
                mail.start(wide_down[k], piece, high.at[k], when=z > 0, fsdp=jnp.maximum(z - 1, 0))
    for k, piece in enumerate(wide_away):
        mail.start(wide_x[k], piece, wide_landed.at[k], cp=1 - c)
    for hop in range(1, count):
        outs.arrive(hop)
        if hop + 1 < count:
            outs.send(hop + 1)
    for hop in range(count):
        heads_across.arrive(hop)
    mail.arrive(rows_core[0], normed_full.at[beside, c], tp=beside)
    mail.arrive(rows_core[1], normed_full.at[beside, 1 - c], tp=beside)
    far = (beside + 2) % 4
    mail.arrive(rows_core[2], normed_full.at[far, c], tp=beside)
    mail.arrive(rows_core[3], normed_full.at[far, 1 - c], tp=beside)
    for k in range(len(wide)):
        mail.arrive(wide_x[k], wide_landed.at[k], cp=1 - c)
    for pair, place in ((low_pair, 1), (high_pair, 3)):
        kept.append(pltpu.make_async_copy(wide_landed, pair.at[1], local.at[place]))
        kept[-1].start()
    for k in range(len(wide)):
        mail.arrive(wide_up[k], low.at[k], when=z > 0, fsdp=z)
        mail.arrive(wide_down[k], high.at[k], when=z < count - 1, fsdp=z)
    for copy in kept:
        copy.wait()
    stage_qkv.end()
    stage_out.end()
    mail.finish()


def first_gather(count, tokens, tokens_away, gain, qkv, turned_out, wide, wide_away):
    slots = 6 * count + 16
    anywhere = pl.BlockSpec(memory_space=pl.ANY)
    vmem = pl.BlockSpec(memory_space=pltpu.VMEM)
    pair = (2,) + tokens.shape
    wide_shape = (3,) + wide[0].shape
    return pl.pallas_call(
        functools.partial(first_gather_kernel, count),
        out_shape=(
            jax.ShapeDtypeStruct(pair, BF),
            jax.ShapeDtypeStruct((4,) + pair, BF),
            jax.ShapeDtypeStruct((count, 2) + qkv.shape, BF),
            jax.ShapeDtypeStruct((count,) + turned_out.shape, BF),
            jax.ShapeDtypeStruct((2,) + wide_shape, BF),
            jax.ShapeDtypeStruct((2,) + wide_shape, BF),
        ),
        in_specs=[vmem, anywhere, vmem] + [anywhere] * 8,
        out_specs=(vmem,) + (anywhere,) * 5,
        scratch_shapes=[
            pltpu.VMEM(tokens.shape, BF),
            pltpu.VMEM(pair, BF),
            pltpu.VMEM(wide_shape, BF),
            pltpu.VMEM((1,) + qkv.shape, BF),
            pltpu.VMEM((1,) + turned_out.shape, BF),
            pltpu.SemaphoreType.DMA((slots,)),
            pltpu.SemaphoreType.DMA((slots,)),
            pltpu.SemaphoreType.DMA((4,)),
            pltpu.SemaphoreType.DMA((2, 1)),
            pltpu.SemaphoreType.DMA((2, 1)),
        ],
        cost_estimate=COST,
        compiler_params=pltpu.CompilerParams(
            collective_id=1, has_side_effects=True, vmem_limit_bytes=60 << 20
        ),
    )(tokens, tokens_away, gain, qkv, turned_out, *wide, *wide_away)


def in_pieces(rows, body, size=16):
    if rows % size:
        body(pl.ds(0, rows))
        return
    lax.fori_loop(0, rows // size, lambda i, carry: (body(pl.ds(i * size, size)), carry)[1], 0)


class Spread:
    def __init__(self, mail, own, at):
        self.mail, self.own, self.at = mail, own, at
        self.c, self.t = lax.axis_index("cp"), lax.axis_index("tp")
        self.beside, self.yonder = self.t + 1 - 2 * (self.t % 2), (self.t + 2) % 4
        self.x = [mail.slot() for _ in range(3)]
        self.y = [mail.slot() for _ in range(3)]
        self.core = {}

    def to_core(self, c_is_own, t_is_own, piece):
        slot = self.core[c_is_own, t_is_own, piece] = self.mail.slot()
        c = self.c if c_is_own else 1 - self.c
        t = self.t if t_is_own else self.yonder
        source = self.own(piece) if c_is_own and t_is_own else self.at(c, t, piece)
        self.mail.start(slot, source, self.at(c, t, piece), tp=self.beside)

    def begin(self, piece):
        c, t = self.c, self.t
        if piece == 0:
            self.mail.start(self.x[0], self.own(0), self.at(c, t, 0), cp=1 - c)
        else:
            self.mail.start(self.y[0], self.own(1), self.at(c, t, 1), tp=self.yonder)
            self.mail.start(self.x[1], self.own(1), self.at(c, t, 1), cp=1 - c)
            self.mail.start(self.y[1], self.own(0), self.at(c, t, 0), tp=self.yonder)
        self.to_core(True, True, piece)

    def turn(self):
        c, t, mail, yonder = self.c, self.t, self.mail, self.yonder
        mail.arrive(self.x[0], self.at(1 - c, t, 0), cp=1 - c)
        mail.start(self.y[2], self.at(1 - c, t, 0), self.at(1 - c, t, 0), tp=yonder)
        self.to_core(False, True, 0)
        mail.arrive(self.y[0], self.at(c, yonder, 1), tp=yonder)
        mail.start(self.x[2], self.at(c, yonder, 1), self.at(c, yonder, 1), cp=1 - c)
        self.to_core(True, False, 1)

    def end(self):
        c, t, mail, yonder = self.c, self.t, self.mail, self.yonder
        mail.arrive(self.x[1], self.at(1 - c, t, 1), cp=1 - c)
        self.to_core(False, True, 1)
        mail.arrive(self.y[1], self.at(c, yonder, 0), tp=yonder)
        self.to_core(True, False, 0)
        mail.arrive(self.x[2], self.at(1 - c, yonder, 1), cp=1 - c)
        self.to_core(False, False, 1)
        mail.arrive(self.y[2], self.at(1 - c, yonder, 0), tp=yonder)
        self.to_core(False, False, 0)
        far = (self.beside + 2) % 4
        for (c_is_own, t_is_own, piece), slot in self.core.items():
            place = self.at(
                c if c_is_own else 1 - c, self.beside if t_is_own else far, piece
            )
            mail.arrive(slot, place, tp=self.beside)


def second_gather_kernel(
    count, part, tokens, gain, wide_0, wide_1, wide_2,
    first_low, first_high, second_low, second_high, *refs
):
    hops_mine, hops_other = min(2, count - 1), 1
    wide = (wide_0, wide_1, wide_2)
    wide_other = [first_low.at[1, which] for which in range(3)]
    ready_mine = [first_low.at[0], first_high.at[0], second_low.at[0], second_high.at[0]]
    ready_mine = ready_mine[: 2 * hops_mine]
    ready_other = [second_low.at[1], second_high.at[1]]
    middle, middle_home, normed_full, gate_full, up_full, down_full = refs[:6]
    own, from_core, to_yonder, from_yonder, normed, stage, send, recv, local, local_line = refs[6:]
    c, t = lax.axis_index("cp"), lax.axis_index("tp")
    rows = tokens.shape[0]
    half = rows // 2
    mail = Mail(send, recv)
    greet(count)

    mine, other = [], []
    for which, full in enumerate((gate_full, up_full, down_full)):
        for lines, side, piece, ready in (
            (mine, c, wide, ready_mine), (other, 1 - c, wide_other, ready_other),
        ):
            arrived = [
                (ready[2 * hop].at[which], ready[2 * hop + 1].at[which])
                for hop in range(len(ready) // 2)
            ]
            lines.append(
                Line(
                    mail, count, piece[which],
                    lambda j, full=full, side=side: full.at[j, side], arrived,
                )
            )
    summed = TensorSum(mail, part, own, from_core, to_yonder, from_yonder, local)
    spread = Spread(
        mail, lambda piece: normed.at[piece], lambda c, t, piece: normed_full.at[piece, t, c]
    )

    summed.begin()
    placing = Stage([piece for line in mine + other for piece in line.keep()], stage, local_line)
    placing.begin()

    def send_hop(lines, hop):
        for line in lines:
            if hop < count:
                line.send(hop)

    def arrive_hop(lines, hop):
        for line in lines:
            if hop < count:
                line.arrive(hop)

    send_hop(other, hops_other + 1)
    send_hop(mine, hops_mine + 1)
    summed.turn()
    placing.turn()
    for piece in range(2):
        summed.arrive(piece)

        def norm(place, piece=piece):
            row = pl.ds(place.start + piece * half, place.size)
            values = tokens[row, :].astype(F32) + BRANCH * summed.rows(row)
            middle[row, :] = values
            normed[piece, place, :] = (normalize(values) * gain[...]).astype(BF)

        in_pieces(half, norm)
        spread.begin(piece)
    keep_normed = pltpu.make_async_copy(normed, normed_full.at[:, t, c], local.at[0])
    keep_normed.start()
    home = mail.slot()
    stay, go = pl.ds(c * half, half), pl.ds((1 - c) * half, half)
    keep_home = pltpu.make_async_copy(middle.at[stay], middle_home.at[c], local.at[1])
    keep_home.start()
    spread.turn()
    mail.start(home, middle.at[go], middle_home.at[c], cp=1 - c)
    for step in range(1, count):
        hop = hops_other + step
        if hop < count:
            for line_other, line_mine in zip(other, mine):
                line_other.arrive(hop)
                if hop + 1 < count:
                    line_other.send(hop + 1)
                if hops_mine + step < count:
                    line_mine.arrive(hops_mine + step)
                    if hops_mine + step + 1 < count:
                        line_mine.send(hops_mine + step + 1)
        if step == 1:
            spread.end()
    if count == 1:
        spread.end()
    mail.arrive(home, middle_home.at[1 - c], cp=1 - c)
    keep_home.wait()
    keep_normed.wait()
    placing.end()
    mail.finish()


def second_gather(count, part, tokens, gain, wide, first_low, first_high, second_low, second_high):
    slots = 12 * count + 24
    rows, width = tokens.shape
    anywhere = pl.BlockSpec(memory_space=pl.ANY)
    vmem = pl.BlockSpec(memory_space=pltpu.VMEM)
    full = jax.ShapeDtypeStruct((count, 2) + wide[0].shape, BF)
    return pl.pallas_call(
        functools.partial(second_gather_kernel, count),
        out_shape=(
            jax.ShapeDtypeStruct((rows, width), F32),
            jax.ShapeDtypeStruct((2, rows // 2, width), F32),
            jax.ShapeDtypeStruct((2, 4, 2, rows // 2, width), BF),
            full,
            full,
            full,
        ),
        in_specs=[anywhere, vmem, vmem] + [anywhere] * 7,
        out_specs=(vmem,) + (anywhere,) * 5,
        scratch_shapes=[
            pltpu.VMEM((2, rows, width), BF),
            pltpu.VMEM((2, rows, width), BF),
            pltpu.VMEM((rows, width), BF),
            pltpu.VMEM((rows, width), BF),
            pltpu.VMEM((2, rows // 2, width), BF),
            pltpu.VMEM((24,) + wide[0].shape, BF),
            pltpu.SemaphoreType.DMA((slots,)),
            pltpu.SemaphoreType.DMA((slots,)),
            pltpu.SemaphoreType.DMA((2,)),
            pltpu.SemaphoreType.DMA((2, 24)),
        ],
        cost_estimate=COST,
        compiler_params=pltpu.CompilerParams(
            collective_id=2, has_side_effects=True, vmem_limit_bytes=60 << 20
        ),
    )(part, tokens, gain, *wide, first_low, first_high, second_low, second_high)


class TensorSum:
    def __init__(self, mail, part, own, from_core, to_yonder, from_yonder, local):
        self.mail, self.part, self.own, self.from_core = mail, part, own, from_core
        self.to_yonder, self.from_yonder, self.local = to_yonder, from_yonder, local
        self.t = t = lax.axis_index("tp")
        self.beside, self.yonder = t + 1 - 2 * (t % 2), (t + 2) % 4
        self.core = [mail.slot() for _ in range(2)]
        self.across = [mail.slot() for _ in range(2)]
        self.half = from_yonder.shape[0] // 2

    def begin(self):
        part, far = self.part, (self.beside + 2) % 4
        self.mail.start(self.core[1], part.at[far], self.from_core.at[1], tp=self.beside)
        self.mail.start(self.core[0], part.at[self.beside], self.from_core.at[0], tp=self.beside)
        self.kept = [
            pltpu.make_async_copy(part.at[self.yonder], self.own.at[1], self.local.at[0]),
            pltpu.make_async_copy(part.at[self.t], self.own.at[0], self.local.at[1]),
        ]
        for copy in self.kept:
            copy.start()

    def turn(self):
        own, from_core = self.own, self.from_core
        self.kept[0].wait()
        self.mail.arrive(self.core[1], from_core.at[1], tp=self.beside)
        for piece in range(2):

            def add(place, piece=piece):
                place = pl.ds(place.start + piece * self.half, place.size)
                self.to_yonder[place, :] = (
                    own[1, place, :].astype(F32) + from_core[1, place, :].astype(F32)
                ).astype(BF)

            in_pieces(self.half, add)
            block = pl.ds(piece * self.half, self.half)
            self.mail.start(
                self.across[piece], self.to_yonder.at[block], self.from_yonder.at[block],
                tp=self.yonder,
            )
        self.kept[1].wait()
        self.mail.arrive(self.core[0], from_core.at[0], tp=self.beside)

    def arrive(self, piece):
        block = pl.ds(piece * self.half, self.half)
        self.mail.arrive(self.across[piece], self.from_yonder.at[block], tp=self.yonder)

    def rows(self, row):
        return (
            self.own[0, row, :].astype(F32)
            + self.from_core[0, row, :].astype(F32)
            + self.from_yonder[row, :].astype(F32)
        )


class Drain:
    def __init__(self, mail, count, fill, total, landed):
        self.mail, self.count, self.fill, self.total, self.landed = mail, count, fill, total, landed
        self.z = lax.axis_index("fsdp")
        self.slots = [[mail.slot() for _ in range(count)] for _ in range(2)]

    def sends(self, hop, up):
        z, count = self.z, self.count
        return (z <= hop - 1) & (z < count - 1) if up else (z >= count - hop) & (z > 0)

    def gets(self, hop, up):
        z, count = self.z, self.count
        return (z >= 1) & (z <= hop) if up else (z <= count - 2) & (z >= count - 1 - hop)

    def block(self, hop, up):
        z, count = self.z, self.count
        return jnp.minimum(z + count - hop, count - 1) if up else jnp.maximum(z - count + hop, 0)

    def arrive(self, hop):
        for side, up in enumerate((True, False)):
            self.mail.arrive(
                self.slots[side][hop], self.landed(side, hop), when=self.gets(hop, up), fsdp=self.z
            )

    def gather(self, hop):
        for side, up in enumerate((True, False)):
            target = self.total(side, hop)

            def work(side=side, up=up, target=target):
                self.fill(hop, up, self.block(hop, up), target)
                if hop > 1:

                    def add():
                        landed = self.landed(side, hop - 1)

                        def one(place):
                            target[place, :] = (
                                target[place, :].astype(F32) + landed[place, :].astype(F32)
                            ).astype(BF)

                        in_pieces(target.shape[0], one)

                    pl.when(self.gets(hop - 1, up))(add)

            pl.when(self.sends(hop, up))(work)

    def send(self, hop):
        z, count = self.z, self.count
        for side, up in enumerate((True, False)):
            to = jnp.minimum(z + 1, count - 1) if up else jnp.maximum(z - 1, 0)
            self.mail.start(
                self.slots[side][hop], self.total(side, hop), self.landed(side, hop),
                when=self.sends(hop, up), fsdp=to,
            )


def norm_back(values, gain, upstream):
    scale = lax.rsqrt(jnp.mean(values * values, axis=-1, keepdims=True) + EPSILON)
    norm = values * scale
    scaled = upstream * gain
    mean = jnp.mean(scaled * norm, axis=-1, keepdims=True)
    return scale * (scaled - norm * mean), upstream * norm


def first_sum_kernel(
    count, part, gate_grad, up_grad, hidden, middle_from, cotangent_from, down_from, gain,
    grad_middle, attention_full, gain_rows, leaving_up, leaving_down, feedforward,
    own, from_core, first, second, grad_attention, totals, landed, hidden_rows, product, middle, cotangent, down,
    send, recv, local, hidden_local, loads_local,
):
    z, c, t = lax.axis_index("fsdp"), lax.axis_index("cp"), lax.axis_index("tp")
    beside, yonder = t + 1 - 2 * (t % 2), (t + 2) % 4
    far = (beside + 2) % 4
    half = middle.shape[0] // 2
    width = middle.shape[1]
    loads = [
        pltpu.make_async_copy(source, target, loads_local.at[k])
        for k, (source, target) in enumerate(
            ((down_from, down), (middle_from, middle), (cotangent_from, cotangent))
        )
    ]
    mail = Mail(send, recv)
    greet(count)
    last = count - 1

    def fill_from(which):
        def fill(hop, up, j, target):
            copy = pltpu.make_async_copy((gate_grad, up_grad)[which].at[j], target, local.at[4])
            copy.start()
            copy.wait()

        return fill

    drains = [
        Drain(
            mail, count, fill_from(which),
            lambda side, hop, which=which: (
                (leaving_up, leaving_down)[side].at[which] if hop == last else totals.at[side, hop - 1, which]
            ),
            lambda side, hop, which=which: landed.at[side, hop - 1, which],
        )
        for which in range(2)
    ]

    core = {}
    mine = {}
    order = ((0, 0), (0, 1), (1, 0), (1, 1))
    for index, (c_own, t_own) in enumerate(order):
        block_c = c if c_own else 1 - c
        core[c_own, t_own] = mail.slot()
        mail.start(
            core[c_own, t_own], part.at[:, beside if t_own else far, block_c],
            from_core.at[c_own, t_own], tp=beside,
        )
        mine[c_own, t_own] = pltpu.make_async_copy(
            part.at[:, t if t_own else yonder, block_c], own.at[c_own, t_own], local.at[index]
        )
        mine[c_own, t_own].start()
    if last > 1:
        for drain in drains:
            drain.gather(1)
            drain.send(1)

    block_rows = product.shape[1]
    blocks = hidden.shape[0] // block_rows

    def hidden_copy(block):
        return pltpu.make_async_copy(
            hidden.at[pl.ds(block * block_rows, block_rows)], hidden_rows.at[block % 2],
            hidden_local.at[0, block % 2],
        )

    def product_copy(block):
        return pltpu.make_async_copy(
            product.at[block % 2], feedforward.at[pl.ds(block * block_rows, block_rows)],
            hidden_local.at[1, block % 2],
        )

    def product_block(block):
        hidden_copy(block).wait()
        if block + 1 < blocks:
            hidden_copy(block + 1).start()
        if block > 1:
            product_copy(block - 2).wait()

        def one(k, carry):
            columns = pl.ds(pl.multiple_of(k * 2 * TILE, 2 * TILE), 2 * TILE)
            value = lax.dot_general(
                hidden_rows[block % 2], down[columns, :], (((1,), (1,)), ((), ())),
                preferred_element_type=F32,
            )
            product[block % 2, :, columns] = value.astype(BF)
            return carry

        lax.fori_loop(0, width // (2 * TILE), one, 0)
        product_copy(block).start()

    hidden_copy(0).start()
    for copy in loads:
        copy.start()
    loads[0].wait()
    product_block(0)

    quarter = half // 2
    quarters = [(piece, pl.ds(side * quarter, quarter)) for piece in range(2) for side in range(2)]
    x_first = [[mail.slot() for _ in range(2)] for _ in quarters]
    y_second = [mail.slot() for _ in quarters]
    ring_y = [mail.slot() for _ in quarters]
    ring_core = [mail.slot() for _ in quarters]
    ring_far = [mail.slot() for _ in quarters]

    def core_add(c_own, t_own, piece, rows):
        def one(place):
            row = pl.ds(rows.start + place.start, place.size)
            own[c_own, t_own, piece, row, :] = (
                own[c_own, t_own, piece, row, :].astype(F32)
                + from_core[c_own, t_own, piece, row, :].astype(F32)
            ).astype(BF)

        in_pieces(quarter, one)

    for t_own in (0, 1):
        mine[0, t_own].wait()
        mail.arrive(core[0, t_own], from_core.at[0, t_own], tp=beside)
    for k, (piece, rows) in enumerate(quarters):
        for t_own in (0, 1):
            core_add(0, t_own, piece, rows)
            mail.start(
                x_first[k][t_own], own.at[0, t_own, piece, rows], first.at[k, t_own], cp=1 - c
            )
    for t_own in (0, 1):
        mine[1, t_own].wait()
        mail.arrive(core[1, t_own], from_core.at[1, t_own], tp=beside)

    def add_first(k, t_own):
        piece, rows = quarters[k]

        def one(place):
            row = pl.ds(rows.start + place.start, place.size)
            own[1, t_own, piece, row, :] = (
                own[1, t_own, piece, row, :].astype(F32)
                + from_core[1, t_own, piece, row, :].astype(F32)
                + first[k, t_own, place, :].astype(F32)
            ).astype(BF)

        in_pieces(quarter, one)

    gain_rows[...] = jnp.zeros_like(gain_rows)
    loads[1].wait()
    loads[2].wait()

    def finish(k):
        piece, rows = quarters[k]
        mail.arrive(y_second[k], second.at[k], tp=yonder)

        def back(place):
            local_row = pl.ds(rows.start + place.start, place.size)
            row = pl.ds(piece * half + rows.start + place.start, place.size)
            summed = own[1, 1, piece, local_row, :].astype(F32) + second[k, place, :].astype(F32)
            grad, products = norm_back(middle[row, :], gain[...], summed)
            grad = cotangent[row, :].astype(F32) + grad
            grad_middle[row, :] = grad
            grad_attention[piece, local_row, :] = (BRANCH * grad).astype(BF)
            gain_rows[...] += jnp.sum(products, axis=0, keepdims=True)

        in_pieces(quarter, back)
        source = grad_attention.at[piece, rows]
        mail.start(ring_y[k], source, attention_full.at[t, piece, rows], tp=yonder)
        mail.start(ring_core[k], source, attention_full.at[t, piece, rows], tp=beside)

    def z_hop(hop):
        for drain in drains:
            drain.arrive(hop - 1)
            drain.gather(hop)
            drain.send(hop)

    for k, (piece, rows) in enumerate(quarters):
        mail.arrive(x_first[k][0], first.at[k, 0], cp=1 - c)
        add_first(k, 0)
        mail.start(y_second[k], own.at[1, 0, piece, rows], second.at[k], tp=yonder)
        mail.arrive(x_first[k][1], first.at[k, 1], cp=1 - c)
        add_first(k, 1)
        if k > 0:
            finish(k - 1)
        if k == 2 and last > 2:
            z_hop(2)
        product_block(k + 1)
    finish(len(quarters) - 1)
    for block in range(len(quarters) + 1, blocks):
        product_block(block)
    keep = pltpu.make_async_copy(grad_attention, attention_full.at[t], local.at[0])
    keep.start()
    for hop in range(3, last):
        z_hop(hop)
    for k, (piece, rows) in enumerate(quarters):
        arrived = attention_full.at[yonder, piece, rows]
        mail.arrive(ring_y[k], arrived, tp=yonder)
        mail.start(ring_far[k], arrived, arrived, tp=beside)
    for k, (piece, rows) in enumerate(quarters):
        mail.arrive(ring_core[k], attention_full.at[beside, piece, rows], tp=beside)
        mail.arrive(ring_far[k], attention_full.at[far, piece, rows], tp=beside)
    for drain in drains:
        if last > 1:
            drain.arrive(last - 1)
        if last > 0:
            drain.gather(last)
    keep.wait()
    for block in range(blocks - 2, blocks):
        product_copy(block).wait()
    mail.finish()


def first_sum(count, part, gate_grad, up_grad, hidden, middle, cotangent, gain, down):
    slots = 6 * count + 32
    rows, width = middle.shape
    block = gate_grad.shape[1:]
    anywhere = pl.BlockSpec(memory_space=pl.ANY)
    vmem = pl.BlockSpec(memory_space=pltpu.VMEM)
    hops = max(count - 2, 1)
    return pl.pallas_call(
        functools.partial(first_sum_kernel, count),
        out_shape=(
            jax.ShapeDtypeStruct((rows, width), F32),
            jax.ShapeDtypeStruct((4, 2, rows // 2, width), BF),
            jax.ShapeDtypeStruct((1, width), F32),
            jax.ShapeDtypeStruct((2,) + block, BF),
            jax.ShapeDtypeStruct((2,) + block, BF),
            jax.ShapeDtypeStruct((hidden.shape[0], width), BF),
        ),
        in_specs=[anywhere] * 7 + [vmem],
        out_specs=(vmem, anywhere, vmem, vmem, vmem, anywhere),
        scratch_shapes=[
            pltpu.VMEM((2, 2, 2, rows // 2, width), BF),
            pltpu.VMEM((2, 2, 2, rows // 2, width), BF),
            pltpu.VMEM((4, 2, rows // 4, width), BF),
            pltpu.VMEM((4, rows // 4, width), BF),
            pltpu.VMEM((2, rows // 2, width), BF),
            pltpu.VMEM((2, hops, 2) + block, BF),
            pltpu.VMEM((2, hops, 2) + block, BF),
            pltpu.VMEM((2, hidden.shape[0] // 8, hidden.shape[1]), BF),
            pltpu.VMEM((2, hidden.shape[0] // 8, width), BF),
            pltpu.VMEM((rows, width), F32),
            pltpu.VMEM((rows, width), BF),
            pltpu.VMEM(down.shape, BF),
            pltpu.SemaphoreType.DMA((slots,)),
            pltpu.SemaphoreType.DMA((slots,)),
            pltpu.SemaphoreType.DMA((5,)),
            pltpu.SemaphoreType.DMA((2, 2)),
            pltpu.SemaphoreType.DMA((3,)),
        ],
        cost_estimate=COST,
        compiler_params=pltpu.CompilerParams(
            collective_id=3, has_side_effects=True, vmem_limit_bytes=60 << 20
        ),
    )(part, gate_grad, up_grad, hidden, middle, cotangent, down, gain)


AHEAD = 6


def last_sum_kernel(
    count, projected_from, qkv_full, qkv_grad, out_grad, tokens_from, middle_from, gain, gain_rows,
    qkv_total, out_total, grad_tokens, gain_sums,
    own, from_core, to_yonder, from_yonder, pieces,
    from_x, heads_sum, heads_landed, outs_sum, outs_landed, final_out, gains, gain_line,
    part, weights, give_sum, give_landed, give_own, give_total, grad_projected, tokens, grad_middle,
    send, recv, local, weights_local, loads_local,
):
    z, c, t = lax.axis_index("fsdp"), lax.axis_index("cp"), lax.axis_index("tp")
    beside, yonder = t + 1 - 2 * (t % 2), (t + 2) % 4
    half = tokens.shape[0] // 2
    last = count - 1
    mail = Mail(send, recv)
    greet(count)

    summed = TensorSum(mail, part, own, from_core, to_yonder, from_yonder, local)

    columns = qkv_total.shape[1]
    behind = columns * 5 // 6 // TILE * TILE
    split = -(-behind // (2 * TILE)) * TILE
    parts = [pl.ds(0, split), pl.ds(split, behind - split)]
    late = pl.ds(behind, columns - behind)
    cross = [[[mail.slot() for _ in range(count)] for _ in range(2)] for _ in parts]
    cross_own = [mail.slot() for _ in parts]

    def head_drain(lanes):
        def fill(hop, up, j, target):
            side = 0 if up else 1
            copy = pltpu.make_async_copy(qkv_grad.at[j, c, :, lanes], target, local.at[2])
            copy.start()
            copy.wait()
            arrived = from_x.at[side, hop - 1, :, lanes]

            def one(place):
                target[place, :] = (
                    target[place, :].astype(F32) + arrived[place, :].astype(F32)
                ).astype(BF)

            in_pieces(target.shape[0], one)

        return Drain(
            mail, count, fill,
            lambda side, hop: heads_sum.at[side, hop - 1, :, lanes],
            lambda side, hop: heads_landed.at[side, hop - 1, :, lanes],
        )

    heads = [head_drain(lanes) for lanes in parts]

    def late_fill(side_c):
        def fill(hop, up, j, target):
            copy = pltpu.make_async_copy(qkv_grad.at[j, side_c, :, late], target, local.at[2])
            copy.start()
            copy.wait()

        return fill

    stay = Drain(
        mail, count, late_fill(c),
        lambda side, hop: heads_sum.at[side, hop - 1, :, late],
        lambda side, hop: heads_landed.at[side, hop - 1, :, late],
    )
    give = Drain(
        mail, count, late_fill(1 - c),
        lambda side, hop: give_sum.at[side, hop - 1],
        lambda side, hop: give_landed.at[side, hop - 1],
    )
    give_slot = mail.slot()

    def fill_outs(hop, up, j, target):
        copy = pltpu.make_async_copy(out_grad.at[j], target, local.at[3])
        copy.start()
        copy.wait()

    outs = Drain(
        mail, count, fill_outs,
        lambda side, hop: outs_sum.at[side, hop - 1],
        lambda side, hop: outs_landed.at[side, hop - 1],
    )

    steps = [(hop, k) for hop in range(1, count + 1) for k in range(2)]

    def cross_send(step):
        if step >= len(steps):
            return
        hop, k = steps[step]
        lanes = parts[k]
        if hop == count:
            mail.start(
                cross_own[k], qkv_grad.at[z, 1 - c, :, lanes], from_x.at[0, last, :, lanes], cp=1 - c
            )
            return
        for side, up in enumerate((True, False)):
            mail.start(
                cross[k][side][hop], qkv_grad.at[heads[k].block(hop, up), 1 - c, :, lanes],
                from_x.at[side, hop - 1, :, lanes], when=heads[k].sends(hop, up), cp=1 - c,
            )

    def cross_arrive(hop, k):
        for side, up in enumerate((True, False)):
            mail.arrive(
                cross[k][side][hop], from_x.at[side, hop - 1, :, parts[k]],
                when=heads[k].sends(hop, up), cp=1 - c,
            )

    for step in range(AHEAD):
        cross_send(step)
    early_chains = (outs, give, stay)
    if count > 1:
        for drain in early_chains:
            drain.gather(1)
            drain.send(1)

    wide_block = weights.shape[1]
    blocks = qkv_full.shape[0] // wide_block

    def weights_copy(block, slot):
        return pltpu.make_async_copy(
            qkv_full.at[pl.ds(block * wide_block, wide_block)], weights.at[slot],
            weights_local.at[slot],
        )

    def product(block, carry):
        slot = lax.rem(block, 2)
        weights_copy(block, slot).wait()
        pl.when(block + 1 < blocks)(lambda: weights_copy(block + 1, 1 - slot).start())
        columns = pl.ds(pl.multiple_of(block * wide_block, wide_block), wide_block)
        value = lax.dot_general(
            grad_projected[...], weights[slot], (((1,), (1,)), ((), ())),
            preferred_element_type=F32,
        )
        part[:, :, columns] = value.astype(BF).reshape(part.shape[:2] + (wide_block,))
        return carry

    loads = [
        pltpu.make_async_copy(source, target, loads_local.at[k])
        for k, (source, target) in enumerate(
            (
                (projected_from, grad_projected),
                (tokens_from, tokens),
                (middle_from, grad_middle),
            )
        )
    ]
    weights_copy(0, 0).start()
    for copy in loads:
        copy.start()
    loads[0].wait()
    thirds = [blocks * k // 3 for k in range(4)]

    keep = pltpu.make_async_copy(pieces.at[c], grad_tokens.at[c], local.at[0])
    home = mail.slot()
    gain_x, gain_y, gain_core = mail.slot(), mail.slot(), mail.slot()
    line = Line(mail, count, gain_line.at[z], lambda j: gain_line.at[j])

    def finish_rows():
        loads[1].wait()
        loads[2].wait()
        gains[0, 0:1, :] = jnp.zeros_like(gain_rows)
        gains[0, 1:2, :] = gain_rows[...]
        for piece in range(2):
            summed.arrive(piece)

            def back(place, piece=piece):
                row = pl.ds(place.start + piece * half, place.size)
                grad, rows = norm_back(tokens[row, :].astype(F32), gain[...], summed.rows(row))
                pieces[piece, place, :] = (grad_middle[row, :] + grad).astype(BF)
                gains[0, 0:1, :] += jnp.sum(rows, axis=0, keepdims=True)

            in_pieces(half, back)
        mail.start(home, pieces.at[1 - c], grad_tokens.at[c], cp=1 - c)
        keep.start()
        mail.start(gain_core, gains.at[0], gains.at[1], tp=beside)

    def gain_step(k):
        if k == 0:
            mail.arrive(gain_core, gains.at[1], tp=beside)
            gains[2] = gains[0] + gains[1]
            mail.start(gain_y, gains.at[2], gains.at[3], tp=yonder)
        elif k == 1:
            mail.arrive(gain_y, gains.at[3], tp=yonder)
            gains[4] = gains[2] + gains[3]
            mail.start(gain_x, gains.at[4], gains.at[5], cp=1 - c)
        elif k == 2:
            mail.arrive(gain_x, gains.at[5], cp=1 - c)
            gain_line[z] = gains[4] + gains[5]
            if count > 1:
                line.send(1)
        else:
            hop = k - 2
            line.arrive(hop)
            if hop + 1 < count:
                line.send(hop + 1)

    def outs_hop(hop):
        for drain in early_chains:
            drain.arrive(hop - 1)
            drain.gather(hop)
            drain.send(hop)

    def give_away():
        copy = pltpu.make_async_copy(qkv_grad.at[z, 1 - c, :, late], give_own, local.at[3])
        copy.start()
        copy.wait()
        if count > 1:
            give.arrive(last)

        def one(place):
            total = give_own[place, :].astype(F32)
            for side, up in enumerate((True, False)):
                if count > 1:
                    landed = give.landed(side, last)[place, :].astype(F32)
                    total += jnp.where(give.gets(last, up), landed, 0.0)
            give_total[place, :] = total.astype(BF)

        in_pieces(give_own.shape[0], one)
        mail.start(give_slot, give_total, from_x.at[0, last, :, late], cp=1 - c)

    for step, (hop, k) in enumerate(steps[:-2]):
        if step < 3:
            lax.fori_loop(thirds[step], thirds[step + 1], product, 0)
        if count == 2 and step == 1:
            lax.fori_loop(thirds[2], thirds[3], product, 0)
        if step == 2 or count == 2 and step == 1:
            summed.begin()
        cross_arrive(hop, k)
        cross_send(step + AHEAD)
        if hop > 1:
            heads[k].arrive(hop - 1)
        heads[k].gather(hop)
        heads[k].send(hop)
        if k == 1 and hop + 1 < count:
            outs_hop(hop + 1)
        if step == 2 or count == 2 and step == 1:
            summed.turn()
        if step == 3 or count == 2 and step == 1:
            finish_rows()
        if step == 5 or step == 3 and count == 3:
            gain_step(0)
            gain_step(1)
    if count == 1:
        lax.fori_loop(thirds[0], thirds[3], product, 0)
        summed.begin()
        summed.turn()
        finish_rows()
    if count <= 2:
        gain_step(0)
        gain_step(1)
    gain_step(2)
    give_away()

    own_copy = pltpu.make_async_copy(qkv_grad.at[z, c], from_x.at[1, last], local.at[2])
    own_copy.start()
    out_copy = pltpu.make_async_copy(out_grad.at[z], final_out, local.at[3])
    out_copy.start()
    for k, lanes in enumerate(parts):
        mail.arrive(cross_own[k], from_x.at[0, last, :, lanes], cp=1 - c)
    mail.arrive(give_slot, from_x.at[0, last, :, late], cp=1 - c)
    own_copy.wait()
    out_copy.wait()

    def start_heads(place):
        qkv_total[place, :] = from_x[0, last, place, :].astype(F32) + from_x[
            1, last, place, :
        ].astype(F32)

    in_pieces(qkv_total.shape[0], start_heads)

    def start_outs(place):
        out_total[place, :] = final_out[place, :].astype(F32)

    in_pieces(out_total.shape[0], start_outs)
    for hop in range(1, count):
        gain_step(2 + hop)
    if count > 1:
        chains = [(outs, pl.ds(0, out_total.shape[1]), out_total)]
        chains += [(stay, late, qkv_total)]
        chains += [(heads[k], lanes, qkv_total) for k, lanes in enumerate(parts)]
        for drain, lanes, total in chains:
            drain.arrive(last)
            for side, up in enumerate((True, False)):

                def more(drain=drain, total=total, side=side, lanes=lanes):
                    landed = drain.landed(side, last)

                    def one(place):
                        total[place, lanes] += landed[place, :].astype(F32)

                    in_pieces(total.shape[0], one)

                pl.when(drain.gets(last, up))(more)
    gain_sums[...] = jnp.sum(gain_line[...], axis=0)
    mail.arrive(home, grad_tokens.at[1 - c], cp=1 - c)
    keep.wait()
    mail.finish()


def last_sum(count, grad_projected, qkv_full, qkv_grad, out_grad, tokens, grad_middle, gain, gain_rows):
    slots = 17 * count + 17
    rows, width = tokens.shape
    hops = max(count - 1, 1)
    block, out_block = qkv_grad.shape[2:], out_grad.shape[1:]
    columns = block[1]
    give_block = (block[0], columns - columns * 5 // 6 // TILE * TILE)
    anywhere = pl.BlockSpec(memory_space=pl.ANY)
    vmem = pl.BlockSpec(memory_space=pltpu.VMEM)
    return pl.pallas_call(
        functools.partial(last_sum_kernel, count),
        out_shape=(
            jax.ShapeDtypeStruct(block, F32),
            jax.ShapeDtypeStruct(out_block, F32),
            jax.ShapeDtypeStruct((2, rows // 2, width), BF),
            jax.ShapeDtypeStruct((2, width), F32),
        ),
        in_specs=[anywhere] * 6 + [vmem] * 2,
        out_specs=(vmem, vmem, anywhere, vmem),
        scratch_shapes=[
            pltpu.VMEM((2, rows, width), BF),
            pltpu.VMEM((2, rows, width), BF),
            pltpu.VMEM((rows, width), BF),
            pltpu.VMEM((rows, width), BF),
            pltpu.VMEM((2, rows // 2, width), BF),
            pltpu.VMEM((2, count) + block, BF),
            pltpu.VMEM((2, hops) + block, BF),
            pltpu.VMEM((2, hops) + block, BF),
            pltpu.VMEM((2, hops) + out_block, BF),
            pltpu.VMEM((2, hops) + out_block, BF),
            pltpu.VMEM(out_block, BF),
            pltpu.VMEM((6, 2, width), F32),
            pltpu.VMEM((count, 2, width), F32),
            pltpu.VMEM((4, rows, width), BF),
            pltpu.VMEM((2, 2 * TILE, qkv_full.shape[1]), BF),
            pltpu.VMEM((2, hops) + give_block, BF),
            pltpu.VMEM((2, hops) + give_block, BF),
            pltpu.VMEM(give_block, BF),
            pltpu.VMEM(give_block, BF),
            pltpu.VMEM(grad_projected.shape, BF),
            pltpu.VMEM(tokens.shape, BF),
            pltpu.VMEM(grad_middle.shape, F32),
            pltpu.SemaphoreType.DMA((slots,)),
            pltpu.SemaphoreType.DMA((slots,)),
            pltpu.SemaphoreType.DMA((4,)),
            pltpu.SemaphoreType.DMA((2,)),
            pltpu.SemaphoreType.DMA((3,)),
        ],
        cost_estimate=COST,
        compiler_params=pltpu.CompilerParams(
            collective_id=4, has_side_effects=True, vmem_limit_bytes=60 << 20
        ),
    )(grad_projected, qkv_full, qkv_grad, out_grad, tokens, grad_middle, gain, gain_rows)


def normalize(values):
    return values * lax.rsqrt(jnp.mean(values * values, axis=-1, keepdims=True) + EPSILON)


def silu_product(gate_pre, up_pre):
    return gate_pre / (1.0 + jnp.exp(-gate_pre)) * up_pre


def matmul(left, right):
    return jnp.dot(left, right, preferred_element_type=F32)


def rows_inner(left, right):
    return lax.dot_general(left, right, (((0,), (0,)), ((), ())), preferred_element_type=F32)


def cols_inner(left, right):
    return lax.dot_general(left, right, (((1,), (1,)), ((), ())), preferred_element_type=F32)


def row_major(value):
    return with_layout_constraint(value, Layout(major_to_minor=(0, 1)))


def after(value, *earlier):
    return lax.optimization_barrier((value, *earlier))[0]


def swap(value):
    return lax.ppermute(value, "cp", [(0, 1), (1, 0)])


def in_order(place, mine, other, axis):
    return jnp.where(
        place == 0,
        jnp.concatenate([mine, other], axis=axis),
        jnp.concatenate([other, mine], axis=axis),
    )


def on_device(
    tokens,
    seq_lengths,
    attention_gain,
    query_weight,
    key_weight,
    value_weight,
    out_weight,
    feedforward_gain,
    gate_weight,
    up_weight,
    down_weight,
    cotangent,
):
    c = lax.axis_index("cp")
    z = lax.axis_index("fsdp")
    sets = lax.axis_size("cp")
    count = lax.axis_size("fsdp")
    lanes = lax.axis_size("tp")
    slots, local, width = tokens.shape
    share = query_weight.shape[0]
    heads_width = query_weight.shape[1]
    head_count = heads_width // HD
    hidden_width = gate_weight.shape[1] // sets
    rows = sets * local
    seq = rows * lanes
    blocks = row_blocks(seq, sets, local)
    everyone = ("cp", "tp")

    def pick(value, which, axis=0):
        return lax.dynamic_index_in_dim(value, which, axis, keepdims=False)

    length = pick(seq_lengths, c)[None]
    gain_one = attention_gain.astype(F32)
    gain_two = feedforward_gain.astype(F32)

    qkv = jnp.concatenate([query_weight, key_weight, value_weight], axis=1)

    def halves(weight):
        return weight[:, :hidden_width], weight[:, hidden_width:]

    parts = [halves(weight) for weight in (gate_weight, up_weight, down_weight.T)]
    own_wide = [jnp.where(c == 0, low, high) for low, high in parts]
    wide_away = [jnp.where(c == 0, high, low) for low, high in parts]
    token_rows, normed_one, full_qkv, out_half, first_low, first_high = first_gather(
        count, pick(tokens, c), pick(tokens, 1 - c), gain_one[None], qkv, out_weight.T,
        own_wide, wide_away,
    )
    token_rows = token_rows.reshape(rows, width)
    normed_one = normed_one.reshape(seq, width)
    full_qkv = full_qkv.reshape(width, 3 * heads_width)

    out_half, cotangent = after((out_half, cotangent), full_qkv)
    cotangents = lax.all_gather(cotangent, everyone, axis=0).reshape(
        sets, lanes, slots, local, width
    )
    full_out = in_order(c, out_half[:, None], swap(out_half)[:, None], 1)
    full_out = full_out.reshape(width, heads_width)
    up_hop = [(i, i + 1) for i in range(count - 1)]
    down_hop = [(i, i - 1) for i in range(1, count)]
    second_low = lax.ppermute(first_low, "fsdp", up_hop)
    second_high = lax.ppermute(first_high, "fsdp", down_hop)
    cosine_table, sine_table = tables(seq)
    projected = matmul(normed_one, full_qkv)
    context, q_heads, k_heads, v_heads, level = attention(
        blocks, head_count, length, projected, cosine_table, sine_table
    )
    part = cols_inner(context, full_out).astype(BF)

    middle, middle_home, normed_two, full_gate, full_up, full_down = second_gather(
        count, part.reshape(lanes, rows, width), token_rows, gain_two[None], own_wide,
        first_low, first_high, second_low, second_high,
    )
    normed_two = normed_two.reshape(sets * seq, width)
    full_gate, full_up, full_down = (
        full.reshape(width, hidden_width) for full in (full_gate, full_up, full_down)
    )
    t = lax.axis_index("tp")
    cotangents_all = cotangents.reshape(sets * seq, width)
    cotangent_rows = pick(pick(cotangents, t, 1), c, 1).reshape(rows, width)
    gate_pre = matmul(normed_two, full_gate)
    up_pre = matmul(normed_two, full_up)
    hidden_exact, silu_back = jax.vjp(silu_product, gate_pre, up_pre)
    hidden = hidden_exact.astype(BF)

    def blocks_of(gradient):
        gradient = row_major(gradient.astype(BF))
        return gradient.reshape(count, width // count, hidden_width)

    down_blocks = blocks_of(BRANCH * rows_inner(cotangents_all, hidden))
    def leaving(hop, low, high):
        leaving_up = pick(down_blocks, jnp.minimum(z + count - hop, count - 1))
        leaving_down = pick(down_blocks, jnp.maximum(z - count + hop, 0))
        if hop > 1:
            leaving_up = (leaving_up.astype(F32) + low.astype(F32)).astype(BF)
            leaving_down = (leaving_down.astype(F32) + high.astype(F32)).astype(BF)
        return leaving_up, leaving_down

    def sent(hop, leaving_up, leaving_down):
        return (
            lax.ppermute(leaving_up, "fsdp", up_hop[:hop]),
            lax.ppermute(leaving_down, "fsdp", down_hop[count - 1 - hop :]),
        )

    gone = leaving(1, None, None)
    for hop in range(2, count - 1):
        gone = leaving(hop, *sent(hop - 1, *gone))
    grad_hidden = BRANCH * matmul(cotangents_all, full_down)
    grad_gate_exact, grad_up_exact = silu_back(grad_hidden)
    grad_gate_pre = grad_gate_exact.astype(BF)
    grad_up_pre = grad_up_exact.astype(BF)
    gate_part = lax.optimization_barrier(cols_inner(grad_gate_pre, full_gate).astype(BF))
    grad_normed_two = gate_part.astype(F32) + cols_inner(grad_up_pre, full_up)
    gate_blocks = blocks_of(rows_inner(normed_two, grad_gate_pre))
    up_blocks = blocks_of(rows_inner(normed_two, grad_up_pre))
    part = grad_normed_two.astype(BF).reshape(sets, lanes, slots, local, width)
    part, gone = lax.optimization_barrier((part, gone))
    grad_middle, grad_attention, gain_two_rows, pair_up, pair_down, feedforward = first_sum(
        count, part, gate_blocks, up_blocks, hidden, middle, cotangent_rows, gain_two[None],
        full_down,
    )
    grad_attention = grad_attention.reshape(seq, width)

    if count > 1:
        if count > 2:
            arrived = after(sent(count - 2, *gone), grad_attention)
            gone = leaving(count - 1, *arrived)
        leaving_up, leaving_down = after(gone, grad_attention)
        low = [lax.ppermute(pair_up, "fsdp", up_hop), lax.ppermute(leaving_up, "fsdp", up_hop)]
        high = [
            lax.ppermute(pair_down, "fsdp", down_hop), lax.ppermute(leaving_down, "fsdp", down_hop),
        ]
        low = [low[0][0], low[0][1], low[1]]
        high = [high[0][0], high[0][1], high[1]]

    def own_share(which, gradient):
        total = pick(gradient, z).astype(F32)
        if count > 1:
            total = total + low[which].astype(F32) + high[which].astype(F32)
        return total.reshape(sets, share, hidden_width)

    def halved(total):
        return pick(total, c), pick(total, 1 - c).astype(BF)

    gate_kept, gate_given = halved(own_share(0, gate_blocks))
    up_kept, up_given = halved(own_share(1, up_blocks))
    pair_given = jnp.stack([gate_given, up_given])
    pair_got = swap(pair_given).astype(F32)
    grad_gate = in_order(c, gate_kept, pair_got[0], 1)
    grad_up = in_order(c, up_kept, pair_got[1], 1)

    out_pieces = row_major(rows_inner(grad_attention, context).astype(BF))
    out_pieces = out_pieces.reshape(count, sets, share, heads_width)
    out_other = swap(pick(out_pieces, 1 - c, 1))
    out_pieces = (pick(out_pieces, c, 1).astype(F32) + out_other.astype(F32)).astype(BF)
    grad_context = row_major(matmul(grad_attention, full_out).astype(BF))
    feedforward = lax.psum_scatter(feedforward, everyone, scatter_dimension=0, tiled=True)
    feedforward = feedforward.reshape(slots, local, width)
    output = (middle_home + BRANCH * feedforward.astype(F32)).astype(BF)
    grad_projected = attention_back(
        blocks, head_count, length, grad_context, q_heads, k_heads, v_heads, level,
        cosine_table, sine_table,
    )
    grad_projected = after(grad_projected, out_other, pair_given)
    grad_qkv = row_major(rows_inner(normed_one, grad_projected).astype(BF))
    if count > 1:
        low[2], high[2] = after((low[2], high[2]), grad_qkv)
    down_kept, down_given = halved(own_share(2, down_blocks))
    grad_qkv, down_given = lax.optimization_barrier((grad_qkv, down_given))
    grad_down = in_order(c, down_kept, swap(down_given).astype(F32), 1).T
    grad_qkv, grad_out, grad_tokens, gain_sums = last_sum(
        count, grad_projected, full_qkv, grad_qkv.reshape(count, sets, share, 3 * heads_width), out_pieces,
        token_rows, grad_middle, gain_one[None], gain_two_rows,
    )
    return (
        output,
        grad_tokens,
        grad_qkv[:, :heads_width],
        grad_qkv[:, heads_width : 2 * heads_width],
        grad_qkv[:, 2 * heads_width :],
        grad_out.T,
        gain_sums[0],
        grad_gate,
        grad_up,
        grad_down,
        gain_sums[1],
    )


def solution(mesh):
    in_specs = (
        P("fsdp", ("cp", "tp"), None),
        P("fsdp"),
        P(),
        P(("fsdp", "cp"), "tp"),
        P(("fsdp", "cp"), "tp"),
        P(("fsdp", "cp"), "tp"),
        P("tp", ("fsdp", "cp")),
        P(),
        P(("fsdp", "cp"), "tp"),
        P(("fsdp", "cp"), "tp"),
        P("tp", ("fsdp", "cp")),
        P("fsdp", ("cp", "tp"), None),
    )
    out_specs = (
        P("fsdp", ("cp", "tp"), None),
        P("fsdp", ("cp", "tp"), None),
        P(("fsdp", "cp"), "tp"),
        P(("fsdp", "cp"), "tp"),
        P(("fsdp", "cp"), "tp"),
        P("tp", ("fsdp", "cp")),
        P(),
        P(("fsdp", "cp"), "tp"),
        P(("fsdp", "cp"), "tp"),
        P("tp", ("fsdp", "cp")),
        P(),
    )
    return jax.shard_map(
        on_device, mesh=mesh, in_specs=in_specs, out_specs=out_specs, check_vma=False
    )
```

```python
import functools
import math

import jax
import jax.numpy as jnp
import numpy as np
from jax import lax
from jax.experimental import pallas as pl
from jax.experimental.layout import Layout, with_layout_constraint
from jax.experimental.pallas import tpu as pltpu
from jax.sharding import PartitionSpec as P

HD = 64
EPSILON = 1e-05
BRANCH = 1.4 / math.sqrt(40.0)
BF = jnp.bfloat16
F32 = jnp.float32
TILE = 128
QUERY_ROWS = 512


def turned(values, cosine, sine):
    lane = lax.broadcasted_iota(jnp.int32, values.shape, 1)
    partner = jnp.where(
        lane % HD < HD // 2,
        pltpu.roll(values, TILE - HD // 2, 1),
        pltpu.roll(values, HD // 2, 1),
    )
    return values * cosine + partner * sine


def row_blocks(seq, sets, local):
    lanes = seq // sets // local
    return [
        ((t * sets + h) * local, (h * lanes + t) * local)
        for t in range(lanes)
        for h in range(sets)
    ]


def key_mask(length, first, rows, columns):
    place = first + lax.broadcasted_iota(jnp.int32, (rows, columns), 0)
    return place < length


def scores_of(keys, queries, length, first_query):
    raw = lax.dot_general(keys, queries, (((1,), (1,)), ((), ())), preferred_element_type=F32)
    key_place = lax.broadcasted_iota(jnp.int32, raw.shape, 0)
    query_place = first_query + lax.broadcasted_iota(jnp.int32, raw.shape, 1)
    return jnp.where((key_place <= query_place) & (key_place < length), raw, -1e30)


def attention_kernel(
    blocks, length_ref, projected, cosine, sine, context, q_heads, k_heads, v_heads, level, kept
):
    heads, seq, _ = q_heads.shape
    local = seq // len(blocks)
    length = length_ref[0]
    for gathered, ordered in blocks:
        source, target = pl.ds(gathered, local), pl.ds(ordered, local)
        for tile in range(-(-3 * heads // 2)):
            width = min(TILE, 3 * heads * HD - tile * TILE)
            values = projected[source, tile * TILE : tile * TILE + width]
            if tile * 2 < 2 * heads:
                values = turned(values, cosine[target, :], sine[target, :])
            for which in range(width // HD):
                index = tile * 2 + which
                piece = values[:, which * HD : (which + 1) * HD]
                if index < heads:
                    q_heads[index, target, :] = (piece * (1.0 / math.sqrt(HD))).astype(BF)
                elif index < 2 * heads:
                    k_heads[index - heads, target, :] = piece.astype(BF)
                else:
                    v_heads[index - 2 * heads, target, :] = piece.astype(BF)

    def one_head(head, carry):
        for first in range(0, seq, QUERY_ROWS):
            most = first + QUERY_ROWS
            queries = q_heads[head, first:most, :]
            keys = k_heads[head, :most, :]
            values = v_heads[head, :most, :]
            scores = scores_of(keys, queries, length, first)
            top = jnp.max(scores, axis=0, keepdims=True)
            exponent = jnp.exp(scores - top)
            total = jnp.sum(exponent, axis=0, keepdims=True)
            probabilities = exponent.astype(BF)
            level[head, :, first:most] = top + jnp.log(total)
            mixed = lax.dot_general(
                values, probabilities, (((0,), (0,)), ((), ())), preferred_element_type=F32
            )
            kept[head, first:most, :] = (mixed * (1.0 / total)).T.astype(BF)
        return carry

    lax.fori_loop(0, heads, one_head, 0, unroll=True)
    for gathered, ordered in blocks:
        source, target = pl.ds(ordered, local), pl.ds(gathered, local)
        for head in range(0, heads, 2):
            parts = [kept[index, source, :] for index in range(head, min(head + 2, heads))]
            joined = parts[0] if len(parts) == 1 else jnp.concatenate(parts, axis=1)
            context[target, head * HD : head * HD + joined.shape[1]] = joined


def attention(blocks, heads, length, projected, cosine, sine):
    seq = projected.shape[0]
    per_head = jax.ShapeDtypeStruct((heads, seq, HD), BF)
    vmem = pl.BlockSpec(memory_space=pltpu.VMEM)
    return pl.pallas_call(
        functools.partial(attention_kernel, blocks),
        out_shape=(
            jax.ShapeDtypeStruct((seq, heads * HD), BF),
            per_head,
            per_head,
            per_head,
            jax.ShapeDtypeStruct((heads, 1, seq), F32),
        ),
        in_specs=[pl.BlockSpec(memory_space=pltpu.SMEM), vmem, vmem, vmem],
        out_specs=(vmem,) * 5,
        scratch_shapes=[pltpu.VMEM((heads, seq, HD), BF)],
        compiler_params=pltpu.CompilerParams(vmem_limit_bytes=48 << 20),
        cost_estimate=pl.CostEstimate(
            flops=4 * heads * seq * seq * HD, transcendentals=heads * seq * seq, bytes_accessed=20 << 20
        ),
    )(length, projected, cosine, sine)


def attention_back_kernel(
    blocks, length_ref, grad_context, q_heads, k_heads, v_heads, level, cosine, sine,
    grad_projected, g_heads, dq, dk, dv,
):
    heads, seq, _ = q_heads.shape
    local = seq // len(blocks)
    length = length_ref[0]
    for gathered, ordered in blocks:
        source, target = pl.ds(gathered, local), pl.ds(ordered, local)
        for head in range(heads):
            g_heads[head, target, :] = grad_context[source, head * HD : (head + 1) * HD]

    def one_head(head, carry):
        keys_turned = k_heads[head].T
        for first in reversed(range(0, seq, QUERY_ROWS)):
            most = first + QUERY_ROWS
            queries = q_heads[head, first:most, :]
            upstream = g_heads[head, first:most, :]
            keys = k_heads[head, :most, :]
            values = v_heads[head, :most, :]
            scores = scores_of(keys, queries, length, first)
            probabilities = jnp.exp(scores - level[head, :, first:most])
            grad_probabilities = lax.dot_general(
                values, upstream, (((1,), (1,)), ((), ())), preferred_element_type=F32
            )
            weighted = probabilities * grad_probabilities
            balance = jnp.sum(weighted, axis=0, keepdims=True)
            grad_scores = (weighted - probabilities * balance).astype(BF)
            grad_keys = jnp.dot(grad_scores, queries, preferred_element_type=F32)
            grad_values = jnp.dot(
                probabilities.astype(BF), upstream, preferred_element_type=F32
            )
            if most == seq:
                dk[head, :, :] = grad_keys
                dv[head, :, :] = grad_values
            else:
                dk[head, :most, :] += grad_keys
                dv[head, :most, :] += grad_values
            grad_queries = jnp.dot(
                keys_turned[:, :most], grad_scores, preferred_element_type=F32
            )
            dq[head, first:most, :] = grad_queries.T * (1.0 / math.sqrt(HD))
        return carry

    lax.fori_loop(0, heads, one_head, 0, unroll=True)
    sources = [dq] * heads + [dk] * heads + [dv] * heads
    for gathered, ordered in blocks:
        source, target = pl.ds(ordered, local), pl.ds(gathered, local)
        for tile in range(-(-3 * heads // 2)):
            indices = range(tile * 2, min(tile * 2 + 2, 3 * heads))
            parts = [sources[index][index % heads, source, :] for index in indices]
            joined = parts[0] if len(parts) == 1 else jnp.concatenate(parts, axis=1)
            if tile * 2 < 2 * heads:
                joined = turned(joined, cosine[source, :], -sine[source, :])
            grad_projected[target, tile * TILE : tile * TILE + joined.shape[1]] = joined.astype(BF)


def attention_back(blocks, heads, length, grad_context, q_heads, k_heads, v_heads, level, cosine, sine):
    seq = grad_context.shape[0]
    vmem = pl.BlockSpec(memory_space=pltpu.VMEM)
    return pl.pallas_call(
        functools.partial(attention_back_kernel, blocks),
        out_shape=jax.ShapeDtypeStruct((seq, 3 * heads * HD), BF),
        in_specs=[pl.BlockSpec(memory_space=pltpu.SMEM)] + [vmem] * 7,
        out_specs=vmem,
        scratch_shapes=[
            pltpu.VMEM((heads, seq, HD), BF),
            pltpu.VMEM((heads, seq, HD), F32),
            pltpu.VMEM((heads, seq, HD), F32),
            pltpu.VMEM((heads, seq, HD), F32),
        ],
        compiler_params=pltpu.CompilerParams(vmem_limit_bytes=56 << 20),
        cost_estimate=pl.CostEstimate(
            flops=10 * heads * seq * seq * HD, transcendentals=heads * seq * seq, bytes_accessed=20 << 20
        ),
    )(length, grad_context, q_heads, k_heads, v_heads, level, cosine, sine)


def tables(seq):
    step = np.arange(HD // 2, dtype=np.float32)
    frequency = np.power(np.float32(10000.0), np.float32(-2.0) * step / np.float32(HD))
    angle = np.arange(seq, dtype=np.float32)[:, None] * frequency[None, :]
    cosine, sine = np.cos(angle), np.sin(angle)
    signed = np.concatenate([-sine, sine, -sine, sine], axis=1)
    return jnp.asarray(np.tile(cosine, (1, 4))), jnp.asarray(signed)


COST = pl.CostEstimate(flops=0, transcendentals=0, bytes_accessed=300 << 20)
MESH = pl.DeviceIdType.MESH


def greet(count):
    barrier = pltpu.get_barrier_semaphore()
    z, c, t = lax.axis_index("fsdp"), lax.axis_index("cp"), lax.axis_index("tp")

    def hello(**place):
        pl.semaphore_signal(barrier, inc=1, device_id=place, device_id_type=MESH)

    hello(cp=1 - c)
    hello(tp=t + 1 - 2 * (t % 2))
    hello(tp=(t + 2) % 4)
    pl.when(z > 0)(lambda: hello(fsdp=z - 1))
    pl.when(z < count - 1)(lambda: hello(fsdp=z + 1))
    peers = 3 + jnp.minimum(z, 1) + jnp.minimum(count - 1 - z, 1)
    pl.semaphore_wait(barrier, peers)


class Mail:
    def __init__(self, send, recv):
        self.send, self.recv, self.used, self.open = send, recv, 0, []

    def slot(self):
        self.used += 1
        return self.used - 1

    def copy(self, slot, source, target, **place):
        return pltpu.make_async_remote_copy(
            src_ref=source,
            dst_ref=target,
            send_sem=self.send.at[slot],
            recv_sem=self.recv.at[slot],
            device_id=place,
            device_id_type=MESH,
        )

    def start(self, slot, source, target, when=None, **place):
        made = self.copy(slot, source, target, **place)
        if when is None:
            made.start()
        else:
            pl.when(when)(made.start)
        self.open.append((made, when))

    def arrive(self, slot, target, when=None, **place):
        made = self.copy(slot, target, target, **place)
        if when is None:
            made.wait_recv()
        else:
            pl.when(when)(made.wait_recv)

    def finish(self):
        for made, when in self.open:
            if when is None:
                made.wait_send()
            else:
                pl.when(when)(made.wait_send)


class Stage:
    def __init__(self, pieces, stage, sems):
        self.made = []
        for k, (source, target, when) in enumerate(pieces):
            self.made.append(
                (
                    pltpu.make_async_copy(source, stage.at[k], sems.at[0, k]),
                    pltpu.make_async_copy(stage.at[k], target, sems.at[1, k]),
                    when,
                )
            )

    def begin(self):
        for copy, _, when in self.made:
            copy.start() if when is None else pl.when(when)(copy.start)

    def turn(self):
        for first, second, when in self.made:

            def on(first=first, second=second):
                first.wait()
                second.start()

            on() if when is None else pl.when(when)(on)

    def end(self):
        for _, copy, when in self.made:
            copy.wait() if when is None else pl.when(when)(copy.wait)


class Line:
    def __init__(self, mail, count, own, at, ready=()):
        self.mail, self.count, self.own, self.at = mail, count, own, at
        self.ready = ready
        self.z = lax.axis_index("fsdp")
        self.up = [mail.slot() for _ in range(count)]
        self.down = [mail.slot() for _ in range(count)]

    def has_low(self, hop):
        return self.z >= hop

    def has_high(self, hop):
        return self.z <= self.count - 1 - hop

    def send(self, hop):
        z, count, mail = self.z, self.count, self.mail
        low, high = jnp.maximum(z - hop + 1, 0), jnp.minimum(z + hop - 1, count - 1)
        from_low = from_high = self.own
        if hop > 1:
            from_low, from_high = self.at(low), self.at(high)
        if 0 < hop - 1 <= len(self.ready):
            from_low, from_high = self.ready[hop - 2]
        mail.start(
            self.up[hop], from_low, self.at(low),
            when=(z >= hop - 1) & (z < count - 1), fsdp=jnp.minimum(z + 1, count - 1),
        )
        mail.start(
            self.down[hop], from_high, self.at(high),
            when=(z <= count - hop) & (z > 0), fsdp=jnp.maximum(z - 1, 0),
        )

    def arrive(self, hop):
        z, count = self.z, self.count
        self.mail.arrive(
            self.up[hop], self.at(jnp.maximum(z - hop, 0)), when=self.has_low(hop), fsdp=z
        )
        self.mail.arrive(
            self.down[hop], self.at(jnp.minimum(z + hop, count - 1)), when=self.has_high(hop), fsdp=z
        )


    def keep(self):
        z, count = self.z, self.count
        made = [(self.own, self.at(z), None)]
        for index, (low, high) in enumerate(self.ready):
            hop = index + 1
            made.append((low, self.at(jnp.maximum(z - hop, 0)), self.has_low(hop)))
            made.append((high, self.at(jnp.minimum(z + hop, count - 1)), self.has_high(hop)))
        return made


class Across:
    def __init__(self, line, own, mine_at, other_at):
        self.line, self.own, self.mine_at, self.other_at = line, own, mine_at, other_at
        self.c = lax.axis_index("cp")
        self.low = [line.mail.slot() for _ in range(line.count)]
        self.high = [line.mail.slot() for _ in range(line.count)]

    def send(self, hop):
        line, mail = self.line, self.line.mail
        z, count, other = line.z, line.count, 1 - self.c
        if hop == 0:
            mail.start(self.low[0], self.own, self.mine_at(z), cp=other)
            return
        low, high = jnp.maximum(z - hop, 0), jnp.minimum(z + hop, count - 1)
        mail.start(self.low[hop], self.mine_at(low), self.mine_at(low), when=line.has_low(hop), cp=other)
        mail.start(self.high[hop], self.mine_at(high), self.mine_at(high), when=line.has_high(hop), cp=other)

    def arrive(self, hop):
        line, mail = self.line, self.line.mail
        z, count, other = line.z, line.count, 1 - self.c
        if hop == 0:
            mail.arrive(self.low[0], self.other_at(z), cp=other)
            return
        low, high = jnp.maximum(z - hop, 0), jnp.minimum(z + hop, count - 1)
        mail.arrive(self.low[hop], self.other_at(low), when=line.has_low(hop), cp=other)
        mail.arrive(self.high[hop], self.other_at(high), when=line.has_high(hop), cp=other)


def first_gather_kernel(
    count, tokens_all, gain, qkv, turned_out,
    wide_0, wide_1, wide_2, away_0, away_1, away_2,
    token_rows, normed_full, qkv_full, out_half, low_pair, high_pair,
    tokens, landed, normed, wide_landed, qkv_stage, out_stage,
    send, recv, local, qkv_local, out_local,
):
    z, c, t = lax.axis_index("fsdp"), lax.axis_index("cp"), lax.axis_index("tp")
    beside, yonder = t + 1 - 2 * (t % 2), (t + 2) % 4
    low, high = low_pair.at[0], high_pair.at[0]
    wide, wide_away = (wide_0, wide_1, wide_2), (away_0, away_1, away_2)
    mail = Mail(send, recv)
    greet(count)
    stage_qkv = Stage([(qkv, qkv_full.at[z, c], None)], qkv_stage, qkv_local)
    stage_out = Stage([(turned_out, out_half.at[z], None)], out_stage, out_local)
    kept = []

    heads = Line(mail, count, qkv, lambda j: qkv_full.at[j, c])
    heads_across = Across(
        heads, qkv, lambda j: qkv_full.at[j, c], lambda j: qkv_full.at[j, 1 - c]
    )
    outs = Line(mail, count, turned_out, lambda j: out_half.at[j])
    wide_up, wide_down, wide_x = ([mail.slot() for _ in wide] for _ in range(3))
    rows_x = mail.slot()
    rows_y = [mail.slot() for _ in range(2)]
    rows_core = [mail.slot() for _ in range(4)]

    mail.start(rows_x, tokens_all.at[1 - c], landed, cp=1 - c)
    load = pltpu.make_async_copy(tokens_all.at[c], tokens, local.at[0])
    load.start()
    heads.send(1)

    def rows_out(source, side, half):
        def one(place):
            rows = source[place, :]
            token_rows[half, place, :] = rows
            normed[half, place, :] = (normalize(rows.astype(F32)) * gain[...]).astype(BF)

        in_pieces(source.shape[0], one)
        mail.start(rows_y[side], normed.at[half], normed_full.at[t, half], tp=yonder)
        mail.start(rows_core[side], normed.at[half], normed_full.at[t, half], tp=beside)

    stage_qkv.begin()
    stage_out.begin()
    load.wait()
    rows_out(tokens, 0, c)
    stage_qkv.turn()
    stage_out.turn()
    mail.arrive(rows_x, landed, cp=1 - c)
    heads_across.send(0)
    rows_out(landed, 1, 1 - c)
    kept.append(pltpu.make_async_copy(normed, normed_full.at[t], local.at[2]))
    kept[-1].start()

    def rows_on(k, half):
        mail.arrive(rows_y[k], normed_full.at[yonder, half], tp=yonder)
        mail.start(
            rows_core[2 + k], normed_full.at[yonder, half], normed_full.at[yonder, half], tp=beside
        )

    for hop in range(1, count):
        heads.arrive(hop)
        if hop + 1 < count:
            heads.send(hop + 1)
        heads_across.send(hop)
        if hop == 1:
            rows_on(0, c)
            rows_on(1, 1 - c)
            outs.send(1)
        if hop == min(2, count - 1):
            for k, piece in enumerate(wide):
                mail.start(
                    wide_up[k], piece, low.at[k], when=z < count - 1, fsdp=jnp.minimum(z + 1, count - 1)
                )
                mail.start(wide_down[k], piece, high.at[k], when=z > 0, fsdp=jnp.maximum(z - 1, 0))
    for k, piece in enumerate(wide_away):
        mail.start(wide_x[k], piece, wide_landed.at[k], cp=1 - c)
    for hop in range(1, count):
        outs.arrive(hop)
        if hop + 1 < count:
            outs.send(hop + 1)
    for hop in range(count):
        heads_across.arrive(hop)
    mail.arrive(rows_core[0], normed_full.at[beside, c], tp=beside)
    mail.arrive(rows_core[1], normed_full.at[beside, 1 - c], tp=beside)
    far = (beside + 2) % 4
    mail.arrive(rows_core[2], normed_full.at[far, c], tp=beside)
    mail.arrive(rows_core[3], normed_full.at[far, 1 - c], tp=beside)
    for k in range(len(wide)):
        mail.arrive(wide_x[k], wide_landed.at[k], cp=1 - c)
    for pair, place in ((low_pair, 1), (high_pair, 3)):
        kept.append(pltpu.make_async_copy(wide_landed, pair.at[1], local.at[place]))
        kept[-1].start()
    for k in range(len(wide)):
        mail.arrive(wide_up[k], low.at[k], when=z > 0, fsdp=z)
        mail.arrive(wide_down[k], high.at[k], when=z < count - 1, fsdp=z)
    for copy in kept:
        copy.wait()
    stage_qkv.end()
    stage_out.end()
    mail.finish()


def first_gather(count, tokens, gain, qkv, turned_out, wide, wide_away):
    slots = 6 * count + 16
    anywhere = pl.BlockSpec(memory_space=pl.ANY)
    vmem = pl.BlockSpec(memory_space=pltpu.VMEM)
    pair = (2,) + tokens.shape[1:]
    wide_shape = (3,) + wide[0].shape
    return pl.pallas_call(
        functools.partial(first_gather_kernel, count),
        out_shape=(
            jax.ShapeDtypeStruct(pair, BF),
            jax.ShapeDtypeStruct((4,) + pair, BF),
            jax.ShapeDtypeStruct((count, 2) + qkv.shape, BF),
            jax.ShapeDtypeStruct((count,) + turned_out.shape, BF),
            jax.ShapeDtypeStruct((2,) + wide_shape, BF),
            jax.ShapeDtypeStruct((2,) + wide_shape, BF),
        ),
        in_specs=[anywhere, vmem] + [anywhere] * 8,
        out_specs=(vmem,) + (anywhere,) * 5,
        scratch_shapes=[
            pltpu.VMEM(tokens.shape[1:], BF),
            pltpu.VMEM(tokens.shape[1:], BF),
            pltpu.VMEM(pair, BF),
            pltpu.VMEM(wide_shape, BF),
            pltpu.VMEM((1,) + qkv.shape, BF),
            pltpu.VMEM((1,) + turned_out.shape, BF),
            pltpu.SemaphoreType.DMA((slots,)),
            pltpu.SemaphoreType.DMA((slots,)),
            pltpu.SemaphoreType.DMA((4,)),
            pltpu.SemaphoreType.DMA((2, 1)),
            pltpu.SemaphoreType.DMA((2, 1)),
        ],
        cost_estimate=COST,
        compiler_params=pltpu.CompilerParams(
            collective_id=1, has_side_effects=True, vmem_limit_bytes=60 << 20
        ),
    )(tokens, gain, qkv, turned_out, *wide, *wide_away)


def in_pieces(rows, body, size=16):
    if rows % size:
        body(pl.ds(0, rows))
        return
    lax.fori_loop(0, rows // size, lambda i, carry: (body(pl.ds(i * size, size)), carry)[1], 0)


class Spread:
    def __init__(self, mail, own, at):
        self.mail, self.own, self.at = mail, own, at
        self.c, self.t = lax.axis_index("cp"), lax.axis_index("tp")
        self.beside, self.yonder = self.t + 1 - 2 * (self.t % 2), (self.t + 2) % 4
        self.x = [mail.slot() for _ in range(3)]
        self.y = [mail.slot() for _ in range(3)]
        self.core = {}

    def to_core(self, c_is_own, t_is_own, piece):
        slot = self.core[c_is_own, t_is_own, piece] = self.mail.slot()
        c = self.c if c_is_own else 1 - self.c
        t = self.t if t_is_own else self.yonder
        source = self.own(piece) if c_is_own and t_is_own else self.at(c, t, piece)
        self.mail.start(slot, source, self.at(c, t, piece), tp=self.beside)

    def begin(self, piece):
        c, t = self.c, self.t
        if piece == 0:
            self.mail.start(self.x[0], self.own(0), self.at(c, t, 0), cp=1 - c)
        else:
            self.mail.start(self.y[0], self.own(1), self.at(c, t, 1), tp=self.yonder)
            self.mail.start(self.x[1], self.own(1), self.at(c, t, 1), cp=1 - c)
            self.mail.start(self.y[1], self.own(0), self.at(c, t, 0), tp=self.yonder)
        self.to_core(True, True, piece)

    def turn(self):
        c, t, mail, yonder = self.c, self.t, self.mail, self.yonder
        mail.arrive(self.x[0], self.at(1 - c, t, 0), cp=1 - c)
        mail.start(self.y[2], self.at(1 - c, t, 0), self.at(1 - c, t, 0), tp=yonder)
        self.to_core(False, True, 0)
        mail.arrive(self.y[0], self.at(c, yonder, 1), tp=yonder)
        mail.start(self.x[2], self.at(c, yonder, 1), self.at(c, yonder, 1), cp=1 - c)
        self.to_core(True, False, 1)

    def end(self):
        c, t, mail, yonder = self.c, self.t, self.mail, self.yonder
        mail.arrive(self.x[1], self.at(1 - c, t, 1), cp=1 - c)
        self.to_core(False, True, 1)
        mail.arrive(self.y[1], self.at(c, yonder, 0), tp=yonder)
        self.to_core(True, False, 0)
        mail.arrive(self.x[2], self.at(1 - c, yonder, 1), cp=1 - c)
        self.to_core(False, False, 1)
        mail.arrive(self.y[2], self.at(1 - c, yonder, 0), tp=yonder)
        self.to_core(False, False, 0)
        far = (self.beside + 2) % 4
        for (c_is_own, t_is_own, piece), slot in self.core.items():
            place = self.at(
                c if c_is_own else 1 - c, self.beside if t_is_own else far, piece
            )
            mail.arrive(slot, place, tp=self.beside)


def second_gather_kernel(
    count, part, tokens, gain, wide_0, wide_1, wide_2,
    first_low, first_high, second_low, second_high, *refs
):
    hops_mine, hops_other = min(2, count - 1), 1
    wide = (wide_0, wide_1, wide_2)
    wide_other = [first_low.at[1, which] for which in range(3)]
    ready_mine = [first_low.at[0], first_high.at[0], second_low.at[0], second_high.at[0]]
    ready_mine = ready_mine[: 2 * hops_mine]
    ready_other = [second_low.at[1], second_high.at[1]]
    middle, middle_home, normed_full, gate_full, up_full, down_full = refs[:6]
    own, from_core, to_yonder, from_yonder, normed, stage, send, recv, local, local_line = refs[6:]
    c, t = lax.axis_index("cp"), lax.axis_index("tp")
    rows = tokens.shape[0]
    half = rows // 2
    mail = Mail(send, recv)
    greet(count)

    mine, other = [], []
    for which, full in enumerate((gate_full, up_full, down_full)):
        for lines, side, piece, ready in (
            (mine, c, wide, ready_mine), (other, 1 - c, wide_other, ready_other),
        ):
            arrived = [
                (ready[2 * hop].at[which], ready[2 * hop + 1].at[which])
                for hop in range(len(ready) // 2)
            ]
            lines.append(
                Line(
                    mail, count, piece[which],
                    lambda j, full=full, side=side: full.at[j, side], arrived,
                )
            )
    summed = TensorSum(mail, part, own, from_core, to_yonder, from_yonder, local)
    spread = Spread(
        mail, lambda piece: normed.at[piece], lambda c, t, piece: normed_full.at[piece, t, c]
    )

    summed.begin()
    placing = Stage([piece for line in mine + other for piece in line.keep()], stage, local_line)
    placing.begin()

    def send_hop(lines, hop):
        for line in lines:
            if hop < count:
                line.send(hop)

    def arrive_hop(lines, hop):
        for line in lines:
            if hop < count:
                line.arrive(hop)

    send_hop(other, hops_other + 1)
    send_hop(mine, hops_mine + 1)
    summed.turn()
    placing.turn()
    for piece in range(2):
        summed.arrive(piece)

        def norm(place, piece=piece):
            row = pl.ds(place.start + piece * half, place.size)
            values = tokens[row, :].astype(F32) + BRANCH * summed.rows(row)
            middle[row, :] = values
            normed[piece, place, :] = (normalize(values) * gain[...]).astype(BF)

        in_pieces(half, norm)
        spread.begin(piece)
    keep_normed = pltpu.make_async_copy(normed, normed_full.at[:, t, c], local.at[0])
    keep_normed.start()
    home = mail.slot()
    stay, go = pl.ds(c * half, half), pl.ds((1 - c) * half, half)
    keep_home = pltpu.make_async_copy(middle.at[stay], middle_home.at[c], local.at[1])
    keep_home.start()
    spread.turn()
    mail.start(home, middle.at[go], middle_home.at[c], cp=1 - c)
    for step in range(1, count):
        hop = hops_other + step
        if hop < count:
            for line_other, line_mine in zip(other, mine):
                line_other.arrive(hop)
                if hop + 1 < count:
                    line_other.send(hop + 1)
                if hops_mine + step < count:
                    line_mine.arrive(hops_mine + step)
                    if hops_mine + step + 1 < count:
                        line_mine.send(hops_mine + step + 1)
        if step == 1:
            spread.end()
    if count == 1:
        spread.end()
    mail.arrive(home, middle_home.at[1 - c], cp=1 - c)
    keep_home.wait()
    keep_normed.wait()
    placing.end()
    mail.finish()


def second_gather(count, part, tokens, gain, wide, first_low, first_high, second_low, second_high):
    slots = 12 * count + 24
    rows, width = tokens.shape
    anywhere = pl.BlockSpec(memory_space=pl.ANY)
    vmem = pl.BlockSpec(memory_space=pltpu.VMEM)
    full = jax.ShapeDtypeStruct((count, 2) + wide[0].shape, BF)
    return pl.pallas_call(
        functools.partial(second_gather_kernel, count),
        out_shape=(
            jax.ShapeDtypeStruct((rows, width), F32),
            jax.ShapeDtypeStruct((2, rows // 2, width), F32),
            jax.ShapeDtypeStruct((2, 4, 2, rows // 2, width), BF),
            full,
            full,
            full,
        ),
        in_specs=[anywhere, vmem, vmem] + [anywhere] * 7,
        out_specs=(vmem,) + (anywhere,) * 5,
        scratch_shapes=[
            pltpu.VMEM((2, rows, width), BF),
            pltpu.VMEM((2, rows, width), BF),
            pltpu.VMEM((rows, width), BF),
            pltpu.VMEM((rows, width), BF),
            pltpu.VMEM((2, rows // 2, width), BF),
            pltpu.VMEM((24,) + wide[0].shape, BF),
            pltpu.SemaphoreType.DMA((slots,)),
            pltpu.SemaphoreType.DMA((slots,)),
            pltpu.SemaphoreType.DMA((2,)),
            pltpu.SemaphoreType.DMA((2, 24)),
        ],
        cost_estimate=COST,
        compiler_params=pltpu.CompilerParams(
            collective_id=2, has_side_effects=True, vmem_limit_bytes=60 << 20
        ),
    )(part, tokens, gain, *wide, first_low, first_high, second_low, second_high)


class TensorSum:
    def __init__(self, mail, part, own, from_core, to_yonder, from_yonder, local):
        self.mail, self.part, self.own, self.from_core = mail, part, own, from_core
        self.to_yonder, self.from_yonder, self.local = to_yonder, from_yonder, local
        self.t = t = lax.axis_index("tp")
        self.beside, self.yonder = t + 1 - 2 * (t % 2), (t + 2) % 4
        self.core = [mail.slot() for _ in range(2)]
        self.across = [mail.slot() for _ in range(2)]
        self.half = from_yonder.shape[0] // 2

    def begin(self):
        part, far = self.part, (self.beside + 2) % 4
        self.mail.start(self.core[1], part.at[far], self.from_core.at[1], tp=self.beside)
        self.mail.start(self.core[0], part.at[self.beside], self.from_core.at[0], tp=self.beside)
        self.kept = [
            pltpu.make_async_copy(part.at[self.yonder], self.own.at[1], self.local.at[0]),
            pltpu.make_async_copy(part.at[self.t], self.own.at[0], self.local.at[1]),
        ]
        for copy in self.kept:
            copy.start()

    def turn(self):
        own, from_core = self.own, self.from_core
        self.kept[0].wait()
        self.mail.arrive(self.core[1], from_core.at[1], tp=self.beside)
        for piece in range(2):

            def add(place, piece=piece):
                place = pl.ds(place.start + piece * self.half, place.size)
                self.to_yonder[place, :] = (
                    own[1, place, :].astype(F32) + from_core[1, place, :].astype(F32)
                ).astype(BF)

            in_pieces(self.half, add)
            block = pl.ds(piece * self.half, self.half)
            self.mail.start(
                self.across[piece], self.to_yonder.at[block], self.from_yonder.at[block],
                tp=self.yonder,
            )
        self.kept[1].wait()
        self.mail.arrive(self.core[0], from_core.at[0], tp=self.beside)

    def arrive(self, piece):
        block = pl.ds(piece * self.half, self.half)
        self.mail.arrive(self.across[piece], self.from_yonder.at[block], tp=self.yonder)

    def rows(self, row):
        return (
            self.own[0, row, :].astype(F32)
            + self.from_core[0, row, :].astype(F32)
            + self.from_yonder[row, :].astype(F32)
        )


class Drain:
    def __init__(self, mail, count, fill, total, landed):
        self.mail, self.count, self.fill, self.total, self.landed = mail, count, fill, total, landed
        self.z = lax.axis_index("fsdp")
        self.slots = [[mail.slot() for _ in range(count)] for _ in range(2)]

    def sends(self, hop, up):
        z, count = self.z, self.count
        return (z <= hop - 1) & (z < count - 1) if up else (z >= count - hop) & (z > 0)

    def gets(self, hop, up):
        z, count = self.z, self.count
        return (z >= 1) & (z <= hop) if up else (z <= count - 2) & (z >= count - 1 - hop)

    def block(self, hop, up):
        z, count = self.z, self.count
        return jnp.minimum(z + count - hop, count - 1) if up else jnp.maximum(z - count + hop, 0)

    def arrive(self, hop):
        for side, up in enumerate((True, False)):
            self.mail.arrive(
                self.slots[side][hop], self.landed(side, hop), when=self.gets(hop, up), fsdp=self.z
            )

    def gather(self, hop):
        for side, up in enumerate((True, False)):
            target = self.total(side, hop)

            def work(side=side, up=up, target=target):
                self.fill(hop, up, self.block(hop, up), target)
                if hop > 1:

                    def add():
                        landed = self.landed(side, hop - 1)

                        def one(place):
                            target[place, :] = (
                                target[place, :].astype(F32) + landed[place, :].astype(F32)
                            ).astype(BF)

                        in_pieces(target.shape[0], one)

                    pl.when(self.gets(hop - 1, up))(add)

            pl.when(self.sends(hop, up))(work)

    def send(self, hop):
        z, count = self.z, self.count
        for side, up in enumerate((True, False)):
            to = jnp.minimum(z + 1, count - 1) if up else jnp.maximum(z - 1, 0)
            self.mail.start(
                self.slots[side][hop], self.total(side, hop), self.landed(side, hop),
                when=self.sends(hop, up), fsdp=to,
            )


def norm_back(values, gain, upstream):
    scale = lax.rsqrt(jnp.mean(values * values, axis=-1, keepdims=True) + EPSILON)
    norm = values * scale
    scaled = upstream * gain
    mean = jnp.mean(scaled * norm, axis=-1, keepdims=True)
    return scale * (scaled - norm * mean), upstream * norm


def first_sum_kernel(
    count, part, gate_grad, up_grad, hidden, middle_from, cotangent_from, down_from, gain,
    grad_middle, attention_full, gain_rows, leaving_up, leaving_down, feedforward,
    own, from_core, first, second, grad_attention, totals, landed, hidden_rows, product, middle, cotangent, down,
    send, recv, local, hidden_local, loads_local,
):
    z, c, t = lax.axis_index("fsdp"), lax.axis_index("cp"), lax.axis_index("tp")
    beside, yonder = t + 1 - 2 * (t % 2), (t + 2) % 4
    far = (beside + 2) % 4
    half = middle.shape[0] // 2
    width = middle.shape[1]
    loads = [
        pltpu.make_async_copy(source, target, loads_local.at[k])
        for k, (source, target) in enumerate(
            (
                (down_from, down),
                (middle_from, middle),
                (cotangent_from.at[:, t, c], cotangent),
            )
        )
    ]
    mail = Mail(send, recv)
    greet(count)
    last = count - 1

    def fill_from(which):
        def fill(hop, up, j, target):
            copy = pltpu.make_async_copy((gate_grad, up_grad)[which].at[j], target, local.at[4])
            copy.start()
            copy.wait()

        return fill

    drains = [
        Drain(
            mail, count, fill_from(which),
            lambda side, hop, which=which: (
                (leaving_up, leaving_down)[side].at[which] if hop == last else totals.at[side, hop - 1, which]
            ),
            lambda side, hop, which=which: landed.at[side, hop - 1, which],
        )
        for which in range(2)
    ]

    core = {}
    mine = {}
    order = ((0, 0), (0, 1), (1, 0), (1, 1))
    for index, (c_own, t_own) in enumerate(order):
        block_c = c if c_own else 1 - c
        core[c_own, t_own] = mail.slot()
        mail.start(
            core[c_own, t_own], part.at[:, beside if t_own else far, block_c],
            from_core.at[c_own, t_own], tp=beside,
        )
        mine[c_own, t_own] = pltpu.make_async_copy(
            part.at[:, t if t_own else yonder, block_c], own.at[c_own, t_own], local.at[index]
        )
        mine[c_own, t_own].start()
    if last > 1:
        for drain in drains:
            drain.gather(1)
            drain.send(1)

    block_rows = product.shape[1]
    blocks = hidden.shape[0] // block_rows

    def hidden_copy(block):
        return pltpu.make_async_copy(
            hidden.at[pl.ds(block * block_rows, block_rows)], hidden_rows.at[block % 2],
            hidden_local.at[0, block % 2],
        )

    def product_copy(block):
        return pltpu.make_async_copy(
            product.at[block % 2], feedforward.at[pl.ds(block * block_rows, block_rows)],
            hidden_local.at[1, block % 2],
        )

    def product_block(block):
        hidden_copy(block).wait()
        if block + 1 < blocks:
            hidden_copy(block + 1).start()
        if block > 1:
            product_copy(block - 2).wait()

        def one(k, carry):
            columns = pl.ds(pl.multiple_of(k * 2 * TILE, 2 * TILE), 2 * TILE)
            value = lax.dot_general(
                hidden_rows[block % 2], down[columns, :], (((1,), (1,)), ((), ())),
                preferred_element_type=F32,
            )
            product[block % 2, :, columns] = value.astype(BF)
            return carry

        lax.fori_loop(0, width // (2 * TILE), one, 0)
        product_copy(block).start()

    hidden_copy(0).start()
    for copy in loads:
        copy.start()
    loads[0].wait()
    product_block(0)

    quarter = half // 2
    quarters = [(piece, pl.ds(side * quarter, quarter)) for piece in range(2) for side in range(2)]
    x_first = [[mail.slot() for _ in range(2)] for _ in quarters]
    y_second = [mail.slot() for _ in quarters]
    ring_y = [mail.slot() for _ in quarters]
    ring_core = [mail.slot() for _ in quarters]
    ring_far = [mail.slot() for _ in quarters]

    def core_add(c_own, t_own, piece, rows):
        def one(place):
            row = pl.ds(rows.start + place.start, place.size)
            own[c_own, t_own, piece, row, :] = (
                own[c_own, t_own, piece, row, :].astype(F32)
                + from_core[c_own, t_own, piece, row, :].astype(F32)
            ).astype(BF)

        in_pieces(quarter, one)

    for t_own in (0, 1):
        mine[0, t_own].wait()
        mail.arrive(core[0, t_own], from_core.at[0, t_own], tp=beside)
    for k, (piece, rows) in enumerate(quarters):
        for t_own in (0, 1):
            core_add(0, t_own, piece, rows)
            mail.start(
                x_first[k][t_own], own.at[0, t_own, piece, rows], first.at[k, t_own], cp=1 - c
            )
    for t_own in (0, 1):
        mine[1, t_own].wait()
        mail.arrive(core[1, t_own], from_core.at[1, t_own], tp=beside)

    def add_first(k, t_own):
        piece, rows = quarters[k]

        def one(place):
            row = pl.ds(rows.start + place.start, place.size)
            own[1, t_own, piece, row, :] = (
                own[1, t_own, piece, row, :].astype(F32)
                + from_core[1, t_own, piece, row, :].astype(F32)
                + first[k, t_own, place, :].astype(F32)
            ).astype(BF)

        in_pieces(quarter, one)

    gain_rows[...] = jnp.zeros_like(gain_rows)
    loads[1].wait()
    loads[2].wait()

    def finish(k):
        piece, rows = quarters[k]
        mail.arrive(y_second[k], second.at[k], tp=yonder)

        def back(place):
            local_row = pl.ds(rows.start + place.start, place.size)
            row = pl.ds(piece * half + rows.start + place.start, place.size)
            summed = own[1, 1, piece, local_row, :].astype(F32) + second[k, place, :].astype(F32)
            grad, products = norm_back(middle[row, :], gain[...], summed)
            grad = cotangent[piece, local_row, :].astype(F32) + grad
            grad_middle[row, :] = grad
            grad_attention[piece, local_row, :] = (BRANCH * grad).astype(BF)
            gain_rows[...] += jnp.sum(products, axis=0, keepdims=True)

        in_pieces(quarter, back)
        source = grad_attention.at[piece, rows]
        mail.start(ring_y[k], source, attention_full.at[t, piece, rows], tp=yonder)
        mail.start(ring_core[k], source, attention_full.at[t, piece, rows], tp=beside)

    def z_hop(hop):
        for drain in drains:
            drain.arrive(hop - 1)
            drain.gather(hop)
            drain.send(hop)

    for k, (piece, rows) in enumerate(quarters):
        mail.arrive(x_first[k][0], first.at[k, 0], cp=1 - c)
        add_first(k, 0)
        mail.start(y_second[k], own.at[1, 0, piece, rows], second.at[k], tp=yonder)
        mail.arrive(x_first[k][1], first.at[k, 1], cp=1 - c)
        add_first(k, 1)
        if k > 0:
            finish(k - 1)
        if k == 2 and last > 2:
            z_hop(2)
        product_block(k + 1)
    finish(len(quarters) - 1)
    for block in range(len(quarters) + 1, blocks):
        product_block(block)
    keep = pltpu.make_async_copy(grad_attention, attention_full.at[t], local.at[0])
    keep.start()
    for hop in range(3, last):
        z_hop(hop)
    for k, (piece, rows) in enumerate(quarters):
        arrived = attention_full.at[yonder, piece, rows]
        mail.arrive(ring_y[k], arrived, tp=yonder)
        mail.start(ring_far[k], arrived, arrived, tp=beside)
    for k, (piece, rows) in enumerate(quarters):
        mail.arrive(ring_core[k], attention_full.at[beside, piece, rows], tp=beside)
        mail.arrive(ring_far[k], attention_full.at[far, piece, rows], tp=beside)
    for drain in drains:
        if last > 1:
            drain.arrive(last - 1)
        if last > 0:
            drain.gather(last)
    keep.wait()
    for block in range(blocks - 2, blocks):
        product_copy(block).wait()
    mail.finish()


def first_sum(count, part, gate_grad, up_grad, hidden, middle, cotangent, gain, down):
    slots = 6 * count + 32
    rows, width = middle.shape
    block = gate_grad.shape[1:]
    anywhere = pl.BlockSpec(memory_space=pl.ANY)
    vmem = pl.BlockSpec(memory_space=pltpu.VMEM)
    hops = max(count - 2, 1)
    return pl.pallas_call(
        functools.partial(first_sum_kernel, count),
        out_shape=(
            jax.ShapeDtypeStruct((rows, width), F32),
            jax.ShapeDtypeStruct((4, 2, rows // 2, width), BF),
            jax.ShapeDtypeStruct((1, width), F32),
            jax.ShapeDtypeStruct((2,) + block, BF),
            jax.ShapeDtypeStruct((2,) + block, BF),
            jax.ShapeDtypeStruct((hidden.shape[0], width), BF),
        ),
        in_specs=[anywhere] * 7 + [vmem],
        out_specs=(vmem, anywhere, vmem, vmem, vmem, anywhere),
        scratch_shapes=[
            pltpu.VMEM((2, 2, 2, rows // 2, width), BF),
            pltpu.VMEM((2, 2, 2, rows // 2, width), BF),
            pltpu.VMEM((4, 2, rows // 4, width), BF),
            pltpu.VMEM((4, rows // 4, width), BF),
            pltpu.VMEM((2, rows // 2, width), BF),
            pltpu.VMEM((2, hops, 2) + block, BF),
            pltpu.VMEM((2, hops, 2) + block, BF),
            pltpu.VMEM((2, hidden.shape[0] // 8, hidden.shape[1]), BF),
            pltpu.VMEM((2, hidden.shape[0] // 8, width), BF),
            pltpu.VMEM((rows, width), F32),
            pltpu.VMEM((2, rows // 2, width), BF),
            pltpu.VMEM(down.shape, BF),
            pltpu.SemaphoreType.DMA((slots,)),
            pltpu.SemaphoreType.DMA((slots,)),
            pltpu.SemaphoreType.DMA((5,)),
            pltpu.SemaphoreType.DMA((2, 2)),
            pltpu.SemaphoreType.DMA((3,)),
        ],
        cost_estimate=COST,
        compiler_params=pltpu.CompilerParams(
            collective_id=3, has_side_effects=True, vmem_limit_bytes=60 << 20
        ),
    )(part, gate_grad, up_grad, hidden, middle, cotangent, down, gain)


AHEAD = 6


def last_sum_kernel(
    count, projected_from, qkv_full, qkv_grad, out_grad, tokens_from, middle_from, gain, gain_rows,
    qkv_total, out_total, grad_tokens, gain_sums,
    own, from_core, to_yonder, from_yonder, pieces,
    from_x, heads_sum, heads_landed, outs_sum, outs_landed, final_out, gains, gain_line,
    part, weights, give_sum, give_landed, give_own, give_total, grad_projected, tokens, grad_middle,
    send, recv, local, weights_local, loads_local,
):
    z, c, t = lax.axis_index("fsdp"), lax.axis_index("cp"), lax.axis_index("tp")
    beside, yonder = t + 1 - 2 * (t % 2), (t + 2) % 4
    half = tokens.shape[0] // 2
    last = count - 1
    mail = Mail(send, recv)
    greet(count)

    summed = TensorSum(mail, part, own, from_core, to_yonder, from_yonder, local)

    columns = qkv_total.shape[1]
    behind = columns * 5 // 6 // TILE * TILE
    split = -(-behind // (2 * TILE)) * TILE
    parts = [pl.ds(0, split), pl.ds(split, behind - split)]
    late = pl.ds(behind, columns - behind)
    cross = [[[mail.slot() for _ in range(count)] for _ in range(2)] for _ in parts]
    cross_own = [mail.slot() for _ in parts]

    def head_drain(lanes):
        def fill(hop, up, j, target):
            side = 0 if up else 1
            copy = pltpu.make_async_copy(qkv_grad.at[j, c, :, lanes], target, local.at[2])
            copy.start()
            copy.wait()
            arrived = from_x.at[side, hop - 1, :, lanes]

            def one(place):
                target[place, :] = (
                    target[place, :].astype(F32) + arrived[place, :].astype(F32)
                ).astype(BF)

            in_pieces(target.shape[0], one)

        return Drain(
            mail, count, fill,
            lambda side, hop: heads_sum.at[side, hop - 1, :, lanes],
            lambda side, hop: heads_landed.at[side, hop - 1, :, lanes],
        )

    heads = [head_drain(lanes) for lanes in parts]

    def late_fill(side_c):
        def fill(hop, up, j, target):
            copy = pltpu.make_async_copy(qkv_grad.at[j, side_c, :, late], target, local.at[2])
            copy.start()
            copy.wait()

        return fill

    stay = Drain(
        mail, count, late_fill(c),
        lambda side, hop: heads_sum.at[side, hop - 1, :, late],
        lambda side, hop: heads_landed.at[side, hop - 1, :, late],
    )
    give = Drain(
        mail, count, late_fill(1 - c),
        lambda side, hop: give_sum.at[side, hop - 1],
        lambda side, hop: give_landed.at[side, hop - 1],
    )
    give_slot = mail.slot()

    def fill_outs(hop, up, j, target):
        copy = pltpu.make_async_copy(out_grad.at[j], target, local.at[3])
        copy.start()
        copy.wait()

    outs = Drain(
        mail, count, fill_outs,
        lambda side, hop: outs_sum.at[side, hop - 1],
        lambda side, hop: outs_landed.at[side, hop - 1],
    )

    steps = [(hop, k) for hop in range(1, count + 1) for k in range(2)]

    def cross_send(step):
        if step >= len(steps):
            return
        hop, k = steps[step]
        lanes = parts[k]
        if hop == count:
            mail.start(
                cross_own[k], qkv_grad.at[z, 1 - c, :, lanes], from_x.at[0, last, :, lanes], cp=1 - c
            )
            return
        for side, up in enumerate((True, False)):
            mail.start(
                cross[k][side][hop], qkv_grad.at[heads[k].block(hop, up), 1 - c, :, lanes],
                from_x.at[side, hop - 1, :, lanes], when=heads[k].sends(hop, up), cp=1 - c,
            )

    def cross_arrive(hop, k):
        for side, up in enumerate((True, False)):
            mail.arrive(
                cross[k][side][hop], from_x.at[side, hop - 1, :, parts[k]],
                when=heads[k].sends(hop, up), cp=1 - c,
            )

    for step in range(AHEAD):
        cross_send(step)
    early_chains = (outs, give, stay)
    if count > 1:
        for drain in early_chains:
            drain.gather(1)
            drain.send(1)

    wide_block = weights.shape[1]
    blocks = qkv_full.shape[0] // wide_block

    def weights_copy(block, slot):
        return pltpu.make_async_copy(
            qkv_full.at[pl.ds(block * wide_block, wide_block)], weights.at[slot],
            weights_local.at[slot],
        )

    def product(block, carry):
        slot = lax.rem(block, 2)
        weights_copy(block, slot).wait()
        pl.when(block + 1 < blocks)(lambda: weights_copy(block + 1, 1 - slot).start())
        columns = pl.ds(pl.multiple_of(block * wide_block, wide_block), wide_block)
        value = lax.dot_general(
            grad_projected[...], weights[slot], (((1,), (1,)), ((), ())),
            preferred_element_type=F32,
        )
        part[:, :, columns] = value.astype(BF).reshape(part.shape[:2] + (wide_block,))
        return carry

    loads = [
        pltpu.make_async_copy(source, target, loads_local.at[k])
        for k, (source, target) in enumerate(
            (
                (projected_from, grad_projected),
                (tokens_from, tokens),
                (middle_from, grad_middle),
            )
        )
    ]
    weights_copy(0, 0).start()
    for copy in loads:
        copy.start()
    loads[0].wait()
    thirds = [blocks * k // 3 for k in range(4)]

    keep = pltpu.make_async_copy(pieces.at[c], grad_tokens.at[c], local.at[0])
    home = mail.slot()
    gain_x, gain_y, gain_core = mail.slot(), mail.slot(), mail.slot()
    line = Line(mail, count, gain_line.at[z], lambda j: gain_line.at[j])

    def finish_rows():
        loads[1].wait()
        loads[2].wait()
        gains[0, 0:1, :] = jnp.zeros_like(gain_rows)
        gains[0, 1:2, :] = gain_rows[...]
        for piece in range(2):
            summed.arrive(piece)

            def back(place, piece=piece):
                row = pl.ds(place.start + piece * half, place.size)
                grad, rows = norm_back(tokens[row, :].astype(F32), gain[...], summed.rows(row))
                pieces[piece, place, :] = (grad_middle[row, :] + grad).astype(BF)
                gains[0, 0:1, :] += jnp.sum(rows, axis=0, keepdims=True)

            in_pieces(half, back)
        mail.start(home, pieces.at[1 - c], grad_tokens.at[c], cp=1 - c)
        keep.start()
        mail.start(gain_core, gains.at[0], gains.at[1], tp=beside)

    def gain_step(k):
        if k == 0:
            mail.arrive(gain_core, gains.at[1], tp=beside)
            gains[2] = gains[0] + gains[1]
            mail.start(gain_y, gains.at[2], gains.at[3], tp=yonder)
        elif k == 1:
            mail.arrive(gain_y, gains.at[3], tp=yonder)
            gains[4] = gains[2] + gains[3]
            mail.start(gain_x, gains.at[4], gains.at[5], cp=1 - c)
        elif k == 2:
            mail.arrive(gain_x, gains.at[5], cp=1 - c)
            gain_line[z] = gains[4] + gains[5]
            if count > 1:
                line.send(1)
        else:
            hop = k - 2
            line.arrive(hop)
            if hop + 1 < count:
                line.send(hop + 1)

    def outs_hop(hop):
        for drain in early_chains:
            drain.arrive(hop - 1)
            drain.gather(hop)
            drain.send(hop)

    def give_away():
        copy = pltpu.make_async_copy(qkv_grad.at[z, 1 - c, :, late], give_own, local.at[3])
        copy.start()
        copy.wait()
        if count > 1:
            give.arrive(last)

        def one(place):
            total = give_own[place, :].astype(F32)
            for side, up in enumerate((True, False)):
                if count > 1:
                    landed = give.landed(side, last)[place, :].astype(F32)
                    total += jnp.where(give.gets(last, up), landed, 0.0)
            give_total[place, :] = total.astype(BF)

        in_pieces(give_own.shape[0], one)
        mail.start(give_slot, give_total, from_x.at[0, last, :, late], cp=1 - c)

    for step, (hop, k) in enumerate(steps[:-2]):
        if step < 3:
            lax.fori_loop(thirds[step], thirds[step + 1], product, 0)
        if count == 2 and step == 1:
            lax.fori_loop(thirds[2], thirds[3], product, 0)
        if step == 2 or count == 2 and step == 1:
            summed.begin()
        cross_arrive(hop, k)
        cross_send(step + AHEAD)
        if hop > 1:
            heads[k].arrive(hop - 1)
        heads[k].gather(hop)
        heads[k].send(hop)
        if k == 1 and hop + 1 < count:
            outs_hop(hop + 1)
        if step == 2 or count == 2 and step == 1:
            summed.turn()
        if step == 3 or count == 2 and step == 1:
            finish_rows()
        if step == 5 or step == 3 and count == 3:
            gain_step(0)
            gain_step(1)
    if count == 1:
        lax.fori_loop(thirds[0], thirds[3], product, 0)
        summed.begin()
        summed.turn()
        finish_rows()
    if count <= 2:
        gain_step(0)
        gain_step(1)
    gain_step(2)
    give_away()

    own_copy = pltpu.make_async_copy(qkv_grad.at[z, c], from_x.at[1, last], local.at[2])
    own_copy.start()
    out_copy = pltpu.make_async_copy(out_grad.at[z], final_out, local.at[3])
    out_copy.start()
    for k, lanes in enumerate(parts):
        mail.arrive(cross_own[k], from_x.at[0, last, :, lanes], cp=1 - c)
    mail.arrive(give_slot, from_x.at[0, last, :, late], cp=1 - c)
    own_copy.wait()
    out_copy.wait()

    def start_heads(place):
        qkv_total[place, :] = from_x[0, last, place, :].astype(F32) + from_x[
            1, last, place, :
        ].astype(F32)

    in_pieces(qkv_total.shape[0], start_heads)

    def start_outs(place):
        out_total[place, :] = final_out[place, :].astype(F32)

    in_pieces(out_total.shape[0], start_outs)
    for hop in range(1, count):
        gain_step(2 + hop)
    if count > 1:
        chains = [(outs, pl.ds(0, out_total.shape[1]), out_total)]
        chains += [(stay, late, qkv_total)]
        chains += [(heads[k], lanes, qkv_total) for k, lanes in enumerate(parts)]
        for drain, lanes, total in chains:
            drain.arrive(last)
            for side, up in enumerate((True, False)):

                def more(drain=drain, total=total, side=side, lanes=lanes):
                    landed = drain.landed(side, last)

                    def one(place):
                        total[place, lanes] += landed[place, :].astype(F32)

                    in_pieces(total.shape[0], one)

                pl.when(drain.gets(last, up))(more)
    gain_sums[...] = jnp.sum(gain_line[...], axis=0)
    mail.arrive(home, grad_tokens.at[1 - c], cp=1 - c)
    keep.wait()
    mail.finish()


def last_sum(count, grad_projected, qkv_full, qkv_grad, out_grad, tokens, grad_middle, gain, gain_rows):
    slots = 17 * count + 17
    rows, width = tokens.shape
    hops = max(count - 1, 1)
    block, out_block = qkv_grad.shape[2:], out_grad.shape[1:]
    columns = block[1]
    give_block = (block[0], columns - columns * 5 // 6 // TILE * TILE)
    anywhere = pl.BlockSpec(memory_space=pl.ANY)
    vmem = pl.BlockSpec(memory_space=pltpu.VMEM)
    return pl.pallas_call(
        functools.partial(last_sum_kernel, count),
        out_shape=(
            jax.ShapeDtypeStruct(block, F32),
            jax.ShapeDtypeStruct(out_block, F32),
            jax.ShapeDtypeStruct((2, rows // 2, width), BF),
            jax.ShapeDtypeStruct((2, width), F32),
        ),
        in_specs=[anywhere] * 6 + [vmem] * 2,
        out_specs=(vmem, vmem, anywhere, vmem),
        scratch_shapes=[
            pltpu.VMEM((2, rows, width), BF),
            pltpu.VMEM((2, rows, width), BF),
            pltpu.VMEM((rows, width), BF),
            pltpu.VMEM((rows, width), BF),
            pltpu.VMEM((2, rows // 2, width), BF),
            pltpu.VMEM((2, count) + block, BF),
            pltpu.VMEM((2, hops) + block, BF),
            pltpu.VMEM((2, hops) + block, BF),
            pltpu.VMEM((2, hops) + out_block, BF),
            pltpu.VMEM((2, hops) + out_block, BF),
            pltpu.VMEM(out_block, BF),
            pltpu.VMEM((6, 2, width), F32),
            pltpu.VMEM((count, 2, width), F32),
            pltpu.VMEM((4, rows, width), BF),
            pltpu.VMEM((2, 2 * TILE, qkv_full.shape[1]), BF),
            pltpu.VMEM((2, hops) + give_block, BF),
            pltpu.VMEM((2, hops) + give_block, BF),
            pltpu.VMEM(give_block, BF),
            pltpu.VMEM(give_block, BF),
            pltpu.VMEM(grad_projected.shape, BF),
            pltpu.VMEM(tokens.shape, BF),
            pltpu.VMEM(grad_middle.shape, F32),
            pltpu.SemaphoreType.DMA((slots,)),
            pltpu.SemaphoreType.DMA((slots,)),
            pltpu.SemaphoreType.DMA((4,)),
            pltpu.SemaphoreType.DMA((2,)),
            pltpu.SemaphoreType.DMA((3,)),
        ],
        cost_estimate=COST,
        compiler_params=pltpu.CompilerParams(
            collective_id=4, has_side_effects=True, vmem_limit_bytes=60 << 20
        ),
    )(grad_projected, qkv_full, qkv_grad, out_grad, tokens, grad_middle, gain, gain_rows)


def normalize(values):
    return values * lax.rsqrt(jnp.mean(values * values, axis=-1, keepdims=True) + EPSILON)


def silu_product(gate_pre, up_pre):
    return gate_pre / (1.0 + jnp.exp(-gate_pre)) * up_pre


def matmul(left, right):
    return jnp.dot(left, right, preferred_element_type=F32)


def rows_inner(left, right):
    return lax.dot_general(left, right, (((0,), (0,)), ((), ())), preferred_element_type=F32)


def cols_inner(left, right):
    return lax.dot_general(left, right, (((1,), (1,)), ((), ())), preferred_element_type=F32)


def row_major(value):
    return with_layout_constraint(value, Layout(major_to_minor=(0, 1)))


def after(value, *earlier):
    return lax.optimization_barrier((value, *earlier))[0]


def swap(value):
    return lax.ppermute(value, "cp", [(0, 1), (1, 0)])


def in_order(place, mine, other, axis):
    return jnp.where(
        place == 0,
        jnp.concatenate([mine, other], axis=axis),
        jnp.concatenate([other, mine], axis=axis),
    )


def on_device(
    tokens,
    seq_lengths,
    attention_gain,
    query_weight,
    key_weight,
    value_weight,
    out_weight,
    feedforward_gain,
    gate_weight,
    up_weight,
    down_weight,
    cotangent,
):
    c = lax.axis_index("cp")
    z = lax.axis_index("fsdp")
    sets = lax.axis_size("cp")
    count = lax.axis_size("fsdp")
    lanes = lax.axis_size("tp")
    slots, local, width = tokens.shape
    share = query_weight.shape[0]
    heads_width = query_weight.shape[1]
    head_count = heads_width // HD
    hidden_width = gate_weight.shape[1] // sets
    rows = sets * local
    seq = rows * lanes
    blocks = row_blocks(seq, sets, local)
    everyone = ("cp", "tp")

    def pick(value, which, axis=0):
        return lax.dynamic_index_in_dim(value, which, axis, keepdims=False)

    length = pick(seq_lengths, c)[None]
    gain_one = attention_gain.astype(F32)
    gain_two = feedforward_gain.astype(F32)

    qkv = jnp.concatenate([query_weight, key_weight, value_weight], axis=1)

    def halves(weight):
        return weight[:, :hidden_width], weight[:, hidden_width:]

    parts = [halves(weight) for weight in (gate_weight, up_weight, down_weight.T)]
    own_wide = [jnp.where(c == 0, low, high) for low, high in parts]
    wide_away = [jnp.where(c == 0, high, low) for low, high in parts]
    token_rows, normed_one, full_qkv, out_half, first_low, first_high = first_gather(
        count, tokens, gain_one[None], qkv, out_weight.T,
        own_wide, wide_away,
    )
    token_rows = token_rows.reshape(rows, width)
    normed_one = normed_one.reshape(seq, width)
    full_qkv = full_qkv.reshape(width, 3 * heads_width)

    out_half, cotangent = after((out_half, cotangent), full_qkv)
    cotangents = lax.all_gather(cotangent, everyone, axis=0).reshape(
        sets, lanes, slots, local, width
    )
    full_out = in_order(c, out_half[:, None], swap(out_half)[:, None], 1)
    full_out = full_out.reshape(width, heads_width)
    up_hop = [(i, i + 1) for i in range(count - 1)]
    down_hop = [(i, i - 1) for i in range(1, count)]
    second_low = lax.ppermute(first_low, "fsdp", up_hop)
    second_high = lax.ppermute(first_high, "fsdp", down_hop)
    cosine_table, sine_table = tables(seq)
    projected = matmul(normed_one, full_qkv)
    context, q_heads, k_heads, v_heads, level = attention(
        blocks, head_count, length, projected, cosine_table, sine_table
    )
    part = cols_inner(context, full_out).astype(BF)

    middle, middle_home, normed_two, full_gate, full_up, full_down = second_gather(
        count, part.reshape(lanes, rows, width), token_rows, gain_two[None], own_wide,
        first_low, first_high, second_low, second_high,
    )
    normed_two = normed_two.reshape(sets * seq, width)
    full_gate, full_up, full_down = (
        full.reshape(width, hidden_width) for full in (full_gate, full_up, full_down)
    )
    cotangents_all = cotangents.reshape(sets * seq, width)
    gate_pre = matmul(normed_two, full_gate)
    up_pre = matmul(normed_two, full_up)
    hidden_exact, silu_back = jax.vjp(silu_product, gate_pre, up_pre)
    hidden = hidden_exact.astype(BF)

    def blocks_of(gradient):
        gradient = row_major(gradient.astype(BF))
        return gradient.reshape(count, width // count, hidden_width)

    down_blocks = blocks_of(BRANCH * rows_inner(cotangents_all, hidden))
    def leaving(hop, low, high):
        leaving_up = pick(down_blocks, jnp.minimum(z + count - hop, count - 1))
        leaving_down = pick(down_blocks, jnp.maximum(z - count + hop, 0))
        if hop > 1:
            leaving_up = (leaving_up.astype(F32) + low.astype(F32)).astype(BF)
            leaving_down = (leaving_down.astype(F32) + high.astype(F32)).astype(BF)
        return leaving_up, leaving_down

    def sent(hop, leaving_up, leaving_down):
        return (
            lax.ppermute(leaving_up, "fsdp", up_hop[:hop]),
            lax.ppermute(leaving_down, "fsdp", down_hop[count - 1 - hop :]),
        )

    gone = leaving(1, None, None)
    for hop in range(2, count - 1):
        gone = leaving(hop, *sent(hop - 1, *gone))
    grad_hidden = BRANCH * matmul(cotangents_all, full_down)
    grad_gate_exact, grad_up_exact = silu_back(grad_hidden)
    grad_gate_pre = grad_gate_exact.astype(BF)
    grad_up_pre = grad_up_exact.astype(BF)
    gate_part = lax.optimization_barrier(cols_inner(grad_gate_pre, full_gate).astype(BF))
    grad_normed_two = gate_part.astype(F32) + cols_inner(grad_up_pre, full_up)
    gate_blocks = blocks_of(rows_inner(normed_two, grad_gate_pre))
    up_blocks = blocks_of(rows_inner(normed_two, grad_up_pre))
    part = grad_normed_two.astype(BF).reshape(sets, lanes, slots, local, width)
    part, gone = lax.optimization_barrier((part, gone))
    grad_middle, grad_attention, gain_two_rows, pair_up, pair_down, feedforward = first_sum(
        count, part, gate_blocks, up_blocks, hidden, middle, cotangents, gain_two[None],
        full_down,
    )
    grad_attention = grad_attention.reshape(seq, width)

    if count > 1:
        if count > 2:
            arrived = after(sent(count - 2, *gone), grad_attention)
            gone = leaving(count - 1, *arrived)
        leaving_up, leaving_down = after(gone, grad_attention)
        low = [lax.ppermute(pair_up, "fsdp", up_hop), lax.ppermute(leaving_up, "fsdp", up_hop)]
        high = [
            lax.ppermute(pair_down, "fsdp", down_hop), lax.ppermute(leaving_down, "fsdp", down_hop),
        ]
        low = [low[0][0], low[0][1], low[1]]
        high = [high[0][0], high[0][1], high[1]]

    def own_share(which, gradient):
        total = pick(gradient, z).astype(F32)
        if count > 1:
            total = total + low[which].astype(F32) + high[which].astype(F32)
        return total.reshape(sets, share, hidden_width)

    def halved(total):
        return pick(total, c), pick(total, 1 - c).astype(BF)

    gate_kept, gate_given = halved(own_share(0, gate_blocks))
    up_kept, up_given = halved(own_share(1, up_blocks))
    pair_given = jnp.stack([gate_given, up_given])
    pair_got = swap(pair_given).astype(F32)
    grad_gate = in_order(c, gate_kept, pair_got[0], 1)
    grad_up = in_order(c, up_kept, pair_got[1], 1)

    out_pieces = row_major(rows_inner(grad_attention, context).astype(BF))
    out_pieces = out_pieces.reshape(count, sets, share, heads_width)
    out_other = swap(pick(out_pieces, 1 - c, 1))
    out_pieces = (pick(out_pieces, c, 1).astype(F32) + out_other.astype(F32)).astype(BF)
    grad_context = row_major(matmul(grad_attention, full_out).astype(BF))
    feedforward = lax.psum_scatter(feedforward, everyone, scatter_dimension=0, tiled=True)
    feedforward = feedforward.reshape(slots, local, width)
    output = (middle_home + BRANCH * feedforward.astype(F32)).astype(BF)
    grad_projected = attention_back(
        blocks, head_count, length, grad_context, q_heads, k_heads, v_heads, level,
        cosine_table, sine_table,
    )
    grad_projected = after(grad_projected, out_other, pair_given)
    grad_qkv = row_major(rows_inner(normed_one, grad_projected).astype(BF))
    if count > 1:
        low[2], high[2] = after((low[2], high[2]), grad_qkv)
    down_kept, down_given = halved(own_share(2, down_blocks))
    grad_qkv, down_given = lax.optimization_barrier((grad_qkv, down_given))
    grad_down = in_order(c, down_kept, swap(down_given).astype(F32), 1).T
    grad_qkv, grad_out, grad_tokens, gain_sums = last_sum(
        count, grad_projected, full_qkv, grad_qkv.reshape(count, sets, share, 3 * heads_width), out_pieces,
        token_rows, grad_middle, gain_one[None], gain_two_rows,
    )
    return (
        output,
        grad_tokens,
        grad_qkv[:, :heads_width],
        grad_qkv[:, heads_width : 2 * heads_width],
        grad_qkv[:, 2 * heads_width :],
        grad_out.T,
        gain_sums[0],
        grad_gate,
        grad_up,
        grad_down,
        gain_sums[1],
    )


def solution(mesh):
    in_specs = (
        P("fsdp", ("cp", "tp"), None),
        P("fsdp"),
        P(),
        P(("fsdp", "cp"), "tp"),
        P(("fsdp", "cp"), "tp"),
        P(("fsdp", "cp"), "tp"),
        P("tp", ("fsdp", "cp")),
        P(),
        P(("fsdp", "cp"), "tp"),
        P(("fsdp", "cp"), "tp"),
        P("tp", ("fsdp", "cp")),
        P("fsdp", ("cp", "tp"), None),
    )
    out_specs = (
        P("fsdp", ("cp", "tp"), None),
        P("fsdp", ("cp", "tp"), None),
        P(("fsdp", "cp"), "tp"),
        P(("fsdp", "cp"), "tp"),
        P(("fsdp", "cp"), "tp"),
        P("tp", ("fsdp", "cp")),
        P(),
        P(("fsdp", "cp"), "tp"),
        P(("fsdp", "cp"), "tp"),
        P("tp", ("fsdp", "cp")),
        P(),
    )
    return jax.shard_map(
        on_device, mesh=mesh, in_specs=in_specs, out_specs=out_specs, check_vma=False
    )
```
